32 devices in a mesh: fsdp: 4 (over y, x), ctx: 2 (over core), tp: 4 (over z).
Axes of the slice: x: 2, y: 2, z: 4, core: 2. Of those that a mesh axis runs over, the one named last changes fastest.
Arguments:
- tokens: bfloat16 [8192, 2048], P(('fsdp', 'ctx')), may hold values from -6 to 6
- segments: int32 [8192], P('fsdp'), may hold values from 0 to 171, as said below
- cotangent: bfloat16 [8192, 2048], P(('fsdp', 'ctx')), may hold values from -6 to 6
- w_recur: bfloat16 [2048, 2560], P('fsdp', 'tp'), may hold values from -0.125 to 0.125
- w_gelu: bfloat16 [2048, 2560], P('fsdp', 'tp'), may hold values from -0.125 to 0.125
- w_merge: bfloat16 [2560, 2048], P('tp', 'fsdp'), may hold values from -0.3125 to 0.3125
- w_gate: bfloat16 [2048, 6144], P('fsdp', 'tp'), may hold values from -0.125 to 0.125
- w_up: bfloat16 [2048, 6144], P('fsdp', 'tp'), may hold values from -0.125 to 0.125
- w_down: bfloat16 [6144, 2048], P('tp', 'fsdp'), may hold values from -0.15625 to 0.15625
- norm_mix: bfloat16 [2048], P('fsdp'), may hold values from 0.5 to 1.5
- norm_feed: bfloat16 [2048], P('fsdp'), may hold values from 0.5 to 1.5
- conv_taps: bfloat16 [4, 2560], P(None, 'tp'), may hold values from -3 to 3
- conv_bias: bfloat16 [2560], P('tp'), may hold values from -3 to 3
- rate_gate: bfloat16 [16, 160, 160], P('tp'), may hold values from -0.5 to 0.5
- entry_gate: bfloat16 [16, 160, 160], P('tp'), may hold values from -0.5 to 0.5
- rate_bias: bfloat16 [2560], P('tp'), may hold values from -2 to 4
- entry_bias: bfloat16 [2560], P('tp'), may hold values from -4 to 4
- decay_logit: float32 [2560], P('tp'), may hold values from 4.5 to 8.5
Outputs:
- output: bfloat16 [8192, 2048], P(('fsdp', 'ctx'), 'tp')
- grad_tokens: bfloat16 [8192, 2048], P(('fsdp', 'ctx'), 'tp')
- grad_recur: float32 [2048, 2560], P('fsdp', 'tp')
- grad_gelu: float32 [2048, 2560], P('fsdp', 'tp')
- grad_merge: float32 [2560, 2048], P('tp', 'fsdp')
- grad_gate: float32 [2048, 6144], P('fsdp', 'tp')
- grad_up: float32 [2048, 6144], P('fsdp', 'tp')
- grad_down: float32 [6144, 2048], P('tp', 'fsdp')
- grad_mix: float32 [2048], P('fsdp')
- grad_feed: float32 [2048], P('fsdp')
- grad_taps: float32 [4, 2560], P(None, 'tp')
- grad_conv_bias: float32 [2560], P('tp')
- grad_rate_gate: float32 [16, 160, 160], P('tp')
- grad_entry_gate: float32 [16, 160, 160], P('tp')
- grad_rate_bias: float32 [2560], P('tp')
- grad_entry_bias: float32 [2560], P('tp')
- grad_decay: float32 [2560], P('tp')
The draws below stay inside these ranges and needn't reach their ends.
Inputs may be any that keep to these rules, and one draw needn't show every extreme that they name: `segments`: in each sequence of 2048 tokens the ids never fall and change exactly at each document's first token; the first document has id 0 and the last document has id 2048 // 12 + 1; no document begins within 24 tokens of a border between two pieces of 1024 tokens.
All inputs are finite; a program needn't handle non-finite values.
Results may differ from the reference program's by a relative error of at most 0.019.
Values may be sent and summed in bfloat16 or wider, within the bound.
A program may use at most 256 MiB of HBM per device.

```python
import jax
import jax.numpy as jnp
from jax import lax

D = 2048
RW = 2560
HEADS = 16
FF = 6144
KW = 4
PIECE = 1024
DOC_MIN = 60
DOC_MAX = 800
GAP = 24
BW = 160
LENGTH = 2048
SEQS = 4
TOKENS = 8192


def draw_segments(key, part):
    number = LENGTH // DOC_MIN + 2
    top_id = LENGTH // (DOC_MIN - 2 * GAP) + 1
    keys = jax.random.split(key, SEQS)
    spots = jnp.arange(LENGTH, dtype=jnp.int32)

    def one_sequence(subkey):
        spans = jax.random.randint(subkey, (number,), DOC_MIN, DOC_MAX + 1).astype(jnp.int32)
        starts = jnp.cumsum(spans).astype(jnp.int32)
        border = (starts + PIECE // 2) // PIECE * PIECE
        inner = (border > 0) & (border < LENGTH)
        below = inner & (starts <= border) & (starts > border - GAP)
        above = inner & (starts > border) & (starts < border + GAP)
        starts = jnp.where(below, border - GAP, jnp.where(above, border + GAP, starts))
        counted = jnp.sum((starts[None, :] <= spots[:, None]).astype(jnp.int32), axis=1)
        final = counted[LENGTH - 1]
        return jnp.where(counted == final, top_id, counted).astype(jnp.int32)
    return jax.vmap(one_sequence)(keys).reshape(-1).astype(jnp.int32)


def with_spikes(values, own_key, source, target, shards_of, factor):
    owner, partner = [(jnp.arange(values.shape[position]) // (values.shape[position] // shards_of)).reshape([-1 if axis == position else 1 for axis in range(values.ndim)]) for position in (source, target)]
    chosen = jax.random.permutation(own_key, shards_of)[partner]
    strong = (owner == chosen) | (owner == (partner + shards_of // 2) % shards_of)
    return jnp.where(strong, factor * values, values)


def block_levels(key, dims, cuts, smallest, high):
    level = 1.0
    for dim, blocks in cuts:
        steps = jax.random.uniform(jax.random.fold_in(jax.random.fold_in(key, 6), dim), (blocks,), jnp.float32, smallest / len(cuts), high / len(cuts))
        level = level * jnp.repeat(jnp.exp(steps), dims[dim] // blocks).reshape((-1,) + (1,) * (len(dims) - 1 - dim))
    return level


def centred(key, shape, spread, most, cuts=(), kind=jnp.bfloat16):
    values = spread * jax.random.normal(key, shape, jnp.float32)
    if cuts:
        values = values * block_levels(key, shape, cuts, -0.22, 0.18)
    return jnp.clip(values, -most, most).astype(kind)


def bell_draw_with(own_key, dims, scale, limit, shards, heavy, kind=jnp.bfloat16):
    values = scale * jax.random.normal(own_key, dims, jnp.float32)
    if shards:
        values = values * block_levels(own_key, dims, shards, -0.22, 0.18)
    return jnp.clip(with_spikes(values, jax.random.fold_in(own_key, 3), *heavy), -limit, limit).astype(kind)


def setup_inputs(seed: int = 0) -> dict:
    key_of = jax.random.split(jax.random.key(seed), 19)
    return {
        "tokens": centred(key_of[0], (TOKENS, D), 1.0, 6.0, ((0, 8),)),
        "segments": draw_segments(jax.random.fold_in(key_of[18], 71), 0),
        "cotangent": bell_draw_with(key_of[2], (TOKENS, D), 1.0, 6.0, ((0, 8),), (0, 1, 8, 2.0)),
        "w_recur": centred(key_of[3], (D, RW), D ** -0.5, 0.125, ((0, 4), (1, 4))),
        "w_gelu": centred(key_of[4], (D, RW), D ** -0.5, 0.125, ((0, 4), (1, 4))),
        "w_merge": centred(key_of[5], (RW, D), (RW // 8) ** -0.5, 0.3125, ((0, 4), (1, 4))),
        "w_gate": centred(key_of[6], (D, FF), D ** -0.5, 0.125, ((0, 4), (1, 4))),
        "w_up": centred(key_of[7], (D, FF), D ** -0.5, 0.125, ((0, 4), (1, 4))),
        "w_down": centred(key_of[8], (FF, D), (FF // 4) ** -0.5, 0.15625, ((0, 4), (1, 4))),
        "norm_mix": jnp.clip(1.0 + 0.1 * jax.random.normal(key_of[9], (D,), jnp.float32), 0.5, 1.5).astype(jnp.bfloat16),
        "norm_feed": jnp.clip(1.0 + 0.1 * jax.random.normal(key_of[10], (D,), jnp.float32), 0.5, 1.5).astype(jnp.bfloat16),
        "conv_taps": centred(key_of[11], (KW, RW), KW ** -0.5, 3.0, ((1, 4),)),
        "conv_bias": centred(key_of[12], (RW,), 0.5, 3.0, ((0, 4),)),
        "rate_gate": centred(key_of[13], (HEADS, BW, BW), BW ** -0.5, 0.5, ((0, 4),)),
        "entry_gate": centred(key_of[14], (HEADS, BW, BW), BW ** -0.5, 0.5, ((0, 4),)),
        "rate_bias": jnp.clip(-2.0 + 6.0 * jax.random.uniform(key_of[15], (RW,), jnp.float32) ** block_levels(key_of[15], (RW,), ((0, 4),), -0.2, 0.2), -2.0, 4.0).astype(jnp.bfloat16),
        "entry_bias": centred(key_of[16], (RW,), 1.0, 4.0, ((0, 4),)),
        "decay_logit": jnp.clip(4.5 + 4.0 * jax.random.uniform(key_of[17], (RW,), jnp.float32) ** block_levels(key_of[17], (RW,), ((0, 4),), -0.2, 0.2), 4.5, 8.5),
    }


EPS = 1e-06
CGAIN = 8.0

@jax.custom_vjp
def low(v):
    return lax.optimization_barrier(v.astype(jnp.bfloat16)).astype(jnp.float32)

@jax.custom_vjp
def low_back(v):
    return v

def low_keep(v):
    return (low(v), None)

def low_pass(kept, grad):
    return (grad,)

def back_keep(v):
    return (v, None)

def back_low(kept, grad):
    return (low(grad),)
low.defvjp(low_keep, low_pass)
low_back.defvjp(back_keep, back_low)

def matmul(left, right):
    return jnp.dot(left, right, precision=lax.Precision.HIGHEST)

def combine(first, second):
    return (first[0] * second[0], second[0] * first[1] + second[1])

def block_apply(rows, blocks):
    length = rows.shape[0]
    shaped = rows.reshape(length, blocks.shape[0], blocks.shape[1])
    return jnp.einsum('thi,hij->thj', shaped, blocks, precision=lax.Precision.HIGHEST).reshape(length, -1)

def forward(inputs, seq_ids, w_recur, w_gelu, w_merge, w_gate, w_up, w_down, norm_mix, norm_feed, conv_taps, conv_bias, rate_gate, entry_gate, rate_bias, entry_bias, decay_logit):
    width = conv_taps.shape[0]
    scale_one = lax.rsqrt(lax.optimization_barrier(jnp.mean(inputs * inputs, axis=-1, keepdims=True)) + EPS)
    normed = low(inputs * scale_one * norm_mix)
    branch = low_back(low(matmul(normed, w_recur)))
    pre_gelu = low_back(matmul(normed, w_gelu))
    gelu_out = jax.nn.gelu(pre_gelu)
    before = jnp.concatenate([jnp.full((1,), -1, jnp.int32), seq_ids[:-1]])
    keep = (seq_ids == before)[:, None]
    mixed = conv_bias + conv_taps[0] * branch
    for shift in range(1, width):
        moved = jnp.concatenate([jnp.zeros((shift, branch.shape[1]), jnp.float32), branch[:-shift]], axis=0)
        moved_ids = jnp.concatenate([jnp.full((shift,), -1, jnp.int32), seq_ids[:-shift]])
        mask = (moved_ids == seq_ids).astype(jnp.float32)[:, None]
        mixed = mixed + conv_taps[shift] * moved * mask
    conv_out = low(mixed)
    rate = jax.nn.sigmoid(low_back(block_apply(conv_out, rate_gate) + rate_bias))
    entry = jax.nn.sigmoid(low_back(block_apply(conv_out, entry_gate) + entry_bias))
    log_rate = -CGAIN * rate * jax.nn.softplus(-decay_logit)
    decay_step = jnp.where(keep, jnp.exp(log_rate), 0.0)
    multiplier = jnp.where(keep, jnp.sqrt(-jnp.expm1(2.0 * log_rate)), 1.0)
    _, states = lax.associative_scan(combine, (decay_step, multiplier * entry * conv_out))
    gated = low(states * gelu_out)
    resid = inputs + low_back(matmul(gated, w_merge))
    scale_two = lax.rsqrt(lax.optimization_barrier(jnp.mean(resid * resid, axis=-1, keepdims=True)) + EPS)
    normed_two = low(resid * scale_two * norm_feed)
    gate_pre = low_back(matmul(normed_two, w_gate))
    up_vals = low_back(matmul(normed_two, w_up))
    hidden = low(jax.nn.gelu(gate_pre) * up_vals)
    return resid + matmul(hidden, w_down)

def reference(tokens, segments, cotangent, w_recur, w_gelu, w_merge, w_gate, w_up, w_down, norm_mix, norm_feed, conv_taps, conv_bias, rate_gate, entry_gate, rate_bias, entry_bias, decay_logit):
    weights = tuple((item.astype(jnp.float32) for item in (w_recur, w_gelu, w_merge, w_gate, w_up, w_down, norm_mix, norm_feed, conv_taps, conv_bias, rate_gate, entry_gate, rate_bias, entry_bias, decay_logit)))
    rows = tokens.astype(jnp.float32).reshape(SEQS, LENGTH, D)
    ids = segments.astype(jnp.int32).reshape(SEQS, LENGTH)
    upstream = cotangent.astype(jnp.float32).reshape(SEQS, LENGTH, D)

    def one_sequence(totals, item):
        inputs, seq_ids, seq_up = item

        def apply_block(values, *params):
            return forward(values, seq_ids, *params)
        result, back = jax.vjp(apply_block, inputs, *weights)
        grads = back(seq_up)
        totals = tuple((total + grad for total, grad in zip(totals, grads[1:])))
        return (totals, (result.astype(jnp.bfloat16), grads[0].astype(jnp.bfloat16)))
    initial = tuple((jnp.zeros_like(item) for item in weights))
    totals, (outputs, grad_rows) = lax.scan(one_sequence, initial, (rows, ids, upstream))
    return (outputs.reshape(TOKENS, D), grad_rows.reshape(TOKENS, D), totals[0], totals[1], totals[2], totals[3], totals[4], totals[5], totals[6], totals[7], totals[8], totals[9], totals[10], totals[11], totals[12], totals[13], totals[14])
```

```python
import jax
import jax.numpy as jnp
from jax import lax
from jax.experimental import pallas as pl
from jax.experimental.pallas import tpu as pltpu
from jax.sharding import PartitionSpec as P

EPS = 1e-06
CGAIN = 8.0
ROOT = 0.7978845608
CUBE = 0.044715
TILE = 128
SEGS = 8
F32 = jnp.float32
BF16 = jnp.bfloat16


def swap_cores(block):
    size = lax.axis_size("ctx")
    return lax.ppermute(block, "ctx", [(i, size - 1 - i) for i in range(size)])


def shifted(block, axis, distance):
    devices = range(lax.axis_size(axis))
    route = [(i - distance, i) for i in devices if i - distance in devices]
    return lax.ppermute(block, axis, route)


def gather_rows(shard):
    half = shard.shape[0] // 2
    core = lax.axis_index("ctx")
    mine = lax.dynamic_slice_in_dim(shard, core * half, half, 0)
    mine = lax.all_gather(mine, "fsdp", axis=0)
    other = swap_cores(mine)
    first = jnp.where(core == 0, mine, other)
    second = jnp.where(core == 0, other, mine)
    return jnp.stack([first, second], axis=1).reshape(-1, shard.shape[1])


def scatter_rows(grad):
    shards = lax.axis_size("fsdp")
    core = lax.axis_index("ctx")
    halves = grad.reshape(shards, 2, grad.shape[0] // shards // 2, grad.shape[1])
    mine = lax.dynamic_index_in_dim(halves, core, 1, False)
    send = lax.dynamic_index_in_dim(halves, 1 - core, 1, False).astype(BF16)
    pair = (mine + swap_cores(send).astype(F32)).astype(BF16)
    total = lax.psum_scatter(pair.reshape(-1, grad.shape[1]), "fsdp", scatter_dimension=0, tiled=True)
    other = swap_cores(total)
    first = jnp.where(core == 0, total, other)
    second = jnp.where(core == 0, other, total)
    return jnp.concatenate([first, second], axis=0).astype(F32)


def gelu_pair(q):
    tanh = jnp.tanh(ROOT * (q + CUBE * q * q * q))
    value = 0.5 * q * (1.0 + tanh)
    slope = 0.5 * (1.0 + tanh) + 0.5 * q * (1.0 - tanh * tanh) * ROOT * (1.0 + 3.0 * CUBE * q * q)
    return value, slope


def rms_scale(values):
    return lax.rsqrt(jnp.mean(values * values, axis=-1, keepdims=True) + EPS)


def decay_parts(rate, softer, keep):
    gap = 2.0 * CGAIN * rate * softer
    decay = jnp.exp(-0.5 * gap)
    series = gap * (
        1.0
        - gap / 2.0
        * (1.0 - gap / 3.0 * (1.0 - gap / 4.0 * (1.0 - gap / 5.0 * (1.0 - gap / 6.0 * (1.0 - gap / 7.0)))))
    )
    square = jnp.where(gap < 0.25, series, 1.0 - decay * decay)
    return jnp.where(keep, decay, 0.0), jnp.where(keep, square, 1.0)


LANES = 128


def put_lanes(ref, block, rows):
    for lane in range(ref.shape[0]):
        ref[lane, 0:rows, :] = block[:, lane * LANES : (lane + 1) * LANES]


def sweep(decay_ref, value_ref, state_ref, product_ref, out_ref, run_ref, carry_ref, reverse, offset):
    groups, rows, _ = value_ref.shape
    steps = rows // SEGS
    place = lax.broadcasted_iota(jnp.int32, (SEGS, LANES), 0)
    if reverse:
        place = SEGS - 1 - place

    def moved(block, by, fill):
        turned = pltpu.roll(block, SEGS - by if reverse else by, 0)
        return jnp.where(place >= by, turned, fill)

    for lane in range(groups):
        lanes = slice(lane * LANES, (lane + 1) * LANES)
        state = jnp.zeros((SEGS, LANES), F32)
        product = jnp.ones((SEGS, LANES), F32)
        for step in reversed(range(steps)) if reverse else range(steps):
            spot = pl.ds(step, SEGS, stride=steps)
            decay = decay_ref[lane, pl.ds(step + offset, SEGS, stride=steps), :]
            state = decay * state + value_ref[lane, spot, :]
            product = product * decay
            state_ref[lane, spot, :] = state
            product_ref[lane, spot, :] = product
        for by in (1, 2, 4):
            state = state + product * moved(state, by, 0.0)
            product = product * moved(product, by, 1.0)
        carry = carry_ref[0:1, lanes]
        carry_run = carry_ref[8:9, lanes]
        state = state + product * carry
        product = product * carry_run
        enter = moved(state, 1, carry)
        enter_run = moved(product, 1, carry_run)
        for seg in range(SEGS):
            span = slice(seg * steps, (seg + 1) * steps)
            inner = product_ref[lane, span, :]
            out_ref[span, lanes] = state_ref[lane, span, :] + inner * enter[seg : seg + 1, :]
            run_ref[span, lanes] = inner * enter_run[seg : seg + 1, :]
        last = 0 if reverse else SEGS - 1
        carry_ref[0:1, lanes] = state[last : last + 1, :]
        carry_ref[8:9, lanes] = product[last : last + 1, :]


def forward_kernel(
    branch_ref, halo_ref, mask_ref, taps_ref, bias_ref, gates_ref, gate_bias_ref, softer_ref,
    conv_ref, rate_ref, entry_ref, state_ref, run_ref,
    window, decay, value, inner, product, carry,
):
    rows, chans = conv_ref.shape
    spot = pl.program_id(0)

    @pl.when(spot == 0)
    def _():
        window[0:8, :] = halo_ref[...].astype(F32)
        carry[0:8, :] = jnp.zeros((8, chans), F32)
        carry[8:16, :] = jnp.ones((8, chans), F32)

    @pl.when(spot > 0)
    def _():
        window[0:8, :] = window[rows : rows + 8, :]

    window[8 : rows + 8, :] = branch_ref[...].astype(F32)
    mixed = bias_ref[...] + taps_ref[0:1, :] * window[8 : rows + 8, :]
    for shift in range(1, taps_ref.shape[0]):
        moved = window[8 - shift : 8 - shift + rows, :]
        mixed = mixed + taps_ref[shift : shift + 1, :] * (moved * mask_ref[:, shift : shift + 1])
    conv = mixed.astype(BF16)
    conv_ref[...] = conv
    pre = jnp.dot(conv, gates_ref[...], preferred_element_type=F32) + gate_bias_ref[...]
    rate = jax.nn.sigmoid(pre[:, :chans])
    entry = jax.nn.sigmoid(pre[:, chans:])
    rate_ref[...] = rate
    entry_ref[...] = entry
    keep = jnp.broadcast_to(mask_ref[:, 0:1], (rows, chans)) > 0.5
    step, square = decay_parts(rate, softer_ref[...], keep)
    put_lanes(decay, step, rows)
    put_lanes(value, jnp.sqrt(square) * entry * conv.astype(F32), rows)
    sweep(decay, value, inner, product, state_ref, run_ref, carry, False, 0)


def tile_spec(width, count=None):
    if count is None:
        return pl.BlockSpec((TILE, width), lambda i: (i, 0))
    return pl.BlockSpec((TILE, width), lambda i: (count - 1 - i, 0))


def fixed_spec(shape):
    return pl.BlockSpec(shape, lambda i: (0, 0))


def recur_forward(branch, halo, masks, taps, bias, gates, gate_bias, softer):
    rows, chans = branch.shape
    wide = jax.ShapeDtypeStruct((rows, chans), F32)
    return pl.pallas_call(
        forward_kernel,
        grid=(rows // TILE,),
        out_shape=(jax.ShapeDtypeStruct((rows, chans), BF16), wide, wide, wide, wide),
        in_specs=[
            tile_spec(chans),
            fixed_spec((8, chans)),
            tile_spec(masks.shape[1]),
            fixed_spec(taps.shape),
            fixed_spec((1, chans)),
            fixed_spec(gates.shape),
            fixed_spec((1, 2 * chans)),
            fixed_spec((1, chans)),
        ],
        out_specs=[tile_spec(chans)] * 5,
        scratch_shapes=[
            pltpu.VMEM((TILE + 8, chans), F32),
            pltpu.VMEM((chans // LANES, TILE, LANES), F32),
            pltpu.VMEM((chans // LANES, TILE, LANES), F32),
            pltpu.VMEM((chans // LANES, TILE, LANES), F32),
            pltpu.VMEM((chans // LANES, TILE, LANES), F32),
            pltpu.VMEM((16, chans), F32),
        ],
        cost_estimate=pl.CostEstimate(
            flops=2 * rows * chans * 2 * chans, bytes_accessed=24 * rows * chans, transcendentals=5 * rows * chans
        ),
        name="recur_forward",
    )(branch, halo, masks, taps, bias, gates, gate_bias, softer)


def adjoint_kernel(
    rate_ref, up_ref, mask_ref, softer_ref, grad_ref, run_ref, head_ref, decay, value, inner, product, carry
):
    rows, chans = rate_ref.shape
    groups = chans // LANES
    spot = pl.program_id(0)

    @pl.when(spot == 0)
    def _():
        for lane in range(groups):
            decay[lane, rows : rows + 8, :] = jnp.ones((8, LANES), F32)
        carry[0:8, :] = jnp.zeros((8, chans), F32)
        carry[8:16, :] = jnp.ones((8, chans), F32)

    @pl.when(spot > 0)
    def _():
        for lane in range(groups):
            decay[lane, rows : rows + 8, :] = decay[lane, 0:8, :]

    keep = jnp.broadcast_to(mask_ref[:, 0:1], (rows, chans)) > 0.5
    gap = CGAIN * rate_ref[...] * softer_ref[...]
    step = jnp.where(keep, jnp.exp(-gap), 0.0)
    put_lanes(decay, step, rows)
    put_lanes(value, up_ref[...], rows)
    sweep(decay, value, inner, product, grad_ref, run_ref, carry, True, 1)
    head_ref[...] = jnp.broadcast_to(step[0:1, :] * carry[0:1, :], (8, chans))


def recur_adjoint(rate, up, masks, softer):
    rows, chans = rate.shape
    count = rows // TILE
    wide = jax.ShapeDtypeStruct((rows, chans), F32)
    return pl.pallas_call(
        adjoint_kernel,
        grid=(count,),
        out_shape=(wide, wide, jax.ShapeDtypeStruct((8, chans), F32)),
        in_specs=[
            tile_spec(chans, count),
            tile_spec(chans, count),
            tile_spec(masks.shape[1], count),
            fixed_spec((1, chans)),
        ],
        out_specs=[tile_spec(chans, count), tile_spec(chans, count), fixed_spec((8, chans))],
        scratch_shapes=[
            pltpu.VMEM((chans // LANES, TILE + 8, LANES), F32),
            pltpu.VMEM((chans // LANES, TILE, LANES), F32),
            pltpu.VMEM((chans // LANES, TILE, LANES), F32),
            pltpu.VMEM((chans // LANES, TILE, LANES), F32),
            pltpu.VMEM((16, chans), F32),
        ],
        cost_estimate=pl.CostEstimate(
            flops=8 * rows * chans, bytes_accessed=16 * rows * chans, transcendentals=rows * chans
        ),
        name="recur_adjoint",
    )(rate, up, masks, softer)


def backward_kernel(
    grad_ref, run_ref, enter_ref, rate_ref, entry_ref, conv_ref, state_ref, mask_ref,
    branch_ref, halo_ref, taps_ref, gates_ref, softer_ref,
    back_ref, tail_ref, head_ref, gate_grad_ref, sums_ref,
    shifts, edge,
):
    rows, chans = conv_ref.shape
    width = taps_ref.shape[0]
    spot = pl.program_id(0)
    last = pl.num_programs(0) - 1

    @pl.when(spot == 0)
    def _():
        for shift in range(1, width):
            shifts[shift - 1, rows : rows + 8, :] = jnp.zeros((8, chans), F32)
        gate_grad_ref[...] = jnp.zeros_like(gate_grad_ref)
        sums_ref[...] = jnp.zeros_like(sums_ref)

    @pl.when(spot > 0)
    def _():
        for shift in range(1, width):
            shifts[shift - 1, rows : rows + 8, :] = shifts[shift - 1, 0:8, :]

    keep = jnp.broadcast_to(mask_ref[:, 0:1], (rows, chans)) > 0.5
    softer = softer_ref[...]
    rate = rate_ref[...]
    entry = entry_ref[...]
    conv = conv_ref[...].astype(F32)
    grad = grad_ref[...] + run_ref[...] * enter_ref[0:1, :]
    step, square = decay_parts(rate, softer, keep)
    inverse = lax.rsqrt(square)
    mult = square * inverse
    driven = entry * conv
    carried = state_ref[...] - mult * driven
    d_log = jnp.where(keep, grad * (carried - driven * step * step * inverse), 0.0)
    d_rate = (-CGAIN * softer * d_log * rate * (1.0 - rate)).astype(BF16)
    lifted = grad * mult * entry
    d_entry = (lifted * conv * (1.0 - entry)).astype(BF16)
    both = jnp.concatenate([d_rate, d_entry], axis=1)
    d_conv = lifted + lax.dot_general(
        both, gates_ref[...], (((1,), (1,)), ((), ())), preferred_element_type=F32
    )
    gate_grad_ref[...] += lax.dot_general(
        conv_ref[...], both, (((0,), (0,)), ((), ())), preferred_element_type=F32
    )

    def add_row(row, block):
        sums_ref[row : row + 1, :] += jnp.sum(block, axis=0, keepdims=True)

    branch = branch_ref[...].astype(F32)
    add_row(0, d_log * rate)
    add_row(1, d_rate.astype(F32))
    add_row(2, d_entry.astype(F32))
    add_row(3, d_conv)
    add_row(4, d_conv * branch)
    back = taps_ref[0:1, :] * d_conv
    for shift in range(1, width):
        shifts[shift - 1, 0:rows, :] = d_conv * mask_ref[:, shift : shift + 1]
        moved = shifts[shift - 1, shift : shift + rows, :]
        add_row(4 + shift, moved * branch)
        back = back + taps_ref[shift : shift + 1, :] * moved
    back_ref[...] = back.astype(BF16)

    @pl.when(spot == 0)
    def _():
        tail_ref[...] = back[rows - 8 :, :]

    @pl.when(spot == last)
    def _():
        halo = halo_ref[...].astype(F32)
        head = jnp.zeros((8, chans), F32)
        edge[0:8, :] = head
        for shift in range(1, width):
            edge[8:16, :] = shifts[shift - 1, 0:8, :]
            moved = edge[shift : shift + 8, :]
            add_row(4 + shift, moved * halo)
            head = head + taps_ref[shift : shift + 1, :] * moved
        head_ref[...] = head


def recur_backward(grad, run, enter, rate, entry, conv, state, masks, branch, halo, taps, gates, softer):
    rows, chans = rate.shape
    count = rows // TILE
    edge = jax.ShapeDtypeStruct((8, chans), F32)
    wide = tile_spec(chans, count)
    return pl.pallas_call(
        backward_kernel,
        grid=(count,),
        out_shape=(
            jax.ShapeDtypeStruct((rows, chans), BF16),
            edge,
            edge,
            jax.ShapeDtypeStruct((chans, 2 * chans), F32),
            jax.ShapeDtypeStruct((16, chans), F32),
        ),
        in_specs=[
            wide, wide, fixed_spec((1, chans)), wide, wide, wide, wide,
            tile_spec(masks.shape[1], count),
            wide,
            fixed_spec((8, chans)),
            fixed_spec(taps.shape),
            fixed_spec(gates.shape),
            fixed_spec((1, chans)),
        ],
        out_specs=[
            wide,
            fixed_spec((8, chans)),
            fixed_spec((8, chans)),
            fixed_spec((chans, 2 * chans)),
            fixed_spec((16, chans)),
        ],
        scratch_shapes=[
            pltpu.VMEM((taps.shape[0] - 1, TILE + 8, chans), F32),
            pltpu.VMEM((16, chans), F32),
        ],
        cost_estimate=pl.CostEstimate(
            flops=8 * rows * chans * chans, bytes_accessed=28 * rows * chans, transcendentals=2 * rows * chans
        ),
        name="recur_backward",
    )(grad, run, enter, rate, entry, conv, state, masks, branch, halo, taps, gates, softer)


def spread_blocks(blocks):
    count, size = blocks.shape[0], blocks.shape[1]
    rows = [
        jnp.pad(blocks[i], ((0, 0), (i * size, (count - 1 - i) * size))) for i in range(count)
    ]
    return jnp.concatenate(rows, axis=0)


def shards(
    tokens,
    segments,
    cotangent,
    w_recur,
    w_gelu,
    w_merge,
    w_gate,
    w_up,
    w_down,
    norm_mix,
    norm_feed,
    conv_taps,
    conv_bias,
    rate_gate,
    entry_gate,
    rate_bias,
    entry_bias,
    decay_logit,
):
    piece = tokens.shape[0]
    width = conv_taps.shape[0]
    edge = width - 1
    heads, block = rate_gate.shape[0], rate_gate.shape[1]
    chans = conv_taps.shape[1]
    features = tokens.shape[1]
    feat_local = features // lax.axis_size("tp")
    feat_start = lax.axis_index("tp") * feat_local

    whole_recur = gather_rows(w_recur)
    whole_gelu = gather_rows(w_gelu)
    gains = lax.all_gather(jnp.stack([norm_mix, norm_feed]), "fsdp", axis=1, tiled=True).astype(F32)
    gain_one, gain_two = gains[0:1], gains[1:2]
    whole_merge = gather_rows(w_merge.T)
    whole_gate = gather_rows(w_gate)
    whole_up = gather_rows(w_up)
    whole_down = gather_rows(w_down.T)

    padded_ids = jnp.concatenate([jnp.full((edge,), -1, jnp.int32), segments])
    local_ids = lax.dynamic_slice_in_dim(padded_ids, lax.axis_index("ctx") * piece, piece + edge)
    own_ids = local_ids[edge:]
    masks = jnp.stack(
        [(local_ids[edge - max(shift, 1) : edge - max(shift, 1) + piece] == own_ids) for shift in range(width)],
        axis=1,
    ).astype(F32)
    taps = conv_taps.astype(F32)
    gates = jnp.concatenate([spread_blocks(rate_gate), spread_blocks(entry_gate)], axis=1)
    gate_bias = jnp.concatenate([rate_bias, entry_bias]).astype(F32)[None, :]
    softer = jax.nn.softplus(-decay_logit)[None, :]

    inputs = tokens.astype(F32)
    scale_one = rms_scale(inputs)
    normed = (inputs * scale_one * gain_one).astype(BF16)
    branch = jnp.dot(normed, whole_recur, preferred_element_type=F32).astype(BF16)
    halo = shifted(branch[piece - 8 :], "ctx", 1)
    pre_gelu = jnp.dot(normed, whole_gelu, preferred_element_type=F32)
    conv, rate, entry, local_state, run = recur_forward(
        branch, halo, masks, taps, conv_bias.astype(F32)[None, :], gates, gate_bias, softer
    )
    state_in = shifted(local_state[piece - 8 :], "ctx", 1)[7:8]
    states = local_state + run * state_in
    gelu_out, gelu_slope = gelu_pair(pre_gelu)
    gated = (states * gelu_out).astype(BF16)
    part_merge = lax.dot_general(gated, whole_merge, (((1,), (1,)), ((), ())), preferred_element_type=F32)
    merged = lax.psum(part_merge.astype(BF16), "tp").astype(F32)

    d_hidden = lax.dot_general(cotangent, whole_down, (((1,), (0,)), ((), ())), preferred_element_type=F32)
    resid = inputs + merged
    scale_two = rms_scale(resid)
    normed_two = (resid * scale_two * gain_two).astype(BF16)
    gate_pre = jnp.dot(normed_two, whole_gate, preferred_element_type=F32)
    up_vals = jnp.dot(normed_two, whole_up, preferred_element_type=F32)
    gate_act, gate_slope = gelu_pair(gate_pre)
    hidden = (gate_act * up_vals).astype(BF16)
    d_gate = (d_hidden * up_vals * gate_slope).astype(BF16)
    d_up = (d_hidden * gate_act).astype(BF16)
    part_two = lax.dot_general(
        d_gate, whole_gate, (((1,), (1,)), ((), ())), preferred_element_type=F32
    ) + lax.dot_general(d_up, whole_up, (((1,), (1,)), ((), ())), preferred_element_type=F32)
    d_normed_two = lax.psum(part_two.astype(BF16), "tp").astype(F32)
    feed = lax.psum_scatter(
        lax.dot_general(
            hidden, whole_down, (((1,), (1,)), ((), ())), preferred_element_type=F32
        ).astype(BF16),
        "tp",
        scatter_dimension=1,
        tiled=True,
    ).astype(F32)
    output = (lax.dynamic_slice_in_dim(resid, feat_start, feat_local, 1) + feed).astype(BF16)

    rows_to_rows = (((0,), (0,)), ((), ()))
    grad_down = lax.dot_general(cotangent, hidden, rows_to_rows, preferred_element_type=F32)
    grad_gate = lax.dot_general(normed_two, d_gate, rows_to_rows, preferred_element_type=F32)
    grad_up = lax.dot_general(normed_two, d_up, rows_to_rows, preferred_element_type=F32)
    shard_down = scatter_rows(grad_down).T
    shard_gate = scatter_rows(grad_gate)
    shard_up = scatter_rows(grad_up)

    grad_feed = jnp.sum(d_normed_two * resid * scale_two, axis=0)
    weighted = d_normed_two * gain_two
    d_resid = (
        cotangent.astype(F32)
        + scale_two * weighted
        - resid * scale_two**3 * jnp.mean(resid * weighted, axis=-1, keepdims=True)
    )
    d_merge_in = d_resid.astype(BF16)
    grad_merge = lax.dot_general(d_merge_in, gated, rows_to_rows, preferred_element_type=F32)
    shard_merge = scatter_rows(grad_merge).T
    d_gated = jnp.dot(d_merge_in, whole_merge, preferred_element_type=F32)
    d_states = d_gated * gelu_out
    d_gelu_pre = (d_gated * states * gelu_slope).astype(BF16)
    local_grad, grad_run, first = recur_adjoint(rate, d_states, masks, softer)
    grad_in = shifted(first, "ctx", -1)[0:1]
    back, tail, head, gate_grads, sums = recur_backward(
        local_grad, grad_run, grad_in, rate, entry, conv, states, masks, branch, halo, taps, gates, softer
    )
    returned = shifted(head, "ctx", -1)
    d_branch = lax.dynamic_update_slice_in_dim(back, (tail + returned).astype(BF16), piece - 8, 0)

    part_one = lax.dot_general(
        d_gelu_pre, whole_gelu, (((1,), (1,)), ((), ())), preferred_element_type=F32
    ) + lax.dot_general(d_branch, whole_recur, (((1,), (1,)), ((), ())), preferred_element_type=F32)
    stat_one = jnp.sum(part_one * inputs * gain_one, axis=-1)
    grad_mix = jnp.sum(part_one * inputs * scale_one, axis=0)
    d_normed = lax.psum_scatter(
        part_one.astype(BF16), "tp", scatter_dimension=1, tiled=True
    ).astype(F32)
    stat_one = lax.psum(stat_one, "tp")[:, None] / features
    grad_recur = lax.dot_general(normed, d_branch, rows_to_rows, preferred_element_type=F32)
    grad_gelu = lax.dot_general(normed, d_gelu_pre, rows_to_rows, preferred_element_type=F32)
    shard_recur = scatter_rows(grad_recur)
    shard_gelu = scatter_rows(grad_gelu)

    def own(block):
        return lax.dynamic_slice_in_dim(block, feat_start, feat_local, 1)

    own_inputs = own(inputs)
    grad_tokens = (
        own(d_resid)
        + scale_one * d_normed * own(gain_one)
        - own_inputs * scale_one**3 * stat_one
    ).astype(BF16)

    both_norms = lax.psum(
        jnp.stack([grad_mix, grad_feed / lax.axis_size("tp")]), ("fsdp", "ctx", "tp")
    )
    norm_local = norm_mix.shape[0]
    own_norms = lax.dynamic_slice_in_dim(both_norms, lax.axis_index("fsdp") * norm_local, norm_local, 1)

    diagonal = [
        gate_grads[i * block : (i + 1) * block, part * chans + i * block : part * chans + (i + 1) * block]
        for part in range(2)
        for i in range(heads)
    ]
    gate_sums = lax.psum(jnp.stack(diagonal).astype(BF16), ("fsdp", "ctx")).astype(F32)
    row_sums = lax.psum(sums, ("fsdp", "ctx"))
    return (
        output,
        grad_tokens,
        shard_recur,
        shard_gelu,
        shard_merge,
        shard_gate,
        shard_up,
        shard_down,
        own_norms[0],
        own_norms[1],
        row_sums[4 : 4 + width],
        row_sums[3],
        gate_sums[:heads],
        gate_sums[heads:],
        row_sums[1],
        row_sums[2],
        CGAIN * row_sums[0] * jax.nn.sigmoid(-decay_logit),
    )


def solution(mesh):
    placed = (
        P(("fsdp", "ctx"), None),
        P("fsdp"),
        P(("fsdp", "ctx"), None),
        P("fsdp", "tp"),
        P("fsdp", "tp"),
        P("tp", "fsdp"),
        P("fsdp", "tp"),
        P("fsdp", "tp"),
        P("tp", "fsdp"),
        P("fsdp"),
        P("fsdp"),
        P(None, "tp"),
        P("tp"),
        P("tp", None, None),
        P("tp", None, None),
        P("tp"),
        P("tp"),
        P("tp"),
    )
    return jax.shard_map(
        shards,
        mesh=mesh,
        in_specs=placed,
        out_specs=(
            P(("fsdp", "ctx"), "tp"),
            P(("fsdp", "ctx"), "tp"),
            P("fsdp", "tp"),
            P("fsdp", "tp"),
            P("tp", "fsdp"),
            P("fsdp", "tp"),
            P("fsdp", "tp"),
            P("tp", "fsdp"),
            P("fsdp"),
            P("fsdp"),
            P(None, "tp"),
            P("tp"),
            P("tp", None, None),
            P("tp", None, None),
            P("tp"),
            P("tp"),
            P("tp"),
        ),
        check_vma=False,
    )
```

```python
import jax
import jax.numpy as jnp
from jax import lax
from jax.experimental import pallas as pl
from jax.experimental.pallas import tpu as pltpu
from jax.sharding import PartitionSpec as P

EPS = 1e-06
CGAIN = 8.0
ROOT = 0.7978845608
CUBE = 0.044715
TILE = 128
SEGS = 8
F32 = jnp.float32
BF16 = jnp.bfloat16


def swap_cores(block):
    size = lax.axis_size("ctx")
    return lax.ppermute(block, "ctx", [(i, size - 1 - i) for i in range(size)])


def shifted(block, axis, distance):
    devices = range(lax.axis_size(axis))
    route = [(i - distance, i) for i in devices if i - distance in devices]
    return lax.ppermute(block, axis, route)


def gather_halves(shard, dim):
    half = shard.shape[dim] // 2
    core = lax.axis_index("ctx")
    mine = lax.dynamic_slice_in_dim(shard, core * half, half, dim)
    mine = lax.all_gather(mine, "fsdp", axis=dim)
    other = swap_cores(mine)
    first = jnp.where(core == 0, mine, other)
    second = jnp.where(core == 0, other, mine)
    both = jnp.stack([first, second], axis=dim + 1)
    return both.reshape(shard.shape[:dim] + (-1,) + shard.shape[dim + 1 :])


def split_features(block):
    shards = lax.axis_size("fsdp")
    core = lax.axis_index("ctx")
    parts = block.reshape(block.shape[0], shards, 2, -1)
    return [
        lax.dynamic_index_in_dim(parts, index, 2, False).reshape(block.shape[0], -1)
        for index in (core, 1 - core)
    ]


def pair_sums(left, right, dim):
    rows_to_rows = (((0,), (0,)), ((), ()))

    def product(index):
        pair = (left[index], right) if dim == 0 else (right, left[index])
        return lax.dot_general(*pair, rows_to_rows, preferred_element_type=F32)

    arrived = swap_cores(product(1).astype(BF16))
    return (product(0) + arrived.astype(F32)).astype(BF16)


def to_owners(mine, dim):
    total = lax.psum_scatter(mine, "fsdp", scatter_dimension=dim, tiled=True)
    other = swap_cores(total)
    core = lax.axis_index("ctx")
    first = jnp.where(core == 0, total, other)
    second = jnp.where(core == 0, other, total)
    return jnp.concatenate([first, second], axis=dim).astype(F32)


def after(value, *others):
    return lax.optimization_barrier((value, *others))[0]


class Square:
    def __init__(self):
        me = lax.axis_index("fsdp")
        row, col = me // 2, me % 2
        self.me = me
        self.core = lax.axis_index("ctx")
        self.near = (row * 2 + 1 - col, (1 - row) * 2 + col)
        self.far = (1 - row) * 2 + 1 - col


def remote(source, target, send, arrive, **device):
    return pltpu.make_async_remote_copy(
        source, target, send, arrive, device_id=device, device_id_type=pl.DeviceIdType.MESH
    )


class Gather:
    def __init__(self, items, stages, send, arrive, local):
        self.items, self.stages = items, stages
        self.send, self.arrive, self.local = send, arrive, local
        self.square = Square()

    def piece(self, w, owner, low, size):
        shard, whole, dim, offset = self.items[w]
        low = pl.multiple_of(owner * shard.shape[dim] + low, 128)
        if dim == 0:
            return whole.at[pl.ds(low, size), pl.ds(offset, shard.shape[1])]
        return whole.at[:, pl.ds(low, size)]

    def copy(self, w, k):
        shard, _, dim, _ = self.items[w]
        square = self.square
        half = shard.shape[dim] // 2
        low = pl.multiple_of(square.core * half, 128)
        first, second = square.near
        if k < 2:
            source = shard.at[pl.ds(low, half), :] if dim == 0 else shard.at[:, pl.ds(low, half)]
            target = self.piece(w, square.me, low, half)
            device = {"fsdp": square.near[k]}
        elif k < 4:
            source = target = self.piece(w, square.near[k - 2], low + (k - 2) * (half // 2), half // 2)
            device = {"fsdp": square.near[3 - k]}
        else:
            source = target = self.piece(w, (first, second, square.far)[k - 4], low, half)
            device = {"ctx": 1 - square.core}
        return remote(source, target, self.send.at[w, k], self.arrive.at[w, k], **device)

    def stage(self, w, out):
        shard = self.items[w][0]
        if out:
            target = self.piece(w, self.square.me, 0, shard.shape[self.items[w][2]])
            return pltpu.make_async_copy(self.stages[w], target, self.local.at[w, 1])
        return pltpu.make_async_copy(shard, self.stages[w], self.local.at[w, 0])

    def start(self, w):
        self.copy(w, 0).start()
        self.copy(w, 1).start()
        self.stage(w, False).start()

    def forward(self, w):
        self.copy(w, 0).wait_recv()
        self.copy(w, 2).start()
        self.copy(w, 1).wait_recv()
        self.copy(w, 3).start()
        self.copy(w, 4).start()
        self.copy(w, 5).start()
        self.stage(w, False).wait()
        self.stage(w, True).start()

    def hand_over(self, w):
        self.copy(w, 2).wait_recv()
        self.copy(w, 3).wait_recv()
        self.copy(w, 6).start()

    def finish(self, w):
        for k in (4, 5, 6):
            self.copy(w, k).wait_recv()
        for k in range(7):
            self.copy(w, k).wait_send()
        self.stage(w, True).wait()


def greet(line, square):
    barrier = pltpu.get_barrier_semaphore()

    def call(**device):
        pl.semaphore_signal(barrier, inc=1, device_id=device, device_id_type=pl.DeviceIdType.MESH)

    peers = 0
    if line:
        count, me = lax.axis_size("tp"), lax.axis_index("tp")

        @pl.when(me > 0)
        def _():
            call(tp=me - 1)

        @pl.when(me < count - 1)
        def _():
            call(tp=me + 1)

        peers = jnp.where((me > 0) & (me < count - 1), 2, 1)
    if square:
        place = Square()
        call(fsdp=place.near[0])
        call(fsdp=place.near[1])
        call(fsdp=place.far)
        call(ctx=1 - place.core)
        peers = peers + 4
    pl.semaphore_wait(barrier, peers)


def line_sum(part, whole, inbox, sems, finish, between):
    count, me = lax.axis_size("tp"), lax.axis_index("tp")
    half = part.shape[0] // 2
    chunks = inbox.shape[1]
    rows = half // chunks
    sum_send, sum_arrive, share_send, share_arrive = sems

    def spot(side, c):
        return pl.ds(pl.multiple_of(side * half + c * rows, rows), rows)

    def place(side):
        return count - 1 - me if side else me

    def onward(side, c, source):
        target = me - 1 if side else me + 1
        return remote(source, inbox.at[side, c], sum_send.at[side, c], sum_arrive.at[side, c], tp=target)

    def share(side, c):
        target = me + 1 if side else me - 1
        block = whole.at[spot(side, c), :]
        return remote(block, block, share_send.at[side, c], share_arrive.at[side, c], tp=target)

    for side in (0, 1):
        @pl.when(place(side) == 0)
        def _():
            onward(side, 0, part.at[spot(side, 0), :]).start()

    def step(t, carry):
        for side in (0, 1):
            here = place(side)
            c = t - here

            @pl.when((here == 0) & (t + 1 < chunks))
            def _():
                onward(side, t + 1, part.at[spot(side, t + 1), :]).start()

            @pl.when((c >= 0) & (c < chunks) & (here > 0))
            def _():
                onward(side, c, inbox.at[side, c]).wait_recv()
                total = (inbox[side, c].astype(F32) + part[spot(side, c), :].astype(F32)).astype(BF16)

                @pl.when(here < count - 1)
                def _():
                    inbox[side, c] = total
                    onward(side, c, inbox.at[side, c]).start()

                @pl.when(here == count - 1)
                def _():
                    whole[spot(side, c), :] = total
                    share(side, c).start()
                    finish(spot(side, c))

        for side in (0, 1):
            here = place(side)
            c = t - 2 * (count - 1) + here

            @pl.when((c >= 0) & (c < chunks) & (here < count - 1))
            def _():
                share(side, c).wait_recv()

                @pl.when(here > 0)
                def _():
                    share(side, c).start()

                finish(spot(side, c))

        between(t)
        return carry

    lax.fori_loop(0, chunks + 2 * (count - 1), step, 0)

    def drain(c, carry):
        for side in (0, 1):
            here = place(side)

            @pl.when(here < count - 1)
            def _():
                onward(side, c, inbox.at[side, c]).wait_send()

            @pl.when(here > 0)
            def _():
                share(side, c).wait_send()

        return carry

    lax.fori_loop(0, chunks, drain, 0)


def put_split(ref, rows, block):
    core = lax.axis_index("ctx")
    size = block.shape[1] // 8
    for owner in range(4):
        for index in range(2):
            low = (2 * owner + index) * size
            ref[(index + core) % 2, rows, owner * size : (owner + 1) * size] = block[:, low : low + size]


CHUNK = 32


def enter_kernel(
    tokens, gain_shard, recur, gelu, merge,
    normed, halves, gains, whole_in, whole_merge,
    stage_recur, stage_gelu, stage_merge, send, arrive, local, gain_send, gain_arrive,
):
    square = Square()
    greet(False, True)
    width = gain_shard.shape[1]

    def gain_copy(k, owner, target):
        spot = gains.at[:, pl.ds(pl.multiple_of(owner * width, 128), width)]
        return remote(gain_shard, spot, gain_send.at[k], gain_arrive.at[k], fsdp=target)

    others = (*square.near, square.far)
    for k, target in enumerate(others):
        gain_copy(k, square.me, target).start()
    gather = Gather(
        [(recur, whole_in, 0, 0), (gelu, whole_in, 0, recur.shape[1]), (merge, whole_merge, 1, 0)],
        (stage_recur, stage_gelu, stage_merge), send, arrive, local,
    )
    for w in range(3):
        gather.start(w)
    gains[:, pl.ds(pl.multiple_of(square.me * width, 128), width)] = gain_shard[...]
    for k, owner in enumerate(others):
        gain_copy(k, owner, owner).wait_recv()

    def norm(t, carry):
        rows = pl.ds(pl.multiple_of(t * CHUNK, CHUNK), CHUNK)
        block = tokens[rows, :].astype(F32)
        block = (block * rms_scale(block) * gains[0:1, :]).astype(BF16)
        normed[rows, :] = block
        put_split(halves, rows, block)
        return carry

    lax.fori_loop(0, tokens.shape[0] // CHUNK, norm, 0)
    for w in range(3):
        gather.forward(w)
    for w in range(3):
        gather.hand_over(w)
    for w in range(3):
        gather.finish(w)
    for k, target in enumerate(others):
        gain_copy(k, square.me, target).wait_send()


ANY = pl.BlockSpec(memory_space=pl.ANY)
NEAR = pl.BlockSpec(memory_space=pltpu.VMEM)


def gather_scratch(shards):
    count = len(shards)
    dma = pltpu.SemaphoreType.DMA
    return [pltpu.VMEM(w.shape, w.dtype) for w in shards] + [dma((count, 7)), dma((count, 7)), dma((count, 2))]


def enter(tokens, gain_shard, recur, gelu, merge):
    rows, features = tokens.shape
    shape = jax.ShapeDtypeStruct
    inner = recur.shape[1]
    dma = pltpu.SemaphoreType.DMA
    return pl.pallas_call(
        enter_kernel,
        out_shape=(
            shape((rows, features), BF16),
            shape((2, rows, features // 2), BF16),
            shape((8, features), F32),
            shape((features, 2 * inner), BF16),
            shape((inner, features), BF16),
        ),
        in_specs=[NEAR, NEAR, ANY, ANY, ANY],
        out_specs=[NEAR, NEAR, NEAR, ANY, ANY],
        scratch_shapes=gather_scratch([recur, gelu, merge]) + [dma((3,)), dma((3,))],
        compiler_params=pltpu.CompilerParams(collective_id=1, has_side_effects=True),
        name="enter",
    )(tokens, gain_shard, recur, gelu, merge)


def line_scratch(rows, features):
    chunks = rows // 2 // CHUNK
    dma = pltpu.SemaphoreType.DMA((2, chunks))
    return [pltpu.VMEM((2, chunks, CHUNK, features), BF16), dma, dma, dma, dma]


def middle_kernel(gathers, part, tokens, gains, *refs):
    if gathers:
        gate, up, down, merged, normed, halves, whole_in, whole_down = refs[:8]
        inbox, *rest = refs[8:]
        sems, (stage_gate, stage_up, stage_down, send, arrive, local) = rest[:4], rest[4:]
        gather = Gather(
            [(gate, whole_in, 0, 0), (up, whole_in, 0, gate.shape[1]), (down, whole_down, 1, 0)],
            (stage_gate, stage_up, stage_down), send, arrive, local,
        )
        greet(True, True)
        for w in range(3):
            gather.start(w)
    else:
        merged, normed, inbox, *sems = refs
        greet(True, False)

    def finish(rows):
        block = tokens[rows, :].astype(F32) + merged[rows, :].astype(F32)
        block = (block * rms_scale(block) * gains[1:2, :]).astype(BF16)
        normed[rows, :] = block
        if gathers:
            put_split(halves, rows, block)

    def between(t):
        if gathers:
            for w in range(3):
                @pl.when(t == 5 + 4 * w)
                def _():
                    gather.forward(w)

                @pl.when(t == 17 + w)
                def _():
                    gather.hand_over(w)

    line_sum(part, merged, inbox, sems, finish, between)
    if gathers:
        for w in range(3):
            gather.finish(w)


def middle(part, tokens, gains, shards):
    rows, features = tokens.shape
    shape = jax.ShapeDtypeStruct
    whole = shape((rows, features), BF16)
    outs, specs = [whole, whole], [NEAR, NEAR]
    scratch = line_scratch(rows, features)
    if shards:
        gate, up, down = shards
        outs += [
            shape((2, rows, features // 2), BF16),
            shape((features, 2 * gate.shape[1]), BF16),
            shape((down.shape[0], features), BF16),
        ]
        specs += [NEAR, ANY, ANY]
        scratch += gather_scratch(shards)
    return pl.pallas_call(
        lambda *refs: middle_kernel(bool(shards), *refs),
        out_shape=tuple(outs),
        in_specs=[NEAR, NEAR, NEAR] + [ANY] * len(shards),
        out_specs=specs,
        scratch_shapes=scratch,
        compiler_params=pltpu.CompilerParams(collective_id=2, has_side_effects=True),
        name="middle",
    )(part, tokens, gains, *shards)


def turn_kernel(split, part, tokens, merged, upstream, gains, own, grad_in, gain_sum, *refs):
    if split:
        halves, whole, wide, inbox, *sems = refs
    else:
        whole, wide, inbox, *sems = refs
    greet(True, False)
    gain_sum[...] = jnp.zeros_like(gain_sum)
    width = own.shape[1]
    start = pl.multiple_of(lax.axis_index("tp") * width, 128)

    def finish(rows):
        block = tokens[rows, :].astype(F32) + merged[rows, :].astype(F32)
        scale = rms_scale(block)
        grad = whole[rows, :].astype(F32)
        gain_sum[0:1, :] += jnp.sum(grad * (block * scale), axis=0, keepdims=True)
        grad = grad * gains[1:2, :]
        mean = jnp.mean(block * grad, axis=-1, keepdims=True)
        grad = upstream[rows, :].astype(F32) + scale * grad - block * (scale * scale * scale * mean)
        wide[...] = grad
        own[rows, :] = wide[:, pl.ds(start, width)]
        grad = grad.astype(BF16)
        grad_in[rows, :] = grad
        if split:
            put_split(halves, rows, grad)

    line_sum(part, whole, inbox, sems, finish, lambda t: None)


def turn(part, tokens, merged, upstream, gains, split):
    rows, features = tokens.shape
    shape = jax.ShapeDtypeStruct
    outs = [
        shape((rows, features // lax.axis_size("tp")), F32),
        shape((rows, features), BF16),
        shape((8, features), F32),
    ]
    if split:
        outs.append(shape((2, rows, features // 2), BF16))
    return pl.pallas_call(
        lambda *refs: turn_kernel(split, *refs),
        out_shape=tuple(outs),
        in_specs=[NEAR] * 5,
        out_specs=[NEAR] * len(outs),
        scratch_shapes=[pltpu.VMEM((rows, features), BF16), pltpu.VMEM((CHUNK, features), F32)]
        + line_scratch(rows, features),
        compiler_params=pltpu.CompilerParams(collective_id=3, has_side_effects=True),
        name="turn",
    )(part, tokens, merged, upstream, gains)


def gelu_pair(q):
    tanh = jnp.tanh(ROOT * (q + CUBE * q * q * q))
    value = 0.5 * q * (1.0 + tanh)
    slope = 0.5 * (1.0 + tanh) + 0.5 * q * (1.0 - tanh * tanh) * ROOT * (1.0 + 3.0 * CUBE * q * q)
    return value, slope


def rms_scale(values):
    return lax.rsqrt(jnp.mean(values * values, axis=-1, keepdims=True) + EPS)


def decay_parts(rate, softer, keep):
    gap = 2.0 * CGAIN * rate * softer
    decay = jnp.exp(-0.5 * gap)
    series = gap * (
        1.0
        - gap / 2.0
        * (1.0 - gap / 3.0 * (1.0 - gap / 4.0 * (1.0 - gap / 5.0 * (1.0 - gap / 6.0 * (1.0 - gap / 7.0)))))
    )
    square = jnp.where(gap < 0.25, series, 1.0 - decay * decay)
    return jnp.where(keep, decay, 0.0), jnp.where(keep, square, 1.0)


LANES = 128


def put_lanes(ref, block, rows):
    for lane in range(ref.shape[0]):
        ref[lane, 0:rows, :] = block[:, lane * LANES : (lane + 1) * LANES]


def sweep(decay_ref, value_ref, state_ref, product_ref, out_ref, run_ref, carry_ref, reverse, offset):
    groups, rows, _ = value_ref.shape
    steps = rows // SEGS
    place = lax.broadcasted_iota(jnp.int32, (SEGS, LANES), 0)
    if reverse:
        place = SEGS - 1 - place

    def moved(block, by, fill):
        turned = pltpu.roll(block, SEGS - by if reverse else by, 0)
        return jnp.where(place >= by, turned, fill)

    for lane in range(groups):
        lanes = slice(lane * LANES, (lane + 1) * LANES)
        state = jnp.zeros((SEGS, LANES), F32)
        product = jnp.ones((SEGS, LANES), F32)
        for step in reversed(range(steps)) if reverse else range(steps):
            spot = pl.ds(step, SEGS, stride=steps)
            decay = decay_ref[lane, pl.ds(step + offset, SEGS, stride=steps), :]
            state = decay * state + value_ref[lane, spot, :]
            product = product * decay
            state_ref[lane, spot, :] = state
            product_ref[lane, spot, :] = product
        for by in (1, 2, 4):
            state = state + product * moved(state, by, 0.0)
            product = product * moved(product, by, 1.0)
        carry = carry_ref[0:1, lanes]
        carry_run = carry_ref[8:9, lanes]
        state = state + product * carry
        product = product * carry_run
        enter = moved(state, 1, carry)
        enter_run = moved(product, 1, carry_run)
        for seg in range(SEGS):
            span = slice(seg * steps, (seg + 1) * steps)
            inner = product_ref[lane, span, :]
            out_ref[span, lanes] = state_ref[lane, span, :] + inner * enter[seg : seg + 1, :]
            run_ref[span, lanes] = inner * enter_run[seg : seg + 1, :]
        last = 0 if reverse else SEGS - 1
        carry_ref[0:1, lanes] = state[last : last + 1, :]
        carry_ref[8:9, lanes] = product[last : last + 1, :]


def spread_blocks(blocks_ref, out_ref):
    chans, size = blocks_ref.shape[1:]
    row = lax.broadcasted_iota(jnp.int32, (chans, chans), 0)
    col = lax.broadcasted_iota(jnp.int32, (chans, chans), 1)
    inner = lax.broadcasted_iota(jnp.int32, (size, chans), 0)
    outer = lax.broadcasted_iota(jnp.int32, (size, chans), 1)
    inside = row < 0
    repeat = outer < 0
    for low in range(0, chans, size):
        inside |= (row >= low) & (row < low + size) & (col >= low) & (col < low + size)
        repeat |= outer - low == inner
    repeat = repeat.astype(F32).astype(BF16)
    for gate in range(2):
        wide = jnp.dot(blocks_ref[gate], repeat, preferred_element_type=F32)
        out_ref[:, gate * chans : (gate + 1) * chans] = jnp.where(inside, wide, 0.0).astype(BF16)


def forward_kernel(
    branch_ref, halo_ref, mask_ref, taps_ref, bias_ref, blocks_ref, gate_bias_ref, softer_ref,
    conv_ref, rate_ref, entry_ref, state_ref, run_ref, gates_ref,
    window, decay, value, inner, product, carry,
):
    rows, chans = conv_ref.shape
    spot = pl.program_id(0)

    @pl.when(spot == 0)
    def _():
        spread_blocks(blocks_ref, gates_ref)
        window[0:8, :] = halo_ref[...].astype(F32)
        carry[0:8, :] = jnp.zeros((8, chans), F32)
        carry[8:16, :] = jnp.ones((8, chans), F32)

    @pl.when(spot > 0)
    def _():
        window[0:8, :] = window[rows : rows + 8, :]

    window[8 : rows + 8, :] = branch_ref[...].astype(F32)
    mixed = bias_ref[...] + taps_ref[0:1, :] * window[8 : rows + 8, :]
    for shift in range(1, taps_ref.shape[0]):
        moved = window[8 - shift : 8 - shift + rows, :]
        mixed = mixed + taps_ref[shift : shift + 1, :] * (moved * mask_ref[:, shift : shift + 1])
    conv = mixed.astype(BF16)
    conv_ref[...] = conv
    pre = jnp.dot(conv, gates_ref[...], preferred_element_type=F32) + gate_bias_ref[...]
    rate = jax.nn.sigmoid(pre[:, :chans])
    entry = jax.nn.sigmoid(pre[:, chans:])
    rate_ref[...] = rate
    entry_ref[...] = entry
    keep = jnp.broadcast_to(mask_ref[:, 0:1], (rows, chans)) > 0.5
    step, square = decay_parts(rate, softer_ref[...], keep)
    put_lanes(decay, step, rows)
    put_lanes(value, jnp.sqrt(square) * entry * conv.astype(F32), rows)
    sweep(decay, value, inner, product, state_ref, run_ref, carry, False, 0)


def tile_spec(width, count=None):
    if count is None:
        return pl.BlockSpec((TILE, width), lambda i: (i, 0))
    return pl.BlockSpec((TILE, width), lambda i: (count - 1 - i, 0))


def fixed_spec(shape):
    return pl.BlockSpec(shape, lambda i: (0, 0))


def recur_forward(branch, halo, masks, taps, bias, blocks, gate_bias, softer):
    rows, chans = branch.shape[0], halo.shape[1]
    wide = jax.ShapeDtypeStruct((rows, chans), F32)
    return pl.pallas_call(
        forward_kernel,
        grid=(rows // TILE,),
        out_shape=(
            jax.ShapeDtypeStruct((rows, chans), BF16), wide, wide, wide, wide,
            jax.ShapeDtypeStruct((chans, 2 * chans), BF16),
        ),
        in_specs=[
            tile_spec(chans),
            fixed_spec((8, chans)),
            tile_spec(masks.shape[1]),
            fixed_spec(taps.shape),
            fixed_spec((1, chans)),
            pl.BlockSpec(blocks.shape, lambda i: (0, 0, 0)),
            fixed_spec((1, 2 * chans)),
            fixed_spec((1, chans)),
        ],
        out_specs=[tile_spec(chans)] * 5 + [fixed_spec((chans, 2 * chans))],
        scratch_shapes=[
            pltpu.VMEM((TILE + 8, chans), F32),
            pltpu.VMEM((chans // LANES, TILE, LANES), F32),
            pltpu.VMEM((chans // LANES, TILE, LANES), F32),
            pltpu.VMEM((chans // LANES, TILE, LANES), F32),
            pltpu.VMEM((chans // LANES, TILE, LANES), F32),
            pltpu.VMEM((16, chans), F32),
        ],
        cost_estimate=pl.CostEstimate(
            flops=2 * rows * chans * 2 * chans, bytes_accessed=24 * rows * chans, transcendentals=5 * rows * chans
        ),
        name="recur_forward",
    )(branch, halo, masks, taps, bias, blocks, gate_bias, softer)


def merge_kernel(local_ref, run_ref, enter_ref, pre_ref, weight_ref, state_ref, gated_ref, part_ref):
    state = local_ref[...] + run_ref[...] * enter_ref[0:1, :]
    state_ref[...] = state
    pre = pre_ref[...].astype(F32)
    gated = (state * gelu_pair(pre)[0]).astype(BF16)
    gated_ref[...] = gated
    part_ref[...] = jnp.dot(gated, weight_ref[...], preferred_element_type=F32).astype(BF16)


def merge_states(local, run, enter, branches, weight):
    rows, chans = local.shape
    features = weight.shape[1]
    shape = jax.ShapeDtypeStruct
    return pl.pallas_call(
        merge_kernel,
        grid=(rows // TILE,),
        out_shape=(shape((rows, chans), F32), shape((rows, chans), BF16), shape((rows, features), BF16)),
        in_specs=[
            tile_spec(chans), tile_spec(chans), fixed_spec((1, chans)),
            pl.BlockSpec((TILE, chans), lambda i: (i, 1)),
            fixed_spec(weight.shape),
        ],
        out_specs=[tile_spec(chans), tile_spec(chans), tile_spec(features)],
        cost_estimate=pl.CostEstimate(
            flops=2 * rows * chans * features, bytes_accessed=16 * rows * chans, transcendentals=rows * chans
        ),
        name="merge_states",
    )(local, run, enter, branches, weight)


def adjoint_kernel(
    rate_ref, up_ref, pre_ref, state_ref, mask_ref, softer_ref,
    grad_ref, run_ref, head_ref, pre_grad_ref,
    decay, value, inner, product, carry,
):
    rows, chans = rate_ref.shape
    groups = chans // LANES
    spot = pl.program_id(0)

    @pl.when(spot == 0)
    def _():
        for lane in range(groups):
            decay[lane, rows : rows + 8, :] = jnp.ones((8, LANES), F32)
        carry[0:8, :] = jnp.zeros((8, chans), F32)
        carry[8:16, :] = jnp.ones((8, chans), F32)

    @pl.when(spot > 0)
    def _():
        for lane in range(groups):
            decay[lane, rows : rows + 8, :] = decay[lane, 0:8, :]

    keep = jnp.broadcast_to(mask_ref[:, 0:1], (rows, chans)) > 0.5
    gap = CGAIN * rate_ref[...] * softer_ref[...]
    step = jnp.where(keep, jnp.exp(-gap), 0.0)
    put_lanes(decay, step, rows)
    gate, slope = gelu_pair(pre_ref[...].astype(F32))
    up = up_ref[...]
    pre_grad_ref[...] = (up * state_ref[...] * slope).astype(BF16)
    put_lanes(value, up * gate, rows)
    sweep(decay, value, inner, product, grad_ref, run_ref, carry, True, 1)
    head_ref[...] = jnp.broadcast_to(step[0:1, :] * carry[0:1, :], (8, chans))


def recur_adjoint(rate, up, branches, state, masks, softer):
    rows, chans = rate.shape
    count = rows // TILE
    wide = jax.ShapeDtypeStruct((rows, chans), F32)
    return pl.pallas_call(
        adjoint_kernel,
        grid=(count,),
        out_shape=(
            wide, wide, jax.ShapeDtypeStruct((8, chans), F32), jax.ShapeDtypeStruct((rows, chans), BF16)
        ),
        in_specs=[
            tile_spec(chans, count),
            tile_spec(chans, count),
            pl.BlockSpec((TILE, chans), lambda i: (count - 1 - i, 1)),
            tile_spec(chans, count),
            tile_spec(masks.shape[1], count),
            fixed_spec((1, chans)),
        ],
        out_specs=[tile_spec(chans, count), tile_spec(chans, count), fixed_spec((8, chans)), tile_spec(chans, count)],
        scratch_shapes=[
            pltpu.VMEM((chans // LANES, TILE + 8, LANES), F32),
            pltpu.VMEM((chans // LANES, TILE, LANES), F32),
            pltpu.VMEM((chans // LANES, TILE, LANES), F32),
            pltpu.VMEM((chans // LANES, TILE, LANES), F32),
            pltpu.VMEM((16, chans), F32),
        ],
        cost_estimate=pl.CostEstimate(
            flops=8 * rows * chans, bytes_accessed=16 * rows * chans, transcendentals=rows * chans
        ),
        name="recur_adjoint",
    )(rate, up, branches, state, masks, softer)


def backward_kernel(
    grad_ref, run_ref, enter_ref, rate_ref, entry_ref, conv_ref, state_ref, mask_ref,
    branch_ref, pre_grad_ref, halo_ref, taps_ref, gates_ref, softer_ref,
    back_ref, tail_ref, head_ref, gate_grad_ref, sums_ref,
    shifts, edge,
):
    rows, chans = conv_ref.shape
    width = taps_ref.shape[0]
    spot = pl.program_id(0)
    last = pl.num_programs(0) - 1

    @pl.when(spot == 0)
    def _():
        for shift in range(1, width):
            shifts[shift - 1, rows : rows + 8, :] = jnp.zeros((8, chans), F32)
        gate_grad_ref[...] = jnp.zeros_like(gate_grad_ref)
        sums_ref[...] = jnp.zeros_like(sums_ref)

    @pl.when(spot > 0)
    def _():
        for shift in range(1, width):
            shifts[shift - 1, rows : rows + 8, :] = shifts[shift - 1, 0:8, :]

    keep = jnp.broadcast_to(mask_ref[:, 0:1], (rows, chans)) > 0.5
    softer = softer_ref[...]
    rate = rate_ref[...]
    entry = entry_ref[...]
    conv = conv_ref[...].astype(F32)
    grad = grad_ref[...] + run_ref[...] * enter_ref[0:1, :]
    step, square = decay_parts(rate, softer, keep)
    inverse = lax.rsqrt(square)
    mult = square * inverse
    driven = entry * conv
    carried = state_ref[...] - mult * driven
    d_log = jnp.where(keep, grad * (carried - driven * step * step * inverse), 0.0)
    d_rate = (-CGAIN * softer * d_log * rate * (1.0 - rate)).astype(BF16)
    lifted = grad * mult * entry
    d_entry = (lifted * conv * (1.0 - entry)).astype(BF16)
    both = jnp.concatenate([d_rate, d_entry], axis=1)
    d_conv = lifted + lax.dot_general(
        both, gates_ref[...], (((1,), (1,)), ((), ())), preferred_element_type=F32
    )
    gate_grad_ref[...] += lax.dot_general(
        conv_ref[...], both, (((0,), (0,)), ((), ())), preferred_element_type=F32
    )

    def add_row(row, block):
        sums_ref[row : row + 1, :] += jnp.sum(block, axis=0, keepdims=True)

    branch = branch_ref[...].astype(F32)
    add_row(0, d_log * rate)
    add_row(1, d_rate.astype(F32))
    add_row(2, d_entry.astype(F32))
    add_row(3, d_conv)
    add_row(4, d_conv * branch)
    back = taps_ref[0:1, :] * d_conv
    for shift in range(1, width):
        shifts[shift - 1, 0:rows, :] = d_conv * mask_ref[:, shift : shift + 1]
        moved = shifts[shift - 1, shift : shift + rows, :]
        add_row(4 + shift, moved * branch)
        back = back + taps_ref[shift : shift + 1, :] * moved
    back_ref[:, 0:chans] = back.astype(BF16)
    back_ref[:, chans:] = pre_grad_ref[...]

    @pl.when(spot == 0)
    def _():
        tail_ref[...] = back[rows - 8 :, :]

    @pl.when(spot == last)
    def _():
        halo = halo_ref[...].astype(F32)
        head = jnp.zeros((8, chans), F32)
        edge[0:8, :] = head
        for shift in range(1, width):
            edge[8:16, :] = shifts[shift - 1, 0:8, :]
            moved = edge[shift : shift + 8, :]
            add_row(4 + shift, moved * halo)
            head = head + taps_ref[shift : shift + 1, :] * moved
        head_ref[...] = head


def recur_backward(grad, run, enter, rate, entry, conv, state, masks, branch, pre_grad, halo, taps, gates, softer):
    rows, chans = rate.shape
    count = rows // TILE
    edge = jax.ShapeDtypeStruct((8, chans), F32)
    wide = tile_spec(chans, count)
    return pl.pallas_call(
        backward_kernel,
        grid=(count,),
        out_shape=(
            jax.ShapeDtypeStruct((rows, 2 * chans), BF16),
            edge,
            edge,
            jax.ShapeDtypeStruct((chans, 2 * chans), F32),
            jax.ShapeDtypeStruct((16, chans), F32),
        ),
        in_specs=[
            wide, wide, fixed_spec((1, chans)), wide, wide, wide, wide,
            tile_spec(masks.shape[1], count),
            wide,
            wide,
            fixed_spec((8, chans)),
            fixed_spec(taps.shape),
            fixed_spec(gates.shape),
            fixed_spec((1, chans)),
        ],
        out_specs=[
            tile_spec(2 * chans, count),
            fixed_spec((8, chans)),
            fixed_spec((8, chans)),
            fixed_spec((chans, 2 * chans)),
            fixed_spec((16, chans)),
        ],
        scratch_shapes=[
            pltpu.VMEM((taps.shape[0] - 1, TILE + 8, chans), F32),
            pltpu.VMEM((16, chans), F32),
        ],
        cost_estimate=pl.CostEstimate(
            flops=8 * rows * chans * chans, bytes_accessed=28 * rows * chans, transcendentals=2 * rows * chans
        ),
        name="recur_backward",
    )(grad, run, enter, rate, entry, conv, state, masks, branch, pre_grad, halo, taps, gates, softer)


def shards(
    tokens,
    segments,
    cotangent,
    w_recur,
    w_gelu,
    w_merge,
    w_gate,
    w_up,
    w_down,
    norm_mix,
    norm_feed,
    conv_taps,
    conv_bias,
    rate_gate,
    entry_gate,
    rate_bias,
    entry_bias,
    decay_logit,
):
    piece = tokens.shape[0]
    width = conv_taps.shape[0]
    edge = width - 1
    heads, block = rate_gate.shape[0], rate_gate.shape[1]
    chans = conv_taps.shape[1]
    features = tokens.shape[1]
    feat_local = features // lax.axis_size("tp")
    feat_start = lax.axis_index("tp") * feat_local

    square = lax.axis_size("fsdp") == 4
    gain_shard = jnp.concatenate(
        [jnp.stack([norm_mix, norm_feed]).astype(F32), jnp.zeros((6, norm_mix.shape[0]), F32)], axis=0
    )
    if square:
        normed, normed_split, gains, whole_in, whole_merge = enter(tokens, gain_shard, w_recur, w_gelu, w_merge)
    else:
        whole_in = gather_halves(jnp.concatenate([w_recur, w_gelu], axis=1), 0)
        whole_merge = gather_halves(w_merge, 1)
        gains = lax.all_gather(gain_shard, "fsdp", axis=1, tiled=True)
        inputs = tokens.astype(F32)
        normed = (inputs * rms_scale(inputs) * gains[0:1]).astype(BF16)
        normed_split = split_features(normed)
    gain_one = gains[0:1]

    padded_ids = jnp.concatenate([jnp.full((edge,), -1, jnp.int32), segments])
    local_ids = lax.dynamic_slice_in_dim(padded_ids, lax.axis_index("ctx") * piece, piece + edge)
    own_ids = local_ids[edge:]
    masks = jnp.stack(
        [(local_ids[edge - max(shift, 1) : edge - max(shift, 1) + piece] == own_ids) for shift in range(width)],
        axis=1,
    ).astype(F32)
    taps = conv_taps.astype(F32)
    blocks = jnp.stack([rate_gate.reshape(chans, block), entry_gate.reshape(chans, block)])
    gate_bias = jnp.concatenate([rate_bias, entry_bias]).astype(F32)[None, :]
    softer = jax.nn.softplus(-decay_logit)[None, :]

    rows_to_features = (((1,), (1,)), ((), ()))
    branches = jnp.dot(normed, whole_in, preferred_element_type=F32).astype(BF16)
    halo = shifted(branches[piece - 8 :, :chans], "ctx", 1)
    conv, rate, entry, local_state, run, gates = recur_forward(
        branches, halo, masks, taps, conv_bias.astype(F32)[None, :], blocks, gate_bias, softer
    )
    state_in = shifted(local_state[piece - 8 :], "ctx", 1)[7:8]
    states, gated, part_merge = merge_states(local_state, run, state_in, branches, whole_merge)

    if square:
        merged, normed_two, normed_two_split, whole_mid, whole_down = middle(
            part_merge, tokens, gains, (w_gate, w_up, w_down)
        )
    else:
        merged, normed_two = middle(part_merge, tokens, gains, ())
        normed_two_split = split_features(normed_two)
        whole_mid = gather_halves(jnp.concatenate([w_gate, w_up], axis=1), 0)
        whole_down = gather_halves(w_down, 1)
    cotangent_split = split_features(cotangent)

    units = w_gate.shape[1]
    pre_mid = jnp.dot(normed_two, whole_mid, preferred_element_type=F32).astype(BF16)
    d_hidden = lax.dot_general(cotangent, whole_down, rows_to_features, preferred_element_type=F32).astype(BF16)
    gate_act, gate_slope = gelu_pair(pre_mid[:, :units].astype(F32))
    up_vals = pre_mid[:, units:].astype(F32)
    wide_hidden = d_hidden.astype(F32)
    hidden = (gate_act * up_vals).astype(BF16)
    d_mid = jnp.concatenate(
        [(wide_hidden * up_vals * gate_slope).astype(BF16), (wide_hidden * gate_act).astype(BF16)], axis=1
    )
    part_two = lax.dot_general(d_mid, whole_mid, rows_to_features, preferred_element_type=F32).astype(BF16)
    pair_down = pair_sums(cotangent_split, hidden, 1)
    pair_mid = pair_sums(normed_two_split, d_mid, 0)
    part_two = after(part_two, pair_down, pair_mid)
    turned = turn(part_two, tokens, merged, cotangent, gains, square)
    own_resid_grad, d_merge_in, feed_sums = turned[:3]
    d_merge_split = turned[3] if square else split_features(d_merge_in)
    grad_feed = feed_sums[0]

    feed = lax.psum_scatter(
        jnp.dot(after(hidden, d_merge_in), whole_down, preferred_element_type=F32).astype(BF16),
        "tp",
        scatter_dimension=1,
        tiled=True,
    ).astype(F32)
    shard_down = to_owners(pair_down, 1)
    shard_mid = to_owners(pair_mid, 0)

    d_gated = lax.dot_general(d_merge_in, whole_merge, rows_to_features, preferred_element_type=F32)
    local_grad, grad_run, first, d_gelu_pre = recur_adjoint(rate, d_gated, branches, states, masks, softer)
    grad_in = shifted(first, "ctx", -1)[0:1]
    back, tail, head, gate_grads, sums = recur_backward(
        local_grad, grad_run, grad_in, rate, entry, conv, states, masks, branches, d_gelu_pre,
        halo, taps, gates, softer
    )
    returned = shifted(head, "ctx", -1)
    shard_merge = to_owners(pair_sums(d_merge_split, after(gated, back), 1), 1)
    d_in = lax.dynamic_update_slice(back, (tail + returned).astype(BF16), (piece - 8, 0))

    inputs = tokens.astype(F32)
    scale_one = rms_scale(inputs)
    part_one = lax.dot_general(d_in, whole_in, rows_to_features, preferred_element_type=F32)
    stat_one = jnp.sum(part_one * inputs * gain_one, axis=-1)
    grad_mix = jnp.sum(part_one * inputs * scale_one, axis=0)
    d_normed = lax.psum_scatter(
        part_one.astype(BF16), "tp", scatter_dimension=1, tiled=True
    ).astype(F32)
    stat_one = lax.psum(stat_one, "tp")[:, None] / features
    shard_in = to_owners(pair_sums(normed_split, d_in, 0), 0)

    def own(block):
        return lax.dynamic_slice_in_dim(block, feat_start, feat_local, 1)

    own_inputs = own(inputs)
    output = (own_inputs + own(merged).astype(F32) + feed).astype(BF16)
    grad_tokens = (
        own_resid_grad
        + scale_one * d_normed * own(gain_one)
        - own_inputs * scale_one**3 * stat_one
    ).astype(BF16)

    both_norms = lax.psum(
        jnp.stack([grad_mix, grad_feed / lax.axis_size("tp")]), ("fsdp", "ctx", "tp")
    )
    norm_local = norm_mix.shape[0]
    own_norms = lax.dynamic_slice_in_dim(both_norms, lax.axis_index("fsdp") * norm_local, norm_local, 1)

    diagonal = [
        gate_grads[i * block : (i + 1) * block, part * chans + i * block : part * chans + (i + 1) * block]
        for part in range(2)
        for i in range(heads)
    ]
    gate_sums = lax.psum(jnp.stack(diagonal).astype(BF16), ("fsdp", "ctx")).astype(F32)
    row_sums = lax.psum(sums, ("fsdp", "ctx"))
    return (
        output,
        grad_tokens,
        shard_in[:, :chans],
        shard_in[:, chans:],
        shard_merge,
        shard_mid[:, :units],
        shard_mid[:, units:],
        shard_down,
        own_norms[0],
        own_norms[1],
        row_sums[4 : 4 + width],
        row_sums[3],
        gate_sums[:heads],
        gate_sums[heads:],
        row_sums[1],
        row_sums[2],
        CGAIN * row_sums[0] * jax.nn.sigmoid(-decay_logit),
    )


def solution(mesh):
    placed = (
        P(("fsdp", "ctx"), None),
        P("fsdp"),
        P(("fsdp", "ctx"), None),
        P("fsdp", "tp"),
        P("fsdp", "tp"),
        P("tp", "fsdp"),
        P("fsdp", "tp"),
        P("fsdp", "tp"),
        P("tp", "fsdp"),
        P("fsdp"),
        P("fsdp"),
        P(None, "tp"),
        P("tp"),
        P("tp", None, None),
        P("tp", None, None),
        P("tp"),
        P("tp"),
        P("tp"),
    )
    return jax.shard_map(
        shards,
        mesh=mesh,
        in_specs=placed,
        out_specs=(
            P(("fsdp", "ctx"), "tp"),
            P(("fsdp", "ctx"), "tp"),
            P("fsdp", "tp"),
            P("fsdp", "tp"),
            P("tp", "fsdp"),
            P("fsdp", "tp"),
            P("fsdp", "tp"),
            P("tp", "fsdp"),
            P("fsdp"),
            P("fsdp"),
            P(None, "tp"),
            P("tp"),
            P("tp", None, None),
            P("tp", None, None),
            P("tp"),
            P("tp"),
            P("tp"),
        ),
        check_vma=False,
    )
```

```python
import jax
import jax.numpy as jnp
from jax import lax
from jax.experimental import pallas as pl
from jax.experimental.pallas import tpu as pltpu
from jax.sharding import PartitionSpec as P

EPS = 1e-06
CGAIN = 8.0
ROOT = 0.7978845608
CUBE = 0.044715
TILE = 128
SEGS = 8
F32 = jnp.float32
BF16 = jnp.bfloat16


def swap_cores(block):
    size = lax.axis_size("ctx")
    return lax.ppermute(block, "ctx", [(i, size - 1 - i) for i in range(size)])


def shifted(block, axis, distance):
    devices = range(lax.axis_size(axis))
    route = [(i - distance, i) for i in devices if i - distance in devices]
    return lax.ppermute(block, axis, route)


def gather_halves(shard, dim):
    half = shard.shape[dim] // 2
    core = lax.axis_index("ctx")
    mine = lax.dynamic_slice_in_dim(shard, core * half, half, dim)
    mine = lax.all_gather(mine, "fsdp", axis=dim)
    other = swap_cores(mine)
    first = jnp.where(core == 0, mine, other)
    second = jnp.where(core == 0, other, mine)
    both = jnp.stack([first, second], axis=dim + 1)
    return both.reshape(shard.shape[:dim] + (-1,) + shard.shape[dim + 1 :])


def split_features(block):
    shards = lax.axis_size("fsdp")
    core = lax.axis_index("ctx")
    parts = block.reshape(block.shape[0], shards, 2, -1)
    return [
        lax.dynamic_index_in_dim(parts, index, 2, False).reshape(block.shape[0], -1)
        for index in (core, 1 - core)
    ]


def pair_sums(left, right, dim):
    rows_to_rows = (((0,), (0,)), ((), ()))

    def product(index):
        pair = (left[index], right) if dim == 0 else (right, left[index])
        return lax.dot_general(*pair, rows_to_rows, preferred_element_type=F32)

    arrived = swap_cores(product(1).astype(BF16))
    return (product(0) + arrived.astype(F32)).astype(BF16)


def half_to_owners(mine, dim):
    return lax.psum_scatter(mine, "fsdp", scatter_dimension=dim, tiled=True)


def both_halves(total, dim):
    other = swap_cores(total)
    core = lax.axis_index("ctx")
    first = jnp.where(core == 0, total, other)
    second = jnp.where(core == 0, other, total)
    return jnp.concatenate([first, second], axis=dim).astype(F32)


def after(value, *others):
    return lax.optimization_barrier((value, *others))[0]


class Square:
    def __init__(self):
        me = lax.axis_index("fsdp")
        row, col = me // 2, me % 2
        self.me = me
        self.core = lax.axis_index("ctx")
        self.near = (row * 2 + 1 - col, (1 - row) * 2 + col)
        self.far = (1 - row) * 2 + 1 - col


def remote(source, target, send, arrive, **device):
    return pltpu.make_async_remote_copy(
        source, target, send, arrive, device_id=device, device_id_type=pl.DeviceIdType.MESH
    )


class Gather:
    def __init__(self, items, stages, send, arrive, local):
        self.items, self.stages = items, stages
        self.send, self.arrive, self.local = send, arrive, local
        self.square = Square()

    def piece(self, w, owner, low, size):
        shard, whole, dim, offset = self.items[w]
        low = pl.multiple_of(owner * shard.shape[dim] + low, 128)
        if dim == 0:
            return whole.at[pl.ds(low, size), pl.ds(offset, shard.shape[1])]
        return whole.at[:, pl.ds(low, size)]

    def copy(self, w, k):
        shard, _, dim, _ = self.items[w]
        square = self.square
        half = shard.shape[dim] // 2
        low = pl.multiple_of(square.core * half, 128)
        first, second = square.near
        if k < 2:
            source = shard.at[pl.ds(low, half), :] if dim == 0 else shard.at[:, pl.ds(low, half)]
            target = self.piece(w, square.me, low, half)
            device = {"fsdp": square.near[k]}
        elif k < 4:
            source = target = self.piece(w, square.near[k - 2], low + (k - 2) * (half // 2), half // 2)
            device = {"fsdp": square.near[3 - k]}
        else:
            source = target = self.piece(w, (first, second, square.far)[k - 4], low, half)
            device = {"ctx": 1 - square.core}
        return remote(source, target, self.send.at[w, k], self.arrive.at[w, k], **device)

    def stage(self, w, out):
        shard = self.items[w][0]
        if out:
            target = self.piece(w, self.square.me, 0, shard.shape[self.items[w][2]])
            return pltpu.make_async_copy(self.stages[w], target, self.local.at[w, 1])
        return pltpu.make_async_copy(shard, self.stages[w], self.local.at[w, 0])

    def start(self, w):
        self.copy(w, 0).start()
        self.copy(w, 1).start()
        self.stage(w, False).start()

    def forward(self, w):
        self.copy(w, 0).wait_recv()
        self.copy(w, 2).start()
        self.copy(w, 1).wait_recv()
        self.copy(w, 3).start()
        self.copy(w, 4).start()
        self.copy(w, 5).start()
        self.stage(w, False).wait()
        self.stage(w, True).start()

    def hand_over(self, w):
        self.copy(w, 2).wait_recv()
        self.copy(w, 3).wait_recv()
        self.copy(w, 6).start()

    def finish(self, w):
        for k in (4, 5, 6):
            self.copy(w, k).wait_recv()
        for k in range(7):
            self.copy(w, k).wait_send()
        self.stage(w, True).wait()


def greet(line, square):
    barrier = pltpu.get_barrier_semaphore()

    def call(**device):
        pl.semaphore_signal(barrier, inc=1, device_id=device, device_id_type=pl.DeviceIdType.MESH)

    peers = 0
    if line:
        count, me = lax.axis_size("tp"), lax.axis_index("tp")

        @pl.when(me > 0)
        def _():
            call(tp=me - 1)

        @pl.when(me < count - 1)
        def _():
            call(tp=me + 1)

        peers = jnp.where((me > 0) & (me < count - 1), 2, 1)
    if square:
        place = Square()
        call(fsdp=place.near[0])
        call(fsdp=place.near[1])
        call(fsdp=place.far)
        call(ctx=1 - place.core)
        peers = peers + 4
    pl.semaphore_wait(barrier, peers)


def line_sum(part, whole, inbox, sems, finish, between):
    count, me = lax.axis_size("tp"), lax.axis_index("tp")
    half = part.shape[0] // 2
    chunks = inbox.shape[1]
    rows = half // chunks
    sum_send, sum_arrive, share_send, share_arrive = sems

    def spot(side, c):
        return pl.ds(pl.multiple_of(side * half + c * rows, rows), rows)

    def place(side):
        return count - 1 - me if side else me

    def onward(side, c, source):
        target = me - 1 if side else me + 1
        return remote(source, inbox.at[side, c], sum_send.at[side, c], sum_arrive.at[side, c], tp=target)

    def share(side, c):
        target = me + 1 if side else me - 1
        block = whole.at[spot(side, c), :]
        return remote(block, block, share_send.at[side, c], share_arrive.at[side, c], tp=target)

    for side in (0, 1):
        @pl.when(place(side) == 0)
        def _():
            onward(side, 0, part.at[spot(side, 0), :]).start()

    def step(t, carry):
        for side in (0, 1):
            here = place(side)
            c = t - here

            @pl.when((here == 0) & (t + 1 < chunks))
            def _():
                onward(side, t + 1, part.at[spot(side, t + 1), :]).start()

            @pl.when((c >= 0) & (c < chunks) & (here > 0))
            def _():
                onward(side, c, inbox.at[side, c]).wait_recv()
                total = (inbox[side, c].astype(F32) + part[spot(side, c), :].astype(F32)).astype(BF16)

                @pl.when(here < count - 1)
                def _():
                    inbox[side, c] = total
                    onward(side, c, inbox.at[side, c]).start()

                @pl.when(here == count - 1)
                def _():
                    whole[spot(side, c), :] = total
                    share(side, c).start()
                    finish(spot(side, c))

        for side in (0, 1):
            here = place(side)
            c = t - 2 * (count - 1) + here

            @pl.when((c >= 0) & (c < chunks) & (here < count - 1))
            def _():
                share(side, c).wait_recv()

                @pl.when(here > 0)
                def _():
                    share(side, c).start()

                finish(spot(side, c))

        between(t)
        return carry

    lax.fori_loop(0, chunks + 2 * (count - 1), step, 0)

    def drain(c, carry):
        for side in (0, 1):
            here = place(side)

            @pl.when(here < count - 1)
            def _():
                onward(side, c, inbox.at[side, c]).wait_send()

            @pl.when(here > 0)
            def _():
                share(side, c).wait_send()

        return carry

    lax.fori_loop(0, chunks, drain, 0)


def put_split(ref, rows, block):
    core = lax.axis_index("ctx")
    size = block.shape[1] // 8
    for owner in range(4):
        for index in range(2):
            low = (2 * owner + index) * size
            ref[(index + core) % 2, rows, owner * size : (owner + 1) * size] = block[:, low : low + size]


CHUNK = 32
LINE_COST = pl.CostEstimate(flops=0, bytes_accessed=400_000_000, transcendentals=0)


def enter_kernel(
    tokens, upstream, gain_shard, recur, gelu, merge,
    normed, halves, upstream_halves, gains, whole_in, whole_merge,
    stage_recur, stage_gelu, stage_merge, send, arrive, local, gain_send, gain_arrive,
):
    square = Square()
    greet(False, True)
    width = gain_shard.shape[1]

    def gain_copy(k, owner, target):
        spot = gains.at[:, pl.ds(pl.multiple_of(owner * width, 128), width)]
        return remote(gain_shard, spot, gain_send.at[k], gain_arrive.at[k], fsdp=target)

    others = (*square.near, square.far)
    for k, target in enumerate(others):
        gain_copy(k, square.me, target).start()
    gather = Gather(
        [(recur, whole_in, 0, 0), (gelu, whole_in, 0, recur.shape[1]), (merge, whole_merge, 1, 0)],
        (stage_recur, stage_gelu, stage_merge), send, arrive, local,
    )
    for w in range(3):
        gather.start(w)
    gains[:, pl.ds(pl.multiple_of(square.me * width, 128), width)] = gain_shard[...]
    for k, owner in enumerate(others):
        gain_copy(k, owner, owner).wait_recv()

    def norm(t, carry):
        rows = pl.ds(pl.multiple_of(t * CHUNK, CHUNK), CHUNK)
        block = tokens[rows, :].astype(F32)
        block = (block * rms_scale(block) * gains[0:1, :]).astype(BF16)
        normed[rows, :] = block
        put_split(halves, rows, block)
        put_split(upstream_halves, rows, upstream[rows, :])
        return carry

    lax.fori_loop(0, tokens.shape[0] // CHUNK, norm, 0)
    for w in range(3):
        gather.forward(w)
    for w in range(3):
        gather.hand_over(w)
    for w in range(3):
        gather.finish(w)
    for k, target in enumerate(others):
        gain_copy(k, square.me, target).wait_send()


ANY = pl.BlockSpec(memory_space=pl.ANY)
NEAR = pl.BlockSpec(memory_space=pltpu.VMEM)


def gather_scratch(shards):
    count = len(shards)
    dma = pltpu.SemaphoreType.DMA
    return [pltpu.VMEM(w.shape, w.dtype) for w in shards] + [dma((count, 7)), dma((count, 7)), dma((count, 2))]


def enter(tokens, upstream, gain_shard, recur, gelu, merge):
    rows, features = tokens.shape
    shape = jax.ShapeDtypeStruct
    inner = recur.shape[1]
    dma = pltpu.SemaphoreType.DMA
    return pl.pallas_call(
        enter_kernel,
        out_shape=(
            shape((rows, features), BF16),
            shape((2, rows, features // 2), BF16),
            shape((2, rows, features // 2), BF16),
            shape((8, features), F32),
            shape((features, 2 * inner), BF16),
            shape((inner, features), BF16),
        ),
        in_specs=[NEAR, NEAR, NEAR, ANY, ANY, ANY],
        out_specs=[NEAR, NEAR, NEAR, NEAR, ANY, ANY],
        scratch_shapes=gather_scratch([recur, gelu, merge]) + [dma((3,)), dma((3,))],
        compiler_params=pltpu.CompilerParams(collective_id=1, has_side_effects=True),
        name="enter",
    )(tokens, upstream, gain_shard, recur, gelu, merge)


def line_scratch(rows, features):
    chunks = rows // 2 // CHUNK
    dma = pltpu.SemaphoreType.DMA((2, chunks))
    return [pltpu.VMEM((2, chunks, CHUNK, features), BF16), dma, dma, dma, dma]


def middle_kernel(gathers, part, tokens, gains, *refs):
    if gathers:
        gate, up, down, merged, normed, halves, whole_in, whole_down = refs[:8]
        inbox, *rest = refs[8:]
        sems, (stage_gate, stage_up, stage_down, send, arrive, local) = rest[:4], rest[4:]
        gather = Gather(
            [(gate, whole_in, 0, 0), (up, whole_in, 0, gate.shape[1]), (down, whole_down, 1, 0)],
            (stage_gate, stage_up, stage_down), send, arrive, local,
        )
        greet(True, True)
        for w in range(3):
            gather.start(w)
    else:
        merged, normed, inbox, *sems = refs
        greet(True, False)

    def finish(rows):
        block = tokens[rows, :].astype(F32) + merged[rows, :].astype(F32)
        block = (block * rms_scale(block) * gains[1:2, :]).astype(BF16)
        normed[rows, :] = block
        if gathers:
            put_split(halves, rows, block)

    def between(t):
        if gathers:
            for w in range(3):
                @pl.when(t == 5 + 4 * w)
                def _():
                    gather.forward(w)

                @pl.when(t == 17 + w)
                def _():
                    gather.hand_over(w)

    line_sum(part, merged, inbox, sems, finish, between)
    if gathers:
        for w in range(3):
            gather.finish(w)


def middle(part, tokens, gains, shards):
    rows, features = tokens.shape
    shape = jax.ShapeDtypeStruct
    whole = shape((rows, features), BF16)
    outs, specs = [whole, whole], [NEAR, NEAR]
    scratch = line_scratch(rows, features)
    if shards:
        gate, up, down = shards
        outs += [
            shape((2, rows, features // 2), BF16),
            shape((features, 2 * gate.shape[1]), BF16),
            shape((down.shape[0], features), BF16),
        ]
        specs += [NEAR, ANY, ANY]
        scratch += gather_scratch(shards)
    return pl.pallas_call(
        lambda *refs: middle_kernel(bool(shards), *refs),
        out_shape=tuple(outs),
        in_specs=[NEAR, NEAR, NEAR] + [ANY] * len(shards),
        out_specs=specs,
        scratch_shapes=scratch,
        compiler_params=pltpu.CompilerParams(collective_id=2, has_side_effects=True),
        cost_estimate=LINE_COST,
        name="middle",
    )(part, tokens, gains, *shards)


def turn_kernel(split, part, tokens, merged, upstream, gains, own, grad_in, gain_sum, *refs):
    if split:
        halves, whole, wide, inbox, *sems = refs
    else:
        whole, wide, inbox, *sems = refs
    greet(True, False)
    gain_sum[...] = jnp.zeros_like(gain_sum)
    width = own.shape[1]
    start = pl.multiple_of(lax.axis_index("tp") * width, 128)

    def finish(rows):
        block = tokens[rows, :].astype(F32) + merged[rows, :].astype(F32)
        scale = rms_scale(block)
        grad = whole[rows, :].astype(F32)
        gain_sum[0:1, :] += jnp.sum(grad * (block * scale), axis=0, keepdims=True)
        grad = grad * gains[1:2, :]
        mean = jnp.mean(block * grad, axis=-1, keepdims=True)
        grad = upstream[rows, :].astype(F32) + scale * grad - block * (scale * scale * scale * mean)
        wide[...] = grad
        own[rows, :] = wide[:, pl.ds(start, width)]
        grad = grad.astype(BF16)
        grad_in[rows, :] = grad
        if split:
            put_split(halves, rows, grad)

    line_sum(part, whole, inbox, sems, finish, lambda t: None)


def turn(part, tokens, merged, upstream, gains, split):
    rows, features = tokens.shape
    shape = jax.ShapeDtypeStruct
    outs = [
        shape((rows, features // lax.axis_size("tp")), F32),
        shape((rows, features), BF16),
        shape((8, features), F32),
    ]
    if split:
        outs.append(shape((2, rows, features // 2), BF16))
    return pl.pallas_call(
        lambda *refs: turn_kernel(split, *refs),
        out_shape=tuple(outs),
        in_specs=[NEAR] * 5,
        out_specs=[NEAR] * len(outs),
        scratch_shapes=[pltpu.VMEM((rows, features), BF16), pltpu.VMEM((CHUNK, features), F32)]
        + line_scratch(rows, features),
        compiler_params=pltpu.CompilerParams(collective_id=3, has_side_effects=True),
        cost_estimate=LINE_COST,
        name="turn",
    )(part, tokens, merged, upstream, gains)


def gelu_pair(q):
    tanh = jnp.tanh(ROOT * (q + CUBE * q * q * q))
    value = 0.5 * q * (1.0 + tanh)
    slope = 0.5 * (1.0 + tanh) + 0.5 * q * (1.0 - tanh * tanh) * ROOT * (1.0 + 3.0 * CUBE * q * q)
    return value, slope


def rms_scale(values):
    return lax.rsqrt(jnp.mean(values * values, axis=-1, keepdims=True) + EPS)


def decay_parts(rate, softer, keep):
    gap = 2.0 * CGAIN * rate * softer
    decay = jnp.exp(-0.5 * gap)
    series = gap * (
        1.0
        - gap / 2.0
        * (1.0 - gap / 3.0 * (1.0 - gap / 4.0 * (1.0 - gap / 5.0 * (1.0 - gap / 6.0 * (1.0 - gap / 7.0)))))
    )
    square = jnp.where(gap < 0.25, series, 1.0 - decay * decay)
    return jnp.where(keep, decay, 0.0), jnp.where(keep, square, 1.0)


LANES = 128


def put_lanes(ref, block, rows):
    for lane in range(ref.shape[0]):
        ref[lane, 0:rows, :] = block[:, lane * LANES : (lane + 1) * LANES]


def sweep(decay_ref, value_ref, state_ref, product_ref, out_ref, run_ref, carry_ref, reverse, offset):
    groups, rows, _ = value_ref.shape
    steps = rows // SEGS
    place = lax.broadcasted_iota(jnp.int32, (SEGS, LANES), 0)
    if reverse:
        place = SEGS - 1 - place

    def moved(block, by, fill):
        turned = pltpu.roll(block, SEGS - by if reverse else by, 0)
        return jnp.where(place >= by, turned, fill)

    for lane in range(groups):
        lanes = slice(lane * LANES, (lane + 1) * LANES)
        state = jnp.zeros((SEGS, LANES), F32)
        product = jnp.ones((SEGS, LANES), F32)
        for step in reversed(range(steps)) if reverse else range(steps):
            spot = pl.ds(step, SEGS, stride=steps)
            decay = decay_ref[lane, pl.ds(step + offset, SEGS, stride=steps), :]
            state = decay * state + value_ref[lane, spot, :]
            product = product * decay
            state_ref[lane, spot, :] = state
            product_ref[lane, spot, :] = product
        for by in (1, 2, 4):
            state = state + product * moved(state, by, 0.0)
            product = product * moved(product, by, 1.0)
        carry = carry_ref[0:1, lanes]
        carry_run = carry_ref[8:9, lanes]
        state = state + product * carry
        product = product * carry_run
        enter = moved(state, 1, carry)
        enter_run = moved(product, 1, carry_run)
        for seg in range(SEGS):
            span = slice(seg * steps, (seg + 1) * steps)
            inner = product_ref[lane, span, :]
            out_ref[span, lanes] = state_ref[lane, span, :] + inner * enter[seg : seg + 1, :]
            run_ref[span, lanes] = inner * enter_run[seg : seg + 1, :]
        last = 0 if reverse else SEGS - 1
        carry_ref[0:1, lanes] = state[last : last + 1, :]
        carry_ref[8:9, lanes] = product[last : last + 1, :]


def spread_blocks(blocks_ref, out_ref):
    chans, size = blocks_ref.shape[1:]
    row = lax.broadcasted_iota(jnp.int32, (chans, chans), 0)
    col = lax.broadcasted_iota(jnp.int32, (chans, chans), 1)
    inner = lax.broadcasted_iota(jnp.int32, (size, chans), 0)
    outer = lax.broadcasted_iota(jnp.int32, (size, chans), 1)
    inside = row < 0
    repeat = outer < 0
    for low in range(0, chans, size):
        inside |= (row >= low) & (row < low + size) & (col >= low) & (col < low + size)
        repeat |= outer - low == inner
    repeat = repeat.astype(F32).astype(BF16)
    for gate in range(2):
        wide = jnp.dot(blocks_ref[gate], repeat, preferred_element_type=F32)
        out_ref[:, gate * chans : (gate + 1) * chans] = jnp.where(inside, wide, 0.0).astype(BF16)


def forward_kernel(
    branch_ref, halo_ref, mask_ref, taps_ref, bias_ref, blocks_ref, gate_bias_ref, softer_ref,
    conv_ref, rate_ref, entry_ref, state_ref, run_ref, gates_ref,
    window, decay, value, inner, product, carry,
):
    rows, chans = conv_ref.shape
    spot = pl.program_id(0)

    @pl.when(spot == 0)
    def _():
        spread_blocks(blocks_ref, gates_ref)
        window[0:8, :] = halo_ref[...].astype(F32)
        carry[0:8, :] = jnp.zeros((8, chans), F32)
        carry[8:16, :] = jnp.ones((8, chans), F32)

    @pl.when(spot > 0)
    def _():
        window[0:8, :] = window[rows : rows + 8, :]

    window[8 : rows + 8, :] = branch_ref[...].astype(F32)
    mixed = bias_ref[...] + taps_ref[0:1, :] * window[8 : rows + 8, :]
    for shift in range(1, taps_ref.shape[0]):
        moved = window[8 - shift : 8 - shift + rows, :]
        mixed = mixed + taps_ref[shift : shift + 1, :] * (moved * mask_ref[:, shift : shift + 1])
    conv = mixed.astype(BF16)
    conv_ref[...] = conv
    pre = jnp.dot(conv, gates_ref[...], preferred_element_type=F32) + gate_bias_ref[...]
    rate = jax.nn.sigmoid(pre[:, :chans])
    entry = jax.nn.sigmoid(pre[:, chans:])
    rate_ref[...] = rate
    entry_ref[...] = entry
    keep = jnp.broadcast_to(mask_ref[:, 0:1], (rows, chans)) > 0.5
    step, square = decay_parts(rate, softer_ref[...], keep)
    put_lanes(decay, step, rows)
    put_lanes(value, jnp.sqrt(square) * entry * conv.astype(F32), rows)
    sweep(decay, value, inner, product, state_ref, run_ref, carry, False, 0)


def tile_spec(width, count=None):
    if count is None:
        return pl.BlockSpec((TILE, width), lambda i: (i, 0))
    return pl.BlockSpec((TILE, width), lambda i: (count - 1 - i, 0))


def fixed_spec(shape):
    return pl.BlockSpec(shape, lambda i: (0, 0))


def recur_forward(branch, halo, masks, taps, bias, blocks, gate_bias, softer):
    rows, chans = branch.shape[0], halo.shape[1]
    wide = jax.ShapeDtypeStruct((rows, chans), F32)
    return pl.pallas_call(
        forward_kernel,
        grid=(rows // TILE,),
        out_shape=(
            jax.ShapeDtypeStruct((rows, chans), BF16), wide, wide, wide, wide,
            jax.ShapeDtypeStruct((chans, 2 * chans), BF16),
        ),
        in_specs=[
            tile_spec(chans),
            fixed_spec((8, chans)),
            tile_spec(masks.shape[1]),
            fixed_spec(taps.shape),
            fixed_spec((1, chans)),
            pl.BlockSpec(blocks.shape, lambda i: (0, 0, 0)),
            fixed_spec((1, 2 * chans)),
            fixed_spec((1, chans)),
        ],
        out_specs=[tile_spec(chans)] * 5 + [fixed_spec((chans, 2 * chans))],
        scratch_shapes=[
            pltpu.VMEM((TILE + 8, chans), F32),
            pltpu.VMEM((chans // LANES, TILE, LANES), F32),
            pltpu.VMEM((chans // LANES, TILE, LANES), F32),
            pltpu.VMEM((chans // LANES, TILE, LANES), F32),
            pltpu.VMEM((chans // LANES, TILE, LANES), F32),
            pltpu.VMEM((16, chans), F32),
        ],
        cost_estimate=pl.CostEstimate(
            flops=2 * rows * chans * 2 * chans, bytes_accessed=24 * rows * chans, transcendentals=5 * rows * chans
        ),
        name="recur_forward",
    )(branch, halo, masks, taps, bias, blocks, gate_bias, softer)


def merge_kernel(local_ref, run_ref, enter_ref, pre_ref, weight_ref, state_ref, gated_ref, part_ref):
    state = local_ref[...] + run_ref[...] * enter_ref[0:1, :]
    state_ref[...] = state
    pre = pre_ref[...].astype(F32)
    gated = (state * gelu_pair(pre)[0]).astype(BF16)
    gated_ref[...] = gated
    part_ref[...] = jnp.dot(gated, weight_ref[...], preferred_element_type=F32).astype(BF16)


def merge_states(local, run, enter, branches, weight):
    rows, chans = local.shape
    features = weight.shape[1]
    shape = jax.ShapeDtypeStruct
    return pl.pallas_call(
        merge_kernel,
        grid=(rows // TILE,),
        out_shape=(shape((rows, chans), F32), shape((rows, chans), BF16), shape((rows, features), BF16)),
        in_specs=[
            tile_spec(chans), tile_spec(chans), fixed_spec((1, chans)),
            pl.BlockSpec((TILE, chans), lambda i: (i, 1)),
            fixed_spec(weight.shape),
        ],
        out_specs=[tile_spec(chans), tile_spec(chans), tile_spec(features)],
        cost_estimate=pl.CostEstimate(
            flops=2 * rows * chans * features, bytes_accessed=16 * rows * chans, transcendentals=rows * chans
        ),
        name="merge_states",
    )(local, run, enter, branches, weight)


def adjoint_kernel(
    rate_ref, up_ref, pre_ref, state_ref, mask_ref, softer_ref,
    grad_ref, run_ref, head_ref, pre_grad_ref,
    decay, value, inner, product, carry,
):
    rows, chans = rate_ref.shape
    groups = chans // LANES
    spot = pl.program_id(0)

    @pl.when(spot == 0)
    def _():
        for lane in range(groups):
            decay[lane, rows : rows + 8, :] = jnp.ones((8, LANES), F32)
        carry[0:8, :] = jnp.zeros((8, chans), F32)
        carry[8:16, :] = jnp.ones((8, chans), F32)

    @pl.when(spot > 0)
    def _():
        for lane in range(groups):
            decay[lane, rows : rows + 8, :] = decay[lane, 0:8, :]

    keep = jnp.broadcast_to(mask_ref[:, 0:1], (rows, chans)) > 0.5
    gap = CGAIN * rate_ref[...] * softer_ref[...]
    step = jnp.where(keep, jnp.exp(-gap), 0.0)
    put_lanes(decay, step, rows)
    gate, slope = gelu_pair(pre_ref[...].astype(F32))
    up = up_ref[...]
    pre_grad_ref[...] = (up * state_ref[...] * slope).astype(BF16)
    put_lanes(value, up * gate, rows)
    sweep(decay, value, inner, product, grad_ref, run_ref, carry, True, 1)
    head_ref[...] = jnp.broadcast_to(step[0:1, :] * carry[0:1, :], (8, chans))


def recur_adjoint(rate, up, branches, state, masks, softer):
    rows, chans = rate.shape
    count = rows // TILE
    wide = jax.ShapeDtypeStruct((rows, chans), F32)
    return pl.pallas_call(
        adjoint_kernel,
        grid=(count,),
        out_shape=(
            wide, wide, jax.ShapeDtypeStruct((8, chans), F32), jax.ShapeDtypeStruct((rows, chans), BF16)
        ),
        in_specs=[
            tile_spec(chans, count),
            tile_spec(chans, count),
            pl.BlockSpec((TILE, chans), lambda i: (count - 1 - i, 1)),
            tile_spec(chans, count),
            tile_spec(masks.shape[1], count),
            fixed_spec((1, chans)),
        ],
        out_specs=[tile_spec(chans, count), tile_spec(chans, count), fixed_spec((8, chans)), tile_spec(chans, count)],
        scratch_shapes=[
            pltpu.VMEM((chans // LANES, TILE + 8, LANES), F32),
            pltpu.VMEM((chans // LANES, TILE, LANES), F32),
            pltpu.VMEM((chans // LANES, TILE, LANES), F32),
            pltpu.VMEM((chans // LANES, TILE, LANES), F32),
            pltpu.VMEM((16, chans), F32),
        ],
        cost_estimate=pl.CostEstimate(
            flops=8 * rows * chans, bytes_accessed=16 * rows * chans, transcendentals=rows * chans
        ),
        name="recur_adjoint",
    )(rate, up, branches, state, masks, softer)


def backward_kernel(
    grad_ref, run_ref, enter_ref, rate_ref, entry_ref, conv_ref, state_ref, mask_ref,
    branch_ref, pre_grad_ref, halo_ref, taps_ref, gates_ref, softer_ref,
    back_ref, tail_ref, head_ref, gate_grad_ref, sums_ref,
    shifts, edge,
):
    rows, chans = conv_ref.shape
    width = taps_ref.shape[0]
    spot = pl.program_id(0)
    last = pl.num_programs(0) - 1

    @pl.when(spot == 0)
    def _():
        for shift in range(1, width):
            shifts[shift - 1, rows : rows + 8, :] = jnp.zeros((8, chans), F32)
        gate_grad_ref[...] = jnp.zeros_like(gate_grad_ref)
        sums_ref[...] = jnp.zeros_like(sums_ref)

    @pl.when(spot > 0)
    def _():
        for shift in range(1, width):
            shifts[shift - 1, rows : rows + 8, :] = shifts[shift - 1, 0:8, :]

    keep = jnp.broadcast_to(mask_ref[:, 0:1], (rows, chans)) > 0.5
    softer = softer_ref[...]
    rate = rate_ref[...]
    entry = entry_ref[...]
    conv = conv_ref[...].astype(F32)
    grad = grad_ref[...] + run_ref[...] * enter_ref[0:1, :]
    step, square = decay_parts(rate, softer, keep)
    inverse = lax.rsqrt(square)
    mult = square * inverse
    driven = entry * conv
    carried = state_ref[...] - mult * driven
    d_log = jnp.where(keep, grad * (carried - driven * step * step * inverse), 0.0)
    d_rate = (-CGAIN * softer * d_log * rate * (1.0 - rate)).astype(BF16)
    lifted = grad * mult * entry
    d_entry = (lifted * conv * (1.0 - entry)).astype(BF16)
    both = jnp.concatenate([d_rate, d_entry], axis=1)
    d_conv = lifted + lax.dot_general(
        both, gates_ref[...], (((1,), (1,)), ((), ())), preferred_element_type=F32
    )
    gate_grad_ref[...] += lax.dot_general(
        conv_ref[...], both, (((0,), (0,)), ((), ())), preferred_element_type=F32
    )

    def add_row(row, block):
        sums_ref[row : row + 1, :] += jnp.sum(block, axis=0, keepdims=True)

    branch = branch_ref[...].astype(F32)
    add_row(0, d_log * rate)
    add_row(1, d_rate.astype(F32))
    add_row(2, d_entry.astype(F32))
    add_row(3, d_conv)
    add_row(4, d_conv * branch)
    back = taps_ref[0:1, :] * d_conv
    for shift in range(1, width):
        shifts[shift - 1, 0:rows, :] = d_conv * mask_ref[:, shift : shift + 1]
        moved = shifts[shift - 1, shift : shift + rows, :]
        add_row(4 + shift, moved * branch)
        back = back + taps_ref[shift : shift + 1, :] * moved
    back_ref[:, 0:chans] = back.astype(BF16)
    back_ref[:, chans:] = pre_grad_ref[...]

    @pl.when(spot == 0)
    def _():
        tail_ref[...] = back[rows - 8 :, :]

    @pl.when(spot == last)
    def _():
        halo = halo_ref[...].astype(F32)
        head = jnp.zeros((8, chans), F32)
        edge[0:8, :] = head
        for shift in range(1, width):
            edge[8:16, :] = shifts[shift - 1, 0:8, :]
            moved = edge[shift : shift + 8, :]
            add_row(4 + shift, moved * halo)
            head = head + taps_ref[shift : shift + 1, :] * moved
        head_ref[...] = head


def recur_backward(grad, run, enter, rate, entry, conv, state, masks, branch, pre_grad, halo, taps, gates, softer):
    rows, chans = rate.shape
    count = rows // TILE
    edge = jax.ShapeDtypeStruct((8, chans), F32)
    wide = tile_spec(chans, count)
    return pl.pallas_call(
        backward_kernel,
        grid=(count,),
        out_shape=(
            jax.ShapeDtypeStruct((rows, 2 * chans), BF16),
            edge,
            edge,
            jax.ShapeDtypeStruct((chans, 2 * chans), F32),
            jax.ShapeDtypeStruct((16, chans), F32),
        ),
        in_specs=[
            wide, wide, fixed_spec((1, chans)), wide, wide, wide, wide,
            tile_spec(masks.shape[1], count),
            wide,
            wide,
            fixed_spec((8, chans)),
            fixed_spec(taps.shape),
            fixed_spec(gates.shape),
            fixed_spec((1, chans)),
        ],
        out_specs=[
            tile_spec(2 * chans, count),
            fixed_spec((8, chans)),
            fixed_spec((8, chans)),
            fixed_spec((chans, 2 * chans)),
            fixed_spec((16, chans)),
        ],
        scratch_shapes=[
            pltpu.VMEM((taps.shape[0] - 1, TILE + 8, chans), F32),
            pltpu.VMEM((16, chans), F32),
        ],
        cost_estimate=pl.CostEstimate(
            flops=8 * rows * chans * chans, bytes_accessed=28 * rows * chans, transcendentals=2 * rows * chans
        ),
        name="recur_backward",
    )(grad, run, enter, rate, entry, conv, state, masks, branch, pre_grad, halo, taps, gates, softer)


def shards(
    tokens,
    segments,
    cotangent,
    w_recur,
    w_gelu,
    w_merge,
    w_gate,
    w_up,
    w_down,
    norm_mix,
    norm_feed,
    conv_taps,
    conv_bias,
    rate_gate,
    entry_gate,
    rate_bias,
    entry_bias,
    decay_logit,
):
    piece = tokens.shape[0]
    width = conv_taps.shape[0]
    edge = width - 1
    heads, block = rate_gate.shape[0], rate_gate.shape[1]
    chans = conv_taps.shape[1]
    features = tokens.shape[1]
    feat_local = features // lax.axis_size("tp")
    feat_start = lax.axis_index("tp") * feat_local

    square = lax.axis_size("fsdp") == 4
    gain_shard = jnp.concatenate(
        [jnp.stack([norm_mix, norm_feed]).astype(F32), jnp.zeros((6, norm_mix.shape[0]), F32)], axis=0
    )
    if square:
        normed, normed_split, cotangent_split, gains, whole_in, whole_merge = enter(
            tokens, cotangent, gain_shard, w_recur, w_gelu, w_merge
        )
    else:
        whole_in = gather_halves(jnp.concatenate([w_recur, w_gelu], axis=1), 0)
        whole_merge = gather_halves(w_merge, 1)
        gains = lax.all_gather(gain_shard, "fsdp", axis=1, tiled=True)
        inputs = tokens.astype(F32)
        normed = (inputs * rms_scale(inputs) * gains[0:1]).astype(BF16)
        normed_split = split_features(normed)
        cotangent_split = split_features(cotangent)
    gain_one = gains[0:1]

    padded_ids = jnp.concatenate([jnp.full((edge,), -1, jnp.int32), segments])
    local_ids = lax.dynamic_slice_in_dim(padded_ids, lax.axis_index("ctx") * piece, piece + edge)
    own_ids = local_ids[edge:]
    masks = jnp.stack(
        [(local_ids[edge - max(shift, 1) : edge - max(shift, 1) + piece] == own_ids) for shift in range(width)],
        axis=1,
    ).astype(F32)
    taps = conv_taps.astype(F32)
    blocks = jnp.stack([rate_gate.reshape(chans, block), entry_gate.reshape(chans, block)])
    gate_bias = jnp.concatenate([rate_bias, entry_bias]).astype(F32)[None, :]
    softer = jax.nn.softplus(-decay_logit)[None, :]

    rows_to_features = (((1,), (1,)), ((), ()))
    branches = jnp.dot(normed, whole_in, preferred_element_type=F32).astype(BF16)
    halo = shifted(branches[piece - 8 :, :chans], "ctx", 1)
    conv, rate, entry, local_state, run, gates = recur_forward(
        branches, halo, masks, taps, conv_bias.astype(F32)[None, :], blocks, gate_bias, softer
    )
    state_in = shifted(local_state[piece - 8 :], "ctx", 1)[7:8]
    states, gated, part_merge = merge_states(local_state, run, state_in, branches, whole_merge)

    if square:
        merged, normed_two, normed_two_split, whole_mid, whole_down = middle(
            part_merge, tokens, gains, (w_gate, w_up, w_down)
        )
    else:
        merged, normed_two = middle(part_merge, tokens, gains, ())
        normed_two_split = split_features(normed_two)
        whole_mid = gather_halves(jnp.concatenate([w_gate, w_up], axis=1), 0)
        whole_down = gather_halves(w_down, 1)

    units = w_gate.shape[1]
    pre_mid = jnp.dot(normed_two, whole_mid, preferred_element_type=F32).astype(BF16)
    d_hidden = lax.dot_general(cotangent, whole_down, rows_to_features, preferred_element_type=F32).astype(BF16)
    gate_act, gate_slope = gelu_pair(pre_mid[:, :units].astype(F32))
    up_vals = pre_mid[:, units:].astype(F32)
    wide_hidden = d_hidden.astype(F32)
    hidden = (gate_act * up_vals).astype(BF16)
    d_mid = jnp.concatenate(
        [(wide_hidden * up_vals * gate_slope).astype(BF16), (wide_hidden * gate_act).astype(BF16)], axis=1
    )
    part_two = lax.dot_general(d_mid, whole_mid, rows_to_features, preferred_element_type=F32).astype(BF16)
    pair_down = pair_sums(cotangent_split, hidden, 1)
    pair_mid = pair_sums(normed_two_split, d_mid, 0)
    part_two = after(part_two, pair_down, pair_mid)
    turned = turn(part_two, tokens, merged, cotangent, gains, square)
    own_resid_grad, d_merge_in, feed_sums = turned[:3]
    d_merge_split = turned[3] if square else split_features(d_merge_in)
    half_down = half_to_owners(pair_down, 1)
    half_mid = half_to_owners(pair_mid, 0)
    d_merge_in = after(d_merge_in, half_down, half_mid)

    part_feed = jnp.dot(after(hidden, d_merge_in), whole_down, preferred_element_type=F32).astype(BF16)
    feed = lax.psum_scatter(part_feed, "tp", scatter_dimension=1, tiled=True)
    d_merge_in = after(d_merge_in, part_feed)
    d_gated = lax.dot_general(d_merge_in, whole_merge, rows_to_features, preferred_element_type=F32)
    local_grad, grad_run, first, d_gelu_pre = recur_adjoint(rate, d_gated, branches, states, masks, softer)
    grad_in = shifted(first, "ctx", -1)[0:1]
    back, tail, head, gate_grads, sums = recur_backward(
        local_grad, grad_run, grad_in, rate, entry, conv, states, masks, branches, d_gelu_pre,
        halo, taps, gates, softer
    )
    returned = shifted(head, "ctx", -1)
    d_in = lax.dynamic_update_slice(back, (tail + returned).astype(BF16), (piece - 8, 0))
    part_one = lax.dot_general(d_in, whole_in, rows_to_features, preferred_element_type=F32).astype(BF16)
    part_one = after(part_one, feed)
    d_normed = lax.psum_scatter(part_one, "tp", scatter_dimension=1, tiled=True)

    pair_merge = pair_sums(d_merge_split, after(gated, part_one), 1)
    pair_in = pair_sums(normed_split, after(d_in, part_one), 0)
    half_in = half_to_owners(after(pair_in, d_normed), 0)
    half_merge = half_to_owners(after(pair_merge, d_normed), 1)
    inputs = tokens.astype(F32)
    scale_one = rms_scale(inputs)
    wide_part = part_one.astype(F32)
    stat_one = jnp.sum(wide_part * inputs * gain_one, axis=-1)
    grad_mix = jnp.sum(wide_part * inputs * scale_one, axis=0)
    norm_sums = jnp.stack([grad_mix, feed_sums[0] / lax.axis_size("tp")])
    lines = -(-norm_sums.size // chans)
    flat = jnp.pad(norm_sums.reshape(-1), (0, lines * chans - norm_sums.size)).reshape(lines, chans)
    row_sums = lax.psum(jnp.concatenate([sums, flat], axis=0), ("fsdp", "ctx"))
    norm_sums = row_sums[sums.shape[0] :].reshape(-1)[: norm_sums.size]
    line_sums = lax.psum(jnp.concatenate([stat_one, norm_sums]), "tp")
    stat_one = line_sums[:piece][:, None] / features
    both_norms = line_sums[piece:].reshape(2, features)

    shard_down = both_halves(half_down, 1)
    shard_mid = both_halves(half_mid, 0)
    shard_merge = both_halves(half_merge, 1)
    shard_in = both_halves(half_in, 0)

    def own(block):
        return lax.dynamic_slice_in_dim(block, feat_start, feat_local, 1)

    own_inputs = own(inputs)
    output = (own_inputs + own(merged).astype(F32) + feed.astype(F32)).astype(BF16)
    grad_tokens = (
        own_resid_grad
        + scale_one * d_normed.astype(F32) * own(gain_one)
        - own_inputs * scale_one**3 * stat_one
    ).astype(BF16)

    norm_local = norm_mix.shape[0]
    own_norms = lax.dynamic_slice_in_dim(both_norms, lax.axis_index("fsdp") * norm_local, norm_local, 1)

    diagonal = [
        gate_grads[i * block : (i + 1) * block, part * chans + i * block : part * chans + (i + 1) * block]
        for part in range(2)
        for i in range(heads)
    ]
    gate_sums = lax.psum(jnp.stack(diagonal).astype(BF16), ("fsdp", "ctx")).astype(F32)
    return (
        output,
        grad_tokens,
        shard_in[:, :chans],
        shard_in[:, chans:],
        shard_merge,
        shard_mid[:, :units],
        shard_mid[:, units:],
        shard_down,
        own_norms[0],
        own_norms[1],
        row_sums[4 : 4 + width],
        row_sums[3],
        gate_sums[:heads],
        gate_sums[heads:],
        row_sums[1],
        row_sums[2],
        CGAIN * row_sums[0] * jax.nn.sigmoid(-decay_logit),
    )


def solution(mesh):
    placed = (
        P(("fsdp", "ctx"), None),
        P("fsdp"),
        P(("fsdp", "ctx"), None),
        P("fsdp", "tp"),
        P("fsdp", "tp"),
        P("tp", "fsdp"),
        P("fsdp", "tp"),
        P("fsdp", "tp"),
        P("tp", "fsdp"),
        P("fsdp"),
        P("fsdp"),
        P(None, "tp"),
        P("tp"),
        P("tp", None, None),
        P("tp", None, None),
        P("tp"),
        P("tp"),
        P("tp"),
    )
    return jax.shard_map(
        shards,
        mesh=mesh,
        in_specs=placed,
        out_specs=(
            P(("fsdp", "ctx"), "tp"),
            P(("fsdp", "ctx"), "tp"),
            P("fsdp", "tp"),
            P("fsdp", "tp"),
            P("tp", "fsdp"),
            P("fsdp", "tp"),
            P("fsdp", "tp"),
            P("tp", "fsdp"),
            P("fsdp"),
            P("fsdp"),
            P(None, "tp"),
            P("tp"),
            P("tp", None, None),
            P("tp", None, None),
            P("tp"),
            P("tp"),
            P("tp"),
        ),
        check_vma=False,
    )
```

```python
import jax
import jax.numpy as jnp
from jax import lax
from jax.experimental import pallas as pl
from jax.experimental.pallas import tpu as pltpu
from jax.sharding import PartitionSpec as P

EPS = 1e-06
CGAIN = 8.0
ROOT = 0.7978845608
CUBE = 0.044715
TILE = 128
SEGS = 8
F32 = jnp.float32
BF16 = jnp.bfloat16


def swap_cores(block):
    size = lax.axis_size("ctx")
    return lax.ppermute(block, "ctx", [(i, size - 1 - i) for i in range(size)])


def shifted(block, axis, distance):
    devices = range(lax.axis_size(axis))
    route = [(i - distance, i) for i in devices if i - distance in devices]
    return lax.ppermute(block, axis, route)


def gather_halves(shard, dim):
    half = shard.shape[dim] // 2
    core = lax.axis_index("ctx")
    mine = lax.dynamic_slice_in_dim(shard, core * half, half, dim)
    mine = lax.all_gather(mine, "fsdp", axis=dim)
    other = swap_cores(mine)
    first = jnp.where(core == 0, mine, other)
    second = jnp.where(core == 0, other, mine)
    both = jnp.stack([first, second], axis=dim + 1)
    return both.reshape(shard.shape[:dim] + (-1,) + shard.shape[dim + 1 :])


def split_features(block):
    shards = lax.axis_size("fsdp")
    core = lax.axis_index("ctx")
    parts = block.reshape(block.shape[0], shards, 2, -1)
    return [
        lax.dynamic_index_in_dim(parts, index, 2, False).reshape(block.shape[0], -1)
        for index in (core, 1 - core)
    ]


def pair_sums(left, right, dim):
    rows_to_rows = (((0,), (0,)), ((), ()))

    def product(index):
        pair = (left[index], right) if dim == 0 else (right, left[index])
        return lax.dot_general(*pair, rows_to_rows, preferred_element_type=F32)

    arrived = swap_cores(product(1).astype(BF16))
    return (product(0) + arrived.astype(F32)).astype(BF16)


def half_to_owners(mine, dim):
    return lax.psum_scatter(mine, "fsdp", scatter_dimension=dim, tiled=True)


def both_halves(total, dim):
    other = swap_cores(total)
    core = lax.axis_index("ctx")
    first = jnp.where(core == 0, total, other)
    second = jnp.where(core == 0, other, total)
    return jnp.concatenate([first, second], axis=dim).astype(F32)


def after(value, *others):
    return lax.optimization_barrier((value, *others))[0]


class Square:
    def __init__(self):
        me = lax.axis_index("fsdp")
        row, col = me // 2, me % 2
        self.me = me
        self.core = lax.axis_index("ctx")
        self.near = (row * 2 + 1 - col, (1 - row) * 2 + col)
        self.far = (1 - row) * 2 + 1 - col


def remote(source, target, send, arrive, **device):
    return pltpu.make_async_remote_copy(
        source, target, send, arrive, device_id=device, device_id_type=pl.DeviceIdType.MESH
    )


class Gather:
    def __init__(self, items, stages, send, arrive, local):
        self.items, self.stages = items, stages
        self.send, self.arrive, self.local = send, arrive, local
        self.square = Square()

    def piece(self, w, owner, low, size):
        shard, whole, dim, offset = self.items[w]
        low = pl.multiple_of(owner * shard.shape[dim] + low, 128)
        if dim == 0:
            return whole.at[pl.ds(low, size), pl.ds(offset, shard.shape[1])]
        return whole.at[:, pl.ds(low, size)]

    def copy(self, w, k):
        shard, _, dim, _ = self.items[w]
        square = self.square
        half = shard.shape[dim] // 2
        low = pl.multiple_of(square.core * half, 128)
        first, second = square.near
        if k < 2:
            source = shard.at[pl.ds(low, half), :] if dim == 0 else shard.at[:, pl.ds(low, half)]
            target = self.piece(w, square.me, low, half)
            device = {"fsdp": square.near[k]}
        elif k < 4:
            source = target = self.piece(w, square.near[k - 2], low + (k - 2) * (half // 2), half // 2)
            device = {"fsdp": square.near[3 - k]}
        else:
            source = target = self.piece(w, (first, second, square.far)[k - 4], low, half)
            device = {"ctx": 1 - square.core}
        return remote(source, target, self.send.at[w, k], self.arrive.at[w, k], **device)

    def stage(self, w, out):
        shard = self.items[w][0]
        if out:
            target = self.piece(w, self.square.me, 0, shard.shape[self.items[w][2]])
            return pltpu.make_async_copy(self.stages[w], target, self.local.at[w, 1])
        return pltpu.make_async_copy(shard, self.stages[w], self.local.at[w, 0])

    def start(self, w):
        self.copy(w, 0).start()
        self.copy(w, 1).start()
        self.stage(w, False).start()

    def forward(self, w):
        self.copy(w, 0).wait_recv()
        self.copy(w, 2).start()
        self.copy(w, 1).wait_recv()
        self.copy(w, 3).start()
        self.copy(w, 4).start()
        self.copy(w, 5).start()
        self.stage(w, False).wait()
        self.stage(w, True).start()

    def hand_over(self, w):
        self.copy(w, 2).wait_recv()
        self.copy(w, 3).wait_recv()
        self.copy(w, 6).start()

    def finish(self, w):
        for k in (4, 5, 6):
            self.copy(w, k).wait_recv()
        for k in range(7):
            self.copy(w, k).wait_send()
        self.stage(w, True).wait()


def greet(line, square, whole_line=False):
    barrier = pltpu.get_barrier_semaphore()

    def call(**device):
        pl.semaphore_signal(barrier, inc=1, device_id=device, device_id_type=pl.DeviceIdType.MESH)

    peers = 0
    if line:
        count, me = lax.axis_size("tp"), lax.axis_index("tp")

        @pl.when(me > 0)
        def _():
            call(tp=me - 1)

        @pl.when(me < count - 1)
        def _():
            call(tp=me + 1)

        peers = jnp.where((me > 0) & (me < count - 1), 2, 1)
    if whole_line:
        count, me = lax.axis_size("tp"), lax.axis_index("tp")
        for other in range(count):
            @pl.when(me != other)
            def _():
                call(tp=other)

        peers = peers + (count - 1)
    if square:
        place = Square()
        call(fsdp=place.near[0])
        call(fsdp=place.near[1])
        call(fsdp=place.far)
        call(ctx=1 - place.core)
        peers = peers + 4
    pl.semaphore_wait(barrier, peers)


def line_sum(part, whole, inbox, sems, finish, between):
    count, me = lax.axis_size("tp"), lax.axis_index("tp")
    half = part.shape[0] // 2
    chunks = inbox.shape[1]
    rows = half // chunks
    sum_send, sum_arrive, share_send, share_arrive = sems

    def spot(side, c):
        return pl.ds(pl.multiple_of(side * half + c * rows, rows), rows)

    def place(side):
        return count - 1 - me if side else me

    def onward(side, c, source):
        target = me - 1 if side else me + 1
        return remote(source, inbox.at[side, c], sum_send.at[side, c], sum_arrive.at[side, c], tp=target)

    def share(side, c):
        target = me + 1 if side else me - 1
        block = whole.at[spot(side, c), :]
        return remote(block, block, share_send.at[side, c], share_arrive.at[side, c], tp=target)

    for side in (0, 1):
        @pl.when(place(side) == 0)
        def _():
            onward(side, 0, part.at[spot(side, 0), :]).start()

    def step(t, carry):
        for side in (0, 1):
            here = place(side)
            c = t - here

            @pl.when((here == 0) & (t + 1 < chunks))
            def _():
                onward(side, t + 1, part.at[spot(side, t + 1), :]).start()

            @pl.when((c >= 0) & (c < chunks) & (here > 0))
            def _():
                onward(side, c, inbox.at[side, c]).wait_recv()
                total = (inbox[side, c].astype(F32) + part[spot(side, c), :].astype(F32)).astype(BF16)

                @pl.when(here < count - 1)
                def _():
                    inbox[side, c] = total
                    onward(side, c, inbox.at[side, c]).start()

                @pl.when(here == count - 1)
                def _():
                    whole[spot(side, c), :] = total
                    share(side, c).start()
                    finish(spot(side, c))

        for side in (0, 1):
            here = place(side)
            c = t - 2 * (count - 1) + here

            @pl.when((c >= 0) & (c < chunks) & (here < count - 1))
            def _():
                share(side, c).wait_recv()

                @pl.when(here > 0)
                def _():
                    share(side, c).start()

                finish(spot(side, c))

        between(t)
        return carry

    lax.fori_loop(0, chunks + 2 * (count - 1), step, 0)

    def drain(c, carry):
        for side in (0, 1):
            here = place(side)

            @pl.when(here < count - 1)
            def _():
                onward(side, c, inbox.at[side, c]).wait_send()

            @pl.when(here > 0)
            def _():
                share(side, c).wait_send()

        return carry

    lax.fori_loop(0, chunks, drain, 0)


def put_split(ref, rows, block):
    core = lax.axis_index("ctx")
    size = block.shape[1] // 8
    for owner in range(4):
        for index in range(2):
            low = (2 * owner + index) * size
            ref[(index + core) % 2, rows, owner * size : (owner + 1) * size] = block[:, low : low + size]


CHUNK = 32
LINE_COST = pl.CostEstimate(flops=0, bytes_accessed=400_000_000, transcendentals=0)


def enter_kernel(
    tokens, upstream, gain_shard, recur, gelu, merge,
    normed, halves, upstream_halves, gains, whole_in, whole_merge,
    stage_recur, stage_gelu, stage_merge, send, arrive, local, gain_send, gain_arrive,
):
    square = Square()
    greet(False, True)
    width = gain_shard.shape[1]

    def gain_copy(k, owner, target):
        spot = gains.at[:, pl.ds(pl.multiple_of(owner * width, 128), width)]
        return remote(gain_shard, spot, gain_send.at[k], gain_arrive.at[k], fsdp=target)

    others = (*square.near, square.far)
    for k, target in enumerate(others):
        gain_copy(k, square.me, target).start()
    gather = Gather(
        [(recur, whole_in, 0, 0), (gelu, whole_in, 0, recur.shape[1]), (merge, whole_merge, 1, 0)],
        (stage_recur, stage_gelu, stage_merge), send, arrive, local,
    )
    for w in range(3):
        gather.start(w)
    gains[:, pl.ds(pl.multiple_of(square.me * width, 128), width)] = gain_shard[...]
    for k, owner in enumerate(others):
        gain_copy(k, owner, owner).wait_recv()

    def norm(t, carry):
        rows = pl.ds(pl.multiple_of(t * CHUNK, CHUNK), CHUNK)
        block = tokens[rows, :].astype(F32)
        block = (block * rms_scale(block) * gains[0:1, :]).astype(BF16)
        normed[rows, :] = block
        put_split(halves, rows, block)
        put_split(upstream_halves, rows, upstream[rows, :])
        return carry

    lax.fori_loop(0, tokens.shape[0] // CHUNK, norm, 0)
    for w in range(3):
        gather.forward(w)
    for w in range(3):
        gather.hand_over(w)
    for w in range(3):
        gather.finish(w)
    for k, target in enumerate(others):
        gain_copy(k, square.me, target).wait_send()


ANY = pl.BlockSpec(memory_space=pl.ANY)
NEAR = pl.BlockSpec(memory_space=pltpu.VMEM)


def gather_scratch(shards):
    count = len(shards)
    dma = pltpu.SemaphoreType.DMA
    return [pltpu.VMEM(w.shape, w.dtype) for w in shards] + [dma((count, 7)), dma((count, 7)), dma((count, 2))]


def enter(tokens, upstream, gain_shard, recur, gelu, merge):
    rows, features = tokens.shape
    shape = jax.ShapeDtypeStruct
    inner = recur.shape[1]
    dma = pltpu.SemaphoreType.DMA
    return pl.pallas_call(
        enter_kernel,
        out_shape=(
            shape((rows, features), BF16),
            shape((2, rows, features // 2), BF16),
            shape((2, rows, features // 2), BF16),
            shape((8, features), F32),
            shape((features, 2 * inner), BF16),
            shape((inner, features), BF16),
        ),
        in_specs=[NEAR, NEAR, NEAR, ANY, ANY, ANY],
        out_specs=[NEAR, NEAR, NEAR, NEAR, ANY, ANY],
        scratch_shapes=gather_scratch([recur, gelu, merge]) + [dma((3,)), dma((3,))],
        compiler_params=pltpu.CompilerParams(collective_id=1, has_side_effects=True),
        name="enter",
    )(tokens, upstream, gain_shard, recur, gelu, merge)


def line_scratch(rows, features):
    chunks = rows // 2 // CHUNK
    dma = pltpu.SemaphoreType.DMA((2, chunks))
    return [pltpu.VMEM((2, chunks, CHUNK, features), BF16), dma, dma, dma, dma]


def middle_kernel(gathers, part, tokens, gains, *refs):
    if gathers:
        gate, up, down, merged, normed, halves, whole_in, whole_down = refs[:8]
        inbox, *rest = refs[8:]
        sems, (stage_gate, stage_up, stage_down, send, arrive, local) = rest[:4], rest[4:]
        gather = Gather(
            [(gate, whole_in, 0, 0), (up, whole_in, 0, gate.shape[1]), (down, whole_down, 1, 0)],
            (stage_gate, stage_up, stage_down), send, arrive, local,
        )
        greet(True, True)
        for w in range(3):
            gather.start(w)
    else:
        merged, normed, inbox, *sems = refs
        greet(True, False)

    def finish(rows):
        block = tokens[rows, :].astype(F32) + merged[rows, :].astype(F32)
        block = (block * rms_scale(block) * gains[1:2, :]).astype(BF16)
        normed[rows, :] = block
        if gathers:
            put_split(halves, rows, block)

    def between(t):
        if gathers:
            for w in range(3):
                @pl.when(t == 5 + 4 * w)
                def _():
                    gather.forward(w)

                @pl.when(t == 17 + w)
                def _():
                    gather.hand_over(w)

    line_sum(part, merged, inbox, sems, finish, between)
    if gathers:
        for w in range(3):
            gather.finish(w)


def middle(part, tokens, gains, shards):
    rows, features = tokens.shape
    shape = jax.ShapeDtypeStruct
    whole = shape((rows, features), BF16)
    outs, specs = [whole, whole], [NEAR, NEAR]
    scratch = line_scratch(rows, features)
    if shards:
        gate, up, down = shards
        outs += [
            shape((2, rows, features // 2), BF16),
            shape((features, 2 * gate.shape[1]), BF16),
            shape((down.shape[0], features), BF16),
        ]
        specs += [NEAR, ANY, ANY]
        scratch += gather_scratch(shards)
    return pl.pallas_call(
        lambda *refs: middle_kernel(bool(shards), *refs),
        out_shape=tuple(outs),
        in_specs=[NEAR, NEAR, NEAR] + [ANY] * len(shards),
        out_specs=specs,
        scratch_shapes=scratch,
        compiler_params=pltpu.CompilerParams(collective_id=2, has_side_effects=True),
        cost_estimate=LINE_COST,
        name="middle",
    )(part, tokens, gains, *shards)


def turn_kernel(split, part, tokens, merged, upstream, gains, own, grad_in, gain_sum, *refs):
    if split:
        halves, whole, wide, inbox, *sems = refs
    else:
        whole, wide, inbox, *sems = refs
    greet(True, False)
    gain_sum[...] = jnp.zeros_like(gain_sum)
    width = own.shape[1]
    start = pl.multiple_of(lax.axis_index("tp") * width, 128)

    def finish(rows):
        block = tokens[rows, :].astype(F32) + merged[rows, :].astype(F32)
        scale = rms_scale(block)
        grad = whole[rows, :].astype(F32)
        gain_sum[0:1, :] += jnp.sum(grad * (block * scale), axis=0, keepdims=True)
        grad = grad * gains[1:2, :]
        mean = jnp.mean(block * grad, axis=-1, keepdims=True)
        grad = upstream[rows, :].astype(F32) + scale * grad - block * (scale * scale * scale * mean)
        wide[...] = grad
        own[rows, :] = wide[:, pl.ds(start, width)]
        grad = grad.astype(BF16)
        grad_in[rows, :] = grad
        if split:
            put_split(halves, rows, grad)

    line_sum(part, whole, inbox, sems, finish, lambda t: None)


def turn(part, tokens, merged, upstream, gains, split):
    rows, features = tokens.shape
    shape = jax.ShapeDtypeStruct
    outs = [
        shape((rows, features // lax.axis_size("tp")), F32),
        shape((rows, features), BF16),
        shape((8, features), F32),
    ]
    if split:
        outs.append(shape((2, rows, features // 2), BF16))
    return pl.pallas_call(
        lambda *refs: turn_kernel(split, *refs),
        out_shape=tuple(outs),
        in_specs=[NEAR] * 5,
        out_specs=[NEAR] * len(outs),
        scratch_shapes=[pltpu.VMEM((rows, features), BF16), pltpu.VMEM((CHUNK, features), F32)]
        + line_scratch(rows, features),
        compiler_params=pltpu.CompilerParams(collective_id=3, has_side_effects=True),
        cost_estimate=LINE_COST,
        name="turn",
    )(part, tokens, merged, upstream, gains)


def rounded_sum(*blocks):
    total = blocks[0].astype(F32)
    for block in blocks[1:]:
        total = total + block.astype(F32)
    return total.astype(BF16)


class Scatter:
    def __init__(self, items, boxes, lasts, send, arrive):
        self.items, self.boxes, self.lasts = items, boxes, lasts
        self.send, self.arrive = send, arrive
        self.square = Square()

    def block(self, w, owner, k):
        part, _, dim = self.items[w]
        size = part.shape[dim] // 4
        if dim == 0:
            low = pl.multiple_of(owner * size + k * (size // 2), 128)
            return part.at[pl.ds(low, size // 2), :]
        half = part.shape[0] // 2
        return part.at[pl.ds(k * half, half), pl.ds(pl.multiple_of(owner * size, 128), size)]

    def spot(self, w, k):
        part, out, dim = self.items[w]
        size = part.shape[dim] // 4
        low = pl.multiple_of(self.square.core * size, 128)
        if dim == 0:
            return out.at[pl.ds(low + k * (size // 2), size // 2), :]
        half = part.shape[0] // 2
        return out.at[pl.ds(k * half, half), pl.ds(low, size)]

    def copy(self, w, k, j):
        square = self.square
        first, second = square.near[k], square.near[1 - k]
        send, arrive = self.send.at[w, 4 * k + j], self.arrive.at[w, 4 * k + j]
        if j < 2:
            owner = square.far if j == 0 else first
            return remote(self.block(w, owner, k), self.boxes[w].at[k, j], send, arrive, fsdp=first)
        if j == 2:
            return remote(self.boxes[w].at[k, 0], self.lasts[w].at[k], send, arrive, fsdp=second)
        return remote(self.spot(w, k), self.spot(w, k), send, arrive, ctx=1 - square.core)

    def start(self, w):
        for j in (0, 1):
            for k in (0, 1):
                self.copy(w, k, j).start()

    def relay(self, w):
        for k in (0, 1):
            self.copy(w, k, 0).wait_recv()
            mine = self.block(w, self.square.near[1 - k], k)
            self.boxes[w][k, 0] = rounded_sum(mine[...], self.boxes[w][k, 0])
            self.copy(w, k, 2).start()

    def finish(self, w):
        for k in (0, 1):
            self.copy(w, k, 1).wait_recv()
            self.copy(w, k, 2).wait_recv()
            mine = self.block(w, self.square.me, k)
            self.spot(w, k)[...] = rounded_sum(mine[...], self.boxes[w][k, 1], self.lasts[w][k])
            self.copy(w, k, 3).start()

    def drain(self, w):
        for k in (0, 1):
            self.copy(w, k, 3).wait_recv()
            for j in range(4):
                self.copy(w, k, j).wait_send()


def scatter_scratch(items):
    blocks = []
    for shape, dim in items:
        rows, cols = (shape[0] // 8, shape[1]) if dim == 0 else (shape[0] // 2, shape[1] // 4)
        blocks.append((rows, cols))
    dma = pltpu.SemaphoreType.DMA((len(items), 8))
    return (
        [pltpu.VMEM((2, 2, *block), BF16) for block in blocks]
        + [pltpu.VMEM((2, *block), BF16) for block in blocks]
        + [dma, dma]
    )


def leave_kernel(
    part_in, part_merge, gates, sums, norms, stats,
    own_in, own_merge, gate_sums, row_sums, norm_sums, stat_sums,
    box_in, box_merge, last_in, last_merge, send, arrive,
    gate_core, gate_half, gate_near, gate_pair, gate_far, gate_send, gate_arrive,
    core_sums, core_norms, box_sums, box_norms, sum_send, sum_arrive,
    line_norms, line_stats, norm_send, norm_arrive, stat_send, stat_arrive,
):
    square = Square()
    count, place = lax.axis_size("tp"), lax.axis_index("tp")
    core = square.core
    others = (*square.near, square.far)
    greet(False, True, True)

    def norm_copy(k, source):
        box = line_norms.at[source]
        return remote(box, box, norm_send.at[k], norm_arrive.at[source], tp=k)

    def stat_copy(k, source):
        return remote(stats, line_stats.at[source], stat_send.at[k], stat_arrive.at[source], tp=k)

    def core_copy(k):
        source, target = ((sums, core_sums), (norms, core_norms))[k]
        return remote(source, target, sum_send.at[k], sum_arrive.at[k], ctx=1 - core)

    def square_copy(k, j):
        box = (box_sums, box_norms)[k].at[square.me]
        at = 2 + 3 * k + j
        return remote(box, box, sum_send.at[at], sum_arrive.at[at], fsdp=others[j])

    gate_rows = gates.shape[0] // 2
    gate_cols = gates.shape[1] // 2
    my_rows = pl.ds(pl.multiple_of(core * gate_rows, 16), gate_rows)
    your_rows = pl.ds(pl.multiple_of((1 - core) * gate_rows, 16), gate_rows)

    def gate_copy(j):
        send, arrive = gate_send.at[j], gate_arrive.at[j]
        if j == 0:
            return remote(gates.at[your_rows, :], gate_core, send, arrive, ctx=1 - core)
        if j == 5:
            spot = gate_sums.at[my_rows, :]
            return remote(spot, spot, send, arrive, ctx=1 - core)
        k = (j - 1) % 2
        if j < 3:
            return remote(gate_half.at[k], gate_near.at[k], send, arrive, fsdp=square.near[k])
        return remote(gate_pair.at[k], gate_far.at[k], send, arrive, fsdp=square.near[1 - k])

    scatter = Scatter(
        [(part_merge, own_merge, 1), (part_in, own_in, 0)], (box_merge, box_in), (last_merge, last_in), send, arrive
    )
    gate_copy(0).start()
    core_copy(0).start()
    core_copy(1).start()
    for k in range(count):
        @pl.when(place != k)
        def _():
            stat_copy(k, place).start()

    line_stats[place] = stats[...]
    core_copy(0).wait_recv()
    core_copy(1).wait_recv()
    box_sums[square.me] = sums[...] + core_sums[...]
    box_norms[square.me] = norms[...] + core_norms[...]
    for k in (0, 1):
        for j in range(3):
            square_copy(k, j).start()
    gate_copy(0).wait_recv()
    for k in (0, 1):
        cols = slice(k * gate_cols, (k + 1) * gate_cols)
        gate_half[k] = rounded_sum(gates[my_rows, cols], gate_core[:, cols])
        gate_copy(1 + k).start()
    scatter.start(0)
    scatter.start(1)
    for k in (0, 1):
        for j in range(3):
            square_copy(k, j).wait_recv()
    row_sums[...] = box_sums[0] + box_sums[1] + box_sums[2] + box_sums[3]
    line_norms[place] = box_norms[0] + box_norms[1] + box_norms[2] + box_norms[3]
    for k in range(count):
        @pl.when(place != k)
        def _():
            norm_copy(k, place).start()

    for k in (0, 1):
        gate_copy(1 + k).wait_recv()
        gate_pair[k] = rounded_sum(gate_half[k], gate_near[k])
        gate_copy(3 + k).start()
    scatter.relay(0)
    scatter.relay(1)
    for k in (0, 1):
        cols = slice(k * gate_cols, (k + 1) * gate_cols)
        gate_copy(3 + k).wait_recv()
        gate_sums[my_rows, cols] = rounded_sum(gate_pair[k], gate_far[k])
    gate_copy(5).start()
    for k in range(count):
        @pl.when(place != k)
        def _():
            norm_copy(k, k).wait_recv()
            stat_copy(k, k).wait_recv()

    total = line_norms[0]
    stat = line_stats[0]
    for k in range(1, count):
        total = total + line_norms[k]
        stat = stat + line_stats[k]
    norm_sums[...] = total
    stat_sums[...] = stat
    scatter.finish(0)
    scatter.finish(1)
    for w in (0, 1):
        scatter.drain(w)
    gate_copy(5).wait_recv()
    for j in range(6):
        gate_copy(j).wait_send()
    for k in (0, 1):
        core_copy(k).wait_send()
        for j in range(3):
            square_copy(k, j).wait_send()
    for k in range(count):
        @pl.when(place != k)
        def _():
            norm_copy(k, place).wait_send()
            stat_copy(k, place).wait_send()


def leave(part_in, part_merge, gates, sums, norms, stats):
    shape = jax.ShapeDtypeStruct
    count = lax.axis_size("tp")
    dma = pltpu.SemaphoreType.DMA
    height, width = gates.shape[0] // 2, gates.shape[1] // 2
    quarter = pltpu.VMEM((2, height, width), BF16)
    return pl.pallas_call(
        leave_kernel,
        out_shape=(
            shape((part_in.shape[0] // 2, part_in.shape[1]), BF16),
            shape((part_merge.shape[0], part_merge.shape[1] // 2), BF16),
            shape(gates.shape, BF16),
            shape(sums.shape, F32),
            shape(norms.shape, F32),
            shape(stats.shape, F32),
        ),
        in_specs=[NEAR] * 6,
        out_specs=[NEAR] * 6,
        scratch_shapes=(
            (lambda boxes: [boxes[1], boxes[0], boxes[3], boxes[2], boxes[4], boxes[5]])(
                scatter_scratch([(part_merge.shape, 1), (part_in.shape, 0)])
            )
            + [pltpu.VMEM((height, 2 * width), BF16), quarter, quarter, quarter, quarter, dma((6,)), dma((6,))]
            + [pltpu.VMEM(sums.shape, F32), pltpu.VMEM(norms.shape, F32)]
            + [pltpu.VMEM((4, *sums.shape), F32), pltpu.VMEM((4, *norms.shape), F32), dma((8,)), dma((8,))]
            + [pltpu.VMEM((count, *norms.shape), F32), pltpu.VMEM((count, *stats.shape), F32)]
            + [dma((count,))] * 4
        ),
        compiler_params=pltpu.CompilerParams(collective_id=4, has_side_effects=True),
        cost_estimate=pl.CostEstimate(flops=0, bytes_accessed=160_000_000, transcendentals=0),
        name="leave",
    )(part_in, part_merge, gates, sums, norms, stats)


def gelu_pair(q):
    tanh = jnp.tanh(ROOT * (q + CUBE * q * q * q))
    value = 0.5 * q * (1.0 + tanh)
    slope = 0.5 * (1.0 + tanh) + 0.5 * q * (1.0 - tanh * tanh) * ROOT * (1.0 + 3.0 * CUBE * q * q)
    return value, slope


def rms_scale(values):
    return lax.rsqrt(jnp.mean(values * values, axis=-1, keepdims=True) + EPS)


def decay_parts(rate, softer, keep):
    gap = 2.0 * CGAIN * rate * softer
    decay = jnp.exp(-0.5 * gap)
    series = gap * (
        1.0
        - gap / 2.0
        * (1.0 - gap / 3.0 * (1.0 - gap / 4.0 * (1.0 - gap / 5.0 * (1.0 - gap / 6.0 * (1.0 - gap / 7.0)))))
    )
    square = jnp.where(gap < 0.25, series, 1.0 - decay * decay)
    return jnp.where(keep, decay, 0.0), jnp.where(keep, square, 1.0)


LANES = 128


def put_lanes(ref, block, rows):
    for lane in range(ref.shape[0]):
        ref[lane, 0:rows, :] = block[:, lane * LANES : (lane + 1) * LANES]


def sweep(decay_ref, value_ref, state_ref, product_ref, out_ref, run_ref, carry_ref, reverse, offset):
    groups, rows, _ = value_ref.shape
    steps = rows // SEGS
    place = lax.broadcasted_iota(jnp.int32, (SEGS, LANES), 0)
    if reverse:
        place = SEGS - 1 - place

    def moved(block, by, fill):
        turned = pltpu.roll(block, SEGS - by if reverse else by, 0)
        return jnp.where(place >= by, turned, fill)

    for lane in range(groups):
        lanes = slice(lane * LANES, (lane + 1) * LANES)
        state = jnp.zeros((SEGS, LANES), F32)
        product = jnp.ones((SEGS, LANES), F32)
        for step in reversed(range(steps)) if reverse else range(steps):
            spot = pl.ds(step, SEGS, stride=steps)
            decay = decay_ref[lane, pl.ds(step + offset, SEGS, stride=steps), :]
            state = decay * state + value_ref[lane, spot, :]
            product = product * decay
            state_ref[lane, spot, :] = state
            product_ref[lane, spot, :] = product
        for by in (1, 2, 4):
            state = state + product * moved(state, by, 0.0)
            product = product * moved(product, by, 1.0)
        carry = carry_ref[0:1, lanes]
        carry_run = carry_ref[8:9, lanes]
        state = state + product * carry
        product = product * carry_run
        enter = moved(state, 1, carry)
        enter_run = moved(product, 1, carry_run)
        for seg in range(SEGS):
            span = slice(seg * steps, (seg + 1) * steps)
            inner = product_ref[lane, span, :]
            out_ref[span, lanes] = state_ref[lane, span, :] + inner * enter[seg : seg + 1, :]
            run_ref[span, lanes] = inner * enter_run[seg : seg + 1, :]
        last = 0 if reverse else SEGS - 1
        carry_ref[0:1, lanes] = state[last : last + 1, :]
        carry_ref[8:9, lanes] = product[last : last + 1, :]


def spread_blocks(blocks_ref, out_ref):
    chans, size = blocks_ref.shape[1:]
    row = lax.broadcasted_iota(jnp.int32, (chans, chans), 0)
    col = lax.broadcasted_iota(jnp.int32, (chans, chans), 1)
    inner = lax.broadcasted_iota(jnp.int32, (size, chans), 0)
    outer = lax.broadcasted_iota(jnp.int32, (size, chans), 1)
    inside = row < 0
    repeat = outer < 0
    for low in range(0, chans, size):
        inside |= (row >= low) & (row < low + size) & (col >= low) & (col < low + size)
        repeat |= outer - low == inner
    repeat = repeat.astype(F32).astype(BF16)
    for gate in range(2):
        wide = jnp.dot(blocks_ref[gate], repeat, preferred_element_type=F32)
        out_ref[:, gate * chans : (gate + 1) * chans] = jnp.where(inside, wide, 0.0).astype(BF16)


def forward_kernel(
    branch_ref, halo_ref, mask_ref, taps_ref, bias_ref, blocks_ref, gate_bias_ref, softer_ref,
    conv_ref, rate_ref, entry_ref, state_ref, run_ref, gates_ref,
    window, decay, value, inner, product, carry,
):
    rows, chans = conv_ref.shape
    spot = pl.program_id(0)

    @pl.when(spot == 0)
    def _():
        spread_blocks(blocks_ref, gates_ref)
        window[0:8, :] = halo_ref[...].astype(F32)
        carry[0:8, :] = jnp.zeros((8, chans), F32)
        carry[8:16, :] = jnp.ones((8, chans), F32)

    @pl.when(spot > 0)
    def _():
        window[0:8, :] = window[rows : rows + 8, :]

    window[8 : rows + 8, :] = branch_ref[...].astype(F32)
    mixed = bias_ref[...] + taps_ref[0:1, :] * window[8 : rows + 8, :]
    for shift in range(1, taps_ref.shape[0]):
        moved = window[8 - shift : 8 - shift + rows, :]
        mixed = mixed + taps_ref[shift : shift + 1, :] * (moved * mask_ref[:, shift : shift + 1])
    conv = mixed.astype(BF16)
    conv_ref[...] = conv
    pre = jnp.dot(conv, gates_ref[...], preferred_element_type=F32) + gate_bias_ref[...]
    rate = jax.nn.sigmoid(pre[:, :chans])
    entry = jax.nn.sigmoid(pre[:, chans:])
    rate_ref[...] = rate
    entry_ref[...] = entry
    keep = jnp.broadcast_to(mask_ref[:, 0:1], (rows, chans)) > 0.5
    step, square = decay_parts(rate, softer_ref[...], keep)
    put_lanes(decay, step, rows)
    put_lanes(value, jnp.sqrt(square) * entry * conv.astype(F32), rows)
    sweep(decay, value, inner, product, state_ref, run_ref, carry, False, 0)


def tile_spec(width, count=None):
    if count is None:
        return pl.BlockSpec((TILE, width), lambda i: (i, 0))
    return pl.BlockSpec((TILE, width), lambda i: (count - 1 - i, 0))


def fixed_spec(shape):
    return pl.BlockSpec(shape, lambda i: (0, 0))


def recur_forward(branch, halo, masks, taps, bias, blocks, gate_bias, softer):
    rows, chans = branch.shape[0], halo.shape[1]
    wide = jax.ShapeDtypeStruct((rows, chans), F32)
    return pl.pallas_call(
        forward_kernel,
        grid=(rows // TILE,),
        out_shape=(
            jax.ShapeDtypeStruct((rows, chans), BF16), wide, wide, wide, wide,
            jax.ShapeDtypeStruct((chans, 2 * chans), BF16),
        ),
        in_specs=[
            tile_spec(chans),
            fixed_spec((8, chans)),
            tile_spec(masks.shape[1]),
            fixed_spec(taps.shape),
            fixed_spec((1, chans)),
            pl.BlockSpec(blocks.shape, lambda i: (0, 0, 0)),
            fixed_spec((1, 2 * chans)),
            fixed_spec((1, chans)),
        ],
        out_specs=[tile_spec(chans)] * 5 + [fixed_spec((chans, 2 * chans))],
        scratch_shapes=[
            pltpu.VMEM((TILE + 8, chans), F32),
            pltpu.VMEM((chans // LANES, TILE, LANES), F32),
            pltpu.VMEM((chans // LANES, TILE, LANES), F32),
            pltpu.VMEM((chans // LANES, TILE, LANES), F32),
            pltpu.VMEM((chans // LANES, TILE, LANES), F32),
            pltpu.VMEM((16, chans), F32),
        ],
        cost_estimate=pl.CostEstimate(
            flops=2 * rows * chans * 2 * chans, bytes_accessed=24 * rows * chans, transcendentals=5 * rows * chans
        ),
        name="recur_forward",
    )(branch, halo, masks, taps, bias, blocks, gate_bias, softer)


def merge_kernel(local_ref, run_ref, enter_ref, pre_ref, weight_ref, state_ref, gated_ref, part_ref):
    state = local_ref[...] + run_ref[...] * enter_ref[0:1, :]
    state_ref[...] = state
    pre = pre_ref[...].astype(F32)
    gated = (state * gelu_pair(pre)[0]).astype(BF16)
    gated_ref[...] = gated
    part_ref[...] = jnp.dot(gated, weight_ref[...], preferred_element_type=F32).astype(BF16)


def merge_states(local, run, enter, branches, weight):
    rows, chans = local.shape
    features = weight.shape[1]
    shape = jax.ShapeDtypeStruct
    return pl.pallas_call(
        merge_kernel,
        grid=(rows // TILE,),
        out_shape=(shape((rows, chans), F32), shape((rows, chans), BF16), shape((rows, features), BF16)),
        in_specs=[
            tile_spec(chans), tile_spec(chans), fixed_spec((1, chans)),
            pl.BlockSpec((TILE, chans), lambda i: (i, 1)),
            fixed_spec(weight.shape),
        ],
        out_specs=[tile_spec(chans), tile_spec(chans), tile_spec(features)],
        cost_estimate=pl.CostEstimate(
            flops=2 * rows * chans * features, bytes_accessed=16 * rows * chans, transcendentals=rows * chans
        ),
        name="merge_states",
    )(local, run, enter, branches, weight)


def adjoint_kernel(
    rate_ref, up_ref, pre_ref, state_ref, mask_ref, softer_ref,
    grad_ref, run_ref, head_ref, pre_grad_ref,
    decay, value, inner, product, carry,
):
    rows, chans = rate_ref.shape
    groups = chans // LANES
    spot = pl.program_id(0)

    @pl.when(spot == 0)
    def _():
        for lane in range(groups):
            decay[lane, rows : rows + 8, :] = jnp.ones((8, LANES), F32)
        carry[0:8, :] = jnp.zeros((8, chans), F32)
        carry[8:16, :] = jnp.ones((8, chans), F32)

    @pl.when(spot > 0)
    def _():
        for lane in range(groups):
            decay[lane, rows : rows + 8, :] = decay[lane, 0:8, :]

    keep = jnp.broadcast_to(mask_ref[:, 0:1], (rows, chans)) > 0.5
    gap = CGAIN * rate_ref[...] * softer_ref[...]
    step = jnp.where(keep, jnp.exp(-gap), 0.0)
    put_lanes(decay, step, rows)
    gate, slope = gelu_pair(pre_ref[...].astype(F32))
    up = up_ref[...]
    pre_grad_ref[...] = (up * state_ref[...] * slope).astype(BF16)
    put_lanes(value, up * gate, rows)
    sweep(decay, value, inner, product, grad_ref, run_ref, carry, True, 1)
    head_ref[...] = jnp.broadcast_to(step[0:1, :] * carry[0:1, :], (8, chans))


def recur_adjoint(rate, up, branches, state, masks, softer):
    rows, chans = rate.shape
    count = rows // TILE
    wide = jax.ShapeDtypeStruct((rows, chans), F32)
    return pl.pallas_call(
        adjoint_kernel,
        grid=(count,),
        out_shape=(
            wide, wide, jax.ShapeDtypeStruct((8, chans), F32), jax.ShapeDtypeStruct((rows, chans), BF16)
        ),
        in_specs=[
            tile_spec(chans, count),
            tile_spec(chans, count),
            pl.BlockSpec((TILE, chans), lambda i: (count - 1 - i, 1)),
            tile_spec(chans, count),
            tile_spec(masks.shape[1], count),
            fixed_spec((1, chans)),
        ],
        out_specs=[tile_spec(chans, count), tile_spec(chans, count), fixed_spec((8, chans)), tile_spec(chans, count)],
        scratch_shapes=[
            pltpu.VMEM((chans // LANES, TILE + 8, LANES), F32),
            pltpu.VMEM((chans // LANES, TILE, LANES), F32),
            pltpu.VMEM((chans // LANES, TILE, LANES), F32),
            pltpu.VMEM((chans // LANES, TILE, LANES), F32),
            pltpu.VMEM((16, chans), F32),
        ],
        cost_estimate=pl.CostEstimate(
            flops=8 * rows * chans, bytes_accessed=16 * rows * chans, transcendentals=rows * chans
        ),
        name="recur_adjoint",
    )(rate, up, branches, state, masks, softer)


def backward_kernel(
    grad_ref, run_ref, enter_ref, rate_ref, entry_ref, conv_ref, state_ref, mask_ref,
    branch_ref, pre_grad_ref, halo_ref, taps_ref, gates_ref, softer_ref,
    back_ref, tail_ref, head_ref, gate_grad_ref, sums_ref,
    shifts, edge,
):
    rows, chans = conv_ref.shape
    width = taps_ref.shape[0]
    spot = pl.program_id(0)
    last = pl.num_programs(0) - 1

    @pl.when(spot == 0)
    def _():
        for shift in range(1, width):
            shifts[shift - 1, rows : rows + 8, :] = jnp.zeros((8, chans), F32)
        gate_grad_ref[...] = jnp.zeros_like(gate_grad_ref)
        sums_ref[...] = jnp.zeros_like(sums_ref)

    @pl.when(spot > 0)
    def _():
        for shift in range(1, width):
            shifts[shift - 1, rows : rows + 8, :] = shifts[shift - 1, 0:8, :]

    keep = jnp.broadcast_to(mask_ref[:, 0:1], (rows, chans)) > 0.5
    softer = softer_ref[...]
    rate = rate_ref[...]
    entry = entry_ref[...]
    conv = conv_ref[...].astype(F32)
    grad = grad_ref[...] + run_ref[...] * enter_ref[0:1, :]
    step, square = decay_parts(rate, softer, keep)
    inverse = lax.rsqrt(square)
    mult = square * inverse
    driven = entry * conv
    carried = state_ref[...] - mult * driven
    d_log = jnp.where(keep, grad * (carried - driven * step * step * inverse), 0.0)
    d_rate = (-CGAIN * softer * d_log * rate * (1.0 - rate)).astype(BF16)
    lifted = grad * mult * entry
    d_entry = (lifted * conv * (1.0 - entry)).astype(BF16)
    both = jnp.concatenate([d_rate, d_entry], axis=1)
    d_conv = lifted + lax.dot_general(
        both, gates_ref[...], (((1,), (1,)), ((), ())), preferred_element_type=F32
    )
    gate_grad_ref[...] += lax.dot_general(
        conv_ref[...], both, (((0,), (0,)), ((), ())), preferred_element_type=F32
    )

    def add_row(row, block):
        sums_ref[row : row + 1, :] += jnp.sum(block, axis=0, keepdims=True)

    branch = branch_ref[...].astype(F32)
    add_row(0, d_log * rate)
    add_row(1, d_rate.astype(F32))
    add_row(2, d_entry.astype(F32))
    add_row(3, d_conv)
    add_row(4, d_conv * branch)
    back = taps_ref[0:1, :] * d_conv
    for shift in range(1, width):
        shifts[shift - 1, 0:rows, :] = d_conv * mask_ref[:, shift : shift + 1]
        moved = shifts[shift - 1, shift : shift + rows, :]
        add_row(4 + shift, moved * branch)
        back = back + taps_ref[shift : shift + 1, :] * moved
    back_ref[:, 0:chans] = back.astype(BF16)
    back_ref[:, chans:] = pre_grad_ref[...]

    @pl.when(spot == 0)
    def _():
        tail_ref[...] = back[rows - 8 :, :]

    @pl.when(spot == last)
    def _():
        halo = halo_ref[...].astype(F32)
        head = jnp.zeros((8, chans), F32)
        edge[0:8, :] = head
        for shift in range(1, width):
            edge[8:16, :] = shifts[shift - 1, 0:8, :]
            moved = edge[shift : shift + 8, :]
            add_row(4 + shift, moved * halo)
            head = head + taps_ref[shift : shift + 1, :] * moved
        head_ref[...] = head


def recur_backward(grad, run, enter, rate, entry, conv, state, masks, branch, pre_grad, halo, taps, gates, softer):
    rows, chans = rate.shape
    count = rows // TILE
    edge = jax.ShapeDtypeStruct((8, chans), F32)
    wide = tile_spec(chans, count)
    return pl.pallas_call(
        backward_kernel,
        grid=(count,),
        out_shape=(
            jax.ShapeDtypeStruct((rows, 2 * chans), BF16),
            edge,
            edge,
            jax.ShapeDtypeStruct((chans, 2 * chans), F32),
            jax.ShapeDtypeStruct((16, chans), F32),
        ),
        in_specs=[
            wide, wide, fixed_spec((1, chans)), wide, wide, wide, wide,
            tile_spec(masks.shape[1], count),
            wide,
            wide,
            fixed_spec((8, chans)),
            fixed_spec(taps.shape),
            fixed_spec(gates.shape),
            fixed_spec((1, chans)),
        ],
        out_specs=[
            tile_spec(2 * chans, count),
            fixed_spec((8, chans)),
            fixed_spec((8, chans)),
            fixed_spec((chans, 2 * chans)),
            fixed_spec((16, chans)),
        ],
        scratch_shapes=[
            pltpu.VMEM((taps.shape[0] - 1, TILE + 8, chans), F32),
            pltpu.VMEM((16, chans), F32),
        ],
        cost_estimate=pl.CostEstimate(
            flops=8 * rows * chans * chans, bytes_accessed=28 * rows * chans, transcendentals=2 * rows * chans
        ),
        name="recur_backward",
    )(grad, run, enter, rate, entry, conv, state, masks, branch, pre_grad, halo, taps, gates, softer)


def shards(
    tokens,
    segments,
    cotangent,
    w_recur,
    w_gelu,
    w_merge,
    w_gate,
    w_up,
    w_down,
    norm_mix,
    norm_feed,
    conv_taps,
    conv_bias,
    rate_gate,
    entry_gate,
    rate_bias,
    entry_bias,
    decay_logit,
):
    piece = tokens.shape[0]
    width = conv_taps.shape[0]
    edge = width - 1
    heads, block = rate_gate.shape[0], rate_gate.shape[1]
    chans = conv_taps.shape[1]
    features = tokens.shape[1]
    feat_local = features // lax.axis_size("tp")
    feat_start = lax.axis_index("tp") * feat_local

    square = lax.axis_size("fsdp") == 4
    gain_shard = jnp.concatenate(
        [jnp.stack([norm_mix, norm_feed]).astype(F32), jnp.zeros((6, norm_mix.shape[0]), F32)], axis=0
    )
    if square:
        normed, normed_split, cotangent_split, gains, whole_in, whole_merge = enter(
            tokens, cotangent, gain_shard, w_recur, w_gelu, w_merge
        )
    else:
        whole_in = gather_halves(jnp.concatenate([w_recur, w_gelu], axis=1), 0)
        whole_merge = gather_halves(w_merge, 1)
        gains = lax.all_gather(gain_shard, "fsdp", axis=1, tiled=True)
        inputs = tokens.astype(F32)
        normed = (inputs * rms_scale(inputs) * gains[0:1]).astype(BF16)
        normed_split = split_features(normed)
        cotangent_split = split_features(cotangent)
    gain_one = gains[0:1]

    padded_ids = jnp.concatenate([jnp.full((edge,), -1, jnp.int32), segments])
    local_ids = lax.dynamic_slice_in_dim(padded_ids, lax.axis_index("ctx") * piece, piece + edge)
    own_ids = local_ids[edge:]
    masks = jnp.stack(
        [(local_ids[edge - max(shift, 1) : edge - max(shift, 1) + piece] == own_ids) for shift in range(width)],
        axis=1,
    ).astype(F32)
    taps = conv_taps.astype(F32)
    blocks = jnp.stack([rate_gate.reshape(chans, block), entry_gate.reshape(chans, block)])
    gate_bias = jnp.concatenate([rate_bias, entry_bias]).astype(F32)[None, :]
    softer = jax.nn.softplus(-decay_logit)[None, :]

    rows_to_features = (((1,), (1,)), ((), ()))
    branches = jnp.dot(normed, whole_in, preferred_element_type=F32).astype(BF16)
    halo = shifted(branches[piece - 8 :, :chans], "ctx", 1)
    conv, rate, entry, local_state, run, gates = recur_forward(
        branches, halo, masks, taps, conv_bias.astype(F32)[None, :], blocks, gate_bias, softer
    )
    state_in = shifted(local_state[piece - 8 :], "ctx", 1)[7:8]
    states, gated, part_merge = merge_states(local_state, run, state_in, branches, whole_merge)

    if square:
        merged, normed_two, normed_two_split, whole_mid, whole_down = middle(
            part_merge, tokens, gains, (w_gate, w_up, w_down)
        )
    else:
        merged, normed_two = middle(part_merge, tokens, gains, ())
        normed_two_split = split_features(normed_two)
        whole_mid = gather_halves(jnp.concatenate([w_gate, w_up], axis=1), 0)
        whole_down = gather_halves(w_down, 1)

    units = w_gate.shape[1]
    pre_mid = jnp.dot(normed_two, whole_mid, preferred_element_type=F32).astype(BF16)
    d_hidden = lax.dot_general(cotangent, whole_down, rows_to_features, preferred_element_type=F32).astype(BF16)
    gate_act, gate_slope = gelu_pair(pre_mid[:, :units].astype(F32))
    up_vals = pre_mid[:, units:].astype(F32)
    wide_hidden = d_hidden.astype(F32)
    hidden = (gate_act * up_vals).astype(BF16)
    d_mid = jnp.concatenate(
        [(wide_hidden * up_vals * gate_slope).astype(BF16), (wide_hidden * gate_act).astype(BF16)], axis=1
    )
    part_feed = jnp.dot(hidden, whole_down, preferred_element_type=F32).astype(BF16)
    feed = lax.psum_scatter(part_feed, "tp", scatter_dimension=1, tiled=True)
    hidden = after(hidden, part_feed)
    part_two = lax.dot_general(d_mid, after(whole_mid, part_feed), rows_to_features, preferred_element_type=F32).astype(BF16)
    pair_down = pair_sums(cotangent_split, hidden, 1)
    pair_mid = pair_sums(after(normed_two_split, part_feed), d_mid, 0)
    part_two = after(part_two, pair_down, pair_mid)
    turned = turn(part_two, tokens, merged, cotangent, gains, square)
    own_resid_grad, d_merge_in, feed_sums = turned[:3]
    d_merge_split = turned[3] if square else split_features(d_merge_in)
    half_down = half_to_owners(pair_down, 1)
    half_mid = half_to_owners(pair_mid, 0)
    d_merge_in = after(d_merge_in, half_down, feed)

    d_gated = lax.dot_general(d_merge_in, whole_merge, rows_to_features, preferred_element_type=F32)
    local_grad, grad_run, first, d_gelu_pre = recur_adjoint(after(rate, half_mid), d_gated, branches, states, masks, softer)
    grad_in = shifted(first, "ctx", -1)[0:1]
    back, tail, head, gate_grads, sums = recur_backward(
        local_grad, grad_run, grad_in, rate, entry, conv, states, masks, branches, d_gelu_pre,
        halo, taps, gates, softer
    )
    returned = shifted(head, "ctx", -1)
    d_in = lax.dynamic_update_slice(back, (tail + returned).astype(BF16), (piece - 8, 0))
    part_one = lax.dot_general(d_in, whole_in, rows_to_features, preferred_element_type=F32).astype(BF16)
    d_normed = lax.psum_scatter(part_one, "tp", scatter_dimension=1, tiled=True)

    pair_merge = pair_sums(d_merge_split, after(gated, part_one), 1)
    pair_in = pair_sums(normed_split, after(d_in, part_one), 0)
    inputs = tokens.astype(F32)
    scale_one = rms_scale(inputs)
    wide_part = part_one.astype(F32)
    stat_one = jnp.sum(wide_part * inputs * gain_one, axis=-1)
    grad_mix = jnp.sum(wide_part * inputs * scale_one, axis=0)
    norm_sums = jnp.stack([grad_mix, feed_sums[0] / lax.axis_size("tp")])
    spread = jnp.arange(2 * chans)[None, :] % chans // block
    diagonal = sum(jnp.where(spread == i, gate_grads[i * block : (i + 1) * block], 0.0) for i in range(heads))
    diagonal = diagonal.astype(BF16)
    if square:
        norm_sums = jnp.pad(norm_sums, ((0, 6), (0, 0)))
        own_in, own_merge, gate_sums, row_sums, both_norms, line_stats = leave(
            pair_in, pair_merge, diagonal, sums, norm_sums, stat_one.reshape(-1, 128)
        )
        shard_in, shard_merge = own_in.astype(F32), own_merge.astype(F32)
        stat_one = line_stats.reshape(-1)
    else:
        shard_in = both_halves(half_to_owners(pair_in, 0), 0)
        shard_merge = both_halves(half_to_owners(pair_merge, 1), 1)
        gate_sums = lax.psum(diagonal, ("fsdp", "ctx"))
        row_sums = lax.psum(sums, ("fsdp", "ctx"))
        both_norms = lax.psum(norm_sums, ("fsdp", "ctx", "tp"))
        stat_one = lax.psum(stat_one, "tp")
    stat_one = stat_one[:, None] / features
    shard_down = both_halves(half_down, 1)
    shard_mid = both_halves(half_mid, 0)
    gate_sums = gate_sums.astype(F32).reshape(block, 2, heads, block).transpose(1, 2, 0, 3)

    def own(block):
        return lax.dynamic_slice_in_dim(block, feat_start, feat_local, 1)

    own_inputs = own(tokens).astype(F32)
    output = (own_inputs + own(merged).astype(F32) + feed.astype(F32)).astype(BF16)
    grad_tokens = (
        own_resid_grad
        + scale_one * d_normed.astype(F32) * own(gain_one)
        - own_inputs * scale_one**3 * stat_one
    ).astype(BF16)

    norm_local = norm_mix.shape[0]
    own_norms = lax.dynamic_slice_in_dim(both_norms, lax.axis_index("fsdp") * norm_local, norm_local, 1)

    return (
        output,
        grad_tokens,
        shard_in[:, :chans],
        shard_in[:, chans:],
        shard_merge,
        shard_mid[:, :units],
        shard_mid[:, units:],
        shard_down,
        own_norms[0],
        own_norms[1],
        row_sums[4 : 4 + width],
        row_sums[3],
        gate_sums[0],
        gate_sums[1],
        row_sums[1],
        row_sums[2],
        CGAIN * row_sums[0] * jax.nn.sigmoid(-decay_logit),
    )


def solution(mesh):
    placed = (
        P(("fsdp", "ctx"), None),
        P("fsdp"),
        P(("fsdp", "ctx"), None),
        P("fsdp", "tp"),
        P("fsdp", "tp"),
        P("tp", "fsdp"),
        P("fsdp", "tp"),
        P("fsdp", "tp"),
        P("tp", "fsdp"),
        P("fsdp"),
        P("fsdp"),
        P(None, "tp"),
        P("tp"),
        P("tp", None, None),
        P("tp", None, None),
        P("tp"),
        P("tp"),
        P("tp"),
    )
    return jax.shard_map(
        shards,
        mesh=mesh,
        in_specs=placed,
        out_specs=(
            P(("fsdp", "ctx"), "tp"),
            P(("fsdp", "ctx"), "tp"),
            P("fsdp", "tp"),
            P("fsdp", "tp"),
            P("tp", "fsdp"),
            P("fsdp", "tp"),
            P("fsdp", "tp"),
            P("tp", "fsdp"),
            P("fsdp"),
            P("fsdp"),
            P(None, "tp"),
            P("tp"),
            P("tp", None, None),
            P("tp", None, None),
            P("tp"),
            P("tp"),
            P("tp"),
        ),
        check_vma=False,
    )
```

```python
import jax
import jax.numpy as jnp
from jax import lax
from jax.experimental import pallas as pl
from jax.experimental.pallas import tpu as pltpu
from jax.sharding import PartitionSpec as P

EPS = 1e-06
CGAIN = 8.0
ROOT = 0.7978845608
CUBE = 0.044715
TILE = 128
SEGS = 8
F32 = jnp.float32
BF16 = jnp.bfloat16


def swap_cores(block):
    size = lax.axis_size("ctx")
    return lax.ppermute(block, "ctx", [(i, size - 1 - i) for i in range(size)])


def shifted(block, axis, distance):
    devices = range(lax.axis_size(axis))
    route = [(i - distance, i) for i in devices if i - distance in devices]
    return lax.ppermute(block, axis, route)


def gather_halves(shard, dim):
    half = shard.shape[dim] // 2
    core = lax.axis_index("ctx")
    mine = lax.dynamic_slice_in_dim(shard, core * half, half, dim)
    mine = lax.all_gather(mine, "fsdp", axis=dim)
    other = swap_cores(mine)
    first = jnp.where(core == 0, mine, other)
    second = jnp.where(core == 0, other, mine)
    both = jnp.stack([first, second], axis=dim + 1)
    return both.reshape(shard.shape[:dim] + (-1,) + shard.shape[dim + 1 :])


def split_features(block):
    shards = lax.axis_size("fsdp")
    core = lax.axis_index("ctx")
    parts = block.reshape(block.shape[0], shards, 2, -1)
    return [
        lax.dynamic_index_in_dim(parts, index, 2, False).reshape(block.shape[0], -1)
        for index in (core, 1 - core)
    ]


def pair_sums(left, right, dim, behind=None):
    rows_to_rows = (((0,), (0,)), ((), ()))

    def product(index):
        pair = (left[index], right) if dim == 0 else (right, left[index])
        return lax.dot_general(*pair, rows_to_rows, preferred_element_type=F32)

    arrived = swap_cores(product(1).astype(BF16))
    if behind is not None:
        arrived, left = after((arrived, left), behind)
    return (product(0) + arrived.astype(F32)).astype(BF16)


def half_to_owners(mine, dim):
    return lax.psum_scatter(mine, "fsdp", scatter_dimension=dim, tiled=True)


def both_halves(total, dim):
    other = swap_cores(total)
    core = lax.axis_index("ctx")
    first = jnp.where(core == 0, total, other)
    second = jnp.where(core == 0, other, total)
    return jnp.concatenate([first, second], axis=dim).astype(F32)


def after(value, *others):
    return lax.optimization_barrier((value, *others))[0]


class Square:
    def __init__(self):
        me = lax.axis_index("fsdp")
        row, col = me // 2, me % 2
        self.me = me
        self.core = lax.axis_index("ctx")
        self.near = (row * 2 + 1 - col, (1 - row) * 2 + col)
        self.far = (1 - row) * 2 + 1 - col


def remote(source, target, send, arrive, **device):
    return pltpu.make_async_remote_copy(
        source, target, send, arrive, device_id=device, device_id_type=pl.DeviceIdType.MESH
    )


class Gather:
    def __init__(self, items, stages, send, arrive, local):
        self.items, self.stages = items, stages
        self.send, self.arrive, self.local = send, arrive, local
        self.square = Square()

    def piece(self, w, owner, low, size):
        shard, whole, dim, offset = self.items[w]
        low = pl.multiple_of(owner * shard.shape[dim] + low, 128)
        if dim == 0:
            return whole.at[pl.ds(low, size), pl.ds(offset, shard.shape[1])]
        return whole.at[:, pl.ds(low, size)]

    def copy(self, w, k):
        shard, _, dim, _ = self.items[w]
        square = self.square
        half = shard.shape[dim] // 2
        low = pl.multiple_of(square.core * half, 128)
        first, second = square.near
        if k < 2:
            source = shard.at[pl.ds(low, half), :] if dim == 0 else shard.at[:, pl.ds(low, half)]
            target = self.piece(w, square.me, low, half)
            device = {"fsdp": square.near[k]}
        elif k < 4:
            source = target = self.piece(w, square.near[k - 2], low + (k - 2) * (half // 2), half // 2)
            device = {"fsdp": square.near[3 - k]}
        else:
            source = target = self.piece(w, (first, second, square.far)[k - 4], low, half)
            device = {"ctx": 1 - square.core}
        return remote(source, target, self.send.at[w, k], self.arrive.at[w, k], **device)

    def stage(self, w, out):
        shard = self.items[w][0]
        if out:
            target = self.piece(w, self.square.me, 0, shard.shape[self.items[w][2]])
            return pltpu.make_async_copy(self.stages[w], target, self.local.at[w, 1])
        return pltpu.make_async_copy(shard, self.stages[w], self.local.at[w, 0])

    def start(self, w):
        self.copy(w, 0).start()
        self.copy(w, 1).start()
        self.stage(w, False).start()

    def forward(self, w):
        self.copy(w, 0).wait_recv()
        self.copy(w, 2).start()
        self.copy(w, 1).wait_recv()
        self.copy(w, 3).start()
        self.copy(w, 4).start()
        self.copy(w, 5).start()
        self.stage(w, False).wait()
        self.stage(w, True).start()

    def hand_over(self, w):
        self.copy(w, 2).wait_recv()
        self.copy(w, 3).wait_recv()
        self.copy(w, 6).start()

    def finish(self, w):
        for k in (4, 5, 6):
            self.copy(w, k).wait_recv()
        for k in range(7):
            self.copy(w, k).wait_send()
        self.stage(w, True).wait()


def greet(line, square, whole_line=False):
    barrier = pltpu.get_barrier_semaphore()

    def call(**device):
        pl.semaphore_signal(barrier, inc=1, device_id=device, device_id_type=pl.DeviceIdType.MESH)

    peers = 0
    if line:
        count, me = lax.axis_size("tp"), lax.axis_index("tp")

        @pl.when(me > 0)
        def _():
            call(tp=me - 1)

        @pl.when(me < count - 1)
        def _():
            call(tp=me + 1)

        peers = jnp.where((me > 0) & (me < count - 1), 2, 1)
    if whole_line:
        count, me = lax.axis_size("tp"), lax.axis_index("tp")
        for other in range(count):
            @pl.when(me != other)
            def _():
                call(tp=other)

        peers = peers + (count - 1)
    if square:
        place = Square()
        call(fsdp=place.near[0])
        call(fsdp=place.near[1])
        call(fsdp=place.far)
        call(ctx=1 - place.core)
        peers = peers + 4
    pl.semaphore_wait(barrier, peers)


def line_sum(part, whole, inbox, sems, finish, between):
    count, me = lax.axis_size("tp"), lax.axis_index("tp")
    half = part.shape[0] // 2
    chunks = inbox.shape[1]
    rows = half // chunks
    sum_send, sum_arrive, share_send, share_arrive = sems

    def spot(side, c):
        return pl.ds(pl.multiple_of(side * half + c * rows, rows), rows)

    def place(side):
        return count - 1 - me if side else me

    def onward(side, c, source):
        target = me - 1 if side else me + 1
        return remote(source, inbox.at[side, c], sum_send.at[side, c], sum_arrive.at[side, c], tp=target)

    def share(side, c):
        target = me + 1 if side else me - 1
        block = whole.at[spot(side, c), :]
        return remote(block, block, share_send.at[side, c], share_arrive.at[side, c], tp=target)

    for side in (0, 1):
        @pl.when(place(side) == 0)
        def _():
            onward(side, 0, part.at[spot(side, 0), :]).start()

    def step(t, carry):
        for side in (0, 1):
            here = place(side)
            c = t - here

            @pl.when((here == 0) & (t + 1 < chunks))
            def _():
                onward(side, t + 1, part.at[spot(side, t + 1), :]).start()

            @pl.when((c >= 0) & (c < chunks) & (here > 0))
            def _():
                onward(side, c, inbox.at[side, c]).wait_recv()
                total = (inbox[side, c].astype(F32) + part[spot(side, c), :].astype(F32)).astype(BF16)

                @pl.when(here < count - 1)
                def _():
                    inbox[side, c] = total
                    onward(side, c, inbox.at[side, c]).start()

                @pl.when(here == count - 1)
                def _():
                    whole[spot(side, c), :] = total
                    share(side, c).start()
                    finish(spot(side, c))

        for side in (0, 1):
            here = place(side)
            c = t - 2 * (count - 1) + here

            @pl.when((c >= 0) & (c < chunks) & (here < count - 1))
            def _():
                share(side, c).wait_recv()

                @pl.when(here > 0)
                def _():
                    share(side, c).start()

                finish(spot(side, c))

        between(t)
        return carry

    lax.fori_loop(0, chunks + 2 * (count - 1), step, 0)

    def drain(c, carry):
        for side in (0, 1):
            here = place(side)

            @pl.when(here < count - 1)
            def _():
                onward(side, c, inbox.at[side, c]).wait_send()

            @pl.when(here > 0)
            def _():
                share(side, c).wait_send()

        return carry

    lax.fori_loop(0, chunks, drain, 0)


def put_split(ref, rows, block):
    core = lax.axis_index("ctx")
    size = block.shape[1] // 8
    for owner in range(4):
        for index in range(2):
            low = (2 * owner + index) * size
            ref[(index + core) % 2, rows, owner * size : (owner + 1) * size] = block[:, low : low + size]


CHUNK = 32
LINE_COST = pl.CostEstimate(flops=0, bytes_accessed=400_000_000, transcendentals=0)


def enter_kernel(
    tokens, upstream, gain_shard, recur, gelu, merge,
    normed, halves, upstream_halves, gains, whole_in, whole_merge,
    stage_recur, stage_gelu, stage_merge, send, arrive, local, gain_send, gain_arrive,
):
    square = Square()
    greet(False, True)
    width = gain_shard.shape[1]

    def gain_copy(k, owner, target):
        spot = gains.at[:, pl.ds(pl.multiple_of(owner * width, 128), width)]
        return remote(gain_shard, spot, gain_send.at[k], gain_arrive.at[k], fsdp=target)

    others = (*square.near, square.far)
    for k, target in enumerate(others):
        gain_copy(k, square.me, target).start()
    gather = Gather(
        [(recur, whole_in, 0, 0), (gelu, whole_in, 0, recur.shape[1]), (merge, whole_merge, 1, 0)],
        (stage_recur, stage_gelu, stage_merge), send, arrive, local,
    )
    for w in range(3):
        gather.start(w)
    gains[:, pl.ds(pl.multiple_of(square.me * width, 128), width)] = gain_shard[...]
    for k, owner in enumerate(others):
        gain_copy(k, owner, owner).wait_recv()

    def norm(t, carry):
        rows = pl.ds(pl.multiple_of(t * CHUNK, CHUNK), CHUNK)
        block = tokens[rows, :].astype(F32)
        block = (block * rms_scale(block) * gains[0:1, :]).astype(BF16)
        normed[rows, :] = block
        put_split(halves, rows, block)
        put_split(upstream_halves, rows, upstream[rows, :])
        return carry

    lax.fori_loop(0, tokens.shape[0] // CHUNK, norm, 0)
    for w in range(3):
        gather.forward(w)
    for w in range(3):
        gather.hand_over(w)
    for w in range(3):
        gather.finish(w)
    for k, target in enumerate(others):
        gain_copy(k, square.me, target).wait_send()


ANY = pl.BlockSpec(memory_space=pl.ANY)
NEAR = pl.BlockSpec(memory_space=pltpu.VMEM)


def gather_scratch(shards):
    count = len(shards)
    dma = pltpu.SemaphoreType.DMA
    return [pltpu.VMEM(w.shape, w.dtype) for w in shards] + [dma((count, 7)), dma((count, 7)), dma((count, 2))]


def enter(tokens, upstream, gain_shard, recur, gelu, merge):
    rows, features = tokens.shape
    shape = jax.ShapeDtypeStruct
    inner = recur.shape[1]
    dma = pltpu.SemaphoreType.DMA
    return pl.pallas_call(
        enter_kernel,
        out_shape=(
            shape((rows, features), BF16),
            shape((2, rows, features // 2), BF16),
            shape((2, rows, features // 2), BF16),
            shape((8, features), F32),
            shape((features, 2 * inner), BF16),
            shape((inner, features), BF16),
        ),
        in_specs=[NEAR, NEAR, NEAR, ANY, ANY, ANY],
        out_specs=[NEAR, NEAR, NEAR, NEAR, ANY, ANY],
        scratch_shapes=gather_scratch([recur, gelu, merge]) + [dma((3,)), dma((3,))],
        compiler_params=pltpu.CompilerParams(collective_id=1, has_side_effects=True),
        name="enter",
    )(tokens, upstream, gain_shard, recur, gelu, merge)


def line_scratch(rows, features):
    chunks = rows // 2 // CHUNK
    dma = pltpu.SemaphoreType.DMA((2, chunks))
    return [pltpu.VMEM((2, chunks, CHUNK, features), BF16), dma, dma, dma, dma]


class Fetch:
    def __init__(self, sources, targets, sems):
        self.copies = [pltpu.make_async_copy(a, b, sems.at[k]) for k, (a, b) in enumerate(zip(sources, targets))]

    def start(self):
        for copy in self.copies:
            copy.start()

    def wait(self):
        for copy in self.copies:
            copy.wait()


def middle_kernel(gathers, part, far_tokens, gains, *refs):
    *refs, tokens, fetch_sems = refs
    fetch = Fetch((far_tokens,), (tokens,), fetch_sems)
    fetch.start()
    if gathers:
        gate, up, down, merged, normed, halves, whole_in, whole_down = refs[:8]
        inbox, *rest = refs[8:]
        sems, (stage_gate, stage_up, stage_down, send, arrive, local) = rest[:4], rest[4:]
        gather = Gather(
            [(gate, whole_in, 0, 0), (up, whole_in, 0, gate.shape[1]), (down, whole_down, 1, 0)],
            (stage_gate, stage_up, stage_down), send, arrive, local,
        )
        greet(True, True)
        for w in range(3):
            gather.start(w)
    else:
        merged, normed, inbox, *sems = refs
        greet(True, False)

    def finish(rows):
        block = tokens[rows, :].astype(F32) + merged[rows, :].astype(F32)
        block = (block * rms_scale(block) * gains[1:2, :]).astype(BF16)
        normed[rows, :] = block
        if gathers:
            put_split(halves, rows, block)

    def between(t):
        @pl.when(t == 0)
        def _():
            fetch.wait()

        if gathers:
            for w in range(3):
                @pl.when(t == 5 + 4 * w)
                def _():
                    gather.forward(w)

                @pl.when(t == 17 + w)
                def _():
                    gather.hand_over(w)

    line_sum(part, merged, inbox, sems, finish, between)
    if gathers:
        for w in range(3):
            gather.finish(w)


def middle(part, tokens, gains, shards):
    rows, features = tokens.shape
    shape = jax.ShapeDtypeStruct
    whole = shape((rows, features), BF16)
    outs, specs = [whole, whole], [NEAR, NEAR]
    scratch = line_scratch(rows, features)
    if shards:
        gate, up, down = shards
        outs += [
            shape((2, rows, features // 2), BF16),
            shape((features, 2 * gate.shape[1]), BF16),
            shape((down.shape[0], features), BF16),
        ]
        specs += [NEAR, ANY, ANY]
        scratch += gather_scratch(shards)
    scratch += [pltpu.VMEM((rows, features), BF16), pltpu.SemaphoreType.DMA((1,))]
    return pl.pallas_call(
        lambda *refs: middle_kernel(bool(shards), *refs),
        out_shape=tuple(outs),
        in_specs=[NEAR, ANY, NEAR] + [ANY] * len(shards),
        out_specs=specs,
        scratch_shapes=scratch,
        compiler_params=pltpu.CompilerParams(collective_id=2, has_side_effects=True),
        cost_estimate=LINE_COST,
        name="middle",
    )(part, tokens, gains, *shards)


def turn_kernel(split, part, far_tokens, far_merged, far_upstream, gains, own, grad_in, gain_sum, *refs):
    if split:
        halves, *refs = refs
    whole, wide, tokens, merged, upstream, fetch_sems, inbox, *sems = refs
    fetch = Fetch((far_tokens, far_merged, far_upstream), (tokens, merged, upstream), fetch_sems)
    fetch.start()
    greet(True, False)
    gain_sum[...] = jnp.zeros_like(gain_sum)
    width = own.shape[1]
    start = pl.multiple_of(lax.axis_index("tp") * width, 128)

    def finish(rows):
        block = tokens[rows, :].astype(F32) + merged[rows, :].astype(F32)
        scale = rms_scale(block)
        grad = whole[rows, :].astype(F32)
        gain_sum[0:1, :] += jnp.sum(grad * (block * scale), axis=0, keepdims=True)
        grad = grad * gains[1:2, :]
        mean = jnp.mean(block * grad, axis=-1, keepdims=True)
        grad = upstream[rows, :].astype(F32) + scale * grad - block * (scale * scale * scale * mean)
        wide[...] = grad
        own[rows, :] = wide[:, pl.ds(start, width)]
        grad = grad.astype(BF16)
        grad_in[rows, :] = grad
        if split:
            put_split(halves, rows, grad)

    def between(t):
        @pl.when(t == 0)
        def _():
            fetch.wait()

    line_sum(part, whole, inbox, sems, finish, between)


def turn(part, tokens, merged, upstream, gains, split):
    rows, features = tokens.shape
    shape = jax.ShapeDtypeStruct
    outs = [
        shape((rows, features // lax.axis_size("tp")), F32),
        shape((rows, features), BF16),
        shape((8, features), F32),
    ]
    if split:
        outs.append(shape((2, rows, features // 2), BF16))
    return pl.pallas_call(
        lambda *refs: turn_kernel(split, *refs),
        out_shape=tuple(outs),
        in_specs=[NEAR, ANY, ANY, ANY, NEAR],
        out_specs=[NEAR] * len(outs),
        scratch_shapes=[pltpu.VMEM((rows, features), BF16), pltpu.VMEM((CHUNK, features), F32)]
        + [pltpu.VMEM((rows, features), BF16)] * 3
        + [pltpu.SemaphoreType.DMA((3,))]
        + line_scratch(rows, features),
        compiler_params=pltpu.CompilerParams(collective_id=3, has_side_effects=True),
        cost_estimate=LINE_COST,
        name="turn",
    )(part, tokens, merged, upstream, gains)


def rounded_sum(*blocks):
    total = blocks[0].astype(F32)
    for block in blocks[1:]:
        total = total + block.astype(F32)
    return total.astype(BF16)


class Scatter:
    def __init__(self, items, boxes, lasts, send, arrive):
        self.items, self.boxes, self.lasts = items, boxes, lasts
        self.send, self.arrive = send, arrive
        self.square = Square()

    def block(self, w, owner, k):
        part, _, dim = self.items[w]
        size = part.shape[dim] // 4
        if dim == 0:
            low = pl.multiple_of(owner * size + k * (size // 2), 128)
            return part.at[pl.ds(low, size // 2), :]
        half = part.shape[0] // 2
        return part.at[pl.ds(k * half, half), pl.ds(pl.multiple_of(owner * size, 128), size)]

    def spot(self, w, k):
        part, out, dim = self.items[w]
        size = part.shape[dim] // 4
        low = pl.multiple_of(self.square.core * size, 128)
        if dim == 0:
            return out.at[pl.ds(low + k * (size // 2), size // 2), :]
        half = part.shape[0] // 2
        return out.at[pl.ds(k * half, half), pl.ds(low, size)]

    def copy(self, w, k, j):
        square = self.square
        first, second = square.near[k], square.near[1 - k]
        send, arrive = self.send.at[w, 4 * k + j], self.arrive.at[w, 4 * k + j]
        if j < 2:
            owner = square.far if j == 0 else first
            return remote(self.block(w, owner, k), self.boxes[w].at[k, j], send, arrive, fsdp=first)
        if j == 2:
            return remote(self.boxes[w].at[k, 0], self.lasts[w].at[k], send, arrive, fsdp=second)
        return remote(self.spot(w, k), self.spot(w, k), send, arrive, ctx=1 - square.core)

    def start(self, w):
        for j in (0, 1):
            for k in (0, 1):
                self.copy(w, k, j).start()

    def relay(self, w):
        for k in (0, 1):
            self.copy(w, k, 0).wait_recv()
            mine = self.block(w, self.square.near[1 - k], k)
            self.boxes[w][k, 0] = rounded_sum(mine[...], self.boxes[w][k, 0])
            self.copy(w, k, 2).start()

    def finish(self, w):
        for k in (0, 1):
            self.copy(w, k, 1).wait_recv()
            self.copy(w, k, 2).wait_recv()
            mine = self.block(w, self.square.me, k)
            self.spot(w, k)[...] = rounded_sum(mine[...], self.boxes[w][k, 1], self.lasts[w][k])
            self.copy(w, k, 3).start()

    def drain(self, w):
        for k in (0, 1):
            self.copy(w, k, 3).wait_recv()
            for j in range(4):
                self.copy(w, k, j).wait_send()


def scatter_scratch(items):
    blocks = []
    for shape, dim in items:
        rows, cols = (shape[0] // 8, shape[1]) if dim == 0 else (shape[0] // 2, shape[1] // 4)
        blocks.append((rows, cols))
    dma = pltpu.SemaphoreType.DMA((len(items), 8))
    return (
        [pltpu.VMEM((2, 2, *block), BF16) for block in blocks]
        + [pltpu.VMEM((2, *block), BF16) for block in blocks]
        + [dma, dma]
    )


def leave_kernel(
    part_in, part_merge, gates, sums, norms, stats,
    own_in, own_merge, gate_sums, row_sums, norm_sums, stat_sums,
    box_in, box_merge, last_in, last_merge, send, arrive,
    gate_core, gate_half, gate_near, gate_pair, gate_far, gate_send, gate_arrive,
    core_sums, core_norms, box_sums, box_norms, sum_send, sum_arrive,
    line_norms, line_stats, norm_send, norm_arrive, stat_send, stat_arrive,
):
    square = Square()
    count, place = lax.axis_size("tp"), lax.axis_index("tp")
    core = square.core
    others = (*square.near, square.far)
    greet(False, True, True)

    def norm_copy(k, source):
        box = line_norms.at[source]
        return remote(box, box, norm_send.at[k], norm_arrive.at[source], tp=k)

    def stat_copy(k, source):
        return remote(stats, line_stats.at[source], stat_send.at[k], stat_arrive.at[source], tp=k)

    def core_copy(k):
        source, target = ((sums, core_sums), (norms, core_norms))[k]
        return remote(source, target, sum_send.at[k], sum_arrive.at[k], ctx=1 - core)

    def square_copy(k, j):
        box = (box_sums, box_norms)[k].at[square.me]
        at = 2 + 3 * k + j
        return remote(box, box, sum_send.at[at], sum_arrive.at[at], fsdp=others[j])

    gate_rows = gates.shape[0] // 2
    gate_cols = gates.shape[1] // 2
    my_rows = pl.ds(pl.multiple_of(core * gate_rows, 16), gate_rows)
    your_rows = pl.ds(pl.multiple_of((1 - core) * gate_rows, 16), gate_rows)

    def gate_copy(j):
        send, arrive = gate_send.at[j], gate_arrive.at[j]
        if j == 0:
            return remote(gates.at[your_rows, :], gate_core, send, arrive, ctx=1 - core)
        if j == 5:
            spot = gate_sums.at[my_rows, :]
            return remote(spot, spot, send, arrive, ctx=1 - core)
        k = (j - 1) % 2
        if j < 3:
            return remote(gate_half.at[k], gate_near.at[k], send, arrive, fsdp=square.near[k])
        return remote(gate_pair.at[k], gate_far.at[k], send, arrive, fsdp=square.near[1 - k])

    scatter = Scatter(
        [(part_merge, own_merge, 1), (part_in, own_in, 0)], (box_merge, box_in), (last_merge, last_in), send, arrive
    )
    gate_copy(0).start()
    core_copy(0).start()
    core_copy(1).start()
    scatter.start(0)
    for k in range(count):
        @pl.when(place != k)
        def _():
            stat_copy(k, place).start()

    line_stats[place] = stats[...]
    core_copy(0).wait_recv()
    core_copy(1).wait_recv()
    box_sums[square.me] = sums[...] + core_sums[...]
    box_norms[square.me] = norms[...] + core_norms[...]
    for k in (0, 1):
        for j in range(3):
            square_copy(k, j).start()
    gate_copy(0).wait_recv()
    for k in (0, 1):
        cols = slice(k * gate_cols, (k + 1) * gate_cols)
        gate_half[k] = rounded_sum(gates[my_rows, cols], gate_core[:, cols])
        gate_copy(1 + k).start()
    scatter.start(1)
    for k in (0, 1):
        for j in range(3):
            square_copy(k, j).wait_recv()
    row_sums[...] = box_sums[0] + box_sums[1] + box_sums[2] + box_sums[3]
    line_norms[place] = box_norms[0] + box_norms[1] + box_norms[2] + box_norms[3]
    for k in range(count):
        @pl.when(place != k)
        def _():
            norm_copy(k, place).start()

    for k in (0, 1):
        gate_copy(1 + k).wait_recv()
        gate_pair[k] = rounded_sum(gate_half[k], gate_near[k])
        gate_copy(3 + k).start()
    scatter.relay(0)
    scatter.relay(1)
    for k in (0, 1):
        cols = slice(k * gate_cols, (k + 1) * gate_cols)
        gate_copy(3 + k).wait_recv()
        gate_sums[my_rows, cols] = rounded_sum(gate_pair[k], gate_far[k])
    gate_copy(5).start()
    for k in range(count):
        @pl.when(place != k)
        def _():
            norm_copy(k, k).wait_recv()
            stat_copy(k, k).wait_recv()

    total = line_norms[0]
    stat = line_stats[0]
    for k in range(1, count):
        total = total + line_norms[k]
        stat = stat + line_stats[k]
    norm_sums[...] = total
    stat_sums[...] = stat
    scatter.finish(0)
    scatter.finish(1)
    for w in (0, 1):
        scatter.drain(w)
    gate_copy(5).wait_recv()
    for j in range(6):
        gate_copy(j).wait_send()
    for k in (0, 1):
        core_copy(k).wait_send()
        for j in range(3):
            square_copy(k, j).wait_send()
    for k in range(count):
        @pl.when(place != k)
        def _():
            norm_copy(k, place).wait_send()
            stat_copy(k, place).wait_send()


def leave(part_in, part_merge, gates, sums, norms, stats):
    shape = jax.ShapeDtypeStruct
    count = lax.axis_size("tp")
    dma = pltpu.SemaphoreType.DMA
    height, width = gates.shape[0] // 2, gates.shape[1] // 2
    quarter = pltpu.VMEM((2, height, width), BF16)
    return pl.pallas_call(
        leave_kernel,
        out_shape=(
            shape((part_in.shape[0] // 2, part_in.shape[1]), BF16),
            shape((part_merge.shape[0], part_merge.shape[1] // 2), BF16),
            shape(gates.shape, BF16),
            shape(sums.shape, F32),
            shape(norms.shape, F32),
            shape(stats.shape, F32),
        ),
        in_specs=[NEAR] * 6,
        out_specs=[NEAR] * 6,
        scratch_shapes=(
            (lambda boxes: [boxes[1], boxes[0], boxes[3], boxes[2], boxes[4], boxes[5]])(
                scatter_scratch([(part_merge.shape, 1), (part_in.shape, 0)])
            )
            + [pltpu.VMEM((height, 2 * width), BF16), quarter, quarter, quarter, quarter, dma((6,)), dma((6,))]
            + [pltpu.VMEM(sums.shape, F32), pltpu.VMEM(norms.shape, F32)]
            + [pltpu.VMEM((4, *sums.shape), F32), pltpu.VMEM((4, *norms.shape), F32), dma((8,)), dma((8,))]
            + [pltpu.VMEM((count, *norms.shape), F32), pltpu.VMEM((count, *stats.shape), F32)]
            + [dma((count,))] * 4
        ),
        compiler_params=pltpu.CompilerParams(collective_id=4, has_side_effects=True),
        cost_estimate=pl.CostEstimate(flops=0, bytes_accessed=160_000_000, transcendentals=0),
        name="leave",
    )(part_in, part_merge, gates, sums, norms, stats)


def gelu_pair(q):
    tanh = jnp.tanh(ROOT * (q + CUBE * q * q * q))
    value = 0.5 * q * (1.0 + tanh)
    slope = 0.5 * (1.0 + tanh) + 0.5 * q * (1.0 - tanh * tanh) * ROOT * (1.0 + 3.0 * CUBE * q * q)
    return value, slope


def rms_scale(values):
    return lax.rsqrt(jnp.mean(values * values, axis=-1, keepdims=True) + EPS)


def decay_parts(rate, softer, keep):
    gap = 2.0 * CGAIN * rate * softer
    decay = jnp.exp(-0.5 * gap)
    series = gap * (
        1.0
        - gap / 2.0
        * (1.0 - gap / 3.0 * (1.0 - gap / 4.0 * (1.0 - gap / 5.0 * (1.0 - gap / 6.0 * (1.0 - gap / 7.0)))))
    )
    square = jnp.where(gap < 0.25, series, 1.0 - decay * decay)
    return jnp.where(keep, decay, 0.0), jnp.where(keep, square, 1.0)


LANES = 128


def put_lanes(ref, block, rows):
    for lane in range(ref.shape[0]):
        ref[lane, 0:rows, :] = block[:, lane * LANES : (lane + 1) * LANES]


def sweep(decay_ref, value_ref, state_ref, product_ref, out_ref, run_ref, carry_ref, reverse, offset):
    groups, rows, _ = value_ref.shape
    steps = rows // SEGS
    place = lax.broadcasted_iota(jnp.int32, (SEGS, LANES), 0)
    if reverse:
        place = SEGS - 1 - place

    def moved(block, by, fill):
        turned = pltpu.roll(block, SEGS - by if reverse else by, 0)
        return jnp.where(place >= by, turned, fill)

    for lane in range(groups):
        lanes = slice(lane * LANES, (lane + 1) * LANES)
        state = jnp.zeros((SEGS, LANES), F32)
        product = jnp.ones((SEGS, LANES), F32)
        for step in reversed(range(steps)) if reverse else range(steps):
            spot = pl.ds(step, SEGS, stride=steps)
            decay = decay_ref[lane, pl.ds(step + offset, SEGS, stride=steps), :]
            state = decay * state + value_ref[lane, spot, :]
            product = product * decay
            state_ref[lane, spot, :] = state
            product_ref[lane, spot, :] = product
        for by in (1, 2, 4):
            state = state + product * moved(state, by, 0.0)
            product = product * moved(product, by, 1.0)
        carry = carry_ref[0:1, lanes]
        carry_run = carry_ref[8:9, lanes]
        state = state + product * carry
        product = product * carry_run
        enter = moved(state, 1, carry)
        enter_run = moved(product, 1, carry_run)
        for seg in range(SEGS):
            span = slice(seg * steps, (seg + 1) * steps)
            inner = product_ref[lane, span, :]
            out_ref[span, lanes] = state_ref[lane, span, :] + inner * enter[seg : seg + 1, :]
            run_ref[span, lanes] = inner * enter_run[seg : seg + 1, :]
        last = 0 if reverse else SEGS - 1
        carry_ref[0:1, lanes] = state[last : last + 1, :]
        carry_ref[8:9, lanes] = product[last : last + 1, :]


def spread_blocks(blocks_ref, out_ref):
    chans, size = blocks_ref.shape[1:]
    row = lax.broadcasted_iota(jnp.int32, (chans, chans), 0)
    col = lax.broadcasted_iota(jnp.int32, (chans, chans), 1)
    inner = lax.broadcasted_iota(jnp.int32, (size, chans), 0)
    outer = lax.broadcasted_iota(jnp.int32, (size, chans), 1)
    inside = row < 0
    repeat = outer < 0
    for low in range(0, chans, size):
        inside |= (row >= low) & (row < low + size) & (col >= low) & (col < low + size)
        repeat |= outer - low == inner
    repeat = repeat.astype(F32).astype(BF16)
    for gate in range(2):
        wide = jnp.dot(blocks_ref[gate], repeat, preferred_element_type=F32)
        out_ref[:, gate * chans : (gate + 1) * chans] = jnp.where(inside, wide, 0.0).astype(BF16)


def forward_kernel(
    branch_ref, halo_ref, mask_ref, taps_ref, bias_ref, blocks_ref, gate_bias_ref, softer_ref,
    conv_ref, rate_ref, entry_ref, state_ref, run_ref, gates_ref,
    window, decay, value, inner, product, carry,
):
    rows, chans = conv_ref.shape
    spot = pl.program_id(0)

    @pl.when(spot == 0)
    def _():
        spread_blocks(blocks_ref, gates_ref)
        window[0:8, :] = halo_ref[...].astype(F32)
        carry[0:8, :] = jnp.zeros((8, chans), F32)
        carry[8:16, :] = jnp.ones((8, chans), F32)

    @pl.when(spot > 0)
    def _():
        window[0:8, :] = window[rows : rows + 8, :]

    window[8 : rows + 8, :] = branch_ref[...].astype(F32)
    mixed = bias_ref[...] + taps_ref[0:1, :] * window[8 : rows + 8, :]
    for shift in range(1, taps_ref.shape[0]):
        moved = window[8 - shift : 8 - shift + rows, :]
        mixed = mixed + taps_ref[shift : shift + 1, :] * (moved * mask_ref[:, shift : shift + 1])
    conv = mixed.astype(BF16)
    conv_ref[...] = conv
    pre = jnp.dot(conv, gates_ref[...], preferred_element_type=F32) + gate_bias_ref[...]
    rate = jax.nn.sigmoid(pre[:, :chans])
    entry = jax.nn.sigmoid(pre[:, chans:])
    rate_ref[...] = rate
    entry_ref[...] = entry
    keep = jnp.broadcast_to(mask_ref[:, 0:1], (rows, chans)) > 0.5
    step, square = decay_parts(rate, softer_ref[...], keep)
    put_lanes(decay, step, rows)
    put_lanes(value, jnp.sqrt(square) * entry * conv.astype(F32), rows)
    sweep(decay, value, inner, product, state_ref, run_ref, carry, False, 0)


def tile_spec(width, count=None):
    if count is None:
        return pl.BlockSpec((TILE, width), lambda i: (i, 0))
    return pl.BlockSpec((TILE, width), lambda i: (count - 1 - i, 0))


def fixed_spec(shape):
    return pl.BlockSpec(shape, lambda i: (0, 0))


def recur_forward(branch, halo, masks, taps, bias, blocks, gate_bias, softer):
    rows, chans = branch.shape[0], halo.shape[1]
    wide = jax.ShapeDtypeStruct((rows, chans), F32)
    return pl.pallas_call(
        forward_kernel,
        grid=(rows // TILE,),
        out_shape=(
            jax.ShapeDtypeStruct((rows, chans), BF16), wide, wide, wide, wide,
            jax.ShapeDtypeStruct((chans, 2 * chans), BF16),
        ),
        in_specs=[
            tile_spec(chans),
            fixed_spec((8, chans)),
            tile_spec(masks.shape[1]),
            fixed_spec(taps.shape),
            fixed_spec((1, chans)),
            pl.BlockSpec(blocks.shape, lambda i: (0, 0, 0)),
            fixed_spec((1, 2 * chans)),
            fixed_spec((1, chans)),
        ],
        out_specs=[tile_spec(chans)] * 5 + [fixed_spec((chans, 2 * chans))],
        scratch_shapes=[
            pltpu.VMEM((TILE + 8, chans), F32),
            pltpu.VMEM((chans // LANES, TILE, LANES), F32),
            pltpu.VMEM((chans // LANES, TILE, LANES), F32),
            pltpu.VMEM((chans // LANES, TILE, LANES), F32),
            pltpu.VMEM((chans // LANES, TILE, LANES), F32),
            pltpu.VMEM((16, chans), F32),
        ],
        cost_estimate=pl.CostEstimate(
            flops=2 * rows * chans * 2 * chans, bytes_accessed=24 * rows * chans, transcendentals=5 * rows * chans
        ),
        name="recur_forward",
    )(branch, halo, masks, taps, bias, blocks, gate_bias, softer)


def merge_kernel(local_ref, run_ref, enter_ref, pre_ref, weight_ref, state_ref, gated_ref, part_ref):
    state = local_ref[...] + run_ref[...] * enter_ref[0:1, :]
    state_ref[...] = state
    pre = pre_ref[...].astype(F32)
    gated = (state * gelu_pair(pre)[0]).astype(BF16)
    gated_ref[...] = gated
    part_ref[...] = jnp.dot(gated, weight_ref[...], preferred_element_type=F32).astype(BF16)


def merge_states(local, run, enter, branches, weight):
    rows, chans = local.shape
    features = weight.shape[1]
    shape = jax.ShapeDtypeStruct
    return pl.pallas_call(
        merge_kernel,
        grid=(rows // TILE,),
        out_shape=(shape((rows, chans), F32), shape((rows, chans), BF16), shape((rows, features), BF16)),
        in_specs=[
            tile_spec(chans), tile_spec(chans), fixed_spec((1, chans)),
            pl.BlockSpec((TILE, chans), lambda i: (i, 1)),
            fixed_spec(weight.shape),
        ],
        out_specs=[tile_spec(chans), tile_spec(chans), tile_spec(features)],
        cost_estimate=pl.CostEstimate(
            flops=2 * rows * chans * features, bytes_accessed=16 * rows * chans, transcendentals=rows * chans
        ),
        name="merge_states",
    )(local, run, enter, branches, weight)


def adjoint_kernel(
    rate_ref, up_ref, pre_ref, state_ref, mask_ref, softer_ref,
    grad_ref, run_ref, head_ref, pre_grad_ref,
    decay, value, inner, product, carry,
):
    rows, chans = rate_ref.shape
    groups = chans // LANES
    spot = pl.program_id(0)

    @pl.when(spot == 0)
    def _():
        for lane in range(groups):
            decay[lane, rows : rows + 8, :] = jnp.ones((8, LANES), F32)
        carry[0:8, :] = jnp.zeros((8, chans), F32)
        carry[8:16, :] = jnp.ones((8, chans), F32)

    @pl.when(spot > 0)
    def _():
        for lane in range(groups):
            decay[lane, rows : rows + 8, :] = decay[lane, 0:8, :]

    keep = jnp.broadcast_to(mask_ref[:, 0:1], (rows, chans)) > 0.5
    gap = CGAIN * rate_ref[...] * softer_ref[...]
    step = jnp.where(keep, jnp.exp(-gap), 0.0)
    put_lanes(decay, step, rows)
    gate, slope = gelu_pair(pre_ref[...].astype(F32))
    up = up_ref[...]
    pre_grad_ref[...] = (up * state_ref[...] * slope).astype(BF16)
    put_lanes(value, up * gate, rows)
    sweep(decay, value, inner, product, grad_ref, run_ref, carry, True, 1)
    head_ref[...] = jnp.broadcast_to(step[0:1, :] * carry[0:1, :], (8, chans))


def recur_adjoint(rate, up, branches, state, masks, softer):
    rows, chans = rate.shape
    count = rows // TILE
    wide = jax.ShapeDtypeStruct((rows, chans), F32)
    return pl.pallas_call(
        adjoint_kernel,
        grid=(count,),
        out_shape=(
            wide, wide, jax.ShapeDtypeStruct((8, chans), F32), jax.ShapeDtypeStruct((rows, chans), BF16)
        ),
        in_specs=[
            tile_spec(chans, count),
            tile_spec(chans, count),
            pl.BlockSpec((TILE, chans), lambda i: (count - 1 - i, 1)),
            tile_spec(chans, count),
            tile_spec(masks.shape[1], count),
            fixed_spec((1, chans)),
        ],
        out_specs=[tile_spec(chans, count), tile_spec(chans, count), fixed_spec((8, chans)), tile_spec(chans, count)],
        scratch_shapes=[
            pltpu.VMEM((chans // LANES, TILE + 8, LANES), F32),
            pltpu.VMEM((chans // LANES, TILE, LANES), F32),
            pltpu.VMEM((chans // LANES, TILE, LANES), F32),
            pltpu.VMEM((chans // LANES, TILE, LANES), F32),
            pltpu.VMEM((16, chans), F32),
        ],
        cost_estimate=pl.CostEstimate(
            flops=8 * rows * chans, bytes_accessed=16 * rows * chans, transcendentals=rows * chans
        ),
        name="recur_adjoint",
    )(rate, up, branches, state, masks, softer)


def backward_kernel(
    grad_ref, run_ref, enter_ref, rate_ref, entry_ref, conv_ref, state_ref, mask_ref,
    branch_ref, pre_grad_ref, halo_ref, taps_ref, gates_ref, softer_ref,
    back_ref, tail_ref, head_ref, gate_grad_ref, sums_ref,
    shifts, edge,
):
    rows, chans = conv_ref.shape
    width = taps_ref.shape[0]
    spot = pl.program_id(0)
    last = pl.num_programs(0) - 1

    @pl.when(spot == 0)
    def _():
        for shift in range(1, width):
            shifts[shift - 1, rows : rows + 8, :] = jnp.zeros((8, chans), F32)
        gate_grad_ref[...] = jnp.zeros_like(gate_grad_ref)
        sums_ref[...] = jnp.zeros_like(sums_ref)

    @pl.when(spot > 0)
    def _():
        for shift in range(1, width):
            shifts[shift - 1, rows : rows + 8, :] = shifts[shift - 1, 0:8, :]

    keep = jnp.broadcast_to(mask_ref[:, 0:1], (rows, chans)) > 0.5
    softer = softer_ref[...]
    rate = rate_ref[...]
    entry = entry_ref[...]
    conv = conv_ref[...].astype(F32)
    grad = grad_ref[...] + run_ref[...] * enter_ref[0:1, :]
    step, square = decay_parts(rate, softer, keep)
    inverse = lax.rsqrt(square)
    mult = square * inverse
    driven = entry * conv
    carried = state_ref[...] - mult * driven
    d_log = jnp.where(keep, grad * (carried - driven * step * step * inverse), 0.0)
    d_rate = (-CGAIN * softer * d_log * rate * (1.0 - rate)).astype(BF16)
    lifted = grad * mult * entry
    d_entry = (lifted * conv * (1.0 - entry)).astype(BF16)
    both = jnp.concatenate([d_rate, d_entry], axis=1)
    d_conv = lifted + lax.dot_general(
        both, gates_ref[...], (((1,), (1,)), ((), ())), preferred_element_type=F32
    )
    gate_grad_ref[...] += lax.dot_general(
        conv_ref[...], both, (((0,), (0,)), ((), ())), preferred_element_type=F32
    )

    def add_row(row, block):
        sums_ref[row : row + 1, :] += jnp.sum(block, axis=0, keepdims=True)

    branch = branch_ref[...].astype(F32)
    add_row(0, d_log * rate)
    add_row(1, d_rate.astype(F32))
    add_row(2, d_entry.astype(F32))
    add_row(3, d_conv)
    add_row(4, d_conv * branch)
    back = taps_ref[0:1, :] * d_conv
    for shift in range(1, width):
        shifts[shift - 1, 0:rows, :] = d_conv * mask_ref[:, shift : shift + 1]
        moved = shifts[shift - 1, shift : shift + rows, :]
        add_row(4 + shift, moved * branch)
        back = back + taps_ref[shift : shift + 1, :] * moved
    back_ref[:, 0:chans] = back.astype(BF16)
    back_ref[:, chans:] = pre_grad_ref[...]

    @pl.when(spot == 0)
    def _():
        tail_ref[...] = back[rows - 8 :, :]

    @pl.when(spot == last)
    def _():
        halo = halo_ref[...].astype(F32)
        head = jnp.zeros((8, chans), F32)
        edge[0:8, :] = head
        for shift in range(1, width):
            edge[8:16, :] = shifts[shift - 1, 0:8, :]
            moved = edge[shift : shift + 8, :]
            add_row(4 + shift, moved * halo)
            head = head + taps_ref[shift : shift + 1, :] * moved
        head_ref[...] = head


def recur_backward(grad, run, enter, rate, entry, conv, state, masks, branch, pre_grad, halo, taps, gates, softer):
    rows, chans = rate.shape
    count = rows // TILE
    edge = jax.ShapeDtypeStruct((8, chans), F32)
    wide = tile_spec(chans, count)
    return pl.pallas_call(
        backward_kernel,
        grid=(count,),
        out_shape=(
            jax.ShapeDtypeStruct((rows, 2 * chans), BF16),
            edge,
            edge,
            jax.ShapeDtypeStruct((chans, 2 * chans), F32),
            jax.ShapeDtypeStruct((16, chans), F32),
        ),
        in_specs=[
            wide, wide, fixed_spec((1, chans)), wide, wide, wide, wide,
            tile_spec(masks.shape[1], count),
            wide,
            wide,
            fixed_spec((8, chans)),
            fixed_spec(taps.shape),
            fixed_spec(gates.shape),
            fixed_spec((1, chans)),
        ],
        out_specs=[
            tile_spec(2 * chans, count),
            fixed_spec((8, chans)),
            fixed_spec((8, chans)),
            fixed_spec((chans, 2 * chans)),
            fixed_spec((16, chans)),
        ],
        scratch_shapes=[
            pltpu.VMEM((taps.shape[0] - 1, TILE + 8, chans), F32),
            pltpu.VMEM((16, chans), F32),
        ],
        cost_estimate=pl.CostEstimate(
            flops=8 * rows * chans * chans, bytes_accessed=28 * rows * chans, transcendentals=2 * rows * chans
        ),
        name="recur_backward",
    )(grad, run, enter, rate, entry, conv, state, masks, branch, pre_grad, halo, taps, gates, softer)


def shards(
    tokens,
    segments,
    cotangent,
    w_recur,
    w_gelu,
    w_merge,
    w_gate,
    w_up,
    w_down,
    norm_mix,
    norm_feed,
    conv_taps,
    conv_bias,
    rate_gate,
    entry_gate,
    rate_bias,
    entry_bias,
    decay_logit,
):
    piece = tokens.shape[0]
    width = conv_taps.shape[0]
    edge = width - 1
    heads, block = rate_gate.shape[0], rate_gate.shape[1]
    chans = conv_taps.shape[1]
    features = tokens.shape[1]
    feat_local = features // lax.axis_size("tp")
    feat_start = lax.axis_index("tp") * feat_local

    square = lax.axis_size("fsdp") == 4
    gain_shard = jnp.concatenate(
        [jnp.stack([norm_mix, norm_feed]).astype(F32), jnp.zeros((6, norm_mix.shape[0]), F32)], axis=0
    )
    if square:
        normed, normed_split, cotangent_split, gains, whole_in, whole_merge = enter(
            tokens, cotangent, gain_shard, w_recur, w_gelu, w_merge
        )
    else:
        whole_in = gather_halves(jnp.concatenate([w_recur, w_gelu], axis=1), 0)
        whole_merge = gather_halves(w_merge, 1)
        gains = lax.all_gather(gain_shard, "fsdp", axis=1, tiled=True)
        inputs = tokens.astype(F32)
        normed = (inputs * rms_scale(inputs) * gains[0:1]).astype(BF16)
        normed_split = split_features(normed)
        cotangent_split = split_features(cotangent)
    gain_one = gains[0:1]

    padded_ids = jnp.concatenate([jnp.full((edge,), -1, jnp.int32), segments])
    local_ids = lax.dynamic_slice_in_dim(padded_ids, lax.axis_index("ctx") * piece, piece + edge)
    own_ids = local_ids[edge:]
    masks = jnp.stack(
        [(local_ids[edge - max(shift, 1) : edge - max(shift, 1) + piece] == own_ids) for shift in range(width)],
        axis=1,
    ).astype(F32)
    taps = conv_taps.astype(F32)
    blocks = jnp.stack([rate_gate.reshape(chans, block), entry_gate.reshape(chans, block)])
    gate_bias = jnp.concatenate([rate_bias, entry_bias]).astype(F32)[None, :]
    softer = jax.nn.softplus(-decay_logit)[None, :]

    rows_to_features = (((1,), (1,)), ((), ()))
    branches = jnp.dot(normed, whole_in, preferred_element_type=F32).astype(BF16)
    halo = shifted(branches[piece - 8 :, :chans], "ctx", 1)
    conv, rate, entry, local_state, run, gates = recur_forward(
        branches, halo, masks, taps, conv_bias.astype(F32)[None, :], blocks, gate_bias, softer
    )
    state_in = shifted(local_state[piece - 8 :], "ctx", 1)[7:8]
    states, gated, part_merge = merge_states(local_state, run, state_in, branches, whole_merge)

    if square:
        merged, normed_two, normed_two_split, whole_mid, whole_down = middle(
            part_merge, tokens, gains, (w_gate, w_up, w_down)
        )
    else:
        merged, normed_two = middle(part_merge, tokens, gains, ())
        normed_two_split = split_features(normed_two)
        whole_mid = gather_halves(jnp.concatenate([w_gate, w_up], axis=1), 0)
        whole_down = gather_halves(w_down, 1)

    units = w_gate.shape[1]
    pre_mid = jnp.dot(normed_two, whole_mid, preferred_element_type=F32).astype(BF16)
    d_hidden = lax.dot_general(cotangent, whole_down, rows_to_features, preferred_element_type=F32).astype(BF16)
    gate_act, gate_slope = gelu_pair(pre_mid[:, :units].astype(F32))
    up_vals = pre_mid[:, units:].astype(F32)
    wide_hidden = d_hidden.astype(F32)
    hidden = (gate_act * up_vals).astype(BF16)
    d_mid = jnp.concatenate(
        [(wide_hidden * up_vals * gate_slope).astype(BF16), (wide_hidden * gate_act).astype(BF16)], axis=1
    )
    part_feed = jnp.dot(hidden, whole_down, preferred_element_type=F32).astype(BF16)
    feed = lax.psum_scatter(part_feed, "tp", scatter_dimension=1, tiled=True)
    hidden = after(hidden, part_feed)
    part_two = lax.dot_general(d_mid, after(whole_mid, part_feed), rows_to_features, preferred_element_type=F32).astype(BF16)
    pair_down = pair_sums(cotangent_split, hidden, 1)
    pair_mid = pair_sums(after(normed_two_split, part_feed), d_mid, 0, part_two)
    part_two = after(part_two, pair_down, pair_mid)
    turned = turn(part_two, tokens, merged, cotangent, gains, square)
    own_resid_grad, d_merge_in, feed_sums = turned[:3]
    d_merge_split = turned[3] if square else split_features(d_merge_in)
    half_down = half_to_owners(pair_down, 1)
    half_mid = half_to_owners(pair_mid, 0)
    d_merge_in = after(d_merge_in, half_down, feed)

    d_gated = lax.dot_general(d_merge_in, whole_merge, rows_to_features, preferred_element_type=F32)
    local_grad, grad_run, first, d_gelu_pre = recur_adjoint(rate, d_gated, branches, states, masks, softer)
    grad_in = shifted(first, "ctx", -1)[0:1]
    back, tail, head, gate_grads, sums = recur_backward(
        local_grad, grad_run, grad_in, rate, after(entry, half_mid), conv, states, masks, branches, d_gelu_pre,
        halo, taps, gates, softer
    )
    returned = shifted(head, "ctx", -1)
    d_in = lax.dynamic_update_slice(back, (tail + returned).astype(BF16), (piece - 8, 0))
    part_one = lax.dot_general(d_in, whole_in, rows_to_features, preferred_element_type=F32).astype(BF16)
    d_normed = lax.psum_scatter(part_one, "tp", scatter_dimension=1, tiled=True)

    pair_merge = pair_sums(d_merge_split, after(gated, part_one), 1)
    pair_in = pair_sums(normed_split, after(d_in, part_one), 0)
    inputs = tokens.astype(F32)
    scale_one = rms_scale(inputs)
    wide_part = part_one.astype(F32)
    stat_one = jnp.sum(wide_part * inputs * gain_one, axis=-1)
    grad_mix = jnp.sum(wide_part * inputs * scale_one, axis=0)
    norm_sums = jnp.stack([grad_mix, feed_sums[0] / lax.axis_size("tp")])
    spread = jnp.arange(2 * chans)[None, :] % chans // block
    diagonal = sum(jnp.where(spread == i, gate_grads[i * block : (i + 1) * block], 0.0) for i in range(heads))
    diagonal = diagonal.astype(BF16)
    if square:
        norm_sums = jnp.pad(norm_sums, ((0, 6), (0, 0)))
        own_in, own_merge, gate_sums, row_sums, both_norms, line_stats = leave(
            pair_in, pair_merge, diagonal, sums, norm_sums, stat_one.reshape(-1, 128)
        )
        shard_in, shard_merge = own_in.astype(F32), own_merge.astype(F32)
        stat_one = line_stats.reshape(-1)
    else:
        shard_in = both_halves(half_to_owners(pair_in, 0), 0)
        shard_merge = both_halves(half_to_owners(pair_merge, 1), 1)
        gate_sums = lax.psum(diagonal, ("fsdp", "ctx"))
        row_sums = lax.psum(sums, ("fsdp", "ctx"))
        both_norms = lax.psum(norm_sums, ("fsdp", "ctx", "tp"))
        stat_one = lax.psum(stat_one, "tp")
    stat_one = stat_one[:, None] / features
    shard_down = both_halves(half_down, 1)
    shard_mid = both_halves(half_mid, 0)
    gate_sums = gate_sums.astype(F32).reshape(block, 2, heads, block).transpose(1, 2, 0, 3)

    def own(block):
        return lax.dynamic_slice_in_dim(block, feat_start, feat_local, 1)

    own_inputs = own(tokens).astype(F32)
    output = (own_inputs + own(merged).astype(F32) + feed.astype(F32)).astype(BF16)
    grad_tokens = (
        own_resid_grad
        + scale_one * d_normed.astype(F32) * own(gain_one)
        - own_inputs * scale_one**3 * stat_one
    ).astype(BF16)

    norm_local = norm_mix.shape[0]
    own_norms = lax.dynamic_slice_in_dim(both_norms, lax.axis_index("fsdp") * norm_local, norm_local, 1)

    return (
        output,
        grad_tokens,
        shard_in[:, :chans],
        shard_in[:, chans:],
        shard_merge,
        shard_mid[:, :units],
        shard_mid[:, units:],
        shard_down,
        own_norms[0],
        own_norms[1],
        row_sums[4 : 4 + width],
        row_sums[3],
        gate_sums[0],
        gate_sums[1],
        row_sums[1],
        row_sums[2],
        CGAIN * row_sums[0] * jax.nn.sigmoid(-decay_logit),
    )


def solution(mesh):
    placed = (
        P(("fsdp", "ctx"), None),
        P("fsdp"),
        P(("fsdp", "ctx"), None),
        P("fsdp", "tp"),
        P("fsdp", "tp"),
        P("tp", "fsdp"),
        P("fsdp", "tp"),
        P("fsdp", "tp"),
        P("tp", "fsdp"),
        P("fsdp"),
        P("fsdp"),
        P(None, "tp"),
        P("tp"),
        P("tp", None, None),
        P("tp", None, None),
        P("tp"),
        P("tp"),
        P("tp"),
    )
    return jax.shard_map(
        shards,
        mesh=mesh,
        in_specs=placed,
        out_specs=(
            P(("fsdp", "ctx"), "tp"),
            P(("fsdp", "ctx"), "tp"),
            P("fsdp", "tp"),
            P("fsdp", "tp"),
            P("tp", "fsdp"),
            P("fsdp", "tp"),
            P("fsdp", "tp"),
            P("tp", "fsdp"),
            P("fsdp"),
            P("fsdp"),
            P(None, "tp"),
            P("tp"),
            P("tp", None, None),
            P("tp", None, None),
            P("tp"),
            P("tp"),
            P("tp"),
        ),
        check_vma=False,
    )
```

```python
import jax
import jax.numpy as jnp
from jax import lax
from jax.experimental import pallas as pl
from jax.experimental.pallas import tpu as pltpu
from jax.sharding import PartitionSpec as P

EPS = 1e-06
CGAIN = 8.0
ROOT = 0.7978845608
CUBE = 0.044715
TILE = 128
SEGS = 8
F32 = jnp.float32
BF16 = jnp.bfloat16


def swap_cores(block):
    size = lax.axis_size("ctx")
    return lax.ppermute(block, "ctx", [(i, size - 1 - i) for i in range(size)])


def shifted(block, axis, distance):
    devices = range(lax.axis_size(axis))
    route = [(i - distance, i) for i in devices if i - distance in devices]
    return lax.ppermute(block, axis, route)


def gather_halves(shard, dim):
    half = shard.shape[dim] // 2
    core = lax.axis_index("ctx")
    mine = lax.dynamic_slice_in_dim(shard, core * half, half, dim)
    mine = lax.all_gather(mine, "fsdp", axis=dim)
    other = swap_cores(mine)
    first = jnp.where(core == 0, mine, other)
    second = jnp.where(core == 0, other, mine)
    both = jnp.stack([first, second], axis=dim + 1)
    return both.reshape(shard.shape[:dim] + (-1,) + shard.shape[dim + 1 :])


def split_features(block):
    shards = lax.axis_size("fsdp")
    core = lax.axis_index("ctx")
    parts = block.reshape(block.shape[0], shards, 2, -1)
    return [
        lax.dynamic_index_in_dim(parts, index, 2, False).reshape(block.shape[0], -1)
        for index in (core, 1 - core)
    ]


def pair_sums(left, right, dim, behind=None):
    rows_to_rows = (((0,), (0,)), ((), ()))

    def product(index):
        pair = (left[index], right) if dim == 0 else (right, left[index])
        return lax.dot_general(*pair, rows_to_rows, preferred_element_type=F32)

    arrived = swap_cores(product(1).astype(BF16))
    if behind is not None:
        arrived, left = after((arrived, left), behind)
    return (product(0) + arrived.astype(F32)).astype(BF16)


def half_to_owners(mine, dim):
    return lax.psum_scatter(mine, "fsdp", scatter_dimension=dim, tiled=True)


def both_halves(total, dim):
    other = swap_cores(total)
    core = lax.axis_index("ctx")
    first = jnp.where(core == 0, total, other)
    second = jnp.where(core == 0, other, total)
    return jnp.concatenate([first, second], axis=dim).astype(F32)


def after(value, *others):
    return lax.optimization_barrier((value, *others))[0]


class Square:
    def __init__(self):
        me = lax.axis_index("fsdp")
        row, col = me // 2, me % 2
        self.me = me
        self.core = lax.axis_index("ctx")
        self.near = (row * 2 + 1 - col, (1 - row) * 2 + col)
        self.far = (1 - row) * 2 + 1 - col


def remote(source, target, send, arrive, **device):
    return pltpu.make_async_remote_copy(
        source, target, send, arrive, device_id=device, device_id_type=pl.DeviceIdType.MESH
    )


class Gather:
    def __init__(self, items, stages, send, arrive, local):
        self.items, self.stages = items, stages
        self.send, self.arrive, self.local = send, arrive, local
        self.square = Square()

    def piece(self, w, owner, low, size):
        shard, whole, dim, offset = self.items[w]
        low = pl.multiple_of(owner * shard.shape[dim] + low, 128)
        if dim == 0:
            return whole.at[pl.ds(low, size), pl.ds(offset, shard.shape[1])]
        return whole.at[:, pl.ds(low, size)]

    def copy(self, w, k):
        shard, _, dim, _ = self.items[w]
        square = self.square
        half = shard.shape[dim] // 2
        low = pl.multiple_of(square.core * half, 128)
        first, second = square.near
        if k < 2:
            source = shard.at[pl.ds(low, half), :] if dim == 0 else shard.at[:, pl.ds(low, half)]
            target = self.piece(w, square.me, low, half)
            device = {"fsdp": square.near[k]}
        elif k < 4:
            source = target = self.piece(w, square.near[k - 2], low + (k - 2) * (half // 2), half // 2)
            device = {"fsdp": square.near[3 - k]}
        else:
            source = target = self.piece(w, (first, second, square.far)[k - 4], low, half)
            device = {"ctx": 1 - square.core}
        return remote(source, target, self.send.at[w, k], self.arrive.at[w, k], **device)

    def stage(self, w, out):
        shard = self.items[w][0]
        if out:
            target = self.piece(w, self.square.me, 0, shard.shape[self.items[w][2]])
            return pltpu.make_async_copy(self.stages[w], target, self.local.at[w, 1])
        return pltpu.make_async_copy(shard, self.stages[w], self.local.at[w, 0])

    def start(self, w):
        self.copy(w, 0).start()
        self.copy(w, 1).start()
        self.stage(w, False).start()

    def forward(self, w):
        self.copy(w, 0).wait_recv()
        self.copy(w, 2).start()
        self.copy(w, 1).wait_recv()
        self.copy(w, 3).start()
        self.copy(w, 4).start()
        self.copy(w, 5).start()
        self.stage(w, False).wait()
        self.stage(w, True).start()

    def hand_over(self, w):
        self.copy(w, 2).wait_recv()
        self.copy(w, 3).wait_recv()
        self.copy(w, 6).start()

    def finish(self, w):
        for k in (4, 5, 6):
            self.copy(w, k).wait_recv()
        for k in range(7):
            self.copy(w, k).wait_send()
        self.stage(w, True).wait()


def greet(line, square, whole_line=False):
    barrier = pltpu.get_barrier_semaphore()

    def call(**device):
        pl.semaphore_signal(barrier, inc=1, device_id=device, device_id_type=pl.DeviceIdType.MESH)

    peers = 0
    if line:
        count, me = lax.axis_size("tp"), lax.axis_index("tp")

        @pl.when(me > 0)
        def _():
            call(tp=me - 1)

        @pl.when(me < count - 1)
        def _():
            call(tp=me + 1)

        peers = jnp.where((me > 0) & (me < count - 1), 2, 1)
    if whole_line:
        count, me = lax.axis_size("tp"), lax.axis_index("tp")
        for other in range(count):
            @pl.when(me != other)
            def _():
                call(tp=other)

        peers = peers + (count - 1)
    if square:
        place = Square()
        call(fsdp=place.near[0])
        call(fsdp=place.near[1])
        call(fsdp=place.far)
        call(ctx=1 - place.core)
        peers = peers + 4
    pl.semaphore_wait(barrier, peers)


def line_sum(part, whole, inbox, sems, finish, between):
    count, me = lax.axis_size("tp"), lax.axis_index("tp")
    half = part.shape[0] // 2
    chunks = inbox.shape[1]
    rows = half // chunks
    sum_send, sum_arrive, share_send, share_arrive = sems

    def spot(side, c):
        return pl.ds(pl.multiple_of(side * half + c * rows, rows), rows)

    def place(side):
        return count - 1 - me if side else me

    def onward(side, c, source):
        target = me - 1 if side else me + 1
        return remote(source, inbox.at[side, c], sum_send.at[side, c], sum_arrive.at[side, c], tp=target)

    def share(side, c):
        target = me + 1 if side else me - 1
        block = whole.at[spot(side, c), :]
        return remote(block, block, share_send.at[side, c], share_arrive.at[side, c], tp=target)

    for side in (0, 1):
        @pl.when(place(side) == 0)
        def _():
            onward(side, 0, part.at[spot(side, 0), :]).start()

    def step(t, carry):
        for side in (0, 1):
            here = place(side)
            c = t - here

            @pl.when((here == 0) & (t + 1 < chunks))
            def _():
                onward(side, t + 1, part.at[spot(side, t + 1), :]).start()

            @pl.when((c >= 0) & (c < chunks) & (here > 0))
            def _():
                onward(side, c, inbox.at[side, c]).wait_recv()
                total = (inbox[side, c].astype(F32) + part[spot(side, c), :].astype(F32)).astype(BF16)

                @pl.when(here < count - 1)
                def _():
                    inbox[side, c] = total
                    onward(side, c, inbox.at[side, c]).start()

                @pl.when(here == count - 1)
                def _():
                    whole[spot(side, c), :] = total
                    share(side, c).start()
                    finish(spot(side, c))

        for side in (0, 1):
            here = place(side)
            c = t - 2 * (count - 1) + here

            @pl.when((c >= 0) & (c < chunks) & (here < count - 1))
            def _():
                share(side, c).wait_recv()

                @pl.when(here > 0)
                def _():
                    share(side, c).start()

                finish(spot(side, c))

        between(t)
        return carry

    lax.fori_loop(0, chunks + 2 * (count - 1), step, 0)

    def drain(c, carry):
        for side in (0, 1):
            here = place(side)

            @pl.when(here < count - 1)
            def _():
                onward(side, c, inbox.at[side, c]).wait_send()

            @pl.when(here > 0)
            def _():
                share(side, c).wait_send()

        return carry

    lax.fori_loop(0, chunks, drain, 0)


def put_split(ref, rows, block):
    core = lax.axis_index("ctx")
    size = block.shape[1] // 8
    for owner in range(4):
        for index in range(2):
            low = (2 * owner + index) * size
            ref[(index + core) % 2, rows, owner * size : (owner + 1) * size] = block[:, low : low + size]


CHUNK = 32
LINE_COST = pl.CostEstimate(flops=0, bytes_accessed=400_000_000, transcendentals=0)


def enter_kernel(
    tokens, upstream, gain_shard, recur, gelu, merge,
    normed, halves, upstream_halves, gains, whole_in, whole_merge,
    stage_recur, stage_gelu, stage_merge, send, arrive, local, gain_send, gain_arrive,
):
    square = Square()
    greet(False, True)
    width = gain_shard.shape[1]

    def gain_copy(k, owner, target):
        spot = gains.at[:, pl.ds(pl.multiple_of(owner * width, 128), width)]
        return remote(gain_shard, spot, gain_send.at[k], gain_arrive.at[k], fsdp=target)

    others = (*square.near, square.far)
    for k, target in enumerate(others):
        gain_copy(k, square.me, target).start()
    gather = Gather(
        [(recur, whole_in, 0, 0), (gelu, whole_in, 0, recur.shape[1]), (merge, whole_merge, 1, 0)],
        (stage_recur, stage_gelu, stage_merge), send, arrive, local,
    )
    for w in range(3):
        gather.start(w)
    gains[:, pl.ds(pl.multiple_of(square.me * width, 128), width)] = gain_shard[...]
    for k, owner in enumerate(others):
        gain_copy(k, owner, owner).wait_recv()

    def norm(t, carry):
        rows = pl.ds(pl.multiple_of(t * CHUNK, CHUNK), CHUNK)
        block = tokens[rows, :].astype(F32)
        block = (block * rms_scale(block) * gains[0:1, :]).astype(BF16)
        normed[rows, :] = block
        put_split(halves, rows, block)
        put_split(upstream_halves, rows, upstream[rows, :])
        return carry

    lax.fori_loop(0, tokens.shape[0] // CHUNK, norm, 0)
    for w in range(3):
        gather.forward(w)
    for w in range(3):
        gather.hand_over(w)
    for w in range(3):
        gather.finish(w)
    for k, target in enumerate(others):
        gain_copy(k, square.me, target).wait_send()


ANY = pl.BlockSpec(memory_space=pl.ANY)
NEAR = pl.BlockSpec(memory_space=pltpu.VMEM)


def gather_scratch(shards):
    count = len(shards)
    dma = pltpu.SemaphoreType.DMA
    return [pltpu.VMEM(w.shape, w.dtype) for w in shards] + [dma((count, 7)), dma((count, 7)), dma((count, 2))]


def enter(tokens, upstream, gain_shard, recur, gelu, merge):
    rows, features = tokens.shape
    shape = jax.ShapeDtypeStruct
    inner = recur.shape[1]
    dma = pltpu.SemaphoreType.DMA
    return pl.pallas_call(
        enter_kernel,
        out_shape=(
            shape((rows, features), BF16),
            shape((2, rows, features // 2), BF16),
            shape((2, rows, features // 2), BF16),
            shape((8, features), F32),
            shape((features, 2 * inner), BF16),
            shape((inner, features), BF16),
        ),
        in_specs=[NEAR, NEAR, NEAR, ANY, ANY, ANY],
        out_specs=[NEAR, NEAR, NEAR, NEAR, ANY, ANY],
        scratch_shapes=gather_scratch([recur, gelu, merge]) + [dma((3,)), dma((3,))],
        compiler_params=pltpu.CompilerParams(collective_id=1, has_side_effects=True),
        name="enter",
    )(tokens, upstream, gain_shard, recur, gelu, merge)


def line_scratch(rows, features):
    chunks = rows // 2 // CHUNK
    dma = pltpu.SemaphoreType.DMA((2, chunks))
    return [pltpu.VMEM((2, chunks, CHUNK, features), BF16), dma, dma, dma, dma]


class Fetch:
    def __init__(self, sources, targets, sems):
        self.copies = [pltpu.make_async_copy(a, b, sems.at[k]) for k, (a, b) in enumerate(zip(sources, targets))]

    def start(self):
        for copy in self.copies:
            copy.start()

    def wait(self):
        for copy in self.copies:
            copy.wait()


def middle_kernel(gathers, part, far_tokens, gains, *refs):
    *refs, tokens, fetch_sems = refs
    fetch = Fetch((far_tokens,), (tokens,), fetch_sems)
    fetch.start()
    if gathers:
        gate, up, down, merged, normed, halves, whole_in, whole_down = refs[:8]
        inbox, *rest = refs[8:]
        sems, (stage_gate, stage_up, stage_down, send, arrive, local) = rest[:4], rest[4:]
        gather = Gather(
            [(gate, whole_in, 0, 0), (up, whole_in, 0, gate.shape[1]), (down, whole_down, 1, 0)],
            (stage_gate, stage_up, stage_down), send, arrive, local,
        )
        greet(True, True)
        for w in range(3):
            gather.start(w)
    else:
        merged, normed, inbox, *sems = refs
        greet(True, False)

    def finish(rows):
        block = tokens[rows, :].astype(F32) + merged[rows, :].astype(F32)
        block = (block * rms_scale(block) * gains[1:2, :]).astype(BF16)
        normed[rows, :] = block
        if gathers:
            put_split(halves, rows, block)

    def between(t):
        @pl.when(t == 0)
        def _():
            fetch.wait()

        if gathers:
            for w in range(3):
                @pl.when(t == 5 + 4 * w)
                def _():
                    gather.forward(w)

                @pl.when(t == 17 + w)
                def _():
                    gather.hand_over(w)

    line_sum(part, merged, inbox, sems, finish, between)
    if gathers:
        for w in range(3):
            gather.finish(w)


def middle(part, tokens, gains, shards):
    rows, features = tokens.shape
    shape = jax.ShapeDtypeStruct
    whole = shape((rows, features), BF16)
    outs, specs = [whole, whole], [NEAR, NEAR]
    scratch = line_scratch(rows, features)
    if shards:
        gate, up, down = shards
        outs += [
            shape((2, rows, features // 2), BF16),
            shape((features, 2 * gate.shape[1]), BF16),
            shape((down.shape[0], features), BF16),
        ]
        specs += [NEAR, ANY, ANY]
        scratch += gather_scratch(shards)
    scratch += [pltpu.VMEM((rows, features), BF16), pltpu.SemaphoreType.DMA((1,))]
    return pl.pallas_call(
        lambda *refs: middle_kernel(bool(shards), *refs),
        out_shape=tuple(outs),
        in_specs=[NEAR, ANY, NEAR] + [ANY] * len(shards),
        out_specs=specs,
        scratch_shapes=scratch,
        compiler_params=pltpu.CompilerParams(collective_id=2, has_side_effects=True),
        cost_estimate=LINE_COST,
        name="middle",
    )(part, tokens, gains, *shards)


def turn_kernel(split, part, far_tokens, far_merged, far_upstream, gains, own, grad_in, gain_sum, *refs):
    if split:
        halves, *refs = refs
    whole, wide, tokens, merged, upstream, fetch_sems, inbox, *sems = refs
    fetch = Fetch((far_tokens, far_merged, far_upstream), (tokens, merged, upstream), fetch_sems)
    fetch.start()
    greet(True, False)
    gain_sum[...] = jnp.zeros_like(gain_sum)
    width = own.shape[1]
    start = pl.multiple_of(lax.axis_index("tp") * width, 128)

    def finish(rows):
        block = tokens[rows, :].astype(F32) + merged[rows, :].astype(F32)
        scale = rms_scale(block)
        grad = whole[rows, :].astype(F32)
        gain_sum[0:1, :] += jnp.sum(grad * (block * scale), axis=0, keepdims=True)
        grad = grad * gains[1:2, :]
        mean = jnp.mean(block * grad, axis=-1, keepdims=True)
        grad = upstream[rows, :].astype(F32) + scale * grad - block * (scale * scale * scale * mean)
        wide[...] = grad
        own[rows, :] = wide[:, pl.ds(start, width)]
        grad = grad.astype(BF16)
        grad_in[rows, :] = grad
        if split:
            put_split(halves, rows, grad)

    def between(t):
        @pl.when(t == 0)
        def _():
            fetch.wait()

    line_sum(part, whole, inbox, sems, finish, between)


def turn(part, tokens, merged, upstream, gains, split):
    rows, features = tokens.shape
    shape = jax.ShapeDtypeStruct
    outs = [
        shape((rows, features // lax.axis_size("tp")), F32),
        shape((rows, features), BF16),
        shape((8, features), F32),
    ]
    if split:
        outs.append(shape((2, rows, features // 2), BF16))
    return pl.pallas_call(
        lambda *refs: turn_kernel(split, *refs),
        out_shape=tuple(outs),
        in_specs=[NEAR, ANY, ANY, ANY, NEAR],
        out_specs=[NEAR] * len(outs),
        scratch_shapes=[pltpu.VMEM((rows, features), BF16), pltpu.VMEM((CHUNK, features), F32)]
        + [pltpu.VMEM((rows, features), BF16)] * 3
        + [pltpu.SemaphoreType.DMA((3,))]
        + line_scratch(rows, features),
        compiler_params=pltpu.CompilerParams(collective_id=3, has_side_effects=True),
        cost_estimate=LINE_COST,
        name="turn",
    )(part, tokens, merged, upstream, gains)


def rounded_sum(*blocks):
    total = blocks[0].astype(F32)
    for block in blocks[1:]:
        total = total + block.astype(F32)
    return total.astype(BF16)


class Scatter:
    def __init__(self, items, boxes, lasts, send, arrive):
        self.items, self.boxes, self.lasts = items, boxes, lasts
        self.send, self.arrive = send, arrive
        self.square = Square()

    def block(self, w, owner, k):
        part, _, dim = self.items[w]
        size = part.shape[dim] // 4
        if dim == 0:
            low = pl.multiple_of(owner * size + k * (size // 2), 128)
            return part.at[pl.ds(low, size // 2), :]
        half = part.shape[0] // 2
        return part.at[pl.ds(k * half, half), pl.ds(pl.multiple_of(owner * size, 128), size)]

    def spot(self, w, k):
        part, out, dim = self.items[w]
        size = part.shape[dim] // 4
        low = pl.multiple_of(self.square.core * size, 128)
        if dim == 0:
            return out.at[pl.ds(low + k * (size // 2), size // 2), :]
        half = part.shape[0] // 2
        return out.at[pl.ds(k * half, half), pl.ds(low, size)]

    def copy(self, w, k, j):
        square = self.square
        first, second = square.near[k], square.near[1 - k]
        send, arrive = self.send.at[w, 4 * k + j], self.arrive.at[w, 4 * k + j]
        if j < 2:
            owner = square.far if j == 0 else first
            return remote(self.block(w, owner, k), self.boxes[w].at[k, j], send, arrive, fsdp=first)
        if j == 2:
            return remote(self.boxes[w].at[k, 0], self.lasts[w].at[k], send, arrive, fsdp=second)
        return remote(self.spot(w, k), self.spot(w, k), send, arrive, ctx=1 - square.core)

    def start(self, w):
        for j in (0, 1):
            for k in (0, 1):
                self.copy(w, k, j).start()

    def relay(self, w):
        for k in (0, 1):
            self.copy(w, k, 0).wait_recv()
            mine = self.block(w, self.square.near[1 - k], k)
            self.boxes[w][k, 0] = rounded_sum(mine[...], self.boxes[w][k, 0])
            self.copy(w, k, 2).start()

    def finish(self, w):
        for k in (0, 1):
            self.copy(w, k, 1).wait_recv()
            self.copy(w, k, 2).wait_recv()
            mine = self.block(w, self.square.me, k)
            self.spot(w, k)[...] = rounded_sum(mine[...], self.boxes[w][k, 1], self.lasts[w][k])
            self.copy(w, k, 3).start()

    def drain(self, w):
        for k in (0, 1):
            self.copy(w, k, 3).wait_recv()
            for j in range(4):
                self.copy(w, k, j).wait_send()


def scatter_scratch(items):
    blocks = []
    for shape, dim in items:
        rows, cols = (shape[0] // 8, shape[1]) if dim == 0 else (shape[0] // 2, shape[1] // 4)
        blocks.append((rows, cols))
    dma = pltpu.SemaphoreType.DMA((len(items), 8))
    return (
        [pltpu.VMEM((2, 2, *block), BF16) for block in blocks]
        + [pltpu.VMEM((2, *block), BF16) for block in blocks]
        + [dma, dma]
    )


def leave_kernel(
    part_in, gates, sums, norms, stats,
    own_in, gate_sums, row_sums, norm_sums, stat_sums,
    box_in, last_in, send, arrive,
    gate_core, gate_half, gate_near, gate_pair, gate_far, gate_send, gate_arrive,
    core_sums, core_norms, box_sums, box_norms, sum_send, sum_arrive,
    line_norms, line_stats, norm_send, norm_arrive, stat_send, stat_arrive,
):
    square = Square()
    count, place = lax.axis_size("tp"), lax.axis_index("tp")
    core = square.core
    others = (*square.near, square.far)
    greet(False, True, True)

    def norm_copy(k, source):
        box = line_norms.at[source]
        return remote(box, box, norm_send.at[k], norm_arrive.at[source], tp=k)

    def stat_copy(k, source):
        return remote(stats, line_stats.at[source], stat_send.at[k], stat_arrive.at[source], tp=k)

    def core_copy(k):
        source, target = ((sums, core_sums), (norms, core_norms))[k]
        return remote(source, target, sum_send.at[k], sum_arrive.at[k], ctx=1 - core)

    def square_copy(k, j):
        box = (box_sums, box_norms)[k].at[square.me]
        at = 2 + 3 * k + j
        return remote(box, box, sum_send.at[at], sum_arrive.at[at], fsdp=others[j])

    gate_rows = gates.shape[0] // 2
    gate_cols = gates.shape[1] // 2
    my_rows = pl.ds(pl.multiple_of(core * gate_rows, 16), gate_rows)
    your_rows = pl.ds(pl.multiple_of((1 - core) * gate_rows, 16), gate_rows)

    def gate_copy(j):
        send, arrive = gate_send.at[j], gate_arrive.at[j]
        if j == 0:
            return remote(gates.at[your_rows, :], gate_core, send, arrive, ctx=1 - core)
        if j == 5:
            spot = gate_sums.at[my_rows, :]
            return remote(spot, spot, send, arrive, ctx=1 - core)
        k = (j - 1) % 2
        if j < 3:
            return remote(gate_half.at[k], gate_near.at[k], send, arrive, fsdp=square.near[k])
        return remote(gate_pair.at[k], gate_far.at[k], send, arrive, fsdp=square.near[1 - k])

    scatter = Scatter([(part_in, own_in, 0)], (box_in,), (last_in,), send, arrive)
    gate_copy(0).start()
    core_copy(0).start()
    core_copy(1).start()
    for k in range(count):
        @pl.when(place != k)
        def _():
            stat_copy(k, place).start()

    line_stats[place] = stats[...]
    core_copy(0).wait_recv()
    core_copy(1).wait_recv()
    box_sums[square.me] = sums[...] + core_sums[...]
    box_norms[square.me] = norms[...] + core_norms[...]
    for k in (0, 1):
        for j in range(3):
            square_copy(k, j).start()
    gate_copy(0).wait_recv()
    for k in (0, 1):
        cols = slice(k * gate_cols, (k + 1) * gate_cols)
        gate_half[k] = rounded_sum(gates[my_rows, cols], gate_core[:, cols])
        gate_copy(1 + k).start()
    scatter.start(0)
    for k in (0, 1):
        for j in range(3):
            square_copy(k, j).wait_recv()
    row_sums[...] = box_sums[0] + box_sums[1] + box_sums[2] + box_sums[3]
    line_norms[place] = box_norms[0] + box_norms[1] + box_norms[2] + box_norms[3]
    for k in range(count):
        @pl.when(place != k)
        def _():
            norm_copy(k, place).start()

    for k in (0, 1):
        gate_copy(1 + k).wait_recv()
        gate_pair[k] = rounded_sum(gate_half[k], gate_near[k])
        gate_copy(3 + k).start()
    scatter.relay(0)
    for k in (0, 1):
        cols = slice(k * gate_cols, (k + 1) * gate_cols)
        gate_copy(3 + k).wait_recv()
        gate_sums[my_rows, cols] = rounded_sum(gate_pair[k], gate_far[k])
    gate_copy(5).start()
    for k in range(count):
        @pl.when(place != k)
        def _():
            norm_copy(k, k).wait_recv()
            stat_copy(k, k).wait_recv()

    total = line_norms[0]
    stat = line_stats[0]
    for k in range(1, count):
        total = total + line_norms[k]
        stat = stat + line_stats[k]
    norm_sums[...] = total
    stat_sums[...] = stat
    scatter.finish(0)
    scatter.drain(0)
    gate_copy(5).wait_recv()
    for j in range(6):
        gate_copy(j).wait_send()
    for k in (0, 1):
        core_copy(k).wait_send()
        for j in range(3):
            square_copy(k, j).wait_send()
    for k in range(count):
        @pl.when(place != k)
        def _():
            norm_copy(k, place).wait_send()
            stat_copy(k, place).wait_send()


def leave(part_in, gates, sums, norms, stats):
    shape = jax.ShapeDtypeStruct
    count = lax.axis_size("tp")
    dma = pltpu.SemaphoreType.DMA
    height, width = gates.shape[0] // 2, gates.shape[1] // 2
    quarter = pltpu.VMEM((2, height, width), BF16)
    return pl.pallas_call(
        leave_kernel,
        out_shape=(
            shape((part_in.shape[0] // 2, part_in.shape[1]), BF16),
            shape(gates.shape, BF16),
            shape(sums.shape, F32),
            shape(norms.shape, F32),
            shape(stats.shape, F32),
        ),
        in_specs=[NEAR] * 5,
        out_specs=[NEAR] * 5,
        scratch_shapes=(
            scatter_scratch([(part_in.shape, 0)])
            + [pltpu.VMEM((height, 2 * width), BF16), quarter, quarter, quarter, quarter, dma((6,)), dma((6,))]
            + [pltpu.VMEM(sums.shape, F32), pltpu.VMEM(norms.shape, F32)]
            + [pltpu.VMEM((4, *sums.shape), F32), pltpu.VMEM((4, *norms.shape), F32), dma((8,)), dma((8,))]
            + [pltpu.VMEM((count, *norms.shape), F32), pltpu.VMEM((count, *stats.shape), F32)]
            + [dma((count,))] * 4
        ),
        compiler_params=pltpu.CompilerParams(collective_id=4, has_side_effects=True),
        cost_estimate=pl.CostEstimate(flops=0, bytes_accessed=160_000_000, transcendentals=0),
        name="leave",
    )(part_in, gates, sums, norms, stats)


def gelu_pair(q):
    tanh = jnp.tanh(ROOT * (q + CUBE * q * q * q))
    value = 0.5 * q * (1.0 + tanh)
    slope = 0.5 * (1.0 + tanh) + 0.5 * q * (1.0 - tanh * tanh) * ROOT * (1.0 + 3.0 * CUBE * q * q)
    return value, slope


def rms_scale(values):
    return lax.rsqrt(jnp.mean(values * values, axis=-1, keepdims=True) + EPS)


def decay_parts(rate, softer, keep):
    gap = 2.0 * CGAIN * rate * softer
    decay = jnp.exp(-0.5 * gap)
    series = gap * (
        1.0
        - gap / 2.0
        * (1.0 - gap / 3.0 * (1.0 - gap / 4.0 * (1.0 - gap / 5.0 * (1.0 - gap / 6.0 * (1.0 - gap / 7.0)))))
    )
    square = jnp.where(gap < 0.25, series, 1.0 - decay * decay)
    return jnp.where(keep, decay, 0.0), jnp.where(keep, square, 1.0)


LANES = 128


def put_lanes(ref, block, rows):
    for lane in range(ref.shape[0]):
        ref[lane, 0:rows, :] = block[:, lane * LANES : (lane + 1) * LANES]


def sweep(decay_ref, value_ref, state_ref, product_ref, out_ref, run_ref, carry_ref, reverse, offset):
    groups, rows, _ = value_ref.shape
    steps = rows // SEGS
    place = lax.broadcasted_iota(jnp.int32, (SEGS, LANES), 0)
    if reverse:
        place = SEGS - 1 - place

    def moved(block, by, fill):
        turned = pltpu.roll(block, SEGS - by if reverse else by, 0)
        return jnp.where(place >= by, turned, fill)

    for lane in range(groups):
        lanes = slice(lane * LANES, (lane + 1) * LANES)
        state = jnp.zeros((SEGS, LANES), F32)
        product = jnp.ones((SEGS, LANES), F32)
        for step in reversed(range(steps)) if reverse else range(steps):
            spot = pl.ds(step, SEGS, stride=steps)
            decay = decay_ref[lane, pl.ds(step + offset, SEGS, stride=steps), :]
            state = decay * state + value_ref[lane, spot, :]
            product = product * decay
            state_ref[lane, spot, :] = state
            product_ref[lane, spot, :] = product
        for by in (1, 2, 4):
            state = state + product * moved(state, by, 0.0)
            product = product * moved(product, by, 1.0)
        carry = carry_ref[0:1, lanes]
        carry_run = carry_ref[8:9, lanes]
        state = state + product * carry
        product = product * carry_run
        enter = moved(state, 1, carry)
        enter_run = moved(product, 1, carry_run)
        for seg in range(SEGS):
            span = slice(seg * steps, (seg + 1) * steps)
            inner = product_ref[lane, span, :]
            out_ref[span, lanes] = state_ref[lane, span, :] + inner * enter[seg : seg + 1, :]
            run_ref[span, lanes] = inner * enter_run[seg : seg + 1, :]
        last = 0 if reverse else SEGS - 1
        carry_ref[0:1, lanes] = state[last : last + 1, :]
        carry_ref[8:9, lanes] = product[last : last + 1, :]


def spread_blocks(blocks_ref, out_ref):
    chans, size = blocks_ref.shape[1:]
    row = lax.broadcasted_iota(jnp.int32, (chans, chans), 0)
    col = lax.broadcasted_iota(jnp.int32, (chans, chans), 1)
    inner = lax.broadcasted_iota(jnp.int32, (size, chans), 0)
    outer = lax.broadcasted_iota(jnp.int32, (size, chans), 1)
    inside = row < 0
    repeat = outer < 0
    for low in range(0, chans, size):
        inside |= (row >= low) & (row < low + size) & (col >= low) & (col < low + size)
        repeat |= outer - low == inner
    repeat = repeat.astype(F32).astype(BF16)
    for gate in range(2):
        wide = jnp.dot(blocks_ref[gate], repeat, preferred_element_type=F32)
        out_ref[:, gate * chans : (gate + 1) * chans] = jnp.where(inside, wide, 0.0).astype(BF16)


def forward_kernel(
    branch_ref, halo_ref, mask_ref, taps_ref, bias_ref, blocks_ref, gate_bias_ref, softer_ref,
    conv_ref, rate_ref, entry_ref, state_ref, run_ref, gates_ref,
    window, decay, value, inner, product, carry,
):
    rows, chans = conv_ref.shape
    spot = pl.program_id(0)

    @pl.when(spot == 0)
    def _():
        spread_blocks(blocks_ref, gates_ref)
        window[0:8, :] = halo_ref[...].astype(F32)
        carry[0:8, :] = jnp.zeros((8, chans), F32)
        carry[8:16, :] = jnp.ones((8, chans), F32)

    @pl.when(spot > 0)
    def _():
        window[0:8, :] = window[rows : rows + 8, :]

    window[8 : rows + 8, :] = branch_ref[...].astype(F32)
    mixed = bias_ref[...] + taps_ref[0:1, :] * window[8 : rows + 8, :]
    for shift in range(1, taps_ref.shape[0]):
        moved = window[8 - shift : 8 - shift + rows, :]
        mixed = mixed + taps_ref[shift : shift + 1, :] * (moved * mask_ref[:, shift : shift + 1])
    conv = mixed.astype(BF16)
    conv_ref[...] = conv
    pre = jnp.dot(conv, gates_ref[...], preferred_element_type=F32) + gate_bias_ref[...]
    rate = jax.nn.sigmoid(pre[:, :chans])
    entry = jax.nn.sigmoid(pre[:, chans:])
    rate_ref[...] = rate
    entry_ref[...] = entry
    keep = jnp.broadcast_to(mask_ref[:, 0:1], (rows, chans)) > 0.5
    step, square = decay_parts(rate, softer_ref[...], keep)
    put_lanes(decay, step, rows)
    put_lanes(value, jnp.sqrt(square) * entry * conv.astype(F32), rows)
    sweep(decay, value, inner, product, state_ref, run_ref, carry, False, 0)


def tile_spec(width, count=None):
    if count is None:
        return pl.BlockSpec((TILE, width), lambda i: (i, 0))
    return pl.BlockSpec((TILE, width), lambda i: (count - 1 - i, 0))


def fixed_spec(shape):
    return pl.BlockSpec(shape, lambda i: (0, 0))


def recur_forward(branch, halo, masks, taps, bias, blocks, gate_bias, softer):
    rows, chans = branch.shape[0], halo.shape[1]
    wide = jax.ShapeDtypeStruct((rows, chans), F32)
    return pl.pallas_call(
        forward_kernel,
        grid=(rows // TILE,),
        out_shape=(
            jax.ShapeDtypeStruct((rows, chans), BF16), wide, wide, wide, wide,
            jax.ShapeDtypeStruct((chans, 2 * chans), BF16),
        ),
        in_specs=[
            tile_spec(chans),
            fixed_spec((8, chans)),
            tile_spec(masks.shape[1]),
            fixed_spec(taps.shape),
            fixed_spec((1, chans)),
            pl.BlockSpec(blocks.shape, lambda i: (0, 0, 0)),
            fixed_spec((1, 2 * chans)),
            fixed_spec((1, chans)),
        ],
        out_specs=[tile_spec(chans)] * 5 + [fixed_spec((chans, 2 * chans))],
        scratch_shapes=[
            pltpu.VMEM((TILE + 8, chans), F32),
            pltpu.VMEM((chans // LANES, TILE, LANES), F32),
            pltpu.VMEM((chans // LANES, TILE, LANES), F32),
            pltpu.VMEM((chans // LANES, TILE, LANES), F32),
            pltpu.VMEM((chans // LANES, TILE, LANES), F32),
            pltpu.VMEM((16, chans), F32),
        ],
        cost_estimate=pl.CostEstimate(
            flops=2 * rows * chans * 2 * chans, bytes_accessed=24 * rows * chans, transcendentals=5 * rows * chans
        ),
        name="recur_forward",
    )(branch, halo, masks, taps, bias, blocks, gate_bias, softer)


def merge_kernel(local_ref, run_ref, enter_ref, pre_ref, weight_ref, state_ref, gated_ref, part_ref):
    state = local_ref[...] + run_ref[...] * enter_ref[0:1, :]
    state_ref[...] = state
    pre = pre_ref[...].astype(F32)
    gated = (state * gelu_pair(pre)[0]).astype(BF16)
    gated_ref[...] = gated
    part_ref[...] = jnp.dot(gated, weight_ref[...], preferred_element_type=F32).astype(BF16)


def merge_states(local, run, enter, branches, weight):
    rows, chans = local.shape
    features = weight.shape[1]
    shape = jax.ShapeDtypeStruct
    return pl.pallas_call(
        merge_kernel,
        grid=(rows // TILE,),
        out_shape=(shape((rows, chans), F32), shape((rows, chans), BF16), shape((rows, features), BF16)),
        in_specs=[
            tile_spec(chans), tile_spec(chans), fixed_spec((1, chans)),
            pl.BlockSpec((TILE, chans), lambda i: (i, 1)),
            fixed_spec(weight.shape),
        ],
        out_specs=[tile_spec(chans), tile_spec(chans), tile_spec(features)],
        cost_estimate=pl.CostEstimate(
            flops=2 * rows * chans * features, bytes_accessed=16 * rows * chans, transcendentals=rows * chans
        ),
        name="merge_states",
    )(local, run, enter, branches, weight)


def adjoint_kernel(
    rate_ref, up_ref, pre_ref, state_ref, mask_ref, softer_ref,
    grad_ref, run_ref, head_ref, pre_grad_ref,
    decay, value, inner, product, carry,
):
    rows, chans = rate_ref.shape
    groups = chans // LANES
    spot = pl.program_id(0)

    @pl.when(spot == 0)
    def _():
        for lane in range(groups):
            decay[lane, rows : rows + 8, :] = jnp.ones((8, LANES), F32)
        carry[0:8, :] = jnp.zeros((8, chans), F32)
        carry[8:16, :] = jnp.ones((8, chans), F32)

    @pl.when(spot > 0)
    def _():
        for lane in range(groups):
            decay[lane, rows : rows + 8, :] = decay[lane, 0:8, :]

    keep = jnp.broadcast_to(mask_ref[:, 0:1], (rows, chans)) > 0.5
    gap = CGAIN * rate_ref[...] * softer_ref[...]
    step = jnp.where(keep, jnp.exp(-gap), 0.0)
    put_lanes(decay, step, rows)
    gate, slope = gelu_pair(pre_ref[...].astype(F32))
    up = up_ref[...]
    pre_grad_ref[...] = (up * state_ref[...] * slope).astype(BF16)
    put_lanes(value, up * gate, rows)
    sweep(decay, value, inner, product, grad_ref, run_ref, carry, True, 1)
    head_ref[...] = jnp.broadcast_to(step[0:1, :] * carry[0:1, :], (8, chans))


def recur_adjoint(rate, up, branches, state, masks, softer):
    rows, chans = rate.shape
    count = rows // TILE
    wide = jax.ShapeDtypeStruct((rows, chans), F32)
    return pl.pallas_call(
        adjoint_kernel,
        grid=(count,),
        out_shape=(
            wide, wide, jax.ShapeDtypeStruct((8, chans), F32), jax.ShapeDtypeStruct((rows, chans), BF16)
        ),
        in_specs=[
            tile_spec(chans, count),
            tile_spec(chans, count),
            pl.BlockSpec((TILE, chans), lambda i: (count - 1 - i, 1)),
            tile_spec(chans, count),
            tile_spec(masks.shape[1], count),
            fixed_spec((1, chans)),
        ],
        out_specs=[tile_spec(chans, count), tile_spec(chans, count), fixed_spec((8, chans)), tile_spec(chans, count)],
        scratch_shapes=[
            pltpu.VMEM((chans // LANES, TILE + 8, LANES), F32),
            pltpu.VMEM((chans // LANES, TILE, LANES), F32),
            pltpu.VMEM((chans // LANES, TILE, LANES), F32),
            pltpu.VMEM((chans // LANES, TILE, LANES), F32),
            pltpu.VMEM((16, chans), F32),
        ],
        cost_estimate=pl.CostEstimate(
            flops=8 * rows * chans, bytes_accessed=16 * rows * chans, transcendentals=rows * chans
        ),
        name="recur_adjoint",
    )(rate, up, branches, state, masks, softer)


def backward_kernel(
    grad_ref, run_ref, enter_ref, rate_ref, entry_ref, conv_ref, state_ref, mask_ref,
    branch_ref, pre_grad_ref, halo_ref, taps_ref, gates_ref, softer_ref,
    back_ref, tail_ref, head_ref, gate_grad_ref, sums_ref,
    shifts, edge,
):
    rows, chans = conv_ref.shape
    width = taps_ref.shape[0]
    spot = pl.program_id(0)
    last = pl.num_programs(0) - 1

    @pl.when(spot == 0)
    def _():
        for shift in range(1, width):
            shifts[shift - 1, rows : rows + 8, :] = jnp.zeros((8, chans), F32)
        gate_grad_ref[...] = jnp.zeros_like(gate_grad_ref)
        sums_ref[...] = jnp.zeros_like(sums_ref)

    @pl.when(spot > 0)
    def _():
        for shift in range(1, width):
            shifts[shift - 1, rows : rows + 8, :] = shifts[shift - 1, 0:8, :]

    keep = jnp.broadcast_to(mask_ref[:, 0:1], (rows, chans)) > 0.5
    softer = softer_ref[...]
    rate = rate_ref[...]
    entry = entry_ref[...]
    conv = conv_ref[...].astype(F32)
    grad = grad_ref[...] + run_ref[...] * enter_ref[0:1, :]
    step, square = decay_parts(rate, softer, keep)
    inverse = lax.rsqrt(square)
    mult = square * inverse
    driven = entry * conv
    carried = state_ref[...] - mult * driven
    d_log = jnp.where(keep, grad * (carried - driven * step * step * inverse), 0.0)
    d_rate = (-CGAIN * softer * d_log * rate * (1.0 - rate)).astype(BF16)
    lifted = grad * mult * entry
    d_entry = (lifted * conv * (1.0 - entry)).astype(BF16)
    both = jnp.concatenate([d_rate, d_entry], axis=1)
    d_conv = lifted + lax.dot_general(
        both, gates_ref[...], (((1,), (1,)), ((), ())), preferred_element_type=F32
    )
    gate_grad_ref[...] += lax.dot_general(
        conv_ref[...], both, (((0,), (0,)), ((), ())), preferred_element_type=F32
    )

    def add_row(row, block):
        sums_ref[row : row + 1, :] += jnp.sum(block, axis=0, keepdims=True)

    branch = branch_ref[...].astype(F32)
    add_row(0, d_log * rate)
    add_row(1, d_rate.astype(F32))
    add_row(2, d_entry.astype(F32))
    add_row(3, d_conv)
    add_row(4, d_conv * branch)
    back = taps_ref[0:1, :] * d_conv
    for shift in range(1, width):
        shifts[shift - 1, 0:rows, :] = d_conv * mask_ref[:, shift : shift + 1]
        moved = shifts[shift - 1, shift : shift + rows, :]
        add_row(4 + shift, moved * branch)
        back = back + taps_ref[shift : shift + 1, :] * moved
    back_ref[:, 0:chans] = back.astype(BF16)
    back_ref[:, chans:] = pre_grad_ref[...]

    @pl.when(spot == 0)
    def _():
        tail_ref[...] = back[rows - 8 :, :]

    @pl.when(spot == last)
    def _():
        halo = halo_ref[...].astype(F32)
        head = jnp.zeros((8, chans), F32)
        edge[0:8, :] = head
        for shift in range(1, width):
            edge[8:16, :] = shifts[shift - 1, 0:8, :]
            moved = edge[shift : shift + 8, :]
            add_row(4 + shift, moved * halo)
            head = head + taps_ref[shift : shift + 1, :] * moved
        head_ref[...] = head


def recur_backward(grad, run, enter, rate, entry, conv, state, masks, branch, pre_grad, halo, taps, gates, softer):
    rows, chans = rate.shape
    count = rows // TILE
    edge = jax.ShapeDtypeStruct((8, chans), F32)
    wide = tile_spec(chans, count)
    return pl.pallas_call(
        backward_kernel,
        grid=(count,),
        out_shape=(
            jax.ShapeDtypeStruct((rows, 2 * chans), BF16),
            edge,
            edge,
            jax.ShapeDtypeStruct((chans, 2 * chans), F32),
            jax.ShapeDtypeStruct((8, chans), F32),
        ),
        in_specs=[
            wide, wide, fixed_spec((1, chans)), wide, wide, wide, wide,
            tile_spec(masks.shape[1], count),
            wide,
            wide,
            fixed_spec((8, chans)),
            fixed_spec(taps.shape),
            fixed_spec(gates.shape),
            fixed_spec((1, chans)),
        ],
        out_specs=[
            tile_spec(2 * chans, count),
            fixed_spec((8, chans)),
            fixed_spec((8, chans)),
            fixed_spec((chans, 2 * chans)),
            fixed_spec((8, chans)),
        ],
        scratch_shapes=[
            pltpu.VMEM((taps.shape[0] - 1, TILE + 8, chans), F32),
            pltpu.VMEM((16, chans), F32),
        ],
        cost_estimate=pl.CostEstimate(
            flops=8 * rows * chans * chans, bytes_accessed=28 * rows * chans, transcendentals=2 * rows * chans
        ),
        name="recur_backward",
    )(grad, run, enter, rate, entry, conv, state, masks, branch, pre_grad, halo, taps, gates, softer)


def shards(
    tokens,
    segments,
    cotangent,
    w_recur,
    w_gelu,
    w_merge,
    w_gate,
    w_up,
    w_down,
    norm_mix,
    norm_feed,
    conv_taps,
    conv_bias,
    rate_gate,
    entry_gate,
    rate_bias,
    entry_bias,
    decay_logit,
):
    piece = tokens.shape[0]
    width = conv_taps.shape[0]
    edge = width - 1
    heads, block = rate_gate.shape[0], rate_gate.shape[1]
    chans = conv_taps.shape[1]
    features = tokens.shape[1]
    feat_local = features // lax.axis_size("tp")
    feat_start = lax.axis_index("tp") * feat_local

    square = lax.axis_size("fsdp") == 4
    gain_shard = jnp.concatenate(
        [jnp.stack([norm_mix, norm_feed]).astype(F32), jnp.zeros((6, norm_mix.shape[0]), F32)], axis=0
    )
    if square:
        normed, normed_split, cotangent_split, gains, whole_in, whole_merge = enter(
            tokens, cotangent, gain_shard, w_recur, w_gelu, w_merge
        )
    else:
        whole_in = gather_halves(jnp.concatenate([w_recur, w_gelu], axis=1), 0)
        whole_merge = gather_halves(w_merge, 1)
        gains = lax.all_gather(gain_shard, "fsdp", axis=1, tiled=True)
        inputs = tokens.astype(F32)
        normed = (inputs * rms_scale(inputs) * gains[0:1]).astype(BF16)
        normed_split = split_features(normed)
        cotangent_split = split_features(cotangent)
    gain_one = gains[0:1]

    padded_ids = jnp.concatenate([jnp.full((edge,), -1, jnp.int32), segments])
    local_ids = lax.dynamic_slice_in_dim(padded_ids, lax.axis_index("ctx") * piece, piece + edge)
    own_ids = local_ids[edge:]
    masks = jnp.stack(
        [(local_ids[edge - max(shift, 1) : edge - max(shift, 1) + piece] == own_ids) for shift in range(width)],
        axis=1,
    ).astype(F32)
    taps = conv_taps.astype(F32)
    blocks = jnp.stack([rate_gate.reshape(chans, block), entry_gate.reshape(chans, block)])
    gate_bias = jnp.concatenate([rate_bias, entry_bias]).astype(F32)[None, :]
    softer = jax.nn.softplus(-decay_logit)[None, :]

    rows_to_features = (((1,), (1,)), ((), ()))
    branches = jnp.dot(normed, whole_in, preferred_element_type=F32).astype(BF16)
    halo = shifted(branches[piece - 8 :, :chans], "ctx", 1)
    conv, rate, entry, local_state, run, gates = recur_forward(
        branches, halo, masks, taps, conv_bias.astype(F32)[None, :], blocks, gate_bias, softer
    )
    state_in = shifted(local_state[piece - 8 :], "ctx", 1)[7:8]
    states, gated, part_merge = merge_states(local_state, run, state_in, branches, whole_merge)

    if square:
        merged, normed_two, normed_two_split, whole_mid, whole_down = middle(
            part_merge, tokens, gains, (w_gate, w_up, w_down)
        )
    else:
        merged, normed_two = middle(part_merge, tokens, gains, ())
        normed_two_split = split_features(normed_two)
        whole_mid = gather_halves(jnp.concatenate([w_gate, w_up], axis=1), 0)
        whole_down = gather_halves(w_down, 1)

    units = w_gate.shape[1]
    pre_mid = jnp.dot(normed_two, whole_mid, preferred_element_type=F32).astype(BF16)
    gate_act = gelu_pair(pre_mid[:, :units].astype(F32))[0]
    hidden = (gate_act * pre_mid[:, units:].astype(F32)).astype(BF16)
    part_feed = jnp.dot(hidden, whole_down, preferred_element_type=F32).astype(BF16)
    feed = lax.psum_scatter(part_feed, "tp", scatter_dimension=1, tiled=True)
    hidden, pre_mid, whole_mid, late_cotangent, normed_two_split = after(
        (hidden, pre_mid, whole_mid, cotangent, normed_two_split), part_feed
    )
    d_hidden = lax.dot_general(late_cotangent, whole_down, rows_to_features, preferred_element_type=F32).astype(BF16)
    gate_act, gate_slope = gelu_pair(pre_mid[:, :units].astype(F32))
    up_vals = pre_mid[:, units:].astype(F32)
    wide_hidden = d_hidden.astype(F32)
    d_mid = jnp.concatenate(
        [(wide_hidden * up_vals * gate_slope).astype(BF16), (wide_hidden * gate_act).astype(BF16)], axis=1
    )
    part_two = lax.dot_general(d_mid, whole_mid, rows_to_features, preferred_element_type=F32).astype(BF16)
    pair_down = pair_sums(cotangent_split, hidden, 1)
    pair_mid = pair_sums(normed_two_split, d_mid, 0, part_two)
    part_two = after(part_two, pair_down, pair_mid)
    turned = turn(part_two, tokens, merged, cotangent, gains, square)
    own_resid_grad, d_merge_in, feed_sums = turned[:3]
    d_merge_split = turned[3] if square else split_features(d_merge_in)
    half_down = half_to_owners(pair_down, 1)
    half_mid = half_to_owners(pair_mid, 0)
    d_merge_in = after(d_merge_in, half_down, feed)

    shard_down = both_halves(half_down, 1)
    pair_merge = pair_sums(d_merge_split, gated, 1)
    half_merge = half_to_owners(pair_merge, 1)
    d_gated = lax.dot_general(d_merge_in, whole_merge, rows_to_features, preferred_element_type=F32)
    local_grad, grad_run, first, d_gelu_pre = recur_adjoint(rate, d_gated, branches, states, masks, softer)
    grad_in = shifted(first, "ctx", -1)[0:1]
    back, tail, head, gate_grads, sums = recur_backward(
        local_grad, grad_run, grad_in, rate, after(entry, half_mid, shard_down, pair_merge), conv, states, masks, branches, d_gelu_pre,
        halo, taps, gates, softer
    )
    returned = shifted(head, "ctx", -1)
    d_in = lax.dynamic_update_slice(back, (tail + returned).astype(BF16), (piece - 8, 0))
    part_one = lax.dot_general(d_in, whole_in, rows_to_features, preferred_element_type=F32).astype(BF16)
    part_one = after(part_one, half_merge)
    d_normed = lax.psum_scatter(part_one, "tp", scatter_dimension=1, tiled=True)

    pair_in = pair_sums(normed_split, after(d_in, part_one), 0)
    inputs = tokens.astype(F32)
    scale_one = rms_scale(inputs)
    wide_part = part_one.astype(F32)
    stat_one = jnp.sum(wide_part * inputs * gain_one, axis=-1)
    grad_mix = jnp.sum(wide_part * inputs * scale_one, axis=0)
    norm_sums = jnp.stack([grad_mix, feed_sums[0] / lax.axis_size("tp")])
    spread = jnp.arange(2 * chans)[None, :] % chans // block
    diagonal = sum(jnp.where(spread == i, gate_grads[i * block : (i + 1) * block], 0.0) for i in range(heads))
    diagonal = diagonal.astype(BF16)
    if square:
        own_in, gate_sums, row_sums, both_norms, line_stats = leave(
            pair_in, diagonal, sums, norm_sums.reshape(-1, 128), stat_one.reshape(-1, 128)
        )
        shard_in = own_in.astype(F32)
        both_norms = both_norms.reshape(2, features)
        stat_one = line_stats.reshape(-1)
    else:
        shard_in = both_halves(half_to_owners(pair_in, 0), 0)
        gate_sums = lax.psum(diagonal, ("fsdp", "ctx"))
        row_sums = lax.psum(sums, ("fsdp", "ctx"))
        both_norms = lax.psum(norm_sums, ("fsdp", "ctx", "tp"))
        stat_one = lax.psum(stat_one, "tp")
    stat_one = stat_one[:, None] / features
    shard_mid = both_halves(half_mid, 0)
    shard_merge = both_halves(half_merge, 1)
    gate_sums = gate_sums.astype(F32).reshape(block, 2, heads, block).transpose(1, 2, 0, 3)

    def own(block):
        return lax.dynamic_slice_in_dim(block, feat_start, feat_local, 1)

    own_inputs = own(tokens).astype(F32)
    output = (own_inputs + own(merged).astype(F32) + feed.astype(F32)).astype(BF16)
    grad_tokens = (
        own_resid_grad
        + scale_one * d_normed.astype(F32) * own(gain_one)
        - own_inputs * scale_one**3 * stat_one
    ).astype(BF16)

    norm_local = norm_mix.shape[0]
    own_norms = lax.dynamic_slice_in_dim(both_norms, lax.axis_index("fsdp") * norm_local, norm_local, 1)

    return (
        output,
        grad_tokens,
        shard_in[:, :chans],
        shard_in[:, chans:],
        shard_merge,
        shard_mid[:, :units],
        shard_mid[:, units:],
        shard_down,
        own_norms[0],
        own_norms[1],
        row_sums[4 : 4 + width],
        row_sums[3],
        gate_sums[0],
        gate_sums[1],
        row_sums[1],
        row_sums[2],
        CGAIN * row_sums[0] * jax.nn.sigmoid(-decay_logit),
    )


def solution(mesh):
    placed = (
        P(("fsdp", "ctx"), None),
        P("fsdp"),
        P(("fsdp", "ctx"), None),
        P("fsdp", "tp"),
        P("fsdp", "tp"),
        P("tp", "fsdp"),
        P("fsdp", "tp"),
        P("fsdp", "tp"),
        P("tp", "fsdp"),
        P("fsdp"),
        P("fsdp"),
        P(None, "tp"),
        P("tp"),
        P("tp", None, None),
        P("tp", None, None),
        P("tp"),
        P("tp"),
        P("tp"),
    )
    return jax.shard_map(
        shards,
        mesh=mesh,
        in_specs=placed,
        out_specs=(
            P(("fsdp", "ctx"), "tp"),
            P(("fsdp", "ctx"), "tp"),
            P("fsdp", "tp"),
            P("fsdp", "tp"),
            P("tp", "fsdp"),
            P("fsdp", "tp"),
            P("fsdp", "tp"),
            P("tp", "fsdp"),
            P("fsdp"),
            P("fsdp"),
            P(None, "tp"),
            P("tp"),
            P("tp", None, None),
            P("tp", None, None),
            P("tp"),
            P("tp"),
            P("tp"),
        ),
        check_vma=False,
    )
```

```python
import jax
import jax.numpy as jnp
from jax import lax
from jax.experimental import pallas as pl
from jax.experimental.pallas import tpu as pltpu
from jax.sharding import PartitionSpec as P

EPS = 1e-06
CGAIN = 8.0
ROOT = 0.7978845608
CUBE = 0.044715
TILE = 128
SEGS = 8
F32 = jnp.float32
BF16 = jnp.bfloat16


def swap_cores(block):
    size = lax.axis_size("ctx")
    return lax.ppermute(block, "ctx", [(i, size - 1 - i) for i in range(size)])


def shifted(block, axis, distance):
    devices = range(lax.axis_size(axis))
    route = [(i - distance, i) for i in devices if i - distance in devices]
    return lax.ppermute(block, axis, route)


def gather_halves(shard, dim):
    half = shard.shape[dim] // 2
    core = lax.axis_index("ctx")
    mine = lax.dynamic_slice_in_dim(shard, core * half, half, dim)
    mine = lax.all_gather(mine, "fsdp", axis=dim)
    other = swap_cores(mine)
    first = jnp.where(core == 0, mine, other)
    second = jnp.where(core == 0, other, mine)
    both = jnp.stack([first, second], axis=dim + 1)
    return both.reshape(shard.shape[:dim] + (-1,) + shard.shape[dim + 1 :])


def split_features(block):
    shards = lax.axis_size("fsdp")
    core = lax.axis_index("ctx")
    parts = block.reshape(block.shape[0], shards, 2, -1)
    return [
        lax.dynamic_index_in_dim(parts, index, 2, False).reshape(block.shape[0], -1)
        for index in (core, 1 - core)
    ]


def pair_sums(left, right, dim, behind=None):
    rows_to_rows = (((0,), (0,)), ((), ()))

    def product(index):
        pair = (left[index], right) if dim == 0 else (right, left[index])
        return lax.dot_general(*pair, rows_to_rows, preferred_element_type=F32)

    arrived = swap_cores(product(1).astype(BF16))
    if behind is not None:
        arrived, left = after((arrived, left), behind)
    return (product(0) + arrived.astype(F32)).astype(BF16)


def half_to_owners(mine, dim):
    return lax.psum_scatter(mine, "fsdp", scatter_dimension=dim, tiled=True)


def both_halves(total, dim):
    other = swap_cores(total)
    core = lax.axis_index("ctx")
    first = jnp.where(core == 0, total, other)
    second = jnp.where(core == 0, other, total)
    return jnp.concatenate([first, second], axis=dim).astype(F32)


def after(value, *others):
    return lax.optimization_barrier((value, *others))[0]


class Square:
    def __init__(self):
        me = lax.axis_index("fsdp")
        row, col = me // 2, me % 2
        self.me = me
        self.core = lax.axis_index("ctx")
        self.near = (row * 2 + 1 - col, (1 - row) * 2 + col)
        self.far = (1 - row) * 2 + 1 - col


def remote(source, target, send, arrive, **device):
    return pltpu.make_async_remote_copy(
        source, target, send, arrive, device_id=device, device_id_type=pl.DeviceIdType.MESH
    )


class Gather:
    def __init__(self, items, stages, send, arrive, local):
        self.items, self.stages = items, stages
        self.send, self.arrive, self.local = send, arrive, local
        self.square = Square()

    def piece(self, w, owner, low, size):
        shard, whole, dim, offset = self.items[w]
        low = pl.multiple_of(owner * shard.shape[dim] + low, 128)
        if dim == 0:
            return whole.at[pl.ds(low, size), pl.ds(offset, shard.shape[1])]
        return whole.at[:, pl.ds(low, size)]

    def copy(self, w, k):
        shard, _, dim, _ = self.items[w]
        square = self.square
        half = shard.shape[dim] // 2
        low = pl.multiple_of(square.core * half, 128)
        first, second = square.near
        if k < 2:
            source = shard.at[pl.ds(low, half), :] if dim == 0 else shard.at[:, pl.ds(low, half)]
            target = self.piece(w, square.me, low, half)
            device = {"fsdp": square.near[k]}
        elif k < 4:
            source = target = self.piece(w, square.near[k - 2], low + (k - 2) * (half // 2), half // 2)
            device = {"fsdp": square.near[3 - k]}
        else:
            source = target = self.piece(w, (first, second, square.far)[k - 4], low, half)
            device = {"ctx": 1 - square.core}
        return remote(source, target, self.send.at[w, k], self.arrive.at[w, k], **device)

    def stage(self, w, out):
        shard = self.items[w][0]
        if out:
            target = self.piece(w, self.square.me, 0, shard.shape[self.items[w][2]])
            return pltpu.make_async_copy(self.stages[w], target, self.local.at[w, 1])
        return pltpu.make_async_copy(shard, self.stages[w], self.local.at[w, 0])

    def start(self, w):
        self.copy(w, 0).start()
        self.copy(w, 1).start()
        self.stage(w, False).start()

    def forward(self, w):
        self.copy(w, 0).wait_recv()
        self.copy(w, 2).start()
        self.copy(w, 1).wait_recv()
        self.copy(w, 3).start()
        self.copy(w, 4).start()
        self.copy(w, 5).start()
        self.stage(w, False).wait()
        self.stage(w, True).start()

    def hand_over(self, w):
        self.copy(w, 2).wait_recv()
        self.copy(w, 3).wait_recv()
        self.copy(w, 6).start()

    def finish(self, w):
        for k in (4, 5, 6):
            self.copy(w, k).wait_recv()
        for k in range(7):
            self.copy(w, k).wait_send()
        self.stage(w, True).wait()


def greet(line, square, whole_line=False):
    barrier = pltpu.get_barrier_semaphore()

    def call(**device):
        pl.semaphore_signal(barrier, inc=1, device_id=device, device_id_type=pl.DeviceIdType.MESH)

    peers = 0
    if line:
        count, me = lax.axis_size("tp"), lax.axis_index("tp")

        @pl.when(me > 0)
        def _():
            call(tp=me - 1)

        @pl.when(me < count - 1)
        def _():
            call(tp=me + 1)

        peers = jnp.where((me > 0) & (me < count - 1), 2, 1)
    if whole_line:
        count, me = lax.axis_size("tp"), lax.axis_index("tp")
        for other in range(count):
            @pl.when(me != other)
            def _():
                call(tp=other)

        peers = peers + (count - 1)
    if square:
        place = Square()
        call(fsdp=place.near[0])
        call(fsdp=place.near[1])
        call(fsdp=place.far)
        call(ctx=1 - place.core)
        peers = peers + 4
    pl.semaphore_wait(barrier, peers)


def line_sum(part, whole, inbox, sems, finish, between):
    count, me = lax.axis_size("tp"), lax.axis_index("tp")
    half = part.shape[0] // 2
    chunks = inbox.shape[1]
    rows = half // chunks
    sum_send, sum_arrive, share_send, share_arrive = sems

    def spot(side, c):
        return pl.ds(pl.multiple_of(side * half + c * rows, rows), rows)

    def place(side):
        return count - 1 - me if side else me

    def onward(side, c, source):
        target = me - 1 if side else me + 1
        return remote(source, inbox.at[side, c], sum_send.at[side, c], sum_arrive.at[side, c], tp=target)

    def share(side, c):
        target = me + 1 if side else me - 1
        block = whole.at[spot(side, c), :]
        return remote(block, block, share_send.at[side, c], share_arrive.at[side, c], tp=target)

    for side in (0, 1):
        @pl.when(place(side) == 0)
        def _():
            onward(side, 0, part.at[spot(side, 0), :]).start()

    def step(t, carry):
        for side in (0, 1):
            here = place(side)
            c = t - here

            @pl.when((here == 0) & (t + 1 < chunks))
            def _():
                onward(side, t + 1, part.at[spot(side, t + 1), :]).start()

            @pl.when((c >= 0) & (c < chunks) & (here > 0))
            def _():
                onward(side, c, inbox.at[side, c]).wait_recv()
                total = (inbox[side, c].astype(F32) + part[spot(side, c), :].astype(F32)).astype(BF16)

                @pl.when(here < count - 1)
                def _():
                    inbox[side, c] = total
                    onward(side, c, inbox.at[side, c]).start()

                @pl.when(here == count - 1)
                def _():
                    whole[spot(side, c), :] = total
                    share(side, c).start()
                    finish(spot(side, c))

        for side in (0, 1):
            here = place(side)
            c = t - 2 * (count - 1) + here

            @pl.when((c >= 0) & (c < chunks) & (here < count - 1))
            def _():
                share(side, c).wait_recv()

                @pl.when(here > 0)
                def _():
                    share(side, c).start()

                finish(spot(side, c))

        between(t)
        return carry

    lax.fori_loop(0, chunks + 2 * (count - 1), step, 0)

    def drain(c, carry):
        for side in (0, 1):
            here = place(side)

            @pl.when(here < count - 1)
            def _():
                onward(side, c, inbox.at[side, c]).wait_send()

            @pl.when(here > 0)
            def _():
                share(side, c).wait_send()

        return carry

    lax.fori_loop(0, chunks, drain, 0)


def put_split(ref, rows, block):
    core = lax.axis_index("ctx")
    size = block.shape[1] // 8
    for owner in range(4):
        for index in range(2):
            low = (2 * owner + index) * size
            ref[(index + core) % 2, rows, owner * size : (owner + 1) * size] = block[:, low : low + size]


CHUNK = 32
LINE_COST = pl.CostEstimate(flops=0, bytes_accessed=400_000_000, transcendentals=0)


def enter_kernel(
    tokens, upstream, gain_shard, recur, gelu,
    normed, halves, upstream_halves, gains, whole_in,
    stage_recur, stage_gelu, send, arrive, local, gain_send, gain_arrive,
):
    square = Square()
    greet(False, True)
    width = gain_shard.shape[1]

    def gain_copy(k, owner, target):
        spot = gains.at[:, pl.ds(pl.multiple_of(owner * width, 128), width)]
        return remote(gain_shard, spot, gain_send.at[k], gain_arrive.at[k], fsdp=target)

    others = (*square.near, square.far)
    for k, target in enumerate(others):
        gain_copy(k, square.me, target).start()
    gather = Gather(
        [(recur, whole_in, 0, 0), (gelu, whole_in, 0, recur.shape[1])],
        (stage_recur, stage_gelu), send, arrive, local,
    )
    for w in range(2):
        gather.start(w)
    gains[:, pl.ds(pl.multiple_of(square.me * width, 128), width)] = gain_shard[...]
    for k, owner in enumerate(others):
        gain_copy(k, owner, owner).wait_recv()

    def norm(t, carry):
        rows = pl.ds(pl.multiple_of(t * CHUNK, CHUNK), CHUNK)
        block = tokens[rows, :].astype(F32)
        block = (block * rms_scale(block) * gains[0:1, :]).astype(BF16)
        normed[rows, :] = block
        put_split(halves, rows, block)
        put_split(upstream_halves, rows, upstream[rows, :])
        return carry

    lax.fori_loop(0, tokens.shape[0] // CHUNK, norm, 0)
    for w in range(2):
        gather.forward(w)
    for w in range(2):
        gather.hand_over(w)
    for w in range(2):
        gather.finish(w)
    for k, target in enumerate(others):
        gain_copy(k, square.me, target).wait_send()


ANY = pl.BlockSpec(memory_space=pl.ANY)
NEAR = pl.BlockSpec(memory_space=pltpu.VMEM)


def gather_scratch(shards):
    count = len(shards)
    dma = pltpu.SemaphoreType.DMA
    return [pltpu.VMEM(w.shape, w.dtype) for w in shards] + [dma((count, 7)), dma((count, 7)), dma((count, 2))]


def enter(tokens, upstream, gain_shard, recur, gelu):
    rows, features = tokens.shape
    shape = jax.ShapeDtypeStruct
    inner = recur.shape[1]
    dma = pltpu.SemaphoreType.DMA
    return pl.pallas_call(
        enter_kernel,
        out_shape=(
            shape((rows, features), BF16),
            shape((2, rows, features // 2), BF16),
            shape((2, rows, features // 2), BF16),
            shape((8, features), F32),
            shape((features, 2 * inner), BF16),
        ),
        in_specs=[NEAR, NEAR, NEAR, ANY, ANY],
        out_specs=[NEAR, NEAR, NEAR, NEAR, ANY],
        scratch_shapes=gather_scratch([recur, gelu]) + [dma((3,)), dma((3,))],
        compiler_params=pltpu.CompilerParams(collective_id=1, has_side_effects=True),
        name="enter",
    )(tokens, upstream, gain_shard, recur, gelu)


def line_scratch(rows, features):
    chunks = rows // 2 // CHUNK
    dma = pltpu.SemaphoreType.DMA((2, chunks))
    return [pltpu.VMEM((2, chunks, CHUNK, features), BF16), dma, dma, dma, dma]


class Fetch:
    def __init__(self, sources, targets, sems):
        self.copies = [pltpu.make_async_copy(a, b, sems.at[k]) for k, (a, b) in enumerate(zip(sources, targets))]

    def start(self):
        for copy in self.copies:
            copy.start()

    def wait(self):
        for copy in self.copies:
            copy.wait()


def middle_kernel(gathers, part, far_tokens, gains, *refs):
    *refs, tokens, fetch_sems = refs
    fetch = Fetch((far_tokens,), (tokens,), fetch_sems)
    fetch.start()
    if gathers:
        gate, up, down, merged, normed, halves, whole_in, whole_down = refs[:8]
        inbox, *rest = refs[8:]
        sems, (stage_gate, stage_up, stage_down, send, arrive, local) = rest[:4], rest[4:]
        gather = Gather(
            [(gate, whole_in, 0, 0), (up, whole_in, 0, gate.shape[1]), (down, whole_down, 1, 0)],
            (stage_gate, stage_up, stage_down), send, arrive, local,
        )
        greet(True, True)
        for w in range(3):
            gather.start(w)
    else:
        merged, normed, inbox, *sems = refs
        greet(True, False)

    def finish(rows):
        block = tokens[rows, :].astype(F32) + merged[rows, :].astype(F32)
        block = (block * rms_scale(block) * gains[1:2, :]).astype(BF16)
        normed[rows, :] = block
        if gathers:
            put_split(halves, rows, block)

    def between(t):
        @pl.when(t == 0)
        def _():
            fetch.wait()

        if gathers:
            for w in range(3):
                @pl.when(t == 5 + 4 * w)
                def _():
                    gather.forward(w)

                @pl.when(t == 17 + w)
                def _():
                    gather.hand_over(w)

    line_sum(part, merged, inbox, sems, finish, between)
    if gathers:
        for w in range(3):
            gather.finish(w)


def middle(part, tokens, gains, shards):
    rows, features = tokens.shape
    shape = jax.ShapeDtypeStruct
    whole = shape((rows, features), BF16)
    outs, specs = [whole, whole], [NEAR, NEAR]
    scratch = line_scratch(rows, features)
    if shards:
        gate, up, down = shards
        outs += [
            shape((2, rows, features // 2), BF16),
            shape((features, 2 * gate.shape[1]), BF16),
            shape((down.shape[0], features), BF16),
        ]
        specs += [NEAR, ANY, ANY]
        scratch += gather_scratch(shards)
    scratch += [pltpu.VMEM((rows, features), BF16), pltpu.SemaphoreType.DMA((1,))]
    return pl.pallas_call(
        lambda *refs: middle_kernel(bool(shards), *refs),
        out_shape=tuple(outs),
        in_specs=[NEAR, ANY, NEAR] + [ANY] * len(shards),
        out_specs=specs,
        scratch_shapes=scratch,
        compiler_params=pltpu.CompilerParams(collective_id=2, has_side_effects=True),
        cost_estimate=LINE_COST,
        name="middle",
    )(part, tokens, gains, *shards)


def turn_kernel(split, part, far_tokens, far_merged, far_upstream, gains, own, grad_in, gain_sum, *refs):
    if split:
        halves, *refs = refs
    whole, wide, tokens, merged, upstream, fetch_sems, inbox, *sems = refs
    fetch = Fetch((far_tokens, far_merged, far_upstream), (tokens, merged, upstream), fetch_sems)
    fetch.start()
    greet(True, False)
    gain_sum[...] = jnp.zeros_like(gain_sum)
    width = own.shape[1]
    start = pl.multiple_of(lax.axis_index("tp") * width, 128)

    def finish(rows):
        block = tokens[rows, :].astype(F32) + merged[rows, :].astype(F32)
        scale = rms_scale(block)
        grad = whole[rows, :].astype(F32)
        gain_sum[0:1, :] += jnp.sum(grad * (block * scale), axis=0, keepdims=True)
        grad = grad * gains[1:2, :]
        mean = jnp.mean(block * grad, axis=-1, keepdims=True)
        grad = upstream[rows, :].astype(F32) + scale * grad - block * (scale * scale * scale * mean)
        wide[...] = grad
        own[rows, :] = wide[:, pl.ds(start, width)]
        grad = grad.astype(BF16)
        grad_in[rows, :] = grad
        if split:
            put_split(halves, rows, grad)

    def between(t):
        @pl.when(t == 0)
        def _():
            fetch.wait()

    line_sum(part, whole, inbox, sems, finish, between)


def turn(part, tokens, merged, upstream, gains, split):
    rows, features = tokens.shape
    shape = jax.ShapeDtypeStruct
    outs = [
        shape((rows, features // lax.axis_size("tp")), F32),
        shape((rows, features), BF16),
        shape((8, features), F32),
    ]
    if split:
        outs.append(shape((2, rows, features // 2), BF16))
    return pl.pallas_call(
        lambda *refs: turn_kernel(split, *refs),
        out_shape=tuple(outs),
        in_specs=[NEAR, ANY, ANY, ANY, NEAR],
        out_specs=[NEAR] * len(outs),
        scratch_shapes=[pltpu.VMEM((rows, features), BF16), pltpu.VMEM((CHUNK, features), F32)]
        + [pltpu.VMEM((rows, features), BF16)] * 3
        + [pltpu.SemaphoreType.DMA((3,))]
        + line_scratch(rows, features),
        compiler_params=pltpu.CompilerParams(collective_id=3, has_side_effects=True),
        cost_estimate=LINE_COST,
        name="turn",
    )(part, tokens, merged, upstream, gains)


def rounded_sum(*blocks):
    total = blocks[0].astype(F32)
    for block in blocks[1:]:
        total = total + block.astype(F32)
    return total.astype(BF16)


class Scatter:
    def __init__(self, items, boxes, lasts, send, arrive):
        self.items, self.boxes, self.lasts = items, boxes, lasts
        self.send, self.arrive = send, arrive
        self.square = Square()

    def block(self, w, owner, k):
        part, _, dim = self.items[w]
        size = part.shape[dim] // 4
        if dim == 0:
            low = pl.multiple_of(owner * size + k * (size // 2), 128)
            return part.at[pl.ds(low, size // 2), :]
        half = part.shape[0] // 2
        return part.at[pl.ds(k * half, half), pl.ds(pl.multiple_of(owner * size, 128), size)]

    def spot(self, w, k):
        part, out, dim = self.items[w]
        size = part.shape[dim] // 4
        low = pl.multiple_of(self.square.core * size, 128)
        if dim == 0:
            return out.at[pl.ds(low + k * (size // 2), size // 2), :]
        half = part.shape[0] // 2
        return out.at[pl.ds(k * half, half), pl.ds(low, size)]

    def copy(self, w, k, j):
        square = self.square
        first, second = square.near[k], square.near[1 - k]
        send, arrive = self.send.at[w, 4 * k + j], self.arrive.at[w, 4 * k + j]
        if j < 2:
            owner = square.far if j == 0 else first
            return remote(self.block(w, owner, k), self.boxes[w].at[k, j], send, arrive, fsdp=first)
        if j == 2:
            return remote(self.boxes[w].at[k, 0], self.lasts[w].at[k], send, arrive, fsdp=second)
        return remote(self.spot(w, k), self.spot(w, k), send, arrive, ctx=1 - square.core)

    def start(self, w):
        for j in (0, 1):
            for k in (0, 1):
                self.copy(w, k, j).start()

    def relay(self, w):
        for k in (0, 1):
            self.copy(w, k, 0).wait_recv()
            mine = self.block(w, self.square.near[1 - k], k)
            self.boxes[w][k, 0] = rounded_sum(mine[...], self.boxes[w][k, 0])
            self.copy(w, k, 2).start()

    def finish(self, w):
        for k in (0, 1):
            self.copy(w, k, 1).wait_recv()
            self.copy(w, k, 2).wait_recv()
            mine = self.block(w, self.square.me, k)
            self.spot(w, k)[...] = rounded_sum(mine[...], self.boxes[w][k, 1], self.lasts[w][k])
            self.copy(w, k, 3).start()

    def drain(self, w):
        for k in (0, 1):
            self.copy(w, k, 3).wait_recv()
            for j in range(4):
                self.copy(w, k, j).wait_send()


def scatter_scratch(items):
    blocks = []
    for shape, dim in items:
        rows, cols = (shape[0] // 8, shape[1]) if dim == 0 else (shape[0] // 2, shape[1] // 4)
        blocks.append((rows, cols))
    dma = pltpu.SemaphoreType.DMA((len(items), 8))
    return (
        [pltpu.VMEM((2, 2, *block), BF16) for block in blocks]
        + [pltpu.VMEM((2, *block), BF16) for block in blocks]
        + [dma, dma]
    )


def leave_kernel(
    part_in, gates, sums, norms, stats,
    own_in, gate_sums, row_sums, norm_sums, stat_sums,
    box_in, last_in, send, arrive,
    gate_core, gate_half, gate_near, gate_pair, gate_far, gate_send, gate_arrive,
    core_sums, core_norms, box_sums, box_norms, sum_send, sum_arrive,
    line_norms, line_stats, norm_send, norm_arrive, stat_send, stat_arrive,
):
    square = Square()
    count, place = lax.axis_size("tp"), lax.axis_index("tp")
    core = square.core
    others = (*square.near, square.far)
    greet(False, True, True)

    def norm_copy(k, source):
        box = line_norms.at[source]
        return remote(box, box, norm_send.at[k], norm_arrive.at[source], tp=k)

    def stat_copy(k, source):
        return remote(stats, line_stats.at[source], stat_send.at[k], stat_arrive.at[source], tp=k)

    def core_copy(k):
        source, target = ((sums, core_sums), (norms, core_norms))[k]
        return remote(source, target, sum_send.at[k], sum_arrive.at[k], ctx=1 - core)

    def square_copy(k, j):
        box = (box_sums, box_norms)[k].at[square.me]
        at = 2 + 3 * k + j
        return remote(box, box, sum_send.at[at], sum_arrive.at[at], fsdp=others[j])

    gate_rows = gates.shape[0] // 2
    gate_cols = gates.shape[1] // 2
    my_rows = pl.ds(pl.multiple_of(core * gate_rows, 16), gate_rows)
    your_rows = pl.ds(pl.multiple_of((1 - core) * gate_rows, 16), gate_rows)

    def gate_copy(j):
        send, arrive = gate_send.at[j], gate_arrive.at[j]
        if j == 0:
            return remote(gates.at[your_rows, :], gate_core, send, arrive, ctx=1 - core)
        if j == 5:
            spot = gate_sums.at[my_rows, :]
            return remote(spot, spot, send, arrive, ctx=1 - core)
        k = (j - 1) % 2
        if j < 3:
            return remote(gate_half.at[k], gate_near.at[k], send, arrive, fsdp=square.near[k])
        return remote(gate_pair.at[k], gate_far.at[k], send, arrive, fsdp=square.near[1 - k])

    scatter = Scatter([(part_in, own_in, 0)], (box_in,), (last_in,), send, arrive)
    gate_copy(0).start()
    core_copy(0).start()
    core_copy(1).start()
    for k in range(count):
        @pl.when(place != k)
        def _():
            stat_copy(k, place).start()

    line_stats[place] = stats[...]
    core_copy(0).wait_recv()
    core_copy(1).wait_recv()
    box_sums[square.me] = sums[...] + core_sums[...]
    box_norms[square.me] = norms[...] + core_norms[...]
    for k in (0, 1):
        for j in range(3):
            square_copy(k, j).start()
    gate_copy(0).wait_recv()
    for k in (0, 1):
        cols = slice(k * gate_cols, (k + 1) * gate_cols)
        gate_half[k] = rounded_sum(gates[my_rows, cols], gate_core[:, cols])
        gate_copy(1 + k).start()
    scatter.start(0)
    for k in (0, 1):
        for j in range(3):
            square_copy(k, j).wait_recv()
    row_sums[...] = box_sums[0] + box_sums[1] + box_sums[2] + box_sums[3]
    line_norms[place] = box_norms[0] + box_norms[1] + box_norms[2] + box_norms[3]
    for k in range(count):
        @pl.when(place != k)
        def _():
            norm_copy(k, place).start()

    for k in (0, 1):
        gate_copy(1 + k).wait_recv()
        gate_pair[k] = rounded_sum(gate_half[k], gate_near[k])
        gate_copy(3 + k).start()
    scatter.relay(0)
    for k in (0, 1):
        cols = slice(k * gate_cols, (k + 1) * gate_cols)
        gate_copy(3 + k).wait_recv()
        gate_sums[my_rows, cols] = rounded_sum(gate_pair[k], gate_far[k])
    gate_copy(5).start()
    for k in range(count):
        @pl.when(place != k)
        def _():
            norm_copy(k, k).wait_recv()
            stat_copy(k, k).wait_recv()

    total = line_norms[0]
    stat = line_stats[0]
    for k in range(1, count):
        total = total + line_norms[k]
        stat = stat + line_stats[k]
    norm_sums[...] = total
    stat_sums[...] = stat
    scatter.finish(0)
    scatter.drain(0)
    gate_copy(5).wait_recv()
    for j in range(6):
        gate_copy(j).wait_send()
    for k in (0, 1):
        core_copy(k).wait_send()
        for j in range(3):
            square_copy(k, j).wait_send()
    for k in range(count):
        @pl.when(place != k)
        def _():
            norm_copy(k, place).wait_send()
            stat_copy(k, place).wait_send()


def leave(part_in, gates, sums, norms, stats):
    shape = jax.ShapeDtypeStruct
    count = lax.axis_size("tp")
    dma = pltpu.SemaphoreType.DMA
    height, width = gates.shape[0] // 2, gates.shape[1] // 2
    quarter = pltpu.VMEM((2, height, width), BF16)
    return pl.pallas_call(
        leave_kernel,
        out_shape=(
            shape((part_in.shape[0] // 2, part_in.shape[1]), BF16),
            shape(gates.shape, BF16),
            shape(sums.shape, F32),
            shape(norms.shape, F32),
            shape(stats.shape, F32),
        ),
        in_specs=[NEAR] * 5,
        out_specs=[NEAR] * 5,
        scratch_shapes=(
            scatter_scratch([(part_in.shape, 0)])
            + [pltpu.VMEM((height, 2 * width), BF16), quarter, quarter, quarter, quarter, dma((6,)), dma((6,))]
            + [pltpu.VMEM(sums.shape, F32), pltpu.VMEM(norms.shape, F32)]
            + [pltpu.VMEM((4, *sums.shape), F32), pltpu.VMEM((4, *norms.shape), F32), dma((8,)), dma((8,))]
            + [pltpu.VMEM((count, *norms.shape), F32), pltpu.VMEM((count, *stats.shape), F32)]
            + [dma((count,))] * 4
        ),
        compiler_params=pltpu.CompilerParams(collective_id=4, has_side_effects=True),
        cost_estimate=pl.CostEstimate(flops=0, bytes_accessed=160_000_000, transcendentals=0),
        name="leave",
    )(part_in, gates, sums, norms, stats)


def gelu_pair(q):
    tanh = jnp.tanh(ROOT * (q + CUBE * q * q * q))
    value = 0.5 * q * (1.0 + tanh)
    slope = 0.5 * (1.0 + tanh) + 0.5 * q * (1.0 - tanh * tanh) * ROOT * (1.0 + 3.0 * CUBE * q * q)
    return value, slope


def rms_scale(values):
    return lax.rsqrt(jnp.mean(values * values, axis=-1, keepdims=True) + EPS)


def decay_parts(rate, softer, keep):
    gap = 2.0 * CGAIN * rate * softer
    decay = jnp.exp(-0.5 * gap)
    series = gap * (
        1.0
        - gap / 2.0
        * (1.0 - gap / 3.0 * (1.0 - gap / 4.0 * (1.0 - gap / 5.0 * (1.0 - gap / 6.0 * (1.0 - gap / 7.0)))))
    )
    square = jnp.where(gap < 0.25, series, 1.0 - decay * decay)
    return jnp.where(keep, decay, 0.0), jnp.where(keep, square, 1.0)


LANES = 128


def put_lanes(ref, block, rows):
    for lane in range(ref.shape[0]):
        ref[lane, 0:rows, :] = block[:, lane * LANES : (lane + 1) * LANES]


def sweep(decay_ref, value_ref, state_ref, product_ref, out_ref, run_ref, carry_ref, reverse, offset):
    groups, rows, _ = value_ref.shape
    steps = rows // SEGS
    place = lax.broadcasted_iota(jnp.int32, (SEGS, LANES), 0)
    if reverse:
        place = SEGS - 1 - place

    def moved(block, by, fill):
        turned = pltpu.roll(block, SEGS - by if reverse else by, 0)
        return jnp.where(place >= by, turned, fill)

    for lane in range(groups):
        lanes = slice(lane * LANES, (lane + 1) * LANES)
        state = jnp.zeros((SEGS, LANES), F32)
        product = jnp.ones((SEGS, LANES), F32)
        for step in reversed(range(steps)) if reverse else range(steps):
            spot = pl.ds(step, SEGS, stride=steps)
            decay = decay_ref[lane, pl.ds(step + offset, SEGS, stride=steps), :]
            state = decay * state + value_ref[lane, spot, :]
            product = product * decay
            state_ref[lane, spot, :] = state
            product_ref[lane, spot, :] = product
        for by in (1, 2, 4):
            state = state + product * moved(state, by, 0.0)
            product = product * moved(product, by, 1.0)
        carry = carry_ref[0:1, lanes]
        carry_run = carry_ref[8:9, lanes]
        state = state + product * carry
        product = product * carry_run
        enter = moved(state, 1, carry)
        enter_run = moved(product, 1, carry_run)
        for seg in range(SEGS):
            span = slice(seg * steps, (seg + 1) * steps)
            inner = product_ref[lane, span, :]
            out_ref[span, lanes] = state_ref[lane, span, :] + inner * enter[seg : seg + 1, :]
            run_ref[span, lanes] = inner * enter_run[seg : seg + 1, :]
        last = 0 if reverse else SEGS - 1
        carry_ref[0:1, lanes] = state[last : last + 1, :]
        carry_ref[8:9, lanes] = product[last : last + 1, :]


BIAS, RATE, ENTRY, SOFTER = slice(4, 5), slice(5, 6), slice(6, 7), slice(7, 8)


def spread_blocks(blocks_ref, out_ref):
    chans, size = blocks_ref.shape[1:]
    row = lax.broadcasted_iota(jnp.int32, (chans, chans), 0)
    col = lax.broadcasted_iota(jnp.int32, (chans, chans), 1)
    inner = lax.broadcasted_iota(jnp.int32, (size, chans), 0)
    outer = lax.broadcasted_iota(jnp.int32, (size, chans), 1)
    inside = row < 0
    repeat = outer < 0
    for low in range(0, chans, size):
        inside |= (row >= low) & (row < low + size) & (col >= low) & (col < low + size)
        repeat |= outer - low == inner
    repeat = repeat.astype(F32).astype(BF16)
    for gate in range(2):
        wide = jnp.dot(blocks_ref[gate], repeat, preferred_element_type=F32)
        out_ref[:, gate * chans : (gate + 1) * chans] = jnp.where(inside, wide, 0.0).astype(BF16)


def forward_kernel(
    branch_ref, halo_ref, mask_ref, chan_ref, blocks_ref,
    conv_ref, rate_ref, entry_ref, state_ref, run_ref, gates_ref,
    window, decay, value, inner, product, carry,
):
    rows, chans = conv_ref.shape
    spot = pl.program_id(0)

    @pl.when(spot == 0)
    def _():
        spread_blocks(blocks_ref, gates_ref)
        window[0:8, :] = halo_ref[...].astype(F32)
        carry[0:8, :] = jnp.zeros((8, chans), F32)
        carry[8:16, :] = jnp.ones((8, chans), F32)

    @pl.when(spot > 0)
    def _():
        window[0:8, :] = window[rows : rows + 8, :]

    window[8 : rows + 8, :] = branch_ref[...].astype(F32)
    mixed = chan_ref[BIAS, :] + chan_ref[0:1, :] * window[8 : rows + 8, :]
    for shift in range(1, mask_ref.shape[1]):
        moved = window[8 - shift : 8 - shift + rows, :]
        mixed = mixed + chan_ref[shift : shift + 1, :] * (moved * mask_ref[:, shift : shift + 1])
    conv = mixed.astype(BF16)
    conv_ref[...] = conv
    pre = jnp.dot(conv, gates_ref[...], preferred_element_type=F32)
    rate = jax.nn.sigmoid(pre[:, :chans] + chan_ref[RATE, :])
    entry = jax.nn.sigmoid(pre[:, chans:] + chan_ref[ENTRY, :])
    rate_ref[...] = rate
    entry_ref[...] = entry
    keep = jnp.broadcast_to(mask_ref[:, 0:1], (rows, chans)) > 0.5
    step, square = decay_parts(rate, chan_ref[SOFTER, :], keep)
    put_lanes(decay, step, rows)
    put_lanes(value, jnp.sqrt(square) * entry * conv.astype(F32), rows)
    sweep(decay, value, inner, product, state_ref, run_ref, carry, False, 0)


def tile_spec(width, count=None):
    if count is None:
        return pl.BlockSpec((TILE, width), lambda i: (i, 0))
    return pl.BlockSpec((TILE, width), lambda i: (count - 1 - i, 0))


def fixed_spec(shape):
    return pl.BlockSpec(shape, lambda i: (0, 0))


def recur_forward(branch, halo, masks, channels, blocks):
    rows, chans = branch.shape[0], halo.shape[1]
    wide = jax.ShapeDtypeStruct((rows, chans), F32)
    return pl.pallas_call(
        forward_kernel,
        grid=(rows // TILE,),
        out_shape=(
            jax.ShapeDtypeStruct((rows, chans), BF16), wide, wide, wide, wide,
            jax.ShapeDtypeStruct((chans, 2 * chans), BF16),
        ),
        in_specs=[
            tile_spec(chans),
            fixed_spec((8, chans)),
            tile_spec(masks.shape[1]),
            fixed_spec(channels.shape),
            pl.BlockSpec(blocks.shape, lambda i: (0, 0, 0)),
        ],
        out_specs=[tile_spec(chans)] * 5 + [fixed_spec((chans, 2 * chans))],
        scratch_shapes=[
            pltpu.VMEM((TILE + 8, chans), F32),
            pltpu.VMEM((chans // LANES, TILE, LANES), F32),
            pltpu.VMEM((chans // LANES, TILE, LANES), F32),
            pltpu.VMEM((chans // LANES, TILE, LANES), F32),
            pltpu.VMEM((chans // LANES, TILE, LANES), F32),
            pltpu.VMEM((16, chans), F32),
        ],
        cost_estimate=pl.CostEstimate(
            flops=2 * rows * chans * 2 * chans, bytes_accessed=24 * rows * chans, transcendentals=5 * rows * chans
        ),
        name="recur_forward",
    )(branch, halo, masks, channels, blocks)


def merge_kernel(local_ref, run_ref, enter_ref, pre_ref, *refs):
    *halves, state_ref, gated_ref, part_ref, weight_ref = refs
    core = lax.axis_index("ctx")

    @pl.when(pl.program_id(0) == 0)
    def _():
        if len(halves) == 1:
            weight_ref[...] = halves[0][...]
        else:
            owners, _, size = halves[0].shape
            for owner in range(owners):
                for index, half in ((core, halves[0]), (1 - core, halves[1])):
                    low = pl.multiple_of((2 * owner + index) * size, 128)
                    weight_ref[:, pl.ds(low, size)] = half[owner]

    state = local_ref[...] + run_ref[...] * enter_ref[0:1, :]
    state_ref[...] = state
    pre = pre_ref[...].astype(F32)
    gated = (state * gelu_pair(pre)[0]).astype(BF16)
    gated_ref[...] = gated
    part_ref[...] = jnp.dot(gated, weight_ref[...], preferred_element_type=F32).astype(BF16)


def merge_states(local, run, enter, branches, weights, features):
    rows, chans = local.shape
    shape = jax.ShapeDtypeStruct
    return pl.pallas_call(
        merge_kernel,
        grid=(rows // TILE,),
        out_shape=(
            shape((rows, chans), F32), shape((rows, chans), BF16), shape((rows, features), BF16),
            shape((chans, features), BF16),
        ),
        in_specs=[
            tile_spec(chans), tile_spec(chans), fixed_spec((1, chans)),
            pl.BlockSpec((TILE, chans), lambda i: (i, 1)),
        ]
        + [pl.BlockSpec(w.shape, lambda i, rank=w.ndim: (0,) * rank) for w in weights],
        out_specs=[tile_spec(chans), tile_spec(chans), tile_spec(features), fixed_spec((chans, features))],
        cost_estimate=pl.CostEstimate(
            flops=2 * rows * chans * features, bytes_accessed=16 * rows * chans, transcendentals=rows * chans
        ),
        name="merge_states",
    )(local, run, enter, branches, *weights)


def adjoint_kernel(
    rate_ref, up_ref, pre_ref, state_ref, mask_ref, chan_ref,
    grad_ref, run_ref, head_ref, pre_grad_ref,
    decay, value, inner, product, carry,
):
    rows, chans = rate_ref.shape
    groups = chans // LANES
    spot = pl.program_id(0)

    @pl.when(spot == 0)
    def _():
        for lane in range(groups):
            decay[lane, rows : rows + 8, :] = jnp.ones((8, LANES), F32)
        carry[0:8, :] = jnp.zeros((8, chans), F32)
        carry[8:16, :] = jnp.ones((8, chans), F32)

    @pl.when(spot > 0)
    def _():
        for lane in range(groups):
            decay[lane, rows : rows + 8, :] = decay[lane, 0:8, :]

    keep = jnp.broadcast_to(mask_ref[:, 0:1], (rows, chans)) > 0.5
    gap = CGAIN * rate_ref[...] * chan_ref[SOFTER, :]
    step = jnp.where(keep, jnp.exp(-gap), 0.0)
    put_lanes(decay, step, rows)
    gate, slope = gelu_pair(pre_ref[...].astype(F32))
    up = up_ref[...]
    pre_grad_ref[...] = (up * state_ref[...] * slope).astype(BF16)
    put_lanes(value, up * gate, rows)
    sweep(decay, value, inner, product, grad_ref, run_ref, carry, True, 1)
    head_ref[...] = jnp.broadcast_to(step[0:1, :] * carry[0:1, :], (8, chans))


def recur_adjoint(rate, up, branches, state, masks, channels):
    rows, chans = rate.shape
    count = rows // TILE
    wide = jax.ShapeDtypeStruct((rows, chans), F32)
    return pl.pallas_call(
        adjoint_kernel,
        grid=(count,),
        out_shape=(
            wide, wide, jax.ShapeDtypeStruct((8, chans), F32), jax.ShapeDtypeStruct((rows, chans), BF16)
        ),
        in_specs=[
            tile_spec(chans, count),
            tile_spec(chans, count),
            pl.BlockSpec((TILE, chans), lambda i: (count - 1 - i, 1)),
            tile_spec(chans, count),
            tile_spec(masks.shape[1], count),
            fixed_spec(channels.shape),
        ],
        out_specs=[tile_spec(chans, count), tile_spec(chans, count), fixed_spec((8, chans)), tile_spec(chans, count)],
        scratch_shapes=[
            pltpu.VMEM((chans // LANES, TILE + 8, LANES), F32),
            pltpu.VMEM((chans // LANES, TILE, LANES), F32),
            pltpu.VMEM((chans // LANES, TILE, LANES), F32),
            pltpu.VMEM((chans // LANES, TILE, LANES), F32),
            pltpu.VMEM((16, chans), F32),
        ],
        cost_estimate=pl.CostEstimate(
            flops=8 * rows * chans, bytes_accessed=16 * rows * chans, transcendentals=rows * chans
        ),
        name="recur_adjoint",
    )(rate, up, branches, state, masks, channels)


def backward_kernel(
    grad_ref, run_ref, enter_ref, rate_ref, entry_ref, conv_ref, state_ref, mask_ref,
    branch_ref, pre_grad_ref, halo_ref, chan_ref, gates_ref,
    back_ref, tail_ref, head_ref, gate_grad_ref, sums_ref,
    shifts, edge,
):
    rows, chans = conv_ref.shape
    width = mask_ref.shape[1]
    spot = pl.program_id(0)
    last = pl.num_programs(0) - 1

    @pl.when(spot == 0)
    def _():
        for shift in range(1, width):
            shifts[shift - 1, rows : rows + 8, :] = jnp.zeros((8, chans), F32)
        gate_grad_ref[...] = jnp.zeros_like(gate_grad_ref)
        sums_ref[...] = jnp.zeros_like(sums_ref)

    @pl.when(spot > 0)
    def _():
        for shift in range(1, width):
            shifts[shift - 1, rows : rows + 8, :] = shifts[shift - 1, 0:8, :]

    keep = jnp.broadcast_to(mask_ref[:, 0:1], (rows, chans)) > 0.5
    softer = chan_ref[SOFTER, :]
    rate = rate_ref[...]
    entry = entry_ref[...]
    conv = conv_ref[...].astype(F32)
    grad = grad_ref[...] + run_ref[...] * enter_ref[0:1, :]
    step, square = decay_parts(rate, softer, keep)
    inverse = lax.rsqrt(square)
    mult = square * inverse
    driven = entry * conv
    carried = state_ref[...] - mult * driven
    d_log = jnp.where(keep, grad * (carried - driven * step * step * inverse), 0.0)
    d_rate = (-CGAIN * softer * d_log * rate * (1.0 - rate)).astype(BF16)
    lifted = grad * mult * entry
    d_entry = (lifted * conv * (1.0 - entry)).astype(BF16)
    both = jnp.concatenate([d_rate, d_entry], axis=1)
    d_conv = lifted + lax.dot_general(
        both, gates_ref[...], (((1,), (1,)), ((), ())), preferred_element_type=F32
    )
    gate_grad_ref[...] += lax.dot_general(
        conv_ref[...], both, (((0,), (0,)), ((), ())), preferred_element_type=F32
    )

    def add_row(row, block):
        sums_ref[row : row + 1, :] += jnp.sum(block, axis=0, keepdims=True)

    branch = branch_ref[...].astype(F32)
    add_row(0, d_log * rate)
    add_row(1, d_rate.astype(F32))
    add_row(2, d_entry.astype(F32))
    add_row(3, d_conv)
    add_row(4, d_conv * branch)
    back = chan_ref[0:1, :] * d_conv
    for shift in range(1, width):
        shifts[shift - 1, 0:rows, :] = d_conv * mask_ref[:, shift : shift + 1]
        moved = shifts[shift - 1, shift : shift + rows, :]
        add_row(4 + shift, moved * branch)
        back = back + chan_ref[shift : shift + 1, :] * moved
    back_ref[:, 0:chans] = back.astype(BF16)
    back_ref[:, chans:] = pre_grad_ref[...]

    @pl.when(spot == 0)
    def _():
        tail_ref[...] = back[rows - 8 :, :]

    @pl.when(spot == last)
    def _():
        halo = halo_ref[...].astype(F32)
        head = jnp.zeros((8, chans), F32)
        edge[0:8, :] = head
        for shift in range(1, width):
            edge[8:16, :] = shifts[shift - 1, 0:8, :]
            moved = edge[shift : shift + 8, :]
            add_row(4 + shift, moved * halo)
            head = head + chan_ref[shift : shift + 1, :] * moved
        head_ref[...] = head


def recur_backward(grad, run, enter, rate, entry, conv, state, masks, branch, pre_grad, halo, channels, gates):
    rows, chans = rate.shape
    count = rows // TILE
    edge = jax.ShapeDtypeStruct((8, chans), F32)
    wide = tile_spec(chans, count)
    return pl.pallas_call(
        backward_kernel,
        grid=(count,),
        out_shape=(
            jax.ShapeDtypeStruct((rows, 2 * chans), BF16),
            edge,
            edge,
            jax.ShapeDtypeStruct((chans, 2 * chans), F32),
            jax.ShapeDtypeStruct((8, chans), F32),
        ),
        in_specs=[
            wide, wide, fixed_spec((1, chans)), wide, wide, wide, wide,
            tile_spec(masks.shape[1], count),
            wide,
            wide,
            fixed_spec((8, chans)),
            fixed_spec(channels.shape),
            fixed_spec(gates.shape),
        ],
        out_specs=[
            tile_spec(2 * chans, count),
            fixed_spec((8, chans)),
            fixed_spec((8, chans)),
            fixed_spec((chans, 2 * chans)),
            fixed_spec((8, chans)),
        ],
        scratch_shapes=[
            pltpu.VMEM((masks.shape[1] - 1, TILE + 8, chans), F32),
            pltpu.VMEM((16, chans), F32),
        ],
        cost_estimate=pl.CostEstimate(
            flops=8 * rows * chans * chans, bytes_accessed=28 * rows * chans, transcendentals=2 * rows * chans
        ),
        name="recur_backward",
    )(grad, run, enter, rate, entry, conv, state, masks, branch, pre_grad, halo, channels, gates)


def shards(
    tokens,
    segments,
    cotangent,
    w_recur,
    w_gelu,
    w_merge,
    w_gate,
    w_up,
    w_down,
    norm_mix,
    norm_feed,
    conv_taps,
    conv_bias,
    rate_gate,
    entry_gate,
    rate_bias,
    entry_bias,
    decay_logit,
):
    piece = tokens.shape[0]
    width = conv_taps.shape[0]
    edge = width - 1
    heads, block = rate_gate.shape[0], rate_gate.shape[1]
    chans = conv_taps.shape[1]
    features = tokens.shape[1]
    feat_local = features // lax.axis_size("tp")
    feat_start = lax.axis_index("tp") * feat_local

    def own(block):
        return lax.dynamic_slice_in_dim(block, feat_start, feat_local, 1)

    square = lax.axis_size("fsdp") == 4
    gain_shard = jnp.concatenate(
        [jnp.stack([norm_mix, norm_feed]).astype(F32), jnp.zeros((6, norm_mix.shape[0]), F32)], axis=0
    )
    if square:
        half = w_merge.shape[1] // 2
        half_shard = lax.dynamic_slice_in_dim(w_merge, lax.axis_index("ctx") * half, half, 1)
        normed, normed_split, cotangent_split, gains, whole_in = enter(
            tokens, cotangent, gain_shard, w_recur, w_gelu
        )
        merge_mine = lax.all_gather(after(half_shard, normed), "fsdp", axis=0)
    else:
        whole_in = gather_halves(jnp.concatenate([w_recur, w_gelu], axis=1), 0)
        whole_merge = gather_halves(w_merge, 1)
        gains = lax.all_gather(gain_shard, "fsdp", axis=1, tiled=True)
        inputs = tokens.astype(F32)
        normed = (inputs * rms_scale(inputs) * gains[0:1]).astype(BF16)
        normed_split = split_features(normed)
        cotangent_split = split_features(cotangent)
    gain_one = gains[0:1]

    padded_ids = jnp.concatenate([jnp.full((edge,), -1, jnp.int32), segments])
    local_ids = lax.dynamic_slice_in_dim(padded_ids, lax.axis_index("ctx") * piece, piece + edge)
    own_ids = local_ids[edge:]
    masks = jnp.stack(
        [(local_ids[edge - max(shift, 1) : edge - max(shift, 1) + piece] == own_ids) for shift in range(width)],
        axis=1,
    ).astype(F32)
    blocks = jnp.stack([rate_gate.reshape(chans, block), entry_gate.reshape(chans, block)])
    channels = jnp.concatenate(
        [conv_taps.astype(F32)]
        + [row.astype(F32)[None, :] for row in (conv_bias, rate_bias, entry_bias, jax.nn.softplus(-decay_logit))]
    )

    rows_to_features = (((1,), (1,)), ((), ()))
    branches = jnp.dot(normed, whole_in, preferred_element_type=F32).astype(BF16)
    halo = shifted(branches[piece - 8 :, :chans], "ctx", 1)
    conv, rate, entry, local_state, run, gates = recur_forward(branches, halo, masks, channels, blocks)
    state_in = shifted(local_state[piece - 8 :], "ctx", 1)[7:8]
    merge_weights = (merge_mine, swap_cores(after(merge_mine, conv))) if square else (whole_merge,)
    states, gated, part_merge, whole_merge = merge_states(
        local_state, run, state_in, branches, merge_weights, features
    )

    if square:
        merged, normed_two, normed_two_split, whole_mid, whole_down = middle(
            part_merge, tokens, gains, (w_gate, w_up, w_down)
        )
    else:
        merged, normed_two = middle(part_merge, tokens, gains, ())
        normed_two_split = split_features(normed_two)
        whole_mid = gather_halves(jnp.concatenate([w_gate, w_up], axis=1), 0)
        whole_down = gather_halves(w_down, 1)

    units = w_gate.shape[1]
    pre_mid = jnp.dot(normed_two, whole_mid, preferred_element_type=F32).astype(BF16)
    gate_act = gelu_pair(pre_mid[:, :units].astype(F32))[0]
    hidden = (gate_act * pre_mid[:, units:].astype(F32)).astype(BF16)
    part_feed = jnp.dot(hidden, whole_down, preferred_element_type=F32).astype(BF16)
    feed = lax.psum_scatter(part_feed, "tp", scatter_dimension=1, tiled=True)
    hidden, pre_mid, whole_mid, late_cotangent, normed_two_split = after(
        (hidden, pre_mid, whole_mid, cotangent, normed_two_split), part_feed
    )
    d_hidden = lax.dot_general(late_cotangent, whole_down, rows_to_features, preferred_element_type=F32).astype(BF16)
    gate_act, gate_slope = gelu_pair(pre_mid[:, :units].astype(F32))
    up_vals = pre_mid[:, units:].astype(F32)
    wide_hidden = d_hidden.astype(F32)
    d_mid = jnp.concatenate(
        [(wide_hidden * up_vals * gate_slope).astype(BF16), (wide_hidden * gate_act).astype(BF16)], axis=1
    )
    part_two = lax.dot_general(d_mid, whole_mid, rows_to_features, preferred_element_type=F32).astype(BF16)
    pair_down = pair_sums(cotangent_split, hidden, 1)
    pair_mid = pair_sums(normed_two_split, d_mid, 0, part_two)
    part_two = after(part_two, pair_down, pair_mid)
    turned = turn(part_two, tokens, merged, cotangent, gains, square)
    own_resid_grad, d_merge_in, feed_sums = turned[:3]
    d_merge_split = turned[3] if square else split_features(d_merge_in)
    half_down = half_to_owners(pair_down, 1)
    half_mid = half_to_owners(pair_mid, 0)
    d_merge_in = after(d_merge_in, half_down, feed)

    shard_down = both_halves(half_down, 1)
    pair_merge = pair_sums(d_merge_split, gated, 1)
    half_merge = half_to_owners(pair_merge, 1)
    d_gated = lax.dot_general(d_merge_in, whole_merge, rows_to_features, preferred_element_type=F32)
    local_grad, grad_run, first, d_gelu_pre = recur_adjoint(rate, d_gated, branches, states, masks, channels)
    grad_in = shifted(first, "ctx", -1)[0:1]
    back, tail, head, gate_grads, sums = recur_backward(
        local_grad, grad_run, grad_in, rate, after(entry, half_mid, shard_down, pair_merge), conv, states, masks, branches, d_gelu_pre,
        halo, channels, gates
    )
    returned = shifted(head, "ctx", -1)
    d_in = lax.dynamic_update_slice(back, (tail + returned).astype(BF16), (piece - 8, 0))
    part_one = lax.dot_general(d_in, whole_in, rows_to_features, preferred_element_type=F32).astype(BF16)
    part_one = after(part_one, half_merge)
    d_normed = lax.psum_scatter(part_one, "tp", scatter_dimension=1, tiled=True)

    output = (own(tokens).astype(F32) + own(merged).astype(F32) + after(feed, part_one).astype(F32)).astype(BF16)
    pair_in = after(pair_sums(normed_split, after(d_in, part_one), 0), output)
    inputs = tokens.astype(F32)
    scale_one = rms_scale(inputs)
    wide_part = part_one.astype(F32)
    stat_one = jnp.sum(wide_part * inputs * gain_one, axis=-1)
    grad_mix = jnp.sum(wide_part * inputs * scale_one, axis=0)
    norm_sums = jnp.stack([grad_mix, feed_sums[0] / lax.axis_size("tp")])
    spread = jnp.arange(2 * chans)[None, :] % chans // block
    diagonal = sum(jnp.where(spread == i, gate_grads[i * block : (i + 1) * block], 0.0) for i in range(heads))
    diagonal = diagonal.astype(BF16)
    if square:
        own_in, gate_sums, row_sums, both_norms, line_stats = leave(
            pair_in, diagonal, sums, norm_sums.reshape(-1, 128), stat_one.reshape(-1, 128)
        )
        shard_in = own_in.astype(F32)
        both_norms = both_norms.reshape(2, features)
        stat_one = line_stats.reshape(-1)
    else:
        shard_in = both_halves(half_to_owners(pair_in, 0), 0)
        gate_sums = lax.psum(diagonal, ("fsdp", "ctx"))
        row_sums = lax.psum(sums, ("fsdp", "ctx"))
        both_norms = lax.psum(norm_sums, ("fsdp", "ctx", "tp"))
        stat_one = lax.psum(stat_one, "tp")
    stat_one = stat_one[:, None] / features
    shard_mid = both_halves(half_mid, 0)
    shard_merge = both_halves(half_merge, 1)
    gate_sums = gate_sums.astype(F32).reshape(block, 2, heads, block).transpose(1, 2, 0, 3)

    own_inputs = own(tokens).astype(F32)
    grad_tokens = (
        own_resid_grad
        + scale_one * d_normed.astype(F32) * own(gain_one)
        - own_inputs * scale_one**3 * stat_one
    ).astype(BF16)

    norm_local = norm_mix.shape[0]
    own_norms = lax.dynamic_slice_in_dim(both_norms, lax.axis_index("fsdp") * norm_local, norm_local, 1)

    return (
        output,
        grad_tokens,
        shard_in[:, :chans],
        shard_in[:, chans:],
        shard_merge,
        shard_mid[:, :units],
        shard_mid[:, units:],
        shard_down,
        own_norms[0],
        own_norms[1],
        row_sums[4 : 4 + width],
        row_sums[3],
        gate_sums[0],
        gate_sums[1],
        row_sums[1],
        row_sums[2],
        CGAIN * row_sums[0] * jax.nn.sigmoid(-decay_logit),
    )


def solution(mesh):
    placed = (
        P(("fsdp", "ctx"), None),
        P("fsdp"),
        P(("fsdp", "ctx"), None),
        P("fsdp", "tp"),
        P("fsdp", "tp"),
        P("tp", "fsdp"),
        P("fsdp", "tp"),
        P("fsdp", "tp"),
        P("tp", "fsdp"),
        P("fsdp"),
        P("fsdp"),
        P(None, "tp"),
        P("tp"),
        P("tp", None, None),
        P("tp", None, None),
        P("tp"),
        P("tp"),
        P("tp"),
    )
    return jax.shard_map(
        shards,
        mesh=mesh,
        in_specs=placed,
        out_specs=(
            P(("fsdp", "ctx"), "tp"),
            P(("fsdp", "ctx"), "tp"),
            P("fsdp", "tp"),
            P("fsdp", "tp"),
            P("tp", "fsdp"),
            P("fsdp", "tp"),
            P("fsdp", "tp"),
            P("tp", "fsdp"),
            P("fsdp"),
            P("fsdp"),
            P(None, "tp"),
            P("tp"),
            P("tp", None, None),
            P("tp", None, None),
            P("tp"),
            P("tp"),
            P("tp"),
        ),
        check_vma=False,
    )
```

```python
import jax
import jax.numpy as jnp
from jax import lax
from jax.experimental import pallas as pl
from jax.experimental.pallas import tpu as pltpu
from jax.sharding import PartitionSpec as P

EPS = 1e-06
CGAIN = 8.0
ROOT = 0.7978845608
CUBE = 0.044715
TILE = 128
SEGS = 8
F32 = jnp.float32
BF16 = jnp.bfloat16


def swap_cores(block):
    size = lax.axis_size("ctx")
    return lax.ppermute(block, "ctx", [(i, size - 1 - i) for i in range(size)])


def shifted(block, axis, distance):
    devices = range(lax.axis_size(axis))
    route = [(i - distance, i) for i in devices if i - distance in devices]
    return lax.ppermute(block, axis, route)


def gather_halves(shard, dim):
    half = shard.shape[dim] // 2
    core = lax.axis_index("ctx")
    mine = lax.dynamic_slice_in_dim(shard, core * half, half, dim)
    mine = lax.all_gather(mine, "fsdp", axis=dim)
    other = swap_cores(mine)
    first = jnp.where(core == 0, mine, other)
    second = jnp.where(core == 0, other, mine)
    both = jnp.stack([first, second], axis=dim + 1)
    return both.reshape(shard.shape[:dim] + (-1,) + shard.shape[dim + 1 :])


def split_features(block):
    shards = lax.axis_size("fsdp")
    core = lax.axis_index("ctx")
    parts = block.reshape(block.shape[0], shards, 2, -1)
    return [
        lax.dynamic_index_in_dim(parts, index, 2, False).reshape(block.shape[0], -1)
        for index in (core, 1 - core)
    ]


def pair_sums(left, right, dim, behind=None):
    rows_to_rows = (((0,), (0,)), ((), ()))

    def product(index):
        pair = (left[index], right) if dim == 0 else (right, left[index])
        return lax.dot_general(*pair, rows_to_rows, preferred_element_type=F32)

    arrived = swap_cores(product(1).astype(BF16))
    if behind is not None:
        arrived, left = after((arrived, left), behind)
    return (product(0) + arrived.astype(F32)).astype(BF16)


def half_to_owners(mine, dim):
    return lax.psum_scatter(mine, "fsdp", scatter_dimension=dim, tiled=True)


def both_halves(total, dim):
    other = swap_cores(total)
    core = lax.axis_index("ctx")
    if dim == 0:
        place = lax.broadcasted_iota(jnp.int32, (2, *total.shape), 0)
        both = jnp.where(place == core, total[None], other[None])
        return both.reshape(2 * total.shape[0], total.shape[1])
    first = jnp.where(core == 0, total, other)
    second = jnp.where(core == 0, other, total)
    return jnp.concatenate([first, second], axis=dim).astype(F32)


def after(value, *others):
    return lax.optimization_barrier((value, *others))[0]


class Square:
    def __init__(self):
        me = lax.axis_index("fsdp")
        row, col = me // 2, me % 2
        self.me = me
        self.core = lax.axis_index("ctx")
        self.near = (row * 2 + 1 - col, (1 - row) * 2 + col)
        self.far = (1 - row) * 2 + 1 - col


def remote(source, target, send, arrive, **device):
    return pltpu.make_async_remote_copy(
        source, target, send, arrive, device_id=device, device_id_type=pl.DeviceIdType.MESH
    )


class Gather:
    def __init__(self, items, stages, send, arrive, local):
        self.items, self.stages = items, stages
        self.send, self.arrive, self.local = send, arrive, local
        self.square = Square()

    def piece(self, w, owner, low, size):
        shard, whole, dim, offset = self.items[w]
        low = pl.multiple_of(owner * shard.shape[dim] + low, 128)
        if dim == 0:
            return whole.at[pl.ds(low, size), pl.ds(offset, shard.shape[1])]
        return whole.at[:, pl.ds(low, size)]

    def copy(self, w, k):
        shard, _, dim, _ = self.items[w]
        square = self.square
        half = shard.shape[dim] // 2
        low = pl.multiple_of(square.core * half, 128)
        first, second = square.near
        if k < 2:
            source = shard.at[pl.ds(low, half), :] if dim == 0 else shard.at[:, pl.ds(low, half)]
            target = self.piece(w, square.me, low, half)
            device = {"fsdp": square.near[k]}
        elif k < 4:
            source = target = self.piece(w, square.near[k - 2], low + (k - 2) * (half // 2), half // 2)
            device = {"fsdp": square.near[3 - k]}
        else:
            source = target = self.piece(w, (first, second, square.far)[k - 4], low, half)
            device = {"ctx": 1 - square.core}
        return remote(source, target, self.send.at[w, k], self.arrive.at[w, k], **device)

    def stage(self, w, out):
        shard = self.items[w][0]
        if out:
            target = self.piece(w, self.square.me, 0, shard.shape[self.items[w][2]])
            return pltpu.make_async_copy(self.stages[w], target, self.local.at[w, 1])
        return pltpu.make_async_copy(shard, self.stages[w], self.local.at[w, 0])

    def start(self, w):
        self.copy(w, 0).start()
        self.copy(w, 1).start()
        self.stage(w, False).start()

    def forward(self, w):
        self.copy(w, 0).wait_recv()
        self.copy(w, 2).start()
        self.copy(w, 1).wait_recv()
        self.copy(w, 3).start()
        self.copy(w, 4).start()
        self.copy(w, 5).start()
        self.stage(w, False).wait()
        self.stage(w, True).start()

    def hand_over(self, w):
        self.copy(w, 2).wait_recv()
        self.copy(w, 3).wait_recv()
        self.copy(w, 6).start()

    def finish(self, w):
        for k in (4, 5, 6):
            self.copy(w, k).wait_recv()
        for k in range(7):
            self.copy(w, k).wait_send()
        self.stage(w, True).wait()


def greet(line, square, whole_line=False):
    barrier = pltpu.get_barrier_semaphore()

    def call(**device):
        pl.semaphore_signal(barrier, inc=1, device_id=device, device_id_type=pl.DeviceIdType.MESH)

    peers = 0
    if line:
        count, me = lax.axis_size("tp"), lax.axis_index("tp")

        @pl.when(me > 0)
        def _():
            call(tp=me - 1)

        @pl.when(me < count - 1)
        def _():
            call(tp=me + 1)

        peers = jnp.where((me > 0) & (me < count - 1), 2, 1)
    if whole_line:
        count, me = lax.axis_size("tp"), lax.axis_index("tp")
        for other in range(count):
            @pl.when(me != other)
            def _():
                call(tp=other)

        peers = peers + (count - 1)
    if square:
        place = Square()
        call(fsdp=place.near[0])
        call(fsdp=place.near[1])
        call(fsdp=place.far)
        call(ctx=1 - place.core)
        peers = peers + 4
    pl.semaphore_wait(barrier, peers)


def line_sum(part, whole, inbox, sems, finish, between):
    count, me = lax.axis_size("tp"), lax.axis_index("tp")
    half = part.shape[0] // 2
    chunks = inbox.shape[1]
    rows = half // chunks
    sum_send, sum_arrive, share_send, share_arrive = sems

    def spot(side, c):
        return pl.ds(pl.multiple_of(side * half + c * rows, rows), rows)

    def place(side):
        return count - 1 - me if side else me

    def onward(side, c, source):
        target = me - 1 if side else me + 1
        return remote(source, inbox.at[side, c], sum_send.at[side, c], sum_arrive.at[side, c], tp=target)

    def share(side, c):
        target = me + 1 if side else me - 1
        block = whole.at[spot(side, c), :]
        return remote(block, block, share_send.at[side, c], share_arrive.at[side, c], tp=target)

    for side in (0, 1):
        @pl.when(place(side) == 0)
        def _():
            onward(side, 0, part.at[spot(side, 0), :]).start()

    def step(t, carry):
        for side in (0, 1):
            here = place(side)
            c = t - here

            @pl.when((here == 0) & (t + 1 < chunks))
            def _():
                onward(side, t + 1, part.at[spot(side, t + 1), :]).start()

            @pl.when((c >= 0) & (c < chunks) & (here > 0))
            def _():
                onward(side, c, inbox.at[side, c]).wait_recv()
                total = (inbox[side, c].astype(F32) + part[spot(side, c), :].astype(F32)).astype(BF16)

                @pl.when(here < count - 1)
                def _():
                    inbox[side, c] = total
                    onward(side, c, inbox.at[side, c]).start()

                @pl.when(here == count - 1)
                def _():
                    whole[spot(side, c), :] = total
                    share(side, c).start()
                    finish(spot(side, c))

        for side in (0, 1):
            here = place(side)
            c = t - 2 * (count - 1) + here

            @pl.when((c >= 0) & (c < chunks) & (here < count - 1))
            def _():
                share(side, c).wait_recv()

                @pl.when(here > 0)
                def _():
                    share(side, c).start()

                finish(spot(side, c))

        between(t)
        return carry

    lax.fori_loop(0, chunks + 2 * (count - 1), step, 0)

    def drain(c, carry):
        for side in (0, 1):
            here = place(side)

            @pl.when(here < count - 1)
            def _():
                onward(side, c, inbox.at[side, c]).wait_send()

            @pl.when(here > 0)
            def _():
                share(side, c).wait_send()

        return carry

    lax.fori_loop(0, chunks, drain, 0)


def put_split(ref, rows, block):
    core = lax.axis_index("ctx")
    size = block.shape[1] // 8
    for owner in range(4):
        for index in range(2):
            low = (2 * owner + index) * size
            ref[(index + core) % 2, rows, owner * size : (owner + 1) * size] = block[:, low : low + size]


CHUNK = 32
LANES = 128
LINE_COST = pl.CostEstimate(flops=0, bytes_accessed=400_000_000, transcendentals=0)


def enter_kernel(
    tokens, upstream, gain_shard, recur, gelu,
    normed, halves, upstream_halves, gains, scales, whole_in,
    stage_recur, stage_gelu, send, arrive, local, gain_send, gain_arrive,
):
    square = Square()
    greet(False, True)
    width = gain_shard.shape[1]

    def gain_copy(k, owner, target):
        spot = gains.at[:, pl.ds(pl.multiple_of(owner * width, 128), width)]
        return remote(gain_shard, spot, gain_send.at[k], gain_arrive.at[k], fsdp=target)

    others = (*square.near, square.far)
    for k, target in enumerate(others):
        gain_copy(k, square.me, target).start()
    gather = Gather(
        [(recur, whole_in, 0, 0), (gelu, whole_in, 0, recur.shape[1])],
        (stage_recur, stage_gelu), send, arrive, local,
    )
    for w in range(2):
        gather.start(w)
    gains[:, pl.ds(pl.multiple_of(square.me * width, 128), width)] = gain_shard[...]
    for k, owner in enumerate(others):
        gain_copy(k, owner, owner).wait_recv()

    def norm(t, carry):
        rows = pl.ds(pl.multiple_of(t * CHUNK, CHUNK), CHUNK)
        block = tokens[rows, :].astype(F32)
        scale = rms_scale(block)
        scales[rows, :] = jnp.broadcast_to(scale, (CHUNK, LANES))
        block = (block * scale * gains[0:1, :]).astype(BF16)
        normed[rows, :] = block
        put_split(halves, rows, block)
        put_split(upstream_halves, rows, upstream[rows, :])
        return carry

    lax.fori_loop(0, tokens.shape[0] // CHUNK, norm, 0)
    for w in range(2):
        gather.forward(w)
    for w in range(2):
        gather.hand_over(w)
    for w in range(2):
        gather.finish(w)
    for k, target in enumerate(others):
        gain_copy(k, square.me, target).wait_send()


ANY = pl.BlockSpec(memory_space=pl.ANY)
NEAR = pl.BlockSpec(memory_space=pltpu.VMEM)


def gather_scratch(shards):
    count = len(shards)
    dma = pltpu.SemaphoreType.DMA
    return [pltpu.VMEM(w.shape, w.dtype) for w in shards] + [dma((count, 7)), dma((count, 7)), dma((count, 2))]


def enter(tokens, upstream, gain_shard, recur, gelu):
    rows, features = tokens.shape
    shape = jax.ShapeDtypeStruct
    inner = recur.shape[1]
    dma = pltpu.SemaphoreType.DMA
    return pl.pallas_call(
        enter_kernel,
        out_shape=(
            shape((rows, features), BF16),
            shape((2, rows, features // 2), BF16),
            shape((2, rows, features // 2), BF16),
            shape((8, features), F32),
            shape((rows, LANES), F32),
            shape((features, 2 * inner), BF16),
        ),
        in_specs=[NEAR, NEAR, NEAR, ANY, ANY],
        out_specs=[NEAR, NEAR, NEAR, NEAR, NEAR, ANY],
        scratch_shapes=gather_scratch([recur, gelu]) + [dma((3,)), dma((3,))],
        compiler_params=pltpu.CompilerParams(collective_id=1, has_side_effects=True),
        name="enter",
    )(tokens, upstream, gain_shard, recur, gelu)


def line_scratch(rows, features):
    chunks = rows // 2 // CHUNK
    dma = pltpu.SemaphoreType.DMA((2, chunks))
    return [pltpu.VMEM((2, chunks, CHUNK, features), BF16), dma, dma, dma, dma]


class Fetch:
    def __init__(self, sources, targets, sems):
        self.copies = [pltpu.make_async_copy(a, b, sems.at[k]) for k, (a, b) in enumerate(zip(sources, targets))]

    def start(self):
        for copy in self.copies:
            copy.start()

    def wait(self):
        for copy in self.copies:
            copy.wait()


def middle_kernel(gathers, part, far_tokens, gains, *refs):
    *refs, tokens, fetch_sems = refs
    fetch = Fetch((far_tokens,), (tokens,), fetch_sems)
    fetch.start()
    if gathers:
        gate, up, down, merged, normed, halves, whole_in, whole_down = refs[:8]
        inbox, *rest = refs[8:]
        sems, (stage_gate, stage_up, stage_down, send, arrive, local) = rest[:4], rest[4:]
        gather = Gather(
            [(gate, whole_in, 0, 0), (up, whole_in, 0, gate.shape[1]), (down, whole_down, 1, 0)],
            (stage_gate, stage_up, stage_down), send, arrive, local,
        )
        greet(True, True)
        for w in range(3):
            gather.start(w)
    else:
        merged, normed, inbox, *sems = refs
        greet(True, False)

    def finish(rows):
        block = tokens[rows, :].astype(F32) + merged[rows, :].astype(F32)
        block = (block * rms_scale(block) * gains[1:2, :]).astype(BF16)
        normed[rows, :] = block
        if gathers:
            put_split(halves, rows, block)

    def between(t):
        @pl.when(t == 0)
        def _():
            fetch.wait()

        if gathers:
            for w in range(3):
                @pl.when(t == 5 + 4 * w)
                def _():
                    gather.forward(w)

                @pl.when(t == 17 + w)
                def _():
                    gather.hand_over(w)

    line_sum(part, merged, inbox, sems, finish, between)
    if gathers:
        for w in range(3):
            gather.finish(w)


def middle(part, tokens, gains, shards):
    rows, features = tokens.shape
    shape = jax.ShapeDtypeStruct
    whole = shape((rows, features), BF16)
    outs, specs = [whole, whole], [NEAR, NEAR]
    scratch = line_scratch(rows, features)
    if shards:
        gate, up, down = shards
        outs += [
            shape((2, rows, features // 2), BF16),
            shape((features, 2 * gate.shape[1]), BF16),
            shape((down.shape[0], features), BF16),
        ]
        specs += [NEAR, ANY, ANY]
        scratch += gather_scratch(shards)
    scratch += [pltpu.VMEM((rows, features), BF16), pltpu.SemaphoreType.DMA((1,))]
    return pl.pallas_call(
        lambda *refs: middle_kernel(bool(shards), *refs),
        out_shape=tuple(outs),
        in_specs=[NEAR, ANY, NEAR] + [ANY] * len(shards),
        out_specs=specs,
        scratch_shapes=scratch,
        compiler_params=pltpu.CompilerParams(collective_id=2, has_side_effects=True),
        cost_estimate=LINE_COST,
        name="middle",
    )(part, tokens, gains, *shards)


def turn_kernel(split, part, far_tokens, far_merged, far_upstream, gains, own, grad_in, gain_sum, *refs):
    if split:
        halves, *refs = refs
    whole, wide, tokens, merged, upstream, fetch_sems, inbox, *sems = refs
    fetch = Fetch((far_tokens, far_merged, far_upstream), (tokens, merged, upstream), fetch_sems)
    fetch.start()
    greet(True, False)
    gain_sum[...] = jnp.zeros_like(gain_sum)
    width = own.shape[1]
    start = pl.multiple_of(lax.axis_index("tp") * width, 128)

    def finish(rows):
        block = tokens[rows, :].astype(F32) + merged[rows, :].astype(F32)
        scale = rms_scale(block)
        grad = whole[rows, :].astype(F32)
        gain_sum[0:1, :] += jnp.sum(grad * (block * scale), axis=0, keepdims=True)
        grad = grad * gains[1:2, :]
        mean = jnp.mean(block * grad, axis=-1, keepdims=True)
        grad = upstream[rows, :].astype(F32) + scale * grad - block * (scale * scale * scale * mean)
        wide[...] = grad
        own[rows, :] = wide[:, pl.ds(start, width)]
        grad = grad.astype(BF16)
        grad_in[rows, :] = grad
        if split:
            put_split(halves, rows, grad)

    def between(t):
        @pl.when(t == 0)
        def _():
            fetch.wait()

    line_sum(part, whole, inbox, sems, finish, between)


def turn(part, tokens, merged, upstream, gains, split):
    rows, features = tokens.shape
    shape = jax.ShapeDtypeStruct
    outs = [
        shape((rows, features // lax.axis_size("tp")), F32),
        shape((rows, features), BF16),
        shape((8, features), F32),
    ]
    if split:
        outs.append(shape((2, rows, features // 2), BF16))
    return pl.pallas_call(
        lambda *refs: turn_kernel(split, *refs),
        out_shape=tuple(outs),
        in_specs=[NEAR, ANY, ANY, ANY, NEAR],
        out_specs=[NEAR] * len(outs),
        scratch_shapes=[pltpu.VMEM((rows, features), BF16), pltpu.VMEM((CHUNK, features), F32)]
        + [pltpu.VMEM((rows, features), BF16)] * 3
        + [pltpu.SemaphoreType.DMA((3,))]
        + line_scratch(rows, features),
        compiler_params=pltpu.CompilerParams(collective_id=3, has_side_effects=True),
        cost_estimate=LINE_COST,
        name="turn",
    )(part, tokens, merged, upstream, gains)


def rounded_sum(*blocks):
    total = blocks[0].astype(F32)
    for block in blocks[1:]:
        total = total + block.astype(F32)
    return total.astype(BF16)


class Scatter:
    def __init__(self, items, boxes, lasts, send, arrive):
        self.items, self.boxes, self.lasts = items, boxes, lasts
        self.send, self.arrive = send, arrive
        self.square = Square()

    def block(self, w, owner, k):
        part, _, dim = self.items[w]
        size = part.shape[dim] // 4
        if dim == 0:
            low = pl.multiple_of(owner * size + k * (size // 2), 128)
            return part.at[pl.ds(low, size // 2), :]
        half = part.shape[0] // 2
        return part.at[pl.ds(k * half, half), pl.ds(pl.multiple_of(owner * size, 128), size)]

    def spot(self, w, k):
        part, out, dim = self.items[w]
        size = part.shape[dim] // 4
        low = pl.multiple_of(self.square.core * size, 128)
        if dim == 0:
            return out.at[pl.ds(low + k * (size // 2), size // 2), :]
        half = part.shape[0] // 2
        return out.at[pl.ds(k * half, half), pl.ds(low, size)]

    def copy(self, w, k, j):
        square = self.square
        first, second = square.near[k], square.near[1 - k]
        send, arrive = self.send.at[w, 4 * k + j], self.arrive.at[w, 4 * k + j]
        if j < 2:
            owner = square.far if j == 0 else first
            return remote(self.block(w, owner, k), self.boxes[w].at[k, j], send, arrive, fsdp=first)
        if j == 2:
            return remote(self.boxes[w].at[k, 0], self.lasts[w].at[k], send, arrive, fsdp=second)
        return remote(self.spot(w, k), self.spot(w, k), send, arrive, ctx=1 - square.core)

    def start(self, w):
        for j in (0, 1):
            for k in (0, 1):
                self.copy(w, k, j).start()

    def relay(self, w):
        for k in (0, 1):
            self.copy(w, k, 0).wait_recv()
            mine = self.block(w, self.square.near[1 - k], k)
            self.boxes[w][k, 0] = rounded_sum(mine[...], self.boxes[w][k, 0])
            self.copy(w, k, 2).start()

    def finish(self, w):
        for k in (0, 1):
            self.copy(w, k, 1).wait_recv()
            self.copy(w, k, 2).wait_recv()
            mine = self.block(w, self.square.me, k)
            self.spot(w, k)[...] = rounded_sum(mine[...], self.boxes[w][k, 1], self.lasts[w][k])
            self.copy(w, k, 3).start()

    def drain(self, w):
        for k in (0, 1):
            self.copy(w, k, 3).wait_recv()
            for j in range(4):
                self.copy(w, k, j).wait_send()


def scatter_scratch(items):
    blocks = []
    for shape, dim in items:
        rows, cols = (shape[0] // 8, shape[1]) if dim == 0 else (shape[0] // 2, shape[1] // 4)
        blocks.append((rows, cols))
    dma = pltpu.SemaphoreType.DMA((len(items), 8))
    return (
        [pltpu.VMEM((2, 2, *block), BF16) for block in blocks]
        + [pltpu.VMEM((2, *block), BF16) for block in blocks]
        + [dma, dma]
    )


def leave_kernel(
    part_in, gates, sums, norms, stats,
    own_in, gate_sums, row_sums, norm_sums, stat_sums,
    box_in, last_in, send, arrive,
    gate_core, gate_half, gate_near, gate_pair, gate_far, gate_send, gate_arrive,
    core_sums, core_norms, box_sums, box_norms, sum_send, sum_arrive,
    line_norms, line_stats, norm_send, norm_arrive, stat_send, stat_arrive,
):
    square = Square()
    count, place = lax.axis_size("tp"), lax.axis_index("tp")
    core = square.core
    others = (*square.near, square.far)
    greet(False, True, True)

    def norm_copy(k, source):
        box = line_norms.at[source]
        return remote(box, box, norm_send.at[k], norm_arrive.at[source], tp=k)

    def stat_copy(k, source):
        return remote(stats, line_stats.at[source], stat_send.at[k], stat_arrive.at[source], tp=k)

    def core_copy(k):
        source, target = ((sums, core_sums), (norms, core_norms))[k]
        return remote(source, target, sum_send.at[k], sum_arrive.at[k], ctx=1 - core)

    def square_copy(k, j):
        box = (box_sums, box_norms)[k].at[square.me]
        at = 2 + 3 * k + j
        return remote(box, box, sum_send.at[at], sum_arrive.at[at], fsdp=others[j])

    gate_rows = gates.shape[0] // 2
    gate_cols = gates.shape[1] // 2
    my_rows = pl.ds(pl.multiple_of(core * gate_rows, 16), gate_rows)
    your_rows = pl.ds(pl.multiple_of((1 - core) * gate_rows, 16), gate_rows)

    def gate_copy(j):
        send, arrive = gate_send.at[j], gate_arrive.at[j]
        if j == 0:
            return remote(gates.at[your_rows, :], gate_core, send, arrive, ctx=1 - core)
        if j == 5:
            spot = gate_sums.at[my_rows, :]
            return remote(spot, spot, send, arrive, ctx=1 - core)
        k = (j - 1) % 2
        if j < 3:
            return remote(gate_half.at[k], gate_near.at[k], send, arrive, fsdp=square.near[k])
        return remote(gate_pair.at[k], gate_far.at[k], send, arrive, fsdp=square.near[1 - k])

    scatter = Scatter([(part_in, own_in, 0)], (box_in,), (last_in,), send, arrive)
    gate_copy(0).start()
    core_copy(0).start()
    core_copy(1).start()
    scatter.start(0)
    for k in range(count):
        @pl.when(place != k)
        def _():
            stat_copy(k, place).start()

    line_stats[place] = stats[...]
    core_copy(0).wait_recv()
    core_copy(1).wait_recv()
    box_sums[square.me] = sums[...] + core_sums[...]
    box_norms[square.me] = norms[...] + core_norms[...]
    for k in (0, 1):
        for j in range(3):
            square_copy(k, j).start()
    gate_copy(0).wait_recv()
    for k in (0, 1):
        cols = slice(k * gate_cols, (k + 1) * gate_cols)
        gate_half[k] = rounded_sum(gates[my_rows, cols], gate_core[:, cols])
        gate_copy(1 + k).start()
    for k in (0, 1):
        for j in range(3):
            square_copy(k, j).wait_recv()
    row_sums[...] = box_sums[0] + box_sums[1] + box_sums[2] + box_sums[3]
    line_norms[place] = box_norms[0] + box_norms[1] + box_norms[2] + box_norms[3]
    for k in range(count):
        @pl.when(place != k)
        def _():
            norm_copy(k, place).start()

    for k in (0, 1):
        gate_copy(1 + k).wait_recv()
        gate_pair[k] = rounded_sum(gate_half[k], gate_near[k])
        gate_copy(3 + k).start()
    scatter.relay(0)
    for k in (0, 1):
        cols = slice(k * gate_cols, (k + 1) * gate_cols)
        gate_copy(3 + k).wait_recv()
        gate_sums[my_rows, cols] = rounded_sum(gate_pair[k], gate_far[k])
    gate_copy(5).start()
    for k in range(count):
        @pl.when(place != k)
        def _():
            norm_copy(k, k).wait_recv()
            stat_copy(k, k).wait_recv()

    total = line_norms[0]
    stat = line_stats[0]
    for k in range(1, count):
        total = total + line_norms[k]
        stat = stat + line_stats[k]
    norm_sums[...] = total
    stat_sums[...] = stat
    scatter.finish(0)
    scatter.drain(0)
    gate_copy(5).wait_recv()
    for j in range(6):
        gate_copy(j).wait_send()
    for k in (0, 1):
        core_copy(k).wait_send()
        for j in range(3):
            square_copy(k, j).wait_send()
    for k in range(count):
        @pl.when(place != k)
        def _():
            norm_copy(k, place).wait_send()
            stat_copy(k, place).wait_send()


def leave(part_in, gates, sums, norms, stats):
    shape = jax.ShapeDtypeStruct
    count = lax.axis_size("tp")
    dma = pltpu.SemaphoreType.DMA
    height, width = gates.shape[0] // 2, gates.shape[1] // 2
    quarter = pltpu.VMEM((2, height, width), BF16)
    return pl.pallas_call(
        leave_kernel,
        out_shape=(
            shape((part_in.shape[0] // 2, part_in.shape[1]), BF16),
            shape(gates.shape, BF16),
            shape(sums.shape, F32),
            shape(norms.shape, F32),
            shape(stats.shape, F32),
        ),
        in_specs=[NEAR] * 5,
        out_specs=[NEAR] * 5,
        scratch_shapes=(
            scatter_scratch([(part_in.shape, 0)])
            + [pltpu.VMEM((height, 2 * width), BF16), quarter, quarter, quarter, quarter, dma((6,)), dma((6,))]
            + [pltpu.VMEM(sums.shape, F32), pltpu.VMEM(norms.shape, F32)]
            + [pltpu.VMEM((4, *sums.shape), F32), pltpu.VMEM((4, *norms.shape), F32), dma((8,)), dma((8,))]
            + [pltpu.VMEM((count, *norms.shape), F32), pltpu.VMEM((count, *stats.shape), F32)]
            + [dma((count,))] * 4
        ),
        compiler_params=pltpu.CompilerParams(collective_id=4, has_side_effects=True),
        cost_estimate=pl.CostEstimate(flops=0, bytes_accessed=160_000_000, transcendentals=0),
        name="leave",
    )(part_in, gates, sums, norms, stats)


def gelu_pair(q):
    tanh = jnp.tanh(ROOT * (q + CUBE * q * q * q))
    value = 0.5 * q * (1.0 + tanh)
    slope = 0.5 * (1.0 + tanh) + 0.5 * q * (1.0 - tanh * tanh) * ROOT * (1.0 + 3.0 * CUBE * q * q)
    return value, slope


def rms_scale(values):
    return lax.rsqrt(jnp.mean(values * values, axis=-1, keepdims=True) + EPS)


def decay_parts(rate, softer, keep):
    gap = 2.0 * CGAIN * rate * softer
    decay = jnp.exp(-0.5 * gap)
    series = gap * (
        1.0
        - gap / 2.0
        * (1.0 - gap / 3.0 * (1.0 - gap / 4.0 * (1.0 - gap / 5.0 * (1.0 - gap / 6.0 * (1.0 - gap / 7.0)))))
    )
    square = jnp.where(gap < 0.25, series, 1.0 - decay * decay)
    return jnp.where(keep, decay, 0.0), jnp.where(keep, square, 1.0)


def put_lanes(ref, block, rows):
    for lane in range(ref.shape[0]):
        ref[lane, 0:rows, :] = block[:, lane * LANES : (lane + 1) * LANES]


def sweep(decay_ref, value_ref, state_ref, product_ref, out_ref, run_ref, carry_ref, reverse, offset):
    groups, rows, _ = value_ref.shape
    steps = rows // SEGS
    place = lax.broadcasted_iota(jnp.int32, (SEGS, LANES), 0)
    if reverse:
        place = SEGS - 1 - place

    def moved(block, by, fill):
        turned = pltpu.roll(block, SEGS - by if reverse else by, 0)
        return jnp.where(place >= by, turned, fill)

    for lane in range(groups):
        lanes = slice(lane * LANES, (lane + 1) * LANES)
        state = jnp.zeros((SEGS, LANES), F32)
        product = jnp.ones((SEGS, LANES), F32)
        for step in reversed(range(steps)) if reverse else range(steps):
            spot = pl.ds(step, SEGS, stride=steps)
            decay = decay_ref[lane, pl.ds(step + offset, SEGS, stride=steps), :]
            state = decay * state + value_ref[lane, spot, :]
            product = product * decay
            state_ref[lane, spot, :] = state
            product_ref[lane, spot, :] = product
        for by in (1, 2, 4):
            state = state + product * moved(state, by, 0.0)
            product = product * moved(product, by, 1.0)
        carry = carry_ref[0:1, lanes]
        carry_run = carry_ref[8:9, lanes]
        state = state + product * carry
        product = product * carry_run
        enter = moved(state, 1, carry)
        enter_run = moved(product, 1, carry_run)
        for seg in range(SEGS):
            span = slice(seg * steps, (seg + 1) * steps)
            inner = product_ref[lane, span, :]
            out_ref[span, lanes] = state_ref[lane, span, :] + inner * enter[seg : seg + 1, :]
            run_ref[span, lanes] = inner * enter_run[seg : seg + 1, :]
        last = 0 if reverse else SEGS - 1
        carry_ref[0:1, lanes] = state[last : last + 1, :]
        carry_ref[8:9, lanes] = product[last : last + 1, :]


BIAS, RATE, ENTRY, SOFTER = slice(4, 5), slice(5, 6), slice(6, 7), slice(7, 8)


def spread_blocks(blocks_ref, out_ref):
    chans, size = blocks_ref.shape[1:]
    row = lax.broadcasted_iota(jnp.int32, (chans, chans), 0)
    col = lax.broadcasted_iota(jnp.int32, (chans, chans), 1)
    inner = lax.broadcasted_iota(jnp.int32, (size, chans), 0)
    outer = lax.broadcasted_iota(jnp.int32, (size, chans), 1)
    inside = row < 0
    repeat = outer < 0
    for low in range(0, chans, size):
        inside |= (row >= low) & (row < low + size) & (col >= low) & (col < low + size)
        repeat |= outer - low == inner
    repeat = repeat.astype(F32).astype(BF16)
    for gate in range(2):
        wide = jnp.dot(blocks_ref[gate], repeat, preferred_element_type=F32)
        out_ref[:, gate * chans : (gate + 1) * chans] = jnp.where(inside, wide, 0.0).astype(BF16)


def forward_kernel(
    branch_ref, halo_ref, mask_ref, chan_ref, blocks_ref,
    conv_ref, rate_ref, entry_ref, state_ref, run_ref, gates_ref, tail_ref,
    window, decay, value, inner, product, carry,
):
    rows, chans = conv_ref.shape
    spot = pl.program_id(0)

    @pl.when(spot == 0)
    def _():
        spread_blocks(blocks_ref, gates_ref)
        window[0:8, :] = halo_ref[...].astype(F32)
        carry[0:8, :] = jnp.zeros((8, chans), F32)
        carry[8:16, :] = jnp.ones((8, chans), F32)

    @pl.when(spot > 0)
    def _():
        window[0:8, :] = window[rows : rows + 8, :]

    window[8 : rows + 8, :] = branch_ref[...].astype(F32)
    mixed = chan_ref[BIAS, :] + chan_ref[0:1, :] * window[8 : rows + 8, :]
    for shift in range(1, mask_ref.shape[1]):
        moved = window[8 - shift : 8 - shift + rows, :]
        mixed = mixed + chan_ref[shift : shift + 1, :] * (moved * mask_ref[:, shift : shift + 1])
    conv = mixed.astype(BF16)
    conv_ref[...] = conv
    pre = jnp.dot(conv, gates_ref[...], preferred_element_type=F32)
    rate = jax.nn.sigmoid(pre[:, :chans] + chan_ref[RATE, :])
    entry = jax.nn.sigmoid(pre[:, chans:] + chan_ref[ENTRY, :])
    rate_ref[...] = rate
    entry_ref[...] = entry
    keep = jnp.broadcast_to(mask_ref[:, 0:1], (rows, chans)) > 0.5
    step, square = decay_parts(rate, chan_ref[SOFTER, :], keep)
    put_lanes(decay, step, rows)
    put_lanes(value, jnp.sqrt(square) * entry * conv.astype(F32), rows)
    sweep(decay, value, inner, product, state_ref, run_ref, carry, False, 0)
    tail_ref[...] = state_ref[rows - 8 :, :]


def tile_spec(width, count=None):
    if count is None:
        return pl.BlockSpec((TILE, width), lambda i: (i, 0))
    return pl.BlockSpec((TILE, width), lambda i: (count - 1 - i, 0))


def fixed_spec(shape):
    return pl.BlockSpec(shape, lambda i: (0, 0))


def recur_forward(branch, halo, masks, channels, blocks):
    rows, chans = branch.shape[0], halo.shape[1]
    wide = jax.ShapeDtypeStruct((rows, chans), F32)
    return pl.pallas_call(
        forward_kernel,
        grid=(rows // TILE,),
        out_shape=(
            jax.ShapeDtypeStruct((rows, chans), BF16), wide, wide, wide, wide,
            jax.ShapeDtypeStruct((chans, 2 * chans), BF16),
            jax.ShapeDtypeStruct((8, chans), F32),
        ),
        in_specs=[
            tile_spec(chans),
            fixed_spec((8, chans)),
            tile_spec(masks.shape[1]),
            fixed_spec(channels.shape),
            pl.BlockSpec(blocks.shape, lambda i: (0, 0, 0)),
        ],
        out_specs=[tile_spec(chans)] * 5 + [fixed_spec((chans, 2 * chans)), fixed_spec((8, chans))],
        scratch_shapes=[
            pltpu.VMEM((TILE + 8, chans), F32),
            pltpu.VMEM((chans // LANES, TILE, LANES), F32),
            pltpu.VMEM((chans // LANES, TILE, LANES), F32),
            pltpu.VMEM((chans // LANES, TILE, LANES), F32),
            pltpu.VMEM((chans // LANES, TILE, LANES), F32),
            pltpu.VMEM((16, chans), F32),
        ],
        cost_estimate=pl.CostEstimate(
            flops=2 * rows * chans * 2 * chans, bytes_accessed=24 * rows * chans, transcendentals=5 * rows * chans
        ),
        name="recur_forward",
    )(branch, halo, masks, channels, blocks)


def merge_kernel(local_ref, run_ref, enter_ref, pre_ref, *refs):
    *halves, state_ref, gated_ref, part_ref, weight_ref = refs
    core = lax.axis_index("ctx")

    @pl.when(pl.program_id(0) == 0)
    def _():
        if len(halves) == 1:
            weight_ref[...] = halves[0][...]
        else:
            owners, _, size = halves[0].shape
            for owner in range(owners):
                for index, half in ((core, halves[0]), (1 - core, halves[1])):
                    low = pl.multiple_of((2 * owner + index) * size, 128)
                    weight_ref[:, pl.ds(low, size)] = half[owner]

    state = local_ref[...] + run_ref[...] * enter_ref[7:8, :]
    state_ref[...] = state
    pre = pre_ref[...].astype(F32)
    gated = (state * gelu_pair(pre)[0]).astype(BF16)
    gated_ref[...] = gated
    part_ref[...] = jnp.dot(gated, weight_ref[...], preferred_element_type=F32).astype(BF16)


def merge_states(local, run, enter, branches, weights, features):
    rows, chans = local.shape
    shape = jax.ShapeDtypeStruct
    return pl.pallas_call(
        merge_kernel,
        grid=(rows // TILE,),
        out_shape=(
            shape((rows, chans), F32), shape((rows, chans), BF16), shape((rows, features), BF16),
            shape((chans, features), BF16),
        ),
        in_specs=[
            tile_spec(chans), tile_spec(chans), fixed_spec((8, chans)),
            pl.BlockSpec((TILE, chans), lambda i: (i, 1)),
        ]
        + [pl.BlockSpec(w.shape, lambda i, rank=w.ndim: (0,) * rank) for w in weights],
        out_specs=[tile_spec(chans), tile_spec(chans), tile_spec(features), fixed_spec((chans, features))],
        cost_estimate=pl.CostEstimate(
            flops=2 * rows * chans * features, bytes_accessed=16 * rows * chans, transcendentals=rows * chans
        ),
        name="merge_states",
    )(local, run, enter, branches, *weights)


def adjoint_kernel(
    rate_ref, up_ref, pre_ref, state_ref, mask_ref, chan_ref,
    grad_ref, run_ref, head_ref, pre_grad_ref,
    decay, value, inner, product, carry,
):
    rows, chans = rate_ref.shape
    groups = chans // LANES
    spot = pl.program_id(0)

    @pl.when(spot == 0)
    def _():
        for lane in range(groups):
            decay[lane, rows : rows + 8, :] = jnp.ones((8, LANES), F32)
        carry[0:8, :] = jnp.zeros((8, chans), F32)
        carry[8:16, :] = jnp.ones((8, chans), F32)

    @pl.when(spot > 0)
    def _():
        for lane in range(groups):
            decay[lane, rows : rows + 8, :] = decay[lane, 0:8, :]

    keep = jnp.broadcast_to(mask_ref[:, 0:1], (rows, chans)) > 0.5
    gap = CGAIN * rate_ref[...] * chan_ref[SOFTER, :]
    step = jnp.where(keep, jnp.exp(-gap), 0.0)
    put_lanes(decay, step, rows)
    gate, slope = gelu_pair(pre_ref[...].astype(F32))
    up = up_ref[...]
    pre_grad_ref[...] = (up * state_ref[...] * slope).astype(BF16)
    put_lanes(value, up * gate, rows)
    sweep(decay, value, inner, product, grad_ref, run_ref, carry, True, 1)
    head_ref[...] = jnp.broadcast_to(step[0:1, :] * carry[0:1, :], (8, chans))


def recur_adjoint(rate, up, branches, state, masks, channels):
    rows, chans = rate.shape
    count = rows // TILE
    wide = jax.ShapeDtypeStruct((rows, chans), F32)
    return pl.pallas_call(
        adjoint_kernel,
        grid=(count,),
        out_shape=(
            wide, wide, jax.ShapeDtypeStruct((8, chans), F32), jax.ShapeDtypeStruct((rows, chans), BF16)
        ),
        in_specs=[
            tile_spec(chans, count),
            tile_spec(chans, count),
            pl.BlockSpec((TILE, chans), lambda i: (count - 1 - i, 1)),
            tile_spec(chans, count),
            tile_spec(masks.shape[1], count),
            fixed_spec(channels.shape),
        ],
        out_specs=[tile_spec(chans, count), tile_spec(chans, count), fixed_spec((8, chans)), tile_spec(chans, count)],
        scratch_shapes=[
            pltpu.VMEM((chans // LANES, TILE + 8, LANES), F32),
            pltpu.VMEM((chans // LANES, TILE, LANES), F32),
            pltpu.VMEM((chans // LANES, TILE, LANES), F32),
            pltpu.VMEM((chans // LANES, TILE, LANES), F32),
            pltpu.VMEM((16, chans), F32),
        ],
        cost_estimate=pl.CostEstimate(
            flops=8 * rows * chans, bytes_accessed=16 * rows * chans, transcendentals=rows * chans
        ),
        name="recur_adjoint",
    )(rate, up, branches, state, masks, channels)


def backward_kernel(
    grad_ref, run_ref, enter_ref, rate_ref, entry_ref, conv_ref, state_ref, mask_ref,
    branch_ref, pre_grad_ref, halo_ref, chan_ref, gates_ref,
    back_ref, tail_ref, head_ref, gate_grad_ref, sums_ref,
    shifts, edge,
):
    rows, chans = conv_ref.shape
    width = mask_ref.shape[1]
    spot = pl.program_id(0)
    last = pl.num_programs(0) - 1

    @pl.when(spot == 0)
    def _():
        for shift in range(1, width):
            shifts[shift - 1, rows : rows + 8, :] = jnp.zeros((8, chans), F32)
        gate_grad_ref[...] = jnp.zeros_like(gate_grad_ref)
        sums_ref[...] = jnp.zeros_like(sums_ref)

    @pl.when(spot > 0)
    def _():
        for shift in range(1, width):
            shifts[shift - 1, rows : rows + 8, :] = shifts[shift - 1, 0:8, :]

    keep = jnp.broadcast_to(mask_ref[:, 0:1], (rows, chans)) > 0.5
    softer = chan_ref[SOFTER, :]
    rate = rate_ref[...]
    entry = entry_ref[...]
    conv = conv_ref[...].astype(F32)
    grad = grad_ref[...] + run_ref[...] * enter_ref[0:1, :]
    step, square = decay_parts(rate, softer, keep)
    inverse = lax.rsqrt(square)
    mult = square * inverse
    driven = entry * conv
    carried = state_ref[...] - mult * driven
    d_log = jnp.where(keep, grad * (carried - driven * step * step * inverse), 0.0)
    d_rate = (-CGAIN * softer * d_log * rate * (1.0 - rate)).astype(BF16)
    lifted = grad * mult * entry
    d_entry = (lifted * conv * (1.0 - entry)).astype(BF16)
    both = jnp.concatenate([d_rate, d_entry], axis=1)
    d_conv = lifted + lax.dot_general(
        both, gates_ref[...], (((1,), (1,)), ((), ())), preferred_element_type=F32
    )
    gate_grad_ref[...] += lax.dot_general(
        conv_ref[...], both, (((0,), (0,)), ((), ())), preferred_element_type=F32
    )

    def add_row(row, block):
        sums_ref[row : row + 1, :] += jnp.sum(block, axis=0, keepdims=True)

    branch = branch_ref[...].astype(F32)
    add_row(0, d_log * rate)
    add_row(1, d_rate.astype(F32))
    add_row(2, d_entry.astype(F32))
    add_row(3, d_conv)
    add_row(4, d_conv * branch)
    back = chan_ref[0:1, :] * d_conv
    for shift in range(1, width):
        shifts[shift - 1, 0:rows, :] = d_conv * mask_ref[:, shift : shift + 1]
        moved = shifts[shift - 1, shift : shift + rows, :]
        add_row(4 + shift, moved * branch)
        back = back + chan_ref[shift : shift + 1, :] * moved
    back_ref[:, 0:chans] = back.astype(BF16)
    back_ref[:, chans:] = pre_grad_ref[...]

    @pl.when(spot == 0)
    def _():
        tail_ref[...] = back[rows - 8 :, :]

    @pl.when(spot == last)
    def _():
        halo = halo_ref[...].astype(F32)
        head = jnp.zeros((8, chans), F32)
        edge[0:8, :] = head
        for shift in range(1, width):
            edge[8:16, :] = shifts[shift - 1, 0:8, :]
            moved = edge[shift : shift + 8, :]
            add_row(4 + shift, moved * halo)
            head = head + chan_ref[shift : shift + 1, :] * moved
        head_ref[...] = head


def recur_backward(grad, run, enter, rate, entry, conv, state, masks, branch, pre_grad, halo, channels, gates):
    rows, chans = rate.shape
    count = rows // TILE
    edge = jax.ShapeDtypeStruct((8, chans), F32)
    wide = tile_spec(chans, count)
    return pl.pallas_call(
        backward_kernel,
        grid=(count,),
        out_shape=(
            jax.ShapeDtypeStruct((rows, 2 * chans), BF16),
            edge,
            edge,
            jax.ShapeDtypeStruct((chans, 2 * chans), F32),
            jax.ShapeDtypeStruct((8, chans), F32),
        ),
        in_specs=[
            wide, wide, fixed_spec((8, chans)), wide, wide, wide, wide,
            tile_spec(masks.shape[1], count),
            wide,
            wide,
            fixed_spec((8, chans)),
            fixed_spec(channels.shape),
            fixed_spec(gates.shape),
        ],
        out_specs=[
            tile_spec(2 * chans, count),
            fixed_spec((8, chans)),
            fixed_spec((8, chans)),
            fixed_spec((chans, 2 * chans)),
            fixed_spec((8, chans)),
        ],
        scratch_shapes=[
            pltpu.VMEM((masks.shape[1] - 1, TILE + 8, chans), F32),
            pltpu.VMEM((16, chans), F32),
        ],
        cost_estimate=pl.CostEstimate(
            flops=8 * rows * chans * chans, bytes_accessed=28 * rows * chans, transcendentals=2 * rows * chans
        ),
        name="recur_backward",
    )(grad, run, enter, rate, entry, conv, state, masks, branch, pre_grad, halo, channels, gates)


def shards(
    tokens,
    segments,
    cotangent,
    w_recur,
    w_gelu,
    w_merge,
    w_gate,
    w_up,
    w_down,
    norm_mix,
    norm_feed,
    conv_taps,
    conv_bias,
    rate_gate,
    entry_gate,
    rate_bias,
    entry_bias,
    decay_logit,
):
    piece = tokens.shape[0]
    width = conv_taps.shape[0]
    edge = width - 1
    heads, block = rate_gate.shape[0], rate_gate.shape[1]
    chans = conv_taps.shape[1]
    features = tokens.shape[1]
    feat_local = features // lax.axis_size("tp")
    feat_start = lax.axis_index("tp") * feat_local

    def own(block):
        return lax.dynamic_slice_in_dim(block, feat_start, feat_local, 1)

    square = lax.axis_size("fsdp") == 4
    gain_shard = jnp.concatenate(
        [jnp.stack([norm_mix, norm_feed]).astype(F32), jnp.zeros((6, norm_mix.shape[0]), F32)], axis=0
    )
    if square:
        half = w_merge.shape[1] // 2
        half_shard = lax.dynamic_slice_in_dim(w_merge, lax.axis_index("ctx") * half, half, 1)
        normed, normed_split, cotangent_split, gains, scales, whole_in = enter(
            tokens, cotangent, gain_shard, w_recur, w_gelu
        )
        merge_mine = lax.all_gather(after(half_shard, normed), "fsdp", axis=0)
    else:
        whole_in = gather_halves(jnp.concatenate([w_recur, w_gelu], axis=1), 0)
        whole_merge = gather_halves(w_merge, 1)
        gains = lax.all_gather(gain_shard, "fsdp", axis=1, tiled=True)
        inputs = tokens.astype(F32)
        normed = (inputs * rms_scale(inputs) * gains[0:1]).astype(BF16)
        normed_split = split_features(normed)
        cotangent_split = split_features(cotangent)
        scales = rms_scale(inputs)
    gain_one = gains[0:1]

    padded_ids = jnp.concatenate([jnp.full((edge,), -1, jnp.int32), segments])
    local_ids = lax.dynamic_slice_in_dim(padded_ids, lax.axis_index("ctx") * piece, piece + edge)
    own_ids = local_ids[edge:]
    masks = jnp.stack(
        [(local_ids[edge - max(shift, 1) : edge - max(shift, 1) + piece] == own_ids) for shift in range(width)],
        axis=1,
    ).astype(F32)
    blocks = jnp.stack([rate_gate.reshape(chans, block), entry_gate.reshape(chans, block)])
    channels = jnp.concatenate(
        [conv_taps.astype(F32)]
        + [row.astype(F32)[None, :] for row in (conv_bias, rate_bias, entry_bias, jax.nn.softplus(-decay_logit))]
    )

    rows_to_features = (((1,), (1,)), ((), ()))
    branches = jnp.dot(normed, whole_in, preferred_element_type=F32).astype(BF16)
    halo = shifted(branches[piece - 8 :, :chans], "ctx", 1)
    conv, rate, entry, local_state, run, gates, state_tail = recur_forward(branches, halo, masks, channels, blocks)
    state_in = shifted(state_tail, "ctx", 1)
    merge_weights = (merge_mine, swap_cores(after(merge_mine, conv))) if square else (whole_merge,)
    states, gated, part_merge, whole_merge = merge_states(
        local_state, run, state_in, branches, merge_weights, features
    )

    if square:
        merged, normed_two, normed_two_split, whole_mid, whole_down = middle(
            part_merge, tokens, gains, (w_gate, w_up, w_down)
        )
    else:
        merged, normed_two = middle(part_merge, tokens, gains, ())
        normed_two_split = split_features(normed_two)
        whole_mid = gather_halves(jnp.concatenate([w_gate, w_up], axis=1), 0)
        whole_down = gather_halves(w_down, 1)

    units = w_gate.shape[1]
    pre_mid = jnp.dot(normed_two, whole_mid, preferred_element_type=F32).astype(BF16)
    gate_act = gelu_pair(pre_mid[:, :units].astype(F32))[0]
    hidden = (gate_act * pre_mid[:, units:].astype(F32)).astype(BF16)
    part_feed = jnp.dot(hidden, whole_down, preferred_element_type=F32).astype(BF16)
    feed = lax.psum_scatter(part_feed, "tp", scatter_dimension=1, tiled=True)
    hidden, pre_mid, whole_mid, late_cotangent, normed_two_split = after(
        (hidden, pre_mid, whole_mid, cotangent, normed_two_split), part_feed
    )
    d_hidden = lax.dot_general(late_cotangent, whole_down, rows_to_features, preferred_element_type=F32).astype(BF16)
    gate_act, gate_slope = gelu_pair(pre_mid[:, :units].astype(F32))
    up_vals = pre_mid[:, units:].astype(F32)
    wide_hidden = d_hidden.astype(F32)
    d_mid = jnp.concatenate(
        [(wide_hidden * up_vals * gate_slope).astype(BF16), (wide_hidden * gate_act).astype(BF16)], axis=1
    )
    part_two = lax.dot_general(d_mid, whole_mid, rows_to_features, preferred_element_type=F32).astype(BF16)
    pair_down = pair_sums(cotangent_split, hidden, 1)
    pair_mid = pair_sums(normed_two_split, d_mid, 0, part_two)
    part_two = after(part_two, pair_down, pair_mid)
    turned = turn(part_two, tokens, merged, cotangent, gains, square)
    own_resid_grad, d_merge_in, feed_sums = turned[:3]
    d_merge_split = turned[3] if square else split_features(d_merge_in)
    half_down = half_to_owners(pair_down, 1)
    half_mid = half_to_owners(pair_mid, 0)
    d_merge_in, d_merge_split = after((d_merge_in, d_merge_split), feed)

    shard_down = both_halves(half_down, 1)
    pair_merge = pair_sums(d_merge_split, gated, 1)
    half_merge = half_to_owners(pair_merge, 1)
    d_gated = lax.dot_general(d_merge_in, whole_merge, rows_to_features, preferred_element_type=F32)
    local_grad, grad_run, first, d_gelu_pre = recur_adjoint(after(rate, half_down), d_gated, branches, states, masks, channels)
    grad_in = shifted(first, "ctx", -1)
    back, tail, head, gate_grads, sums = recur_backward(
        local_grad, grad_run, grad_in, rate, after(entry, half_mid, shard_down, pair_merge), conv, states, masks, branches, d_gelu_pre,
        halo, channels, gates
    )
    returned = shifted(head, "ctx", -1)
    d_in = lax.dynamic_update_slice(back, (tail + returned).astype(BF16), (piece - 8, 0))
    part_one = lax.dot_general(d_in, whole_in, rows_to_features, preferred_element_type=F32).astype(BF16)
    part_one = after(part_one, half_merge)
    d_normed = lax.psum_scatter(part_one, "tp", scatter_dimension=1, tiled=True)

    pair_in = pair_sums(normed_split, after(d_in, part_one), 0)
    inputs = tokens.astype(F32)
    scale_one = scales[:, :1]
    wide_part = part_one.astype(F32)
    stat_one = jnp.sum(wide_part * inputs * gain_one, axis=-1)
    grad_mix = jnp.sum(wide_part * inputs * scale_one, axis=0)
    norm_sums = jnp.stack([grad_mix, feed_sums[0] / lax.axis_size("tp")])
    spread = jnp.arange(2 * chans)[None, :] % chans // block
    diagonal = sum(jnp.where(spread == i, gate_grads[i * block : (i + 1) * block], 0.0) for i in range(heads))
    diagonal = diagonal.astype(BF16)
    if square:
        own_in, gate_sums, row_sums, both_norms, line_stats = leave(
            pair_in, diagonal, sums, norm_sums.reshape(-1, 128), stat_one.reshape(-1, 128)
        )
        shard_in = own_in
        both_norms = both_norms.reshape(2, features)
        stat_one = line_stats.reshape(-1)
    else:
        shard_in = both_halves(half_to_owners(pair_in, 0), 0)
        gate_sums = lax.psum(diagonal, ("fsdp", "ctx"))
        row_sums = lax.psum(sums, ("fsdp", "ctx"))
        both_norms = lax.psum(norm_sums, ("fsdp", "ctx", "tp"))
        stat_one = lax.psum(stat_one, "tp")
    stat_one = stat_one[:, None] / features
    shard_mid = both_halves(half_mid, 0)
    shard_merge = both_halves(half_merge, 1)
    gate_sums = gate_sums.astype(F32).reshape(block, 2, heads, block).transpose(1, 2, 0, 3)

    own_inputs = own(tokens).astype(F32)
    output = (own_inputs + own(merged).astype(F32) + feed.astype(F32)).astype(BF16)
    grad_tokens = (
        own_resid_grad
        + scale_one * d_normed.astype(F32) * own(gain_one)
        - own_inputs * scale_one**3 * stat_one
    ).astype(BF16)

    norm_local = norm_mix.shape[0]
    own_norms = lax.dynamic_slice_in_dim(both_norms, lax.axis_index("fsdp") * norm_local, norm_local, 1)

    return (
        output,
        grad_tokens,
        shard_in[:, :chans].astype(F32),
        shard_in[:, chans:].astype(F32),
        shard_merge,
        shard_mid[:, :units].astype(F32),
        shard_mid[:, units:].astype(F32),
        shard_down,
        own_norms[0],
        own_norms[1],
        row_sums[4 : 4 + width],
        row_sums[3],
        gate_sums[0],
        gate_sums[1],
        row_sums[1],
        row_sums[2],
        CGAIN * row_sums[0] * jax.nn.sigmoid(-decay_logit),
    )


def solution(mesh):
    placed = (
        P(("fsdp", "ctx"), None),
        P("fsdp"),
        P(("fsdp", "ctx"), None),
        P("fsdp", "tp"),
        P("fsdp", "tp"),
        P("tp", "fsdp"),
        P("fsdp", "tp"),
        P("fsdp", "tp"),
        P("tp", "fsdp"),
        P("fsdp"),
        P("fsdp"),
        P(None, "tp"),
        P("tp"),
        P("tp", None, None),
        P("tp", None, None),
        P("tp"),
        P("tp"),
        P("tp"),
    )
    return jax.shard_map(
        shards,
        mesh=mesh,
        in_specs=placed,
        out_specs=(
            P(("fsdp", "ctx"), "tp"),
            P(("fsdp", "ctx"), "tp"),
            P("fsdp", "tp"),
            P("fsdp", "tp"),
            P("tp", "fsdp"),
            P("fsdp", "tp"),
            P("fsdp", "tp"),
            P("tp", "fsdp"),
            P("fsdp"),
            P("fsdp"),
            P(None, "tp"),
            P("tp"),
            P("tp", None, None),
            P("tp", None, None),
            P("tp"),
            P("tp"),
            P("tp"),
        ),
        check_vma=False,
    )
```

```python
import jax
import jax.numpy as jnp
from jax import lax
from jax.experimental import pallas as pl
from jax.experimental.pallas import tpu as pltpu
from jax.sharding import PartitionSpec as P

EPS = 1e-06
CGAIN = 8.0
ROOT = 0.7978845608
CUBE = 0.044715
TILE = 128
SEGS = 8
F32 = jnp.float32
BF16 = jnp.bfloat16


def swap_cores(block):
    size = lax.axis_size("ctx")
    return lax.ppermute(block, "ctx", [(i, size - 1 - i) for i in range(size)])


def shifted(block, axis, distance):
    devices = range(lax.axis_size(axis))
    route = [(i - distance, i) for i in devices if i - distance in devices]
    return lax.ppermute(block, axis, route)


def gather_halves(shard, dim):
    half = shard.shape[dim] // 2
    core = lax.axis_index("ctx")
    mine = lax.dynamic_slice_in_dim(shard, core * half, half, dim)
    mine = lax.all_gather(mine, "fsdp", axis=dim)
    other = swap_cores(mine)
    first = jnp.where(core == 0, mine, other)
    second = jnp.where(core == 0, other, mine)
    both = jnp.stack([first, second], axis=dim + 1)
    return both.reshape(shard.shape[:dim] + (-1,) + shard.shape[dim + 1 :])


def split_features(block):
    shards = lax.axis_size("fsdp")
    core = lax.axis_index("ctx")
    parts = block.reshape(block.shape[0], shards, 2, -1)
    return [
        lax.dynamic_index_in_dim(parts, index, 2, False).reshape(block.shape[0], -1)
        for index in (core, 1 - core)
    ]


def pair_sums(left, right, dim, behind=None):
    rows_to_rows = (((0,), (0,)), ((), ()))

    def product(index):
        pair = (left[index], right) if dim == 0 else (right, left[index])
        return lax.dot_general(*pair, rows_to_rows, preferred_element_type=F32)

    arrived = swap_cores(product(1).astype(BF16))
    if behind is not None:
        arrived, left = after((arrived, left), behind)
    return (product(0) + arrived.astype(F32)).astype(BF16)


def half_to_owners(mine, dim):
    return lax.psum_scatter(mine, "fsdp", scatter_dimension=dim, tiled=True)


def both_halves(total, dim):
    other = swap_cores(total)
    core = lax.axis_index("ctx")
    if dim == 0:
        place = lax.broadcasted_iota(jnp.int32, (2, *total.shape), 0)
        both = jnp.where(place == core, total[None], other[None])
        return both.reshape(2 * total.shape[0], total.shape[1])
    first = jnp.where(core == 0, total, other)
    second = jnp.where(core == 0, other, total)
    return jnp.concatenate([first, second], axis=dim).astype(F32)


def after(value, *others):
    return lax.optimization_barrier((value, *others))[0]


class Square:
    def __init__(self):
        me = lax.axis_index("fsdp")
        row, col = me // 2, me % 2
        self.me = me
        self.core = lax.axis_index("ctx")
        self.near = (row * 2 + 1 - col, (1 - row) * 2 + col)
        self.far = (1 - row) * 2 + 1 - col


def remote(source, target, send, arrive, **device):
    return pltpu.make_async_remote_copy(
        source, target, send, arrive, device_id=device, device_id_type=pl.DeviceIdType.MESH
    )


class Gather:
    def __init__(self, items, stages, send, arrive, local):
        self.items, self.stages = items, stages
        self.send, self.arrive, self.local = send, arrive, local
        self.square = Square()

    def piece(self, w, owner, low, size):
        shard, whole, dim, offset = self.items[w]
        low = pl.multiple_of(owner * shard.shape[dim] + low, 128)
        if dim == 0:
            return whole.at[pl.ds(low, size), pl.ds(offset, shard.shape[1])]
        return whole.at[:, pl.ds(low, size)]

    def copy(self, w, k):
        shard, _, dim, _ = self.items[w]
        square = self.square
        half = shard.shape[dim] // 2
        low = pl.multiple_of(square.core * half, 128)
        first, second = square.near
        if k < 2:
            source = shard.at[pl.ds(low, half), :] if dim == 0 else shard.at[:, pl.ds(low, half)]
            target = self.piece(w, square.me, low, half)
            device = {"fsdp": square.near[k]}
        elif k < 4:
            source = target = self.piece(w, square.near[k - 2], low + (k - 2) * (half // 2), half // 2)
            device = {"fsdp": square.near[3 - k]}
        else:
            source = target = self.piece(w, (first, second, square.far)[k - 4], low, half)
            device = {"ctx": 1 - square.core}
        return remote(source, target, self.send.at[w, k], self.arrive.at[w, k], **device)

    def stage(self, w, out):
        shard = self.items[w][0]
        if out:
            target = self.piece(w, self.square.me, 0, shard.shape[self.items[w][2]])
            return pltpu.make_async_copy(self.stages[w], target, self.local.at[w, 1])
        return pltpu.make_async_copy(shard, self.stages[w], self.local.at[w, 0])

    def start(self, w):
        self.copy(w, 0).start()
        self.copy(w, 1).start()
        self.stage(w, False).start()

    def forward(self, w):
        self.copy(w, 0).wait_recv()
        self.copy(w, 2).start()
        self.copy(w, 1).wait_recv()
        self.copy(w, 3).start()
        self.copy(w, 4).start()
        self.copy(w, 5).start()
        self.stage(w, False).wait()
        self.stage(w, True).start()

    def hand_over(self, w):
        self.copy(w, 2).wait_recv()
        self.copy(w, 3).wait_recv()
        self.copy(w, 6).start()

    def finish(self, w):
        for k in (4, 5, 6):
            self.copy(w, k).wait_recv()
        for k in range(7):
            self.copy(w, k).wait_send()
        self.stage(w, True).wait()


def greet(line, square, whole_line=False):
    barrier = pltpu.get_barrier_semaphore()

    def call(**device):
        pl.semaphore_signal(barrier, inc=1, device_id=device, device_id_type=pl.DeviceIdType.MESH)

    peers = 0
    if line:
        count, me = lax.axis_size("tp"), lax.axis_index("tp")

        @pl.when(me > 0)
        def _():
            call(tp=me - 1)

        @pl.when(me < count - 1)
        def _():
            call(tp=me + 1)

        peers = jnp.where((me > 0) & (me < count - 1), 2, 1)
    if whole_line:
        count, me = lax.axis_size("tp"), lax.axis_index("tp")
        for other in range(count):
            @pl.when(me != other)
            def _():
                call(tp=other)

        peers = peers + (count - 1)
    if square:
        place = Square()
        call(fsdp=place.near[0])
        call(fsdp=place.near[1])
        call(fsdp=place.far)
        call(ctx=1 - place.core)
        peers = peers + 4
    pl.semaphore_wait(barrier, peers)


def line_sum(part, whole, inbox, sems, finish, between):
    count, me = lax.axis_size("tp"), lax.axis_index("tp")
    half = part.shape[0] // 2
    chunks = inbox.shape[1]
    rows = half // chunks
    sum_send, sum_arrive, share_send, share_arrive = sems

    def spot(side, c):
        return pl.ds(pl.multiple_of(side * half + c * rows, rows), rows)

    def place(side):
        return count - 1 - me if side else me

    def onward(side, c, source):
        target = me - 1 if side else me + 1
        return remote(source, inbox.at[side, c], sum_send.at[side, c], sum_arrive.at[side, c], tp=target)

    def share(side, c):
        target = me + 1 if side else me - 1
        block = whole.at[spot(side, c), :]
        return remote(block, block, share_send.at[side, c], share_arrive.at[side, c], tp=target)

    for side in (0, 1):
        @pl.when(place(side) == 0)
        def _():
            onward(side, 0, part.at[spot(side, 0), :]).start()

    def step(t, carry):
        for side in (0, 1):
            here = place(side)
            c = t - here

            @pl.when((here == 0) & (t + 1 < chunks))
            def _():
                onward(side, t + 1, part.at[spot(side, t + 1), :]).start()

            @pl.when((c >= 0) & (c < chunks) & (here > 0))
            def _():
                onward(side, c, inbox.at[side, c]).wait_recv()
                total = (inbox[side, c].astype(F32) + part[spot(side, c), :].astype(F32)).astype(BF16)

                @pl.when(here < count - 1)
                def _():
                    inbox[side, c] = total
                    onward(side, c, inbox.at[side, c]).start()

                @pl.when(here == count - 1)
                def _():
                    whole[spot(side, c), :] = total
                    share(side, c).start()
                    finish(spot(side, c))

        for side in (0, 1):
            here = place(side)
            c = t - 2 * (count - 1) + here

            @pl.when((c >= 0) & (c < chunks) & (here < count - 1))
            def _():
                share(side, c).wait_recv()

                @pl.when(here > 0)
                def _():
                    share(side, c).start()

                finish(spot(side, c))

        between(t)
        return carry

    lax.fori_loop(0, chunks + 2 * (count - 1), step, 0)

    def drain(c, carry):
        for side in (0, 1):
            here = place(side)

            @pl.when(here < count - 1)
            def _():
                onward(side, c, inbox.at[side, c]).wait_send()

            @pl.when(here > 0)
            def _():
                share(side, c).wait_send()

        return carry

    lax.fori_loop(0, chunks, drain, 0)


def put_split(ref, rows, block):
    core = lax.axis_index("ctx")
    size = block.shape[1] // 8
    for owner in range(4):
        for index in range(2):
            low = (2 * owner + index) * size
            ref[(index + core) % 2, rows, owner * size : (owner + 1) * size] = block[:, low : low + size]


CHUNK = 32
LANES = 128
LINE_COST = pl.CostEstimate(flops=0, bytes_accessed=400_000_000, transcendentals=0)


def enter_kernel(
    tokens, upstream, gain_shard, recur, gelu,
    normed, halves, upstream_halves, gains, scales, whole_in,
    stage_recur, stage_gelu, send, arrive, local, gain_send, gain_arrive,
):
    square = Square()
    greet(False, True)
    width = gain_shard.shape[1]

    def gain_copy(k, owner, target):
        spot = gains.at[:, pl.ds(pl.multiple_of(owner * width, 128), width)]
        return remote(gain_shard, spot, gain_send.at[k], gain_arrive.at[k], fsdp=target)

    others = (*square.near, square.far)
    for k, target in enumerate(others):
        gain_copy(k, square.me, target).start()
    gather = Gather(
        [(recur, whole_in, 0, 0), (gelu, whole_in, 0, recur.shape[1])],
        (stage_recur, stage_gelu), send, arrive, local,
    )
    for w in range(2):
        gather.start(w)
    gains[:, pl.ds(pl.multiple_of(square.me * width, 128), width)] = gain_shard[...]
    for k, owner in enumerate(others):
        gain_copy(k, owner, owner).wait_recv()

    steps = tokens.shape[0] // CHUNK

    def norm(t, carry):
        rows = pl.ds(pl.multiple_of(t * CHUNK, CHUNK), CHUNK)
        block = tokens[rows, :].astype(F32)
        scale = rms_scale(block)
        scales[rows, :] = jnp.broadcast_to(scale, (CHUNK, LANES))
        block = (block * scale * gains[0:1, :]).astype(BF16)
        normed[rows, :] = block
        put_split(halves, rows, block)
        put_split(upstream_halves, rows, upstream[rows, :])
        for w in range(2):
            @pl.when(t == (3 + 3 * w) * steps // 8)
            def _():
                gather.forward(w)

        return carry

    lax.fori_loop(0, steps, norm, 0)
    for w in range(2):
        gather.hand_over(w)
    for w in range(2):
        gather.finish(w)
    for k, target in enumerate(others):
        gain_copy(k, square.me, target).wait_send()


ANY = pl.BlockSpec(memory_space=pl.ANY)
NEAR = pl.BlockSpec(memory_space=pltpu.VMEM)


def gather_scratch(shards):
    count = len(shards)
    dma = pltpu.SemaphoreType.DMA
    return [pltpu.VMEM(w.shape, w.dtype) for w in shards] + [dma((count, 7)), dma((count, 7)), dma((count, 2))]


def enter(tokens, upstream, gain_shard, recur, gelu):
    rows, features = tokens.shape
    shape = jax.ShapeDtypeStruct
    inner = recur.shape[1]
    dma = pltpu.SemaphoreType.DMA
    return pl.pallas_call(
        enter_kernel,
        out_shape=(
            shape((rows, features), BF16),
            shape((2, rows, features // 2), BF16),
            shape((2, rows, features // 2), BF16),
            shape((8, features), F32),
            shape((rows, LANES), F32),
            shape((features, 2 * inner), BF16),
        ),
        in_specs=[NEAR, NEAR, NEAR, ANY, ANY],
        out_specs=[NEAR, NEAR, NEAR, NEAR, NEAR, ANY],
        scratch_shapes=gather_scratch([recur, gelu]) + [dma((3,)), dma((3,))],
        compiler_params=pltpu.CompilerParams(collective_id=1, has_side_effects=True),
        name="enter",
    )(tokens, upstream, gain_shard, recur, gelu)


def line_scratch(rows, features):
    chunks = rows // 2 // CHUNK
    dma = pltpu.SemaphoreType.DMA((2, chunks))
    return [pltpu.VMEM((2, chunks, CHUNK, features), BF16), dma, dma, dma, dma]


class Fetch:
    def __init__(self, sources, targets, sems):
        self.copies = [pltpu.make_async_copy(a, b, sems.at[k]) for k, (a, b) in enumerate(zip(sources, targets))]

    def start(self):
        for copy in self.copies:
            copy.start()

    def wait(self):
        for copy in self.copies:
            copy.wait()


def middle_kernel(gathers, part, far_tokens, gains, *refs):
    *refs, tokens, fetch_sems = refs
    fetch = Fetch((far_tokens,), (tokens,), fetch_sems)
    fetch.start()
    if gathers:
        gate, up, down, merged, normed, halves, whole_in, whole_down = refs[:8]
        inbox, *rest = refs[8:]
        sems, (stage_gate, stage_up, stage_down, send, arrive, local) = rest[:4], rest[4:]
        gather = Gather(
            [(gate, whole_in, 0, 0), (up, whole_in, 0, gate.shape[1]), (down, whole_down, 1, 0)],
            (stage_gate, stage_up, stage_down), send, arrive, local,
        )
        greet(True, True)
        for w in range(3):
            gather.start(w)
    else:
        merged, normed, inbox, *sems = refs
        greet(True, False)

    def finish(rows):
        block = tokens[rows, :].astype(F32) + merged[rows, :].astype(F32)
        block = (block * rms_scale(block) * gains[1:2, :]).astype(BF16)
        normed[rows, :] = block
        if gathers:
            put_split(halves, rows, block)

    def between(t):
        @pl.when(t == 0)
        def _():
            fetch.wait()

        if gathers:
            for w in range(3):
                @pl.when(t == 5 + 4 * w)
                def _():
                    gather.forward(w)

                @pl.when(t == 17 + w)
                def _():
                    gather.hand_over(w)

    line_sum(part, merged, inbox, sems, finish, between)
    if gathers:
        for w in range(3):
            gather.finish(w)


def middle(part, tokens, gains, shards):
    rows, features = tokens.shape
    shape = jax.ShapeDtypeStruct
    whole = shape((rows, features), BF16)
    outs, specs = [whole, whole], [NEAR, NEAR]
    scratch = line_scratch(rows, features)
    if shards:
        gate, up, down = shards
        outs += [
            shape((2, rows, features // 2), BF16),
            shape((features, 2 * gate.shape[1]), BF16),
            shape((down.shape[0], features), BF16),
        ]
        specs += [NEAR, ANY, ANY]
        scratch += gather_scratch(shards)
    scratch += [pltpu.VMEM((rows, features), BF16), pltpu.SemaphoreType.DMA((1,))]
    return pl.pallas_call(
        lambda *refs: middle_kernel(bool(shards), *refs),
        out_shape=tuple(outs),
        in_specs=[NEAR, ANY, NEAR] + [ANY] * len(shards),
        out_specs=specs,
        scratch_shapes=scratch,
        compiler_params=pltpu.CompilerParams(collective_id=2, has_side_effects=True),
        cost_estimate=LINE_COST,
        name="middle",
    )(part, tokens, gains, *shards)


def turn_kernel(split, part, far_tokens, far_merged, far_upstream, gains, own, grad_in, gain_sum, *refs):
    if split:
        halves, *refs = refs
    whole, wide, tokens, merged, upstream, fetch_sems, inbox, *sems = refs
    fetch = Fetch((far_tokens, far_merged, far_upstream), (tokens, merged, upstream), fetch_sems)
    fetch.start()
    greet(True, False)
    gain_sum[...] = jnp.zeros_like(gain_sum)
    width = own.shape[1]
    start = pl.multiple_of(lax.axis_index("tp") * width, 128)

    def finish(rows):
        block = tokens[rows, :].astype(F32) + merged[rows, :].astype(F32)
        scale = rms_scale(block)
        grad = whole[rows, :].astype(F32)
        gain_sum[0:1, :] += jnp.sum(grad * (block * scale), axis=0, keepdims=True)
        grad = grad * gains[1:2, :]
        mean = jnp.mean(block * grad, axis=-1, keepdims=True)
        grad = upstream[rows, :].astype(F32) + scale * grad - block * (scale * scale * scale * mean)
        wide[...] = grad
        own[rows, :] = wide[:, pl.ds(start, width)]
        grad = grad.astype(BF16)
        grad_in[rows, :] = grad
        if split:
            put_split(halves, rows, grad)

    def between(t):
        @pl.when(t == 0)
        def _():
            fetch.wait()

    line_sum(part, whole, inbox, sems, finish, between)


def turn(part, tokens, merged, upstream, gains, split):
    rows, features = tokens.shape
    shape = jax.ShapeDtypeStruct
    outs = [
        shape((rows, features // lax.axis_size("tp")), F32),
        shape((rows, features), BF16),
        shape((8, features), F32),
    ]
    if split:
        outs.append(shape((2, rows, features // 2), BF16))
    return pl.pallas_call(
        lambda *refs: turn_kernel(split, *refs),
        out_shape=tuple(outs),
        in_specs=[NEAR, ANY, ANY, ANY, NEAR],
        out_specs=[NEAR] * len(outs),
        scratch_shapes=[pltpu.VMEM((rows, features), BF16), pltpu.VMEM((CHUNK, features), F32)]
        + [pltpu.VMEM((rows, features), BF16)] * 3
        + [pltpu.SemaphoreType.DMA((3,))]
        + line_scratch(rows, features),
        compiler_params=pltpu.CompilerParams(collective_id=3, has_side_effects=True),
        cost_estimate=LINE_COST,
        name="turn",
    )(part, tokens, merged, upstream, gains)


def rounded_sum(*blocks):
    total = blocks[0].astype(F32)
    for block in blocks[1:]:
        total = total + block.astype(F32)
    return total.astype(BF16)


class Scatter:
    def __init__(self, items, boxes, lasts, send, arrive):
        self.items, self.boxes, self.lasts = items, boxes, lasts
        self.send, self.arrive = send, arrive
        self.square = Square()

    def block(self, w, owner, k):
        part, _, dim = self.items[w]
        size = part.shape[dim] // 4
        if dim == 0:
            low = pl.multiple_of(owner * size + k * (size // 2), 128)
            return part.at[pl.ds(low, size // 2), :]
        half = part.shape[0] // 2
        return part.at[pl.ds(k * half, half), pl.ds(pl.multiple_of(owner * size, 128), size)]

    def spot(self, w, k):
        part, out, dim = self.items[w]
        size = part.shape[dim] // 4
        low = pl.multiple_of(self.square.core * size, 128)
        if dim == 0:
            return out.at[pl.ds(low + k * (size // 2), size // 2), :]
        half = part.shape[0] // 2
        return out.at[pl.ds(k * half, half), pl.ds(low, size)]

    def copy(self, w, k, j):
        square = self.square
        first, second = square.near[k], square.near[1 - k]
        send, arrive = self.send.at[w, 4 * k + j], self.arrive.at[w, 4 * k + j]
        if j < 2:
            owner = square.far if j == 0 else first
            return remote(self.block(w, owner, k), self.boxes[w].at[k, j], send, arrive, fsdp=first)
        if j == 2:
            return remote(self.boxes[w].at[k, 0], self.lasts[w].at[k], send, arrive, fsdp=second)
        return remote(self.spot(w, k), self.spot(w, k), send, arrive, ctx=1 - square.core)

    def start(self, w):
        for j in (0, 1):
            for k in (0, 1):
                self.copy(w, k, j).start()

    def relay(self, w):
        for k in (0, 1):
            self.copy(w, k, 0).wait_recv()
            mine = self.block(w, self.square.near[1 - k], k)
            self.boxes[w][k, 0] = rounded_sum(mine[...], self.boxes[w][k, 0])
            self.copy(w, k, 2).start()

    def finish(self, w):
        for k in (0, 1):
            self.copy(w, k, 1).wait_recv()
            self.copy(w, k, 2).wait_recv()
            mine = self.block(w, self.square.me, k)
            self.spot(w, k)[...] = rounded_sum(mine[...], self.boxes[w][k, 1], self.lasts[w][k])
            self.copy(w, k, 3).start()

    def drain(self, w):
        for k in (0, 1):
            self.copy(w, k, 3).wait_recv()
            for j in range(4):
                self.copy(w, k, j).wait_send()


def scatter_scratch(items):
    blocks = []
    for shape, dim in items:
        rows, cols = (shape[0] // 8, shape[1]) if dim == 0 else (shape[0] // 2, shape[1] // 4)
        blocks.append((rows, cols))
    dma = pltpu.SemaphoreType.DMA((len(items), 8))
    return (
        [pltpu.VMEM((2, 2, *block), BF16) for block in blocks]
        + [pltpu.VMEM((2, *block), BF16) for block in blocks]
        + [dma, dma]
    )


def leave_kernel(
    part_in, gates, sums, norms, stats,
    own_in, gate_sums, row_sums, norm_sums, stat_sums,
    box_in, last_in, send, arrive,
    gate_core, gate_half, gate_near, gate_pair, gate_far, gate_send, gate_arrive,
    core_sums, core_norms, box_sums, box_norms, sum_send, sum_arrive,
    line_norms, line_stats, norm_send, norm_arrive, stat_send, stat_arrive,
):
    square = Square()
    count, place = lax.axis_size("tp"), lax.axis_index("tp")
    core = square.core
    others = (*square.near, square.far)
    greet(False, True, True)

    def norm_copy(k, source):
        box = line_norms.at[source]
        return remote(box, box, norm_send.at[k], norm_arrive.at[source], tp=k)

    def stat_copy(k, source):
        return remote(stats, line_stats.at[source], stat_send.at[k], stat_arrive.at[source], tp=k)

    def core_copy(k):
        source, target = ((sums, core_sums), (norms, core_norms))[k]
        return remote(source, target, sum_send.at[k], sum_arrive.at[k], ctx=1 - core)

    def square_copy(k, j):
        box = (box_sums, box_norms)[k].at[square.me]
        at = 2 + 3 * k + j
        return remote(box, box, sum_send.at[at], sum_arrive.at[at], fsdp=others[j])

    gate_rows = gates.shape[0] // 2
    gate_cols = gates.shape[1] // 2
    my_rows = pl.ds(pl.multiple_of(core * gate_rows, 16), gate_rows)
    your_rows = pl.ds(pl.multiple_of((1 - core) * gate_rows, 16), gate_rows)

    def gate_copy(j):
        send, arrive = gate_send.at[j], gate_arrive.at[j]
        if j == 0:
            return remote(gates.at[your_rows, :], gate_core, send, arrive, ctx=1 - core)
        if j == 5:
            spot = gate_sums.at[my_rows, :]
            return remote(spot, spot, send, arrive, ctx=1 - core)
        k = (j - 1) % 2
        if j < 3:
            return remote(gate_half.at[k], gate_near.at[k], send, arrive, fsdp=square.near[k])
        return remote(gate_pair.at[k], gate_far.at[k], send, arrive, fsdp=square.near[1 - k])

    scatter = Scatter([(part_in, own_in, 0)], (box_in,), (last_in,), send, arrive)
    gate_copy(0).start()
    core_copy(0).start()
    core_copy(1).start()
    scatter.start(0)
    for k in range(count):
        @pl.when(place != k)
        def _():
            stat_copy(k, place).start()

    line_stats[place] = stats[...]
    core_copy(0).wait_recv()
    core_copy(1).wait_recv()
    box_sums[square.me] = sums[...] + core_sums[...]
    box_norms[square.me] = norms[...] + core_norms[...]
    for k in (0, 1):
        for j in range(3):
            square_copy(k, j).start()
    gate_copy(0).wait_recv()
    for k in (0, 1):
        cols = slice(k * gate_cols, (k + 1) * gate_cols)
        gate_half[k] = rounded_sum(gates[my_rows, cols], gate_core[:, cols])
        gate_copy(1 + k).start()
    for k in (0, 1):
        for j in range(3):
            square_copy(k, j).wait_recv()
    row_sums[...] = box_sums[0] + box_sums[1] + box_sums[2] + box_sums[3]
    line_norms[place] = box_norms[0] + box_norms[1] + box_norms[2] + box_norms[3]
    for k in range(count):
        @pl.when(place != k)
        def _():
            norm_copy(k, place).start()

    for k in (0, 1):
        gate_copy(1 + k).wait_recv()
        gate_pair[k] = rounded_sum(gate_half[k], gate_near[k])
        gate_copy(3 + k).start()
    scatter.relay(0)
    for k in (0, 1):
        cols = slice(k * gate_cols, (k + 1) * gate_cols)
        gate_copy(3 + k).wait_recv()
        gate_sums[my_rows, cols] = rounded_sum(gate_pair[k], gate_far[k])
    gate_copy(5).start()
    for k in range(count):
        @pl.when(place != k)
        def _():
            norm_copy(k, k).wait_recv()
            stat_copy(k, k).wait_recv()

    total = line_norms[0]
    stat = line_stats[0]
    for k in range(1, count):
        total = total + line_norms[k]
        stat = stat + line_stats[k]
    norm_sums[...] = total
    stat_sums[...] = stat
    scatter.finish(0)
    scatter.drain(0)
    gate_copy(5).wait_recv()
    for j in range(6):
        gate_copy(j).wait_send()
    for k in (0, 1):
        core_copy(k).wait_send()
        for j in range(3):
            square_copy(k, j).wait_send()
    for k in range(count):
        @pl.when(place != k)
        def _():
            norm_copy(k, place).wait_send()
            stat_copy(k, place).wait_send()


def leave(part_in, gates, sums, norms, stats):
    shape = jax.ShapeDtypeStruct
    count = lax.axis_size("tp")
    dma = pltpu.SemaphoreType.DMA
    height, width = gates.shape[0] // 2, gates.shape[1] // 2
    quarter = pltpu.VMEM((2, height, width), BF16)
    return pl.pallas_call(
        leave_kernel,
        out_shape=(
            shape((part_in.shape[0] // 2, part_in.shape[1]), BF16),
            shape(gates.shape, BF16),
            shape(sums.shape, F32),
            shape(norms.shape, F32),
            shape(stats.shape, F32),
        ),
        in_specs=[NEAR] * 5,
        out_specs=[NEAR] * 5,
        scratch_shapes=(
            scatter_scratch([(part_in.shape, 0)])
            + [pltpu.VMEM((height, 2 * width), BF16), quarter, quarter, quarter, quarter, dma((6,)), dma((6,))]
            + [pltpu.VMEM(sums.shape, F32), pltpu.VMEM(norms.shape, F32)]
            + [pltpu.VMEM((4, *sums.shape), F32), pltpu.VMEM((4, *norms.shape), F32), dma((8,)), dma((8,))]
            + [pltpu.VMEM((count, *norms.shape), F32), pltpu.VMEM((count, *stats.shape), F32)]
            + [dma((count,))] * 4
        ),
        compiler_params=pltpu.CompilerParams(collective_id=4, has_side_effects=True),
        cost_estimate=pl.CostEstimate(flops=0, bytes_accessed=160_000_000, transcendentals=0),
        name="leave",
    )(part_in, gates, sums, norms, stats)


def gelu_pair(q):
    tanh = jnp.tanh(ROOT * (q + CUBE * q * q * q))
    value = 0.5 * q * (1.0 + tanh)
    slope = 0.5 * (1.0 + tanh) + 0.5 * q * (1.0 - tanh * tanh) * ROOT * (1.0 + 3.0 * CUBE * q * q)
    return value, slope


def rms_scale(values):
    return lax.rsqrt(jnp.mean(values * values, axis=-1, keepdims=True) + EPS)


def decay_parts(rate, softer, keep):
    gap = 2.0 * CGAIN * rate * softer
    decay = jnp.exp(-0.5 * gap)
    series = gap * (
        1.0
        - gap / 2.0
        * (1.0 - gap / 3.0 * (1.0 - gap / 4.0 * (1.0 - gap / 5.0 * (1.0 - gap / 6.0 * (1.0 - gap / 7.0)))))
    )
    square = jnp.where(gap < 0.25, series, 1.0 - decay * decay)
    return jnp.where(keep, decay, 0.0), jnp.where(keep, square, 1.0)


def put_lanes(ref, block, rows):
    for lane in range(ref.shape[0]):
        ref[lane, 0:rows, :] = block[:, lane * LANES : (lane + 1) * LANES]


def sweep(decay_ref, value_ref, state_ref, product_ref, out_ref, run_ref, carry_ref, reverse, offset):
    groups, rows, _ = value_ref.shape
    steps = rows // SEGS
    place = lax.broadcasted_iota(jnp.int32, (SEGS, LANES), 0)
    if reverse:
        place = SEGS - 1 - place

    def moved(block, by, fill):
        turned = pltpu.roll(block, SEGS - by if reverse else by, 0)
        return jnp.where(place >= by, turned, fill)

    for lane in range(groups):
        lanes = slice(lane * LANES, (lane + 1) * LANES)
        state = jnp.zeros((SEGS, LANES), F32)
        product = jnp.ones((SEGS, LANES), F32)
        for step in reversed(range(steps)) if reverse else range(steps):
            spot = pl.ds(step, SEGS, stride=steps)
            decay = decay_ref[lane, pl.ds(step + offset, SEGS, stride=steps), :]
            state = decay * state + value_ref[lane, spot, :]
            product = product * decay
            state_ref[lane, spot, :] = state
            product_ref[lane, spot, :] = product
        for by in (1, 2, 4):
            state = state + product * moved(state, by, 0.0)
            product = product * moved(product, by, 1.0)
        carry = carry_ref[0:1, lanes]
        carry_run = carry_ref[8:9, lanes]
        state = state + product * carry
        product = product * carry_run
        enter = moved(state, 1, carry)
        enter_run = moved(product, 1, carry_run)
        for seg in range(SEGS):
            span = slice(seg * steps, (seg + 1) * steps)
            inner = product_ref[lane, span, :]
            out_ref[span, lanes] = state_ref[lane, span, :] + inner * enter[seg : seg + 1, :]
            run_ref[span, lanes] = inner * enter_run[seg : seg + 1, :]
        last = 0 if reverse else SEGS - 1
        carry_ref[0:1, lanes] = state[last : last + 1, :]
        carry_ref[8:9, lanes] = product[last : last + 1, :]


BIAS, RATE, ENTRY, SOFTER = slice(4, 5), slice(5, 6), slice(6, 7), slice(7, 8)


def spread_blocks(blocks_ref, out_ref):
    chans, size = blocks_ref.shape[1:]
    row = lax.broadcasted_iota(jnp.int32, (chans, chans), 0)
    col = lax.broadcasted_iota(jnp.int32, (chans, chans), 1)
    inner = lax.broadcasted_iota(jnp.int32, (size, chans), 0)
    outer = lax.broadcasted_iota(jnp.int32, (size, chans), 1)
    inside = row < 0
    repeat = outer < 0
    for low in range(0, chans, size):
        inside |= (row >= low) & (row < low + size) & (col >= low) & (col < low + size)
        repeat |= outer - low == inner
    repeat = repeat.astype(F32).astype(BF16)
    for gate in range(2):
        wide = jnp.dot(blocks_ref[gate], repeat, preferred_element_type=F32)
        out_ref[:, gate * chans : (gate + 1) * chans] = jnp.where(inside, wide, 0.0).astype(BF16)


def forward_kernel(
    branch_ref, halo_ref, mask_ref, chan_ref, blocks_ref,
    conv_ref, rate_ref, entry_ref, state_ref, run_ref, gates_ref, tail_ref,
    window, decay, value, inner, product, carry,
):
    rows, chans = conv_ref.shape
    spot = pl.program_id(0)

    @pl.when(spot == 0)
    def _():
        spread_blocks(blocks_ref, gates_ref)
        window[0:8, :] = halo_ref[...].astype(F32)
        carry[0:8, :] = jnp.zeros((8, chans), F32)
        carry[8:16, :] = jnp.ones((8, chans), F32)

    @pl.when(spot > 0)
    def _():
        window[0:8, :] = window[rows : rows + 8, :]

    window[8 : rows + 8, :] = branch_ref[...].astype(F32)
    mixed = chan_ref[BIAS, :] + chan_ref[0:1, :] * window[8 : rows + 8, :]
    for shift in range(1, mask_ref.shape[1]):
        moved = window[8 - shift : 8 - shift + rows, :]
        mixed = mixed + chan_ref[shift : shift + 1, :] * (moved * mask_ref[:, shift : shift + 1])
    conv = mixed.astype(BF16)
    conv_ref[...] = conv
    pre = jnp.dot(conv, gates_ref[...], preferred_element_type=F32)
    rate = jax.nn.sigmoid(pre[:, :chans] + chan_ref[RATE, :])
    entry = jax.nn.sigmoid(pre[:, chans:] + chan_ref[ENTRY, :])
    rate_ref[...] = rate
    entry_ref[...] = entry
    keep = jnp.broadcast_to(mask_ref[:, 0:1], (rows, chans)) > 0.5
    step, square = decay_parts(rate, chan_ref[SOFTER, :], keep)
    put_lanes(decay, step, rows)
    put_lanes(value, jnp.sqrt(square) * entry * conv.astype(F32), rows)
    sweep(decay, value, inner, product, state_ref, run_ref, carry, False, 0)
    tail_ref[...] = state_ref[rows - 8 :, :]


def tile_spec(width, count=None):
    if count is None:
        return pl.BlockSpec((TILE, width), lambda i: (i, 0))
    return pl.BlockSpec((TILE, width), lambda i: (count - 1 - i, 0))


def fixed_spec(shape):
    return pl.BlockSpec(shape, lambda i: (0, 0))


def recur_forward(branch, halo, masks, channels, blocks):
    rows, chans = branch.shape[0], halo.shape[1]
    wide = jax.ShapeDtypeStruct((rows, chans), F32)
    return pl.pallas_call(
        forward_kernel,
        grid=(rows // TILE,),
        out_shape=(
            jax.ShapeDtypeStruct((rows, chans), BF16), wide, wide, wide, wide,
            jax.ShapeDtypeStruct((chans, 2 * chans), BF16),
            jax.ShapeDtypeStruct((8, chans), F32),
        ),
        in_specs=[
            tile_spec(chans),
            fixed_spec((8, chans)),
            tile_spec(masks.shape[1]),
            fixed_spec(channels.shape),
            pl.BlockSpec(blocks.shape, lambda i: (0, 0, 0)),
        ],
        out_specs=[tile_spec(chans)] * 5 + [fixed_spec((chans, 2 * chans)), fixed_spec((8, chans))],
        scratch_shapes=[
            pltpu.VMEM((TILE + 8, chans), F32),
            pltpu.VMEM((chans // LANES, TILE, LANES), F32),
            pltpu.VMEM((chans // LANES, TILE, LANES), F32),
            pltpu.VMEM((chans // LANES, TILE, LANES), F32),
            pltpu.VMEM((chans // LANES, TILE, LANES), F32),
            pltpu.VMEM((16, chans), F32),
        ],
        cost_estimate=pl.CostEstimate(
            flops=2 * rows * chans * 2 * chans, bytes_accessed=24 * rows * chans, transcendentals=5 * rows * chans
        ),
        name="recur_forward",
    )(branch, halo, masks, channels, blocks)


def merge_kernel(local_ref, run_ref, enter_ref, pre_ref, *refs):
    *halves, state_ref, gated_ref, part_ref, weight_ref = refs
    core = lax.axis_index("ctx")

    @pl.when(pl.program_id(0) == 0)
    def _():
        if len(halves) == 1:
            weight_ref[...] = halves[0][...]
        else:
            owners, _, size = halves[0].shape
            for owner in range(owners):
                for index, half in ((core, halves[0]), (1 - core, halves[1])):
                    low = pl.multiple_of((2 * owner + index) * size, 128)
                    weight_ref[:, pl.ds(low, size)] = half[owner]

    state = local_ref[...] + run_ref[...] * enter_ref[7:8, :]
    state_ref[...] = state
    pre = pre_ref[...].astype(F32)
    gated = (state * gelu_pair(pre)[0]).astype(BF16)
    gated_ref[...] = gated
    part_ref[...] = jnp.dot(gated, weight_ref[...], preferred_element_type=F32).astype(BF16)


def merge_states(local, run, enter, branches, weights, features):
    rows, chans = local.shape
    shape = jax.ShapeDtypeStruct
    return pl.pallas_call(
        merge_kernel,
        grid=(rows // TILE,),
        out_shape=(
            shape((rows, chans), F32), shape((rows, chans), BF16), shape((rows, features), BF16),
            shape((chans, features), BF16),
        ),
        in_specs=[
            tile_spec(chans), tile_spec(chans), fixed_spec((8, chans)),
            pl.BlockSpec((TILE, chans), lambda i: (i, 1)),
        ]
        + [pl.BlockSpec(w.shape, lambda i, rank=w.ndim: (0,) * rank) for w in weights],
        out_specs=[tile_spec(chans), tile_spec(chans), tile_spec(features), fixed_spec((chans, features))],
        cost_estimate=pl.CostEstimate(
            flops=2 * rows * chans * features, bytes_accessed=16 * rows * chans, transcendentals=rows * chans
        ),
        name="merge_states",
    )(local, run, enter, branches, *weights)


def adjoint_kernel(
    rate_ref, up_ref, pre_ref, state_ref, mask_ref, chan_ref,
    grad_ref, run_ref, head_ref, pre_grad_ref,
    decay, value, inner, product, carry,
):
    rows, chans = rate_ref.shape
    groups = chans // LANES
    spot = pl.program_id(0)

    @pl.when(spot == 0)
    def _():
        for lane in range(groups):
            decay[lane, rows : rows + 8, :] = jnp.ones((8, LANES), F32)
        carry[0:8, :] = jnp.zeros((8, chans), F32)
        carry[8:16, :] = jnp.ones((8, chans), F32)

    @pl.when(spot > 0)
    def _():
        for lane in range(groups):
            decay[lane, rows : rows + 8, :] = decay[lane, 0:8, :]

    keep = jnp.broadcast_to(mask_ref[:, 0:1], (rows, chans)) > 0.5
    gap = CGAIN * rate_ref[...] * chan_ref[SOFTER, :]
    step = jnp.where(keep, jnp.exp(-gap), 0.0)
    put_lanes(decay, step, rows)
    gate, slope = gelu_pair(pre_ref[...].astype(F32))
    up = up_ref[...]
    pre_grad_ref[...] = (up * state_ref[...] * slope).astype(BF16)
    put_lanes(value, up * gate, rows)
    sweep(decay, value, inner, product, grad_ref, run_ref, carry, True, 1)
    head_ref[...] = jnp.broadcast_to(step[0:1, :] * carry[0:1, :], (8, chans))


def recur_adjoint(rate, up, branches, state, masks, channels):
    rows, chans = rate.shape
    count = rows // TILE
    wide = jax.ShapeDtypeStruct((rows, chans), F32)
    return pl.pallas_call(
        adjoint_kernel,
        grid=(count,),
        out_shape=(
            wide, wide, jax.ShapeDtypeStruct((8, chans), F32), jax.ShapeDtypeStruct((rows, chans), BF16)
        ),
        in_specs=[
            tile_spec(chans, count),
            tile_spec(chans, count),
            pl.BlockSpec((TILE, chans), lambda i: (count - 1 - i, 1)),
            tile_spec(chans, count),
            tile_spec(masks.shape[1], count),
            fixed_spec(channels.shape),
        ],
        out_specs=[tile_spec(chans, count), tile_spec(chans, count), fixed_spec((8, chans)), tile_spec(chans, count)],
        scratch_shapes=[
            pltpu.VMEM((chans // LANES, TILE + 8, LANES), F32),
            pltpu.VMEM((chans // LANES, TILE, LANES), F32),
            pltpu.VMEM((chans // LANES, TILE, LANES), F32),
            pltpu.VMEM((chans // LANES, TILE, LANES), F32),
            pltpu.VMEM((16, chans), F32),
        ],
        cost_estimate=pl.CostEstimate(
            flops=8 * rows * chans, bytes_accessed=16 * rows * chans, transcendentals=rows * chans
        ),
        name="recur_adjoint",
    )(rate, up, branches, state, masks, channels)


def backward_kernel(
    grad_ref, run_ref, enter_ref, rate_ref, entry_ref, conv_ref, state_ref, mask_ref,
    branch_ref, pre_grad_ref, halo_ref, chan_ref, gates_ref,
    back_ref, tail_ref, head_ref, gate_grad_ref, sums_ref,
    shifts, edge,
):
    rows, chans = conv_ref.shape
    width = mask_ref.shape[1]
    spot = pl.program_id(0)
    last = pl.num_programs(0) - 1

    @pl.when(spot == 0)
    def _():
        for shift in range(1, width):
            shifts[shift - 1, rows : rows + 8, :] = jnp.zeros((8, chans), F32)
        gate_grad_ref[...] = jnp.zeros_like(gate_grad_ref)
        sums_ref[...] = jnp.zeros_like(sums_ref)

    @pl.when(spot > 0)
    def _():
        for shift in range(1, width):
            shifts[shift - 1, rows : rows + 8, :] = shifts[shift - 1, 0:8, :]

    keep = jnp.broadcast_to(mask_ref[:, 0:1], (rows, chans)) > 0.5
    softer = chan_ref[SOFTER, :]
    rate = rate_ref[...]
    entry = entry_ref[...]
    conv = conv_ref[...].astype(F32)
    grad = grad_ref[...] + run_ref[...] * enter_ref[0:1, :]
    step, square = decay_parts(rate, softer, keep)
    inverse = lax.rsqrt(square)
    mult = square * inverse
    driven = entry * conv
    carried = state_ref[...] - mult * driven
    d_log = jnp.where(keep, grad * (carried - driven * step * step * inverse), 0.0)
    d_rate = (-CGAIN * softer * d_log * rate * (1.0 - rate)).astype(BF16)
    lifted = grad * mult * entry
    d_entry = (lifted * conv * (1.0 - entry)).astype(BF16)
    both = jnp.concatenate([d_rate, d_entry], axis=1)
    d_conv = lifted + lax.dot_general(
        both, gates_ref[...], (((1,), (1,)), ((), ())), preferred_element_type=F32
    )
    gate_grad_ref[...] += lax.dot_general(
        conv_ref[...], both, (((0,), (0,)), ((), ())), preferred_element_type=F32
    )

    def add_row(row, block):
        sums_ref[row : row + 1, :] += jnp.sum(block, axis=0, keepdims=True)

    branch = branch_ref[...].astype(F32)
    add_row(0, d_log * rate)
    add_row(1, d_rate.astype(F32))
    add_row(2, d_entry.astype(F32))
    add_row(3, d_conv)
    add_row(4, d_conv * branch)
    back = chan_ref[0:1, :] * d_conv
    for shift in range(1, width):
        shifts[shift - 1, 0:rows, :] = d_conv * mask_ref[:, shift : shift + 1]
        moved = shifts[shift - 1, shift : shift + rows, :]
        add_row(4 + shift, moved * branch)
        back = back + chan_ref[shift : shift + 1, :] * moved
    back_ref[:, 0:chans] = back.astype(BF16)
    back_ref[:, chans:] = pre_grad_ref[...]

    @pl.when(spot == 0)
    def _():
        tail_ref[...] = back[rows - 8 :, :]

    @pl.when(spot == last)
    def _():
        halo = halo_ref[...].astype(F32)
        head = jnp.zeros((8, chans), F32)
        edge[0:8, :] = head
        for shift in range(1, width):
            edge[8:16, :] = shifts[shift - 1, 0:8, :]
            moved = edge[shift : shift + 8, :]
            add_row(4 + shift, moved * halo)
            head = head + chan_ref[shift : shift + 1, :] * moved
        head_ref[...] = head


def recur_backward(grad, run, enter, rate, entry, conv, state, masks, branch, pre_grad, halo, channels, gates):
    rows, chans = rate.shape
    count = rows // TILE
    edge = jax.ShapeDtypeStruct((8, chans), F32)
    wide = tile_spec(chans, count)
    return pl.pallas_call(
        backward_kernel,
        grid=(count,),
        out_shape=(
            jax.ShapeDtypeStruct((rows, 2 * chans), BF16),
            edge,
            edge,
            jax.ShapeDtypeStruct((chans, 2 * chans), F32),
            jax.ShapeDtypeStruct((8, chans), F32),
        ),
        in_specs=[
            wide, wide, fixed_spec((8, chans)), wide, wide, wide, wide,
            tile_spec(masks.shape[1], count),
            wide,
            wide,
            fixed_spec((8, chans)),
            fixed_spec(channels.shape),
            fixed_spec(gates.shape),
        ],
        out_specs=[
            tile_spec(2 * chans, count),
            fixed_spec((8, chans)),
            fixed_spec((8, chans)),
            fixed_spec((chans, 2 * chans)),
            fixed_spec((8, chans)),
        ],
        scratch_shapes=[
            pltpu.VMEM((masks.shape[1] - 1, TILE + 8, chans), F32),
            pltpu.VMEM((16, chans), F32),
        ],
        cost_estimate=pl.CostEstimate(
            flops=8 * rows * chans * chans, bytes_accessed=28 * rows * chans, transcendentals=2 * rows * chans
        ),
        name="recur_backward",
    )(grad, run, enter, rate, entry, conv, state, masks, branch, pre_grad, halo, channels, gates)


def shards(
    tokens,
    segments,
    cotangent,
    w_recur,
    w_gelu,
    w_merge,
    w_gate,
    w_up,
    w_down,
    norm_mix,
    norm_feed,
    conv_taps,
    conv_bias,
    rate_gate,
    entry_gate,
    rate_bias,
    entry_bias,
    decay_logit,
):
    piece = tokens.shape[0]
    width = conv_taps.shape[0]
    edge = width - 1
    heads, block = rate_gate.shape[0], rate_gate.shape[1]
    chans = conv_taps.shape[1]
    features = tokens.shape[1]
    feat_local = features // lax.axis_size("tp")
    feat_start = lax.axis_index("tp") * feat_local

    def own(block):
        return lax.dynamic_slice_in_dim(block, feat_start, feat_local, 1)

    square = lax.axis_size("fsdp") == 4
    gain_shard = jnp.concatenate(
        [jnp.stack([norm_mix, norm_feed]).astype(F32), jnp.zeros((6, norm_mix.shape[0]), F32)], axis=0
    )
    if square:
        half = w_merge.shape[1] // 2
        half_shard = lax.dynamic_slice_in_dim(w_merge, lax.axis_index("ctx") * half, half, 1)
        normed, normed_split, cotangent_split, gains, scales, whole_in = enter(
            tokens, cotangent, gain_shard, w_recur, w_gelu
        )
        merge_mine = lax.all_gather(after(half_shard, normed), "fsdp", axis=0)
    else:
        whole_in = gather_halves(jnp.concatenate([w_recur, w_gelu], axis=1), 0)
        whole_merge = gather_halves(w_merge, 1)
        gains = lax.all_gather(gain_shard, "fsdp", axis=1, tiled=True)
        inputs = tokens.astype(F32)
        normed = (inputs * rms_scale(inputs) * gains[0:1]).astype(BF16)
        normed_split = split_features(normed)
        cotangent_split = split_features(cotangent)
        scales = rms_scale(inputs)
    gain_one = gains[0:1]

    padded_ids = jnp.concatenate([jnp.full((edge,), -1, jnp.int32), segments])
    local_ids = lax.dynamic_slice_in_dim(padded_ids, lax.axis_index("ctx") * piece, piece + edge)
    own_ids = local_ids[edge:]
    masks = jnp.stack(
        [(local_ids[edge - max(shift, 1) : edge - max(shift, 1) + piece] == own_ids) for shift in range(width)],
        axis=1,
    ).astype(F32)
    blocks = jnp.stack([rate_gate.reshape(chans, block), entry_gate.reshape(chans, block)])
    channels = jnp.concatenate(
        [conv_taps.astype(F32)]
        + [row.astype(F32)[None, :] for row in (conv_bias, rate_bias, entry_bias, jax.nn.softplus(-decay_logit))]
    )

    rows_to_features = (((1,), (1,)), ((), ()))
    branches = jnp.dot(normed, whole_in, preferred_element_type=F32).astype(BF16)
    halo = shifted(branches[piece - 8 :, :chans], "ctx", 1)
    conv, rate, entry, local_state, run, gates, state_tail = recur_forward(branches, halo, masks, channels, blocks)
    state_in = shifted(state_tail, "ctx", 1)
    merge_weights = (merge_mine, swap_cores(after(merge_mine, conv))) if square else (whole_merge,)
    states, gated, part_merge, whole_merge = merge_states(
        local_state, run, state_in, branches, merge_weights, features
    )

    if square:
        merged, normed_two, normed_two_split, whole_mid, whole_down = middle(
            part_merge, tokens, gains, (w_gate, w_up, w_down)
        )
    else:
        merged, normed_two = middle(part_merge, tokens, gains, ())
        normed_two_split = split_features(normed_two)
        whole_mid = gather_halves(jnp.concatenate([w_gate, w_up], axis=1), 0)
        whole_down = gather_halves(w_down, 1)

    units = w_gate.shape[1]
    pre_mid = jnp.dot(normed_two, whole_mid, preferred_element_type=F32).astype(BF16)
    gate_act = gelu_pair(pre_mid[:, :units].astype(F32))[0]
    hidden = (gate_act * pre_mid[:, units:].astype(F32)).astype(BF16)
    part_feed = jnp.dot(hidden, whole_down, preferred_element_type=F32).astype(BF16)
    feed = lax.psum_scatter(part_feed, "tp", scatter_dimension=1, tiled=True)
    hidden, pre_mid, whole_mid, late_cotangent, normed_two_split = after(
        (hidden, pre_mid, whole_mid, cotangent, normed_two_split), part_feed
    )
    d_hidden = lax.dot_general(late_cotangent, whole_down, rows_to_features, preferred_element_type=F32).astype(BF16)
    gate_act, gate_slope = gelu_pair(pre_mid[:, :units].astype(F32))
    up_vals = pre_mid[:, units:].astype(F32)
    wide_hidden = d_hidden.astype(F32)
    d_mid = jnp.concatenate(
        [(wide_hidden * up_vals * gate_slope).astype(BF16), (wide_hidden * gate_act).astype(BF16)], axis=1
    )
    part_two = lax.dot_general(d_mid, whole_mid, rows_to_features, preferred_element_type=F32).astype(BF16)
    pair_down = pair_sums(cotangent_split, hidden, 1)
    pair_mid = pair_sums(normed_two_split, d_mid, 0, part_two)
    part_two = after(part_two, pair_down, pair_mid)
    turned = turn(part_two, tokens, merged, cotangent, gains, square)
    own_resid_grad, d_merge_in, feed_sums = turned[:3]
    d_merge_split = turned[3] if square else split_features(d_merge_in)
    half_down = half_to_owners(pair_down, 1)
    half_mid = half_to_owners(pair_mid, 0)
    d_merge_in, d_merge_split = after((d_merge_in, d_merge_split), feed)

    shard_down = both_halves(half_down, 1)
    pair_merge = pair_sums(d_merge_split, gated, 1)
    half_merge = half_to_owners(pair_merge, 1)
    d_gated = lax.dot_general(d_merge_in, whole_merge, rows_to_features, preferred_element_type=F32)
    local_grad, grad_run, first, d_gelu_pre = recur_adjoint(after(rate, half_down), d_gated, branches, states, masks, channels)
    grad_in = shifted(first, "ctx", -1)
    back, tail, head, gate_grads, sums = recur_backward(
        local_grad, grad_run, grad_in, rate, after(entry, half_mid, shard_down, pair_merge), conv, states, masks, branches, d_gelu_pre,
        halo, channels, gates
    )
    returned = shifted(head, "ctx", -1)
    d_in = lax.dynamic_update_slice(back, (tail + returned).astype(BF16), (piece - 8, 0))
    part_one = lax.dot_general(d_in, whole_in, rows_to_features, preferred_element_type=F32).astype(BF16)
    part_one = after(part_one, half_merge)
    d_normed = lax.psum_scatter(part_one, "tp", scatter_dimension=1, tiled=True)

    pair_in = pair_sums(normed_split, after(d_in, part_one), 0)
    inputs = tokens.astype(F32)
    scale_one = scales[:, :1]
    wide_part = part_one.astype(F32)
    stat_one = jnp.sum(wide_part * inputs * gain_one, axis=-1)
    grad_mix = jnp.sum(wide_part * inputs * scale_one, axis=0)
    norm_sums = jnp.stack([grad_mix, feed_sums[0] / lax.axis_size("tp")])
    spread = jnp.arange(2 * chans)[None, :] % chans // block
    diagonal = sum(jnp.where(spread == i, gate_grads[i * block : (i + 1) * block], 0.0) for i in range(heads))
    diagonal = diagonal.astype(BF16)
    if square:
        own_in, gate_sums, row_sums, both_norms, line_stats = leave(
            pair_in, diagonal, sums, norm_sums.reshape(-1, 128), stat_one.reshape(-1, 128)
        )
        shard_in = own_in
        both_norms = both_norms.reshape(2, features)
        stat_one = line_stats.reshape(-1)
    else:
        shard_in = both_halves(half_to_owners(pair_in, 0), 0)
        gate_sums = lax.psum(diagonal, ("fsdp", "ctx"))
        row_sums = lax.psum(sums, ("fsdp", "ctx"))
        both_norms = lax.psum(norm_sums, ("fsdp", "ctx", "tp"))
        stat_one = lax.psum(stat_one, "tp")
    stat_one = stat_one[:, None] / features
    shard_mid = both_halves(half_mid, 0)
    shard_merge = both_halves(half_merge, 1)
    gate_sums = gate_sums.astype(F32).reshape(block, 2, heads, block).transpose(1, 2, 0, 3)

    own_inputs = own(tokens).astype(F32)
    output = (own_inputs + own(merged).astype(F32) + feed.astype(F32)).astype(BF16)
    grad_tokens = (
        own_resid_grad
        + scale_one * d_normed.astype(F32) * own(gain_one)
        - own_inputs * scale_one**3 * stat_one
    ).astype(BF16)

    norm_local = norm_mix.shape[0]
    own_norms = lax.dynamic_slice_in_dim(both_norms, lax.axis_index("fsdp") * norm_local, norm_local, 1)

    return (
        output,
        grad_tokens,
        shard_in[:, :chans].astype(F32),
        shard_in[:, chans:].astype(F32),
        shard_merge,
        shard_mid[:, :units].astype(F32),
        shard_mid[:, units:].astype(F32),
        shard_down,
        own_norms[0],
        own_norms[1],
        row_sums[4 : 4 + width],
        row_sums[3],
        gate_sums[0],
        gate_sums[1],
        row_sums[1],
        row_sums[2],
        CGAIN * row_sums[0] * jax.nn.sigmoid(-decay_logit),
    )


def solution(mesh):
    placed = (
        P(("fsdp", "ctx"), None),
        P("fsdp"),
        P(("fsdp", "ctx"), None),
        P("fsdp", "tp"),
        P("fsdp", "tp"),
        P("tp", "fsdp"),
        P("fsdp", "tp"),
        P("fsdp", "tp"),
        P("tp", "fsdp"),
        P("fsdp"),
        P("fsdp"),
        P(None, "tp"),
        P("tp"),
        P("tp", None, None),
        P("tp", None, None),
        P("tp"),
        P("tp"),
        P("tp"),
    )
    return jax.shard_map(
        shards,
        mesh=mesh,
        in_specs=placed,
        out_specs=(
            P(("fsdp", "ctx"), "tp"),
            P(("fsdp", "ctx"), "tp"),
            P("fsdp", "tp"),
            P("fsdp", "tp"),
            P("tp", "fsdp"),
            P("fsdp", "tp"),
            P("fsdp", "tp"),
            P("tp", "fsdp"),
            P("fsdp"),
            P("fsdp"),
            P(None, "tp"),
            P("tp"),
            P("tp", None, None),
            P("tp", None, None),
            P("tp"),
            P("tp"),
            P("tp"),
        ),
        check_vma=False,
    )
```
